32 devices in a mesh: utt: 2 (over y), seq: 16 (over z, x, core).
Axes of the slice: x: 2, y: 2, z: 4, core: 2. Of those that a mesh axis runs over, the one named last changes fastest.
Arguments:
- frames: bfloat16 [4, 1024, 1024], P('utt', 'seq'), may hold values from -8 to 8
- codes: int32 [4, 1024, 3], P('utt', 'seq'), may hold values from 0 to 1023
- lengths: int32 [4], P('utt'), may hold values from 256 to 1024, as said below
- frame_mask: int32 [4, 1024], P('utt', 'seq'), may hold values 0 or 1
- table: bfloat16 [3072, 1024], replicated, may hold values from -6 to 6
- glob_norm_one: float32 [1024], replicated, may hold values from 0.1 to 1.9
- glob_w_query: bfloat16 [1024, 1024], replicated, may hold values from -0.1875 to 0.1875
- glob_w_key: bfloat16 [1024, 1024], replicated, may hold values from -0.1875 to 0.1875
- glob_w_value: bfloat16 [1024, 1024], replicated, may hold values from -0.1875 to 0.1875
- glob_w_output: bfloat16 [1024, 1024], replicated, may hold values from -0.75 to 0.75
- glob_norm_two: float32 [1024], replicated, may hold values from 0.1 to 1.9
- glob_w_up: bfloat16 [1024, 4096], replicated, may hold values from -0.1875 to 0.1875
- glob_b_up: float32 [4096], replicated, may hold values from -3 to 3
- glob_w_down: bfloat16 [4096, 1024], replicated, may hold values from -0.09375 to 0.09375
- glob_b_down: float32 [1024], replicated, may hold values from -1.75 to 1.75
- local_norm_one: float32 [1024], replicated, may hold values from 0.1 to 1.9
- local_w_query: bfloat16 [1024, 1024], replicated, may hold values from -0.1875 to 0.1875
- local_w_key: bfloat16 [1024, 1024], replicated, may hold values from -0.1875 to 0.1875
- local_w_value: bfloat16 [1024, 1024], replicated, may hold values from -0.1875 to 0.1875
- local_w_output: bfloat16 [1024, 1024], replicated, may hold values from -0.25 to 0.25
- local_norm_two: float32 [1024], replicated, may hold values from 0.1 to 1.9
- local_w_up: bfloat16 [1024, 4096], replicated, may hold values from -0.1875 to 0.1875
- local_b_up: float32 [4096], replicated, may hold values from -3 to 3
- local_w_down: bfloat16 [4096, 1024], replicated, may hold values from -0.09375 to 0.09375
- local_b_down: float32 [1024], replicated, may hold values from -1.75 to 1.75
- cotan_global: bfloat16 [4, 1024, 1024], P('utt', 'seq'), may hold values from -8 to 8
- cotan_local: bfloat16 [4, 1024, 4, 1024], P('utt', 'seq'), may hold values from -8 to 8
Outputs:
- global_out: bfloat16 [4, 1024, 1024], P('utt', 'seq')
- local_out: bfloat16 [4, 1024, 4, 1024], P('utt', 'seq')
- grad_frames: float32 [4, 1024, 1024], P('utt', 'seq')
- grad_table: float32 [3072, 1024], P('seq')
- grad_glob_norm_one: float32 [1024], P('seq')
- grad_glob_w_query: float32 [1024, 1024], P('seq')
- grad_glob_w_key: float32 [1024, 1024], P('seq')
- grad_glob_w_value: float32 [1024, 1024], P('seq')
- grad_glob_w_output: float32 [1024, 1024], P('seq')
- grad_glob_norm_two: float32 [1024], P('seq')
- grad_glob_w_up: float32 [1024, 4096], P('seq')
- grad_glob_b_up: float32 [4096], P('seq')
- grad_glob_w_down: float32 [4096, 1024], P('seq')
- grad_glob_b_down: float32 [1024], P('seq')
- grad_local_norm_one: float32 [1024], P('seq')
- grad_local_w_query: float32 [1024, 1024], P('seq')
- grad_local_w_key: float32 [1024, 1024], P('seq')
- grad_local_w_value: float32 [1024, 1024], P('seq')
- grad_local_w_output: float32 [1024, 1024], P('seq')
- grad_local_norm_two: float32 [1024], P('seq')
- grad_local_w_up: float32 [1024, 4096], P('seq')
- grad_local_b_up: float32 [4096], P('seq')
- grad_local_w_down: float32 [4096, 1024], P('seq')
- grad_local_b_down: float32 [1024], P('seq')
The draws below stay inside these ranges and needn't reach their ends.
Inputs may be any that keep to these rules, and one draw needn't show every extreme that they name: `lengths`: in each aligned group of 2 utterances (those of one index of utt) exactly one, drawn from the seed, has 1024 valid frames; the others have 1024 // 4 or more.
All inputs are finite; a program needn't handle non-finite values. No bound on the sum of `frame_mask` on one device may be relied on, other than what follows from the above.
Results may differ from the reference program's by a relative error of at most 0.025.
Values may be sent and summed in bfloat16 or wider, within the bound.
A program may use at most 384 MiB of HBM per device.

```python
import jax
import jax.numpy as jnp
from jax import lax

D = 1024
H = 16
HD = 64
FF = 4096
CB = 3
VOCAB = 1024
UTT_DEV = 2
LOCAL = 4
UTTS = 4
MAXLEN = 1024


def draw_lengths(key, part):
    base_key, pick_key = jax.random.split(jax.random.fold_in(key, 11))
    drawn = jax.random.randint(base_key, (UTTS,), MAXLEN // 4, MAXLEN + 1, dtype=jnp.int32)
    chosen = jax.random.randint(pick_key, (UTTS // UTT_DEV,), 0, UTT_DEV, dtype=jnp.int32)
    places = jnp.arange(UTTS, dtype=jnp.int32)
    groups = places // UTT_DEV
    within = places % UTT_DEV
    return jnp.where(within == chosen[groups], MAXLEN, drawn).astype(jnp.int32)


def set_ends(array, stream_key, least, largest):
    shape = array.shape
    spot = [jax.random.randint(jax.random.fold_in(stream_key, axis), (), 0, shape[axis]) for axis in range(len(shape))]
    array = array.at[tuple(spot)].set(least)
    longest = shape.index(max(shape))
    spot[longest] = (spot[longest] + 1) % shape[longest]
    return array.at[tuple(spot)].set(largest)


def spiked(entries, key, source, target, blocks, factor):
    def block_of(axis_at):
        return (jnp.arange(entries.shape[axis_at]) // (entries.shape[axis_at] // blocks)).reshape((-1,) + (1,) * (entries.ndim - 1 - axis_at))

    one_side = jax.random.permutation(key, blocks)[block_of(target)]
    far = (block_of(target) + blocks // 2) % blocks
    return jnp.where((block_of(source) == one_side) | (block_of(source) == far), factor * entries, entries)


def levels(rng, dims, cuts, smallest, largest):
    gain, own = 1.0, jax.random.fold_in(rng, 6)
    for position, parts in cuts:
        heights = jnp.exp(jax.random.uniform(jax.random.fold_in(own, position), (parts,), jnp.float32, smallest / len(cuts), largest / len(cuts)))
        gain = gain * jnp.repeat(heights, dims[position] // parts).reshape([-1 if axis == position else 1 for axis in range(len(dims))])
    return gain


def centred(stream_key, dims, scale, reach, cuts=(), kind=jnp.bfloat16):
    entries = jax.random.normal(stream_key, dims, jnp.float32) * scale
    if len(cuts) > 0:
        entries = levels(stream_key, dims, cuts, -0.22, 0.18) * entries
    return jnp.clip(entries, min=-reach, max=reach).astype(kind)


def gaussian_with(key, shape, scale, most, shards, heavy, kind=jnp.bfloat16):
    values = scale * jax.random.normal(key, shape, jnp.float32)
    if shards:
        values = values * levels(key, shape, shards, -0.22, 0.18)
    return jnp.clip(spiked(values, jax.random.fold_in(key, 3), *heavy), -most, most).astype(kind)


def setup_inputs(seed: int = 0) -> dict:
    seeds = jax.random.split(jax.random.key(seed), 28)
    frames = gaussian_with(seeds[0], (UTTS, MAXLEN, D), 1.0, 8.0, ((0, 2), (1, 16)), (1, 2, 16, 2.0))
    codes = set_ends(jax.random.randint(seeds[1], (UTTS, MAXLEN, CB), 0, VOCAB), jax.random.fold_in(seeds[1], 1), 0, VOCAB - 1).astype(jnp.int32)
    lengths = draw_lengths(jax.random.fold_in(seeds[27], 71), 0)
    frame_mask = set_ends((jax.random.randint(seeds[3], (UTTS, MAXLEN), 0, 8) < 7).astype(jnp.int32), jax.random.fold_in(seeds[3], 1), 0, 1)
    table = centred(seeds[4], (CB * VOCAB, D), 1.0, 6.0)
    glob_norm_one = jnp.clip(1.0 + 0.18 * jax.random.normal(seeds[5], (D,), jnp.float32), 0.1, 1.9)
    glob_w_query = centred(seeds[6], (D, D), D ** -0.5, 0.1875)
    glob_w_key = centred(seeds[7], (D, D), D ** -0.5, 0.1875)
    glob_w_value = centred(seeds[8], (D, D), D ** -0.5, 0.1875)
    glob_w_output = centred(seeds[9], (D, D), (D // 16) ** -0.5, 0.75)
    glob_norm_two = jnp.clip(1.0 + 0.18 * jax.random.normal(seeds[10], (D,), jnp.float32), 0.1, 1.9)
    glob_w_up = centred(seeds[11], (D, FF), D ** -0.5, 0.1875)
    glob_b_up = centred(seeds[12], (FF,), 0.5, 3.0, (), jnp.float32)
    glob_w_down = centred(seeds[13], (FF, D), FF ** -0.5, 0.09375)
    glob_b_down = centred(seeds[14], (D,), 0.3, 1.75, (), jnp.float32)
    local_norm_one = jnp.clip(1.0 + 0.18 * jax.random.normal(seeds[15], (D,), jnp.float32), 0.1, 1.9)
    local_w_query = centred(seeds[16], (D, D), D ** -0.5, 0.1875)
    local_w_key = centred(seeds[17], (D, D), D ** -0.5, 0.1875)
    local_w_value = centred(seeds[18], (D, D), D ** -0.5, 0.1875)
    local_w_output = centred(seeds[19], (D, D), (D // 2) ** -0.5, 0.25)
    local_norm_two = jnp.clip(1.0 + 0.18 * jax.random.normal(seeds[20], (D,), jnp.float32), 0.1, 1.9)
    local_w_up = centred(seeds[21], (D, FF), D ** -0.5, 0.1875)
    local_b_up = centred(seeds[22], (FF,), 0.5, 3.0, (), jnp.float32)
    local_w_down = centred(seeds[23], (FF, D), FF ** -0.5, 0.09375)
    local_b_down = centred(seeds[24], (D,), 0.3, 1.75, (), jnp.float32)
    cotan_global = gaussian_with(seeds[25], (UTTS, MAXLEN, D), 1.0, 8.0, ((0, 2), (1, 16)), (1, 2, 16, 2.0))
    cotan_local = gaussian_with(seeds[26], (UTTS, MAXLEN, LOCAL, D), 1.0, 8.0, ((0, 2), (1, 16)), (1, 3, 16, 2.0))
    return {"frames": frames, "codes": codes, "lengths": lengths, "frame_mask": frame_mask, "table": table, "glob_norm_one": glob_norm_one, "glob_w_query": glob_w_query, "glob_w_key": glob_w_key, "glob_w_value": glob_w_value, "glob_w_output": glob_w_output, "glob_norm_two": glob_norm_two, "glob_w_up": glob_w_up, "glob_b_up": glob_b_up, "glob_w_down": glob_w_down, "glob_b_down": glob_b_down, "local_norm_one": local_norm_one, "local_w_query": local_w_query, "local_w_key": local_w_key, "local_w_value": local_w_value, "local_w_output": local_w_output, "local_norm_two": local_norm_two, "local_w_up": local_w_up, "local_b_up": local_b_up, "local_w_down": local_w_down, "local_b_down": local_b_down, "cotan_global": cotan_global, "cotan_local": cotan_local}


EPSILON = 1e-05
NEGATIVE = -1e+30

@jax.custom_vjp
def low(v):
    return lax.optimization_barrier(v.astype(jnp.bfloat16)).astype(jnp.float32)

@jax.custom_vjp
def low_back(v):
    return v

def low_keep(v):
    return (low(v), None)

def low_pass(kept, grad):
    return (grad,)

def back_keep(v):
    return (v, None)

def back_low(kept, grad):
    return (low(grad),)
low.defvjp(low_keep, low_pass)
low_back.defvjp(back_keep, back_low)

def highest(left_side, right_side):
    return jnp.dot(left_side, right_side, precision=lax.Precision.HIGHEST, preferred_element_type=jnp.float32)

def normalize(values, gain_vec):
    return values * lax.rsqrt(lax.optimization_barrier(jnp.mean(values * values, axis=-1, keepdims=True)) + EPSILON) * gain_vec

def softmax_rows(scores):
    row_peak = lax.optimization_barrier(jnp.max(scores, axis=-1, keepdims=True))
    raised = jnp.exp(scores - row_peak)
    return raised / lax.optimization_barrier(jnp.sum(raised, axis=-1, keepdims=True))

def layer_block(inputs, params, attend):
    norm_one, w_query, w_key, w_value, w_output, norm_two, w_up, b_up, w_down, b_down = params
    normed = low(normalize(inputs, norm_one))
    queries = low(low_back(highest(normed, w_query)))
    key_rows = low(low_back(highest(normed, w_key)))
    value_rows = low(low_back(highest(normed, w_value)))
    mixed_rows = low(low_back(attend(queries, key_rows, value_rows)))
    middle = inputs + low_back(highest(mixed_rows, w_output))
    middle_norm = low(normalize(middle, norm_two))
    pre_active = low_back(highest(middle_norm, w_up) + b_up)
    active = low(jax.nn.gelu(pre_active, approximate=True))
    return middle + low_back(highest(active, w_down) + b_down)

def global_attend(usable):

    def attend(queries, key_rows, value_rows):
        head_q = queries.reshape(MAXLEN, H, HD)
        head_k = key_rows.reshape(MAXLEN, H, HD)
        head_v = value_rows.reshape(MAXLEN, H, HD)
        block_rows = min(512, MAXLEN)

        def one_block(offset):
            part = lax.dynamic_slice_in_dim(head_q, offset, block_rows, 0)
            scores = low_back(jnp.einsum('qhd,khd->hqk', part, head_k, precision=lax.Precision.HIGHEST) * HD ** (-0.5))
            row_ids = offset + jnp.arange(block_rows, dtype=jnp.int32)
            col_ids = jnp.arange(MAXLEN, dtype=jnp.int32)
            allowed = (col_ids[None, :] <= row_ids[:, None]) & ((usable[None, :] > 0) | (col_ids[None, :] == row_ids[:, None]))
            weights = softmax_rows(jnp.where(allowed[None], scores, NEGATIVE))
            return jnp.einsum('hqk,khd->qhd', low(weights), head_v, precision=lax.Precision.HIGHEST)
        starts = jnp.arange(MAXLEN // block_rows, dtype=jnp.int32) * block_rows
        return lax.map(jax.checkpoint(one_block), starts).reshape(MAXLEN, H * HD)
    return attend

def local_attend(queries, key_rows, value_rows):
    head_q = queries.reshape(MAXLEN, LOCAL, H, HD)
    head_k = key_rows.reshape(MAXLEN, LOCAL, H, HD)
    head_v = value_rows.reshape(MAXLEN, LOCAL, H, HD)
    scores = low_back(jnp.einsum('nihd,njhd->nhij', head_q, head_k, precision=lax.Precision.HIGHEST) * HD ** (-0.5))
    lower = jnp.arange(LOCAL, dtype=jnp.int32)[:, None] >= jnp.arange(LOCAL, dtype=jnp.int32)[None, :]
    weights = softmax_rows(jnp.where(lower, scores, NEGATIVE))
    mixed_rows = jnp.einsum('nhij,njhd->nihd', low(weights), head_v, precision=lax.Precision.HIGHEST)
    return mixed_rows.reshape(MAXLEN * LOCAL, H * HD)

def utterance(item, table_f, glob_params, local_params):
    inputs, code_ids, length, usable = item
    frame_ids = jnp.arange(MAXLEN, dtype=jnp.int32)
    valid = (frame_ids < length)[:, None]
    result = layer_block(inputs, glob_params, global_attend(usable))
    global_rows = low(jnp.where(valid, result, 0.0))
    table_ids = code_ids + VOCAB * jnp.arange(CB, dtype=jnp.int32)[None, :]
    embedded = jnp.take(table_f, table_ids, axis=0)
    local_in = jnp.concatenate([global_rows[:, None, :], embedded], axis=1).reshape(MAXLEN * LOCAL, D)
    local_result = layer_block(local_in, local_params, local_attend).reshape(MAXLEN, LOCAL, D)
    return (global_rows, jnp.where(valid[:, :, None], local_result, 0.0))

def reference(frames, codes, lengths, frame_mask, table, glob_norm_one, glob_w_query, glob_w_key, glob_w_value, glob_w_output, glob_norm_two, glob_w_up, glob_b_up, glob_w_down, glob_b_down, local_norm_one, local_w_query, local_w_key, local_w_value, local_w_output, local_norm_two, local_w_up, local_b_up, local_w_down, local_b_down, cotan_global, cotan_local):
    glob_params = tuple((item.astype(jnp.float32) for item in (glob_norm_one, glob_w_query, glob_w_key, glob_w_value, glob_w_output, glob_norm_two, glob_w_up, glob_b_up, glob_w_down, glob_b_down)))
    local_params = tuple((item.astype(jnp.float32) for item in (local_norm_one, local_w_query, local_w_key, local_w_value, local_w_output, local_norm_two, local_w_up, local_b_up, local_w_down, local_b_down)))

    def forward(frames_f, table_f, glob_in, local_in):

        def one_utterance(item):
            return utterance(item, table_f, glob_in, local_in)
        return lax.map(jax.checkpoint(one_utterance), (frames_f, codes, lengths, frame_mask))
    outputs, pull_back = jax.vjp(forward, frames.astype(jnp.float32), table.astype(jnp.float32), glob_params, local_params)
    grad_x, grad_tab, glob_grads, local_grads = pull_back((cotan_global.astype(jnp.float32), cotan_local.astype(jnp.float32)))
    return (outputs[0].astype(jnp.bfloat16), outputs[1].astype(jnp.bfloat16), grad_x, grad_tab, glob_grads[0], glob_grads[1], glob_grads[2], glob_grads[3], glob_grads[4], glob_grads[5], glob_grads[6], glob_grads[7], glob_grads[8], glob_grads[9], local_grads[0], local_grads[1], local_grads[2], local_grads[3], local_grads[4], local_grads[5], local_grads[6], local_grads[7], local_grads[8], local_grads[9])
```

```python
import functools

import jax
import jax.numpy as jnp
from jax import lax
from jax.experimental import pallas as pl
from jax.experimental.pallas import tpu as pltpu
from jax.sharding import PartitionSpec as P

H = 16
HD = 64
CB = 3
VOCAB = 1024


EPSILON = 1e-05
NEGATIVE = -1e30
MESH_ID = pl.DeviceIdType.MESH
SLOTS = 4
SROWS = 64
SCOLS = 512
DEEP = 8


def reduce_kernel(plan, total, *refs):
    count = len(plan)
    ins = refs[:count]
    outs = refs[count : 2 * count]
    (
        part, recv_c, half_a, half_b, recv_xa, recv_yb, sum_a, sum_b, recv_xb, line_b,
        right_a, left_a, right_b, left_b, recv_ya, recv_yb2, staged,
        load_sem, out_sem, send_sem, recv_sem,
    ) = refs[2 * count :]
    f32 = jnp.float32
    low = jnp.bfloat16
    utt = lax.axis_index("utt")
    seq = lax.axis_index("seq")
    pos = seq // 4
    col = (seq // 2) % 2
    core = seq % 2
    base = pos * 4 + col * 2
    core_id = (utt, base + 1 - core)
    col_id = (utt, pos * 4 + (1 - col) * 2 + core)
    utt_id = (1 - utt, seq)
    right_id = (utt, lax.rem(seq + 4, 16))
    left_id = (utt, lax.rem(seq + 12, 16))

    barrier = pltpu.get_barrier_semaphore()
    for target in (core_id, col_id, utt_id):
        pl.semaphore_signal(barrier, inc=1, device_id=target, device_id_type=MESH_ID)

    @pl.when(pos < 3)
    def _():
        pl.semaphore_signal(barrier, inc=1, device_id=right_id, device_id_type=MESH_ID)

    @pl.when(pos > 0)
    def _():
        pl.semaphore_signal(barrier, inc=1, device_id=left_id, device_id_type=MESH_ID)

    pl.semaphore_wait(barrier, jnp.where((pos == 0) | (pos == 3), 4, 5))

    def window(ref, spec, slab, lead):
        first, _, wide = spec
        local = slab - first
        rows = pl.ds(pl.multiple_of((local // wide) * SROWS, SROWS), SROWS)
        cols = pl.ds(pl.multiple_of((local % wide) * SCOLS, SCOLS), SCOLS)
        return ref.at[lead + (rows, cols)]

    def load(slab, start):
        slot = slab % SLOTS
        if not start:
            for side in range(2):
                pltpu.make_async_copy(
                    ins[0].at[:, side, pl.ds(0, SROWS), pl.ds(0, SCOLS)],
                    part.at[slot, side],
                    load_sem.at[slot, side],
                ).wait()
            return
        for ref, spec in zip(ins, plan):

            @pl.when((slab >= spec[0]) & (slab < spec[0] + spec[1]))
            def _():
                for side in range(2):
                    pltpu.make_async_copy(
                        window(ref, spec, slab, (slice(None), side)),
                        part.at[slot, side],
                        load_sem.at[slot, side],
                    ).start()

    def send(kind, slot, source, target, device):
        return pltpu.make_async_remote_copy(
            src_ref=source,
            dst_ref=target,
            send_sem=send_sem.at[kind, slot],
            recv_sem=recv_sem.at[kind, slot],
            device_id=device,
            device_id_type=MESH_ID,
        )

    def core_copy(slot):
        return send(0, slot, part.at[slot, 1 - core], recv_c.at[slot], core_id)

    def col_copy_a(slot):
        return send(1, slot, half_a.at[slot, 1 - col], recv_xa.at[slot], col_id)

    def utt_copy_b(slot):
        return send(2, slot, half_b.at[slot, 1 - utt], recv_yb.at[slot], utt_id)

    def col_copy_b(slot):
        return send(3, slot, sum_b.at[slot, 1 - col], recv_xb.at[slot], col_id)

    def utt_copy_a(slot, deep):
        return send(4, slot, sum_a.at[deep, pos], recv_ya.at[slot], utt_id)

    def utt_copy_b2(slot, deep):
        return send(5, slot, line_b.at[deep, pos], recv_yb2.at[slot], utt_id)

    def line_right(kind, slot, deep, step, source, target):
        dest = jnp.minimum(4 - step + pos, 3)
        return send(kind + step - 1, slot, source.at[deep, dest], target.at[slot, step - 1], right_id)

    def line_left(kind, slot, deep, step, source, target):
        dest = jnp.maximum(pos - 4 + step, 0)
        return send(kind + step - 1, slot, source.at[deep, dest], target.at[slot, step - 1], left_id)

    def line_start(slot, deep, step, source, right, left, kind):
        @pl.when((pos <= step - 1) & (pos < 3))
        def _():
            line_right(kind, slot, deep, step, source, right).start()

        @pl.when((pos >= 4 - step) & (pos > 0))
        def _():
            line_left(kind + 3, slot, deep, step, source, left).start()

    def line_finish(slot, deep, step, source, right, left, kind):
        @pl.when((pos <= step - 1) & (pos < 3))
        def _():
            line_right(kind, slot, deep, step, source, right).wait_send()

        @pl.when((pos >= 4 - step) & (pos > 0))
        def _():
            line_left(kind + 3, slot, deep, step, source, left).wait_send()

        @pl.when((pos >= 1) & (pos <= step))
        def _():
            line_right(kind, slot, deep, step, source, right).wait_recv()
            dest = 3 - step + pos
            source[deep, dest] = (
                source[deep, dest].astype(f32) + right[slot, step - 1].astype(f32)
            ).astype(low)

        @pl.when((pos <= 2) & (pos >= 3 - step))
        def _():
            line_left(kind + 3, slot, deep, step, source, left).wait_recv()
            dest = pos + step - 3
            source[deep, dest] = (
                source[deep, dest].astype(f32) + left[slot, step - 1].astype(f32)
            ).astype(low)

    line_a = (sum_a, right_a, left_a, 6)
    line_bb = (line_b, right_b, left_b, 12)

    load(0, True)

    @pl.loop(0, total + 8)
    def _(tick):
        def stage(offset):
            slab = tick - offset
            return slab, lax.rem(slab + SLOTS * 4, SLOTS), pl.when((slab >= 0) & (slab < total))

        slab, slot, guard = stage(0)

        @pl.when(slab + 1 < total)
        def _():
            load(slab + 1, True)

        @guard
        def _():
            load(slab, False)
            core_copy(slot).start()

        slab1, slot1, guard = stage(1)

        @guard
        def _():
            core_copy(slot1).wait()
            for line in range(4):
                for side in range(2):
                    both = part[slot1, core, 2 * line + side].astype(f32) + recv_c[
                        slot1, 2 * line + side
                    ].astype(f32)
                    both = both.astype(low)
                    half_a[slot1, side, line] = both[:32]
                    half_b[slot1, 0, side, line] = both[32:48]
                    half_b[slot1, 1, side, line] = both[48:]
            col_copy_a(slot1).start()
            utt_copy_b(slot1).start()

        slab2, slot2, guard = stage(2)
        deep2 = lax.rem(slab2 + DEEP, DEEP)

        @guard
        def _():
            col_copy_a(slot2).wait()
            sum_a[deep2] = (
                half_a[slot2, col].astype(f32) + recv_xa[slot2].astype(f32)
            ).astype(low)
            line_start(slot2, deep2, 1, *line_a)
            utt_copy_b(slot2).wait()
            sum_b[slot2] = (
                half_b[slot2, utt].astype(f32) + recv_yb[slot2].astype(f32)
            ).astype(low)
            col_copy_b(slot2).start()

        slab3, slot3, guard = stage(3)
        deep3 = lax.rem(slab3 + DEEP, DEEP)

        @guard
        def _():
            line_finish(slot3, deep3, 1, *line_a)
            line_start(slot3, deep3, 2, *line_a)
            col_copy_b(slot3).wait()
            line_b[deep3] = (
                sum_b[slot3, col].astype(f32) + recv_xb[slot3].astype(f32)
            ).astype(low)
            line_start(slot3, deep3, 1, *line_bb)

        slab4, slot4, guard = stage(4)
        deep4 = lax.rem(slab4 + DEEP, DEEP)

        @guard
        def _():
            line_finish(slot4, deep4, 2, *line_a)
            line_start(slot4, deep4, 3, *line_a)
            line_finish(slot4, deep4, 1, *line_bb)
            line_start(slot4, deep4, 2, *line_bb)

        slab5, slot5, guard = stage(5)
        deep5 = lax.rem(slab5 + DEEP, DEEP)

        @guard
        def _():
            line_finish(slot5, deep5, 3, *line_a)
            utt_copy_a(slot5, deep5).start()
            line_finish(slot5, deep5, 2, *line_bb)
            line_start(slot5, deep5, 3, *line_bb)

        slab6, slot6, guard = stage(6)
        deep6 = lax.rem(slab6 + DEEP, DEEP)

        @guard
        def _():
            utt_copy_a(slot6, deep6).wait()
            staged[slot6, 0:32] = sum_a[deep6, pos].astype(f32) + recv_ya[slot6].astype(f32)
            line_finish(slot6, deep6, 3, *line_bb)
            utt_copy_b2(slot6, deep6).start()

        slab7, slot7, guard = stage(7)
        deep7 = lax.rem(slab7 + DEEP, DEEP)

        @guard
        def _():
            utt_copy_b2(slot7, deep7).wait()
            mine = line_b[deep7, pos].astype(f32)
            theirs = recv_yb2[slot7].astype(f32)
            staged[slot7, 32:48] = jnp.where(utt == 0, mine, theirs)
            staged[slot7, 48:64] = jnp.where(utt == 0, theirs, mine)
            for ref, spec in zip(outs, plan):

                @pl.when((slab7 >= spec[0]) & (slab7 < spec[0] + spec[1]))
                def _():
                    pltpu.make_async_copy(
                        staged.at[slot7], window(ref, spec, slab7, ()), out_sem.at[slot7]
                    ).start()

        slab8, slot8, guard = stage(8)

        @guard
        def _():
            pltpu.make_async_copy(
                staged.at[slot8], outs[0].at[pl.ds(0, SROWS), pl.ds(0, SCOLS)], out_sem.at[slot8]
            ).wait()


def reduce_grads(arrays):
    views, plan, shapes, total = [], [], [], 0
    for item in arrays:
        rows, cols = item.shape[0] // 16, item.shape[1]
        views.append(item.reshape(8, 2, rows, cols))
        slabs = (rows // SROWS) * (cols // SCOLS)
        plan.append((total, slabs, cols // SCOLS))
        shapes.append(jax.ShapeDtypeStruct((rows, cols), jnp.float32))
        total += slabs
    low = jnp.bfloat16
    hbm = pl.BlockSpec(memory_space=pl.ANY)
    return pl.pallas_call(
        functools.partial(reduce_kernel, tuple(plan), total),
        out_shape=tuple(shapes),
        in_specs=[hbm] * len(views),
        out_specs=tuple([hbm] * len(views)),
        scratch_shapes=[
            pltpu.VMEM((SLOTS, 2, 8, 64, SCOLS), low),
            pltpu.VMEM((SLOTS, 8, 64, SCOLS), low),
            pltpu.VMEM((SLOTS, 2, 4, 32, SCOLS), low),
            pltpu.VMEM((SLOTS, 2, 2, 4, 16, SCOLS), low),
            pltpu.VMEM((SLOTS, 4, 32, SCOLS), low),
            pltpu.VMEM((SLOTS, 2, 4, 16, SCOLS), low),
            pltpu.VMEM((DEEP, 4, 32, SCOLS), low),
            pltpu.VMEM((SLOTS, 2, 4, 16, SCOLS), low),
            pltpu.VMEM((SLOTS, 4, 16, SCOLS), low),
            pltpu.VMEM((DEEP, 4, 16, SCOLS), low),
            pltpu.VMEM((SLOTS, 3, 32, SCOLS), low),
            pltpu.VMEM((SLOTS, 3, 32, SCOLS), low),
            pltpu.VMEM((SLOTS, 3, 16, SCOLS), low),
            pltpu.VMEM((SLOTS, 3, 16, SCOLS), low),
            pltpu.VMEM((SLOTS, 32, SCOLS), low),
            pltpu.VMEM((SLOTS, 16, SCOLS), low),
            pltpu.VMEM((SLOTS, 64, SCOLS), jnp.float32),
            pltpu.SemaphoreType.DMA((SLOTS, 2)),
            pltpu.SemaphoreType.DMA((SLOTS,)),
            pltpu.SemaphoreType.DMA((18, SLOTS)),
            pltpu.SemaphoreType.DMA((18, SLOTS)),
        ],
        compiler_params=pltpu.CompilerParams(
            collective_id=1, has_side_effects=True, vmem_limit_bytes=40 << 20
        ),
    )(*views)


def reduce_all(grads):
    low = [item.astype(jnp.bfloat16) for item in grads]
    if lax.axis_size("seq") != 16 or lax.axis_size("utt") != 2:
        return tuple(
            lax.psum(
                lax.psum_scatter(item, "seq", scatter_dimension=0, tiled=True), "utt"
            ).astype(jnp.float32)
            for item in low
        )
    wide = [index for index, item in enumerate(low) if item.ndim == 2]
    flat = [index for index, item in enumerate(low) if item.ndim == 1]
    small = jnp.concatenate([low[index].reshape(16, -1) for index in flat], axis=1)
    small = jnp.pad(small, ((0, 0), (0, SROWS * SCOLS - small.shape[1])))
    sums = reduce_grads([low[index] for index in wide] + [small.reshape(16 * SROWS, SCOLS)])
    out = [None] * len(low)
    for index, total in zip(wide, sums):
        out[index] = total
    first = 0
    rest = sums[-1].reshape(-1)
    for index in flat:
        size = low[index].shape[0] // 16
        out[index] = rest[first : first + size]
        first += size
    return tuple(out)


def normalize(values, gain_vec):
    return (
        values * lax.rsqrt(jnp.mean(values * values, axis=-1, keepdims=True) + EPSILON) * gain_vec
    )


def gelu_fn(values):
    return jax.nn.gelu(values, approximate=True)


def softmax_rows(scores):
    row_peak = jnp.max(scores, axis=-1, keepdims=True)
    raised = jnp.exp(scores - row_peak)
    return raised / jnp.sum(raised, axis=-1, keepdims=True)


def project(left_side, weight):
    return jnp.dot(left_side, weight, preferred_element_type=jnp.float32)


def project_back(gradient, weight):
    return lax.dot_general(
        gradient, weight, (((1,), (1,)), ((), ())), preferred_element_type=jnp.float32
    )


def weight_grad(left_side, gradient):
    return lax.dot_general(
        left_side, gradient, (((0,), (0,)), ((), ())), preferred_element_type=jnp.float32
    )


def head_split(matrix):
    return matrix.reshape(matrix.shape[0], matrix.shape[1], H, HD)


def block_inputs(inputs, params):
    normed = normalize(inputs, params[0]).astype(jnp.bfloat16)
    queries = project(normed, params[1]).astype(jnp.bfloat16)
    key_rows = project(normed, params[2]).astype(jnp.bfloat16)
    value_rows = project(normed, params[3]).astype(jnp.bfloat16)
    return (normed, queries, key_rows, value_rows)


def block_outputs(inputs, mixed_rows, params):
    middle = inputs + project(mixed_rows, params[4])
    middle_norm = normalize(middle, params[5]).astype(jnp.bfloat16)
    pre_active = project(middle_norm, params[6]) + params[7]
    active = gelu_fn(pre_active).astype(jnp.bfloat16)
    result = middle + project(active, params[8]) + params[9]
    return (result, (middle, middle_norm, pre_active, active))


def block_back(inputs, front_parts, mixed_rows, kept_parts, params, grad_out, attention_back):
    normed, queries, key_rows, value_rows = front_parts
    middle, middle_norm, pre_active, active = kept_parts
    grad_branch = grad_out.astype(jnp.bfloat16)
    grad_b_down = jnp.sum(grad_branch.astype(jnp.float32), axis=0)
    grad_w_down = weight_grad(active, grad_branch)
    grad_active = project_back(grad_branch, params[8])
    grad_pre = jax.vjp(gelu_fn, pre_active)[1](grad_active)[0].astype(jnp.bfloat16)
    grad_b_up = jnp.sum(grad_pre.astype(jnp.float32), axis=0)
    grad_w_up = weight_grad(middle_norm, grad_pre)
    middle_back = jax.vjp(normalize, middle, params[5])[1]
    grad_middle, grad_norm_two = middle_back(project_back(grad_pre, params[6]))
    grad_middle = grad_middle + grad_out
    grad_attn = grad_middle.astype(jnp.bfloat16)
    grad_w_output = weight_grad(mixed_rows, grad_attn)
    grad_mixed = project_back(grad_attn, params[4]).astype(jnp.bfloat16)
    grad_query, grad_key, grad_value = attention_back(grad_mixed)
    grad_normed = (
        project_back(grad_query, params[1])
        + project_back(grad_key, params[2])
        + project_back(grad_value, params[3])
    )
    input_back = jax.vjp(normalize, inputs, params[0])[1]
    grad_inputs, grad_norm_one = input_back(grad_normed)
    weight_grads = (
        grad_norm_one,
        weight_grad(normed, grad_query),
        weight_grad(normed, grad_key),
        weight_grad(normed, grad_value),
        grad_w_output,
        grad_norm_two,
        grad_w_up,
        grad_b_up,
        grad_w_down,
        grad_b_down,
    )
    return (grad_inputs + grad_middle, weight_grads)


def permitted(row_ids, col_ids, usable_cols):
    causal = col_ids[None, :] <= row_ids[:, None]
    itself = col_ids[None, :] == row_ids[:, None]
    return (causal[None] & ((usable_cols[:, None, :] > 0) | itself[None]))[:, None]


def probs_from(query_heads, key_heads, allowed, log_total):
    scores = jnp.einsum(
        "uqhd,ukhd->uhqk", query_heads, key_heads, preferred_element_type=jnp.float32
    ) * HD ** (-0.5)
    return jnp.where(allowed, jnp.exp(scores - log_total[..., None]), 0.0)


def score_grads(probs, grad_heads, value_heads, delta_rows):
    grad_probs = jnp.einsum(
        "uqhd,ukhd->uhqk", grad_heads, value_heads, preferred_element_type=jnp.float32
    )
    return (probs * (grad_probs - delta_rows[..., None])).astype(jnp.bfloat16)


def on_device(
    frames,
    codes,
    lengths,
    frame_mask,
    table,
    glob_norm_one,
    glob_w_query,
    glob_w_key,
    glob_w_value,
    glob_w_output,
    glob_norm_two,
    glob_w_up,
    glob_b_up,
    glob_w_down,
    glob_b_down,
    local_norm_one,
    local_w_query,
    local_w_key,
    local_w_value,
    local_w_output,
    local_norm_two,
    local_w_up,
    local_b_up,
    local_w_down,
    local_b_down,
    cotan_global,
    cotan_local,
):
    utter_count, frame_count, model_width = frames.shape
    row_count = utter_count * frame_count
    local_len = CB + 1
    positions = lax.axis_index("seq") * frame_count + jnp.arange(frame_count, dtype=jnp.int32)
    valid = positions[None, :] < lengths[:, None]
    usable = frame_mask.astype(jnp.bfloat16)
    glob_params = (
        glob_norm_one,
        glob_w_query,
        glob_w_key,
        glob_w_value,
        glob_w_output,
        glob_norm_two,
        glob_w_up,
        glob_b_up,
        glob_w_down,
        glob_b_down,
    )
    local_params = (
        local_norm_one,
        local_w_query,
        local_w_key,
        local_w_value,
        local_w_output,
        local_norm_two,
        local_w_up,
        local_b_up,
        local_w_down,
        local_b_down,
    )
    global_in = frames.astype(jnp.float32).reshape(row_count, model_width)
    glob_front = block_inputs(global_in, glob_params)
    query_block = glob_front[1].reshape(utter_count, frame_count, model_width)
    key_block = glob_front[2].reshape(utter_count, frame_count, model_width)
    value_block = glob_front[3].reshape(utter_count, frame_count, model_width)
    query_heads = head_split(query_block)
    run_max = jnp.full((utter_count, H, frame_count), NEGATIVE, jnp.float32)
    part_keys = lax.all_gather(key_block, "seq", axis=1, tiled=True)
    part_values = lax.all_gather(value_block, "seq", axis=1, tiled=True)
    part_usable = lax.all_gather(usable, "seq", axis=1, tiled=True)
    span = part_keys.shape[1]
    allowed = permitted(positions, jnp.arange(span, dtype=jnp.int32), part_usable)
    scores = jnp.einsum(
        "uqhd,ukhd->uhqk", query_heads, head_split(part_keys), preferred_element_type=jnp.float32
    ) * HD ** (-0.5)
    scores = jnp.where(allowed, scores, NEGATIVE)
    new_max = jnp.maximum(run_max, jnp.max(scores, axis=-1))
    weights = jnp.where(allowed, jnp.exp(scores - new_max[..., None]), 0.0)
    new_sum = jnp.sum(weights, axis=-1)
    new_accum = jnp.einsum(
        "uhqk,ukhd->uqhd",
        weights.astype(jnp.bfloat16),
        head_split(part_values),
        preferred_element_type=jnp.float32,
    )
    log_total = new_max + jnp.log(new_sum)
    attn_heads = new_accum / new_sum.transpose(0, 2, 1)[..., None]
    glob_mixed = attn_heads.reshape(row_count, model_width).astype(jnp.bfloat16)
    glob_result, glob_kept = block_outputs(global_in, glob_mixed, glob_params)
    global_rows = jnp.where(valid.reshape(row_count, 1), glob_result, 0.0).astype(jnp.bfloat16)
    table_ids = codes + VOCAB * jnp.arange(CB, dtype=jnp.int32)[None, None, :]
    embedded = jnp.take(table, table_ids.reshape(-1), axis=0).reshape(
        utter_count, frame_count, CB, model_width
    )
    local_in = jnp.concatenate(
        [global_rows.reshape(utter_count, frame_count, 1, model_width), embedded], axis=2
    )
    local_in = local_in.astype(jnp.float32).reshape(row_count * local_len, model_width)
    local_front = block_inputs(local_in, local_params)
    local_q = local_front[1].reshape(row_count, local_len, H, HD)
    local_k = local_front[2].reshape(row_count, local_len, H, HD)
    local_v = local_front[3].reshape(row_count, local_len, H, HD)
    lower = (
        jnp.arange(local_len, dtype=jnp.int32)[:, None]
        >= jnp.arange(local_len, dtype=jnp.int32)[None, :]
    )
    local_scores = jnp.einsum(
        "nihd,njhd->nhij", local_q, local_k, preferred_element_type=jnp.float32
    ) * HD ** (-0.5)
    local_probs = softmax_rows(jnp.where(lower, local_scores, NEGATIVE))
    local_mixed = jnp.einsum(
        "nhij,njhd->nihd",
        local_probs.astype(jnp.bfloat16),
        local_v,
        preferred_element_type=jnp.float32,
    )
    local_mixed = local_mixed.reshape(row_count * local_len, model_width).astype(jnp.bfloat16)
    local_result, local_kept = block_outputs(local_in, local_mixed, local_params)
    local_valid = jnp.repeat(valid.reshape(-1), local_len)[:, None]
    local_rows = jnp.where(local_valid, local_result, 0.0).astype(jnp.bfloat16)

    def local_back(grad_mixed):
        grad_heads = grad_mixed.reshape(row_count, local_len, H, HD)
        grad_probs = jnp.einsum(
            "nihd,njhd->nhij", grad_heads, local_v, preferred_element_type=jnp.float32
        )
        grads_s = (
            local_probs * (grad_probs - jnp.sum(local_probs * grad_probs, axis=-1, keepdims=True))
        ).astype(jnp.bfloat16)
        grad_query = jnp.einsum(
            "nhij,njhd->nihd", grads_s, local_k, preferred_element_type=jnp.float32
        ) * HD ** (-0.5)
        grad_key = jnp.einsum(
            "nhij,nihd->njhd", grads_s, local_q, preferred_element_type=jnp.float32
        ) * HD ** (-0.5)
        grad_value = jnp.einsum(
            "nhij,nihd->njhd",
            local_probs.astype(jnp.bfloat16),
            grad_heads,
            preferred_element_type=jnp.float32,
        )
        return (
            grad_query.reshape(-1, model_width).astype(jnp.bfloat16),
            grad_key.reshape(-1, model_width).astype(jnp.bfloat16),
            grad_value.reshape(-1, model_width).astype(jnp.bfloat16),
        )

    local_cotan = jnp.where(
        local_valid, cotan_local.astype(jnp.float32).reshape(-1, model_width), 0.0
    )
    grad_local_in, local_grads = block_back(
        local_in, local_front, local_mixed, local_kept, local_params, local_cotan, local_back
    )
    grad_local_in = grad_local_in.reshape(utter_count, frame_count, local_len, model_width)
    grad_tab = jax.ops.segment_sum(
        grad_local_in[:, :, 1:].reshape(-1, model_width),
        table_ids.reshape(-1),
        num_segments=CB * VOCAB,
    )
    glob_cotan = jnp.where(
        valid[:, :, None], cotan_global.astype(jnp.float32) + grad_local_in[:, :, 0], 0.0
    )
    glob_cotan = glob_cotan.reshape(row_count, model_width)

    def global_back(grad_mixed):
        grad_block = grad_mixed.reshape(utter_count, frame_count, model_width)
        grad_heads = head_split(grad_block)
        delta_rows = jnp.sum(grad_heads.astype(jnp.float32) * attn_heads, axis=-1).transpose(
            0, 2, 1
        )
        all_keys, all_values, all_usable = (
            lax.all_gather(key_block, "seq", axis=1, tiled=True),
            lax.all_gather(value_block, "seq", axis=1, tiled=True),
            lax.all_gather(usable, "seq", axis=1, tiled=True),
        )
        every_col = jnp.arange(all_keys.shape[1], dtype=jnp.int32)
        probs = probs_from(
            query_heads,
            head_split(all_keys),
            permitted(positions, every_col, all_usable),
            log_total,
        )
        grads_s = score_grads(probs, grad_heads, head_split(all_values), delta_rows)
        grad_query = jnp.einsum(
            "uhqk,ukhd->uqhd", grads_s, head_split(all_keys), preferred_element_type=jnp.float32
        ) * HD ** (-0.5)
        span = frame_count * lax.axis_size("seq")
        col_ids = jnp.arange(span, dtype=jnp.int32)
        part_probs = probs_from(
            query_heads, head_split(all_keys), permitted(positions, col_ids, all_usable), log_total
        )
        part_grads = score_grads(part_probs, grad_heads, head_split(all_values), delta_rows)
        term_keys = jnp.einsum(
            "uhqk,uqhd->ukhd", part_grads, query_heads, preferred_element_type=jnp.float32
        ) * HD ** (-0.5)
        term_values = jnp.einsum(
            "uhqk,uqhd->ukhd",
            part_probs.astype(jnp.bfloat16),
            grad_heads,
            preferred_element_type=jnp.float32,
        )
        joined = jnp.concatenate(
            [
                term_keys.reshape(utter_count, span, model_width),
                term_values.reshape(utter_count, span, model_width),
            ],
            axis=-1,
        )
        summed = (
            lax.psum_scatter(
                joined.transpose(1, 0, 2).astype(jnp.bfloat16),
                "seq",
                scatter_dimension=0,
                tiled=True,
            )
            .astype(jnp.float32)
            .transpose(1, 0, 2)
        )
        grad_key = summed[:, :, :model_width]
        grad_value = summed[:, :, model_width:]
        return (
            grad_query.reshape(row_count, model_width).astype(jnp.bfloat16),
            grad_key.reshape(row_count, model_width).astype(jnp.bfloat16),
            grad_value.reshape(row_count, model_width).astype(jnp.bfloat16),
        )

    grad_inputs, glob_grads = block_back(
        global_in, glob_front, glob_mixed, glob_kept, glob_params, glob_cotan, global_back
    )
    reduced = reduce_all((grad_tab,) + glob_grads + local_grads)
    return (
        global_rows.reshape(utter_count, frame_count, model_width),
        local_rows.reshape(utter_count, frame_count, local_len, model_width),
        grad_inputs.reshape(utter_count, frame_count, model_width),
    ) + reduced


def solution(mesh):
    return jax.shard_map(
        on_device,
        mesh=mesh,
        in_specs=(
            P("utt", "seq", None),
            P("utt", "seq", None),
            P("utt"),
            P("utt", "seq"),
            P(),
            P(),
            P(),
            P(),
            P(),
            P(),
            P(),
            P(),
            P(),
            P(),
            P(),
            P(),
            P(),
            P(),
            P(),
            P(),
            P(),
            P(),
            P(),
            P(),
            P(),
            P("utt", "seq", None),
            P("utt", "seq", None, None),
        ),
        out_specs=(
            P("utt", "seq", None),
            P("utt", "seq", None, None),
            P("utt", "seq", None),
            P("seq", None),
            P("seq"),
            P("seq", None),
            P("seq", None),
            P("seq", None),
            P("seq", None),
            P("seq"),
            P("seq", None),
            P("seq"),
            P("seq", None),
            P("seq"),
            P("seq"),
            P("seq", None),
            P("seq", None),
            P("seq", None),
            P("seq", None),
            P("seq"),
            P("seq", None),
            P("seq"),
            P("seq", None),
            P("seq"),
        ),
        check_vma=False,
    )
```

```python
import functools

import jax
import jax.numpy as jnp
from jax import lax
from jax.experimental import pallas as pl
from jax.experimental.pallas import tpu as pltpu
from jax.sharding import PartitionSpec as P

H = 16
HD = 64
CB = 3
VOCAB = 1024


EPSILON = 1e-05
NEGATIVE = -1e30
F32 = jnp.float32
LOW = jnp.bfloat16
MESH_ID = pl.DeviceIdType.MESH
SLOTS = 4
SROWS = 64
SCOLS = 512
DEEP = 8


def reduce_kernel(plan, total, *refs):
    count = len(plan)
    ins = refs[:count]
    outs = refs[count : 2 * count]
    (
        part, recv_c, half_a, half_b, recv_xa, recv_yb, sum_a, sum_b, recv_xb, line_b,
        right_a, left_a, right_b, left_b, recv_ya, recv_yb2, staged,
        load_sem, out_sem, send_sem, recv_sem,
    ) = refs[2 * count :]
    f32 = jnp.float32
    low = jnp.bfloat16
    utt = lax.axis_index("utt")
    seq = lax.axis_index("seq")
    pos = seq // 4
    col = (seq // 2) % 2
    core = seq % 2
    base = pos * 4 + col * 2
    core_id = (utt, base + 1 - core)
    col_id = (utt, pos * 4 + (1 - col) * 2 + core)
    utt_id = (1 - utt, seq)
    right_id = (utt, lax.rem(seq + 4, 16))
    left_id = (utt, lax.rem(seq + 12, 16))

    barrier = pltpu.get_barrier_semaphore()
    for target in (core_id, col_id, utt_id):
        pl.semaphore_signal(barrier, inc=1, device_id=target, device_id_type=MESH_ID)

    @pl.when(pos < 3)
    def _():
        pl.semaphore_signal(barrier, inc=1, device_id=right_id, device_id_type=MESH_ID)

    @pl.when(pos > 0)
    def _():
        pl.semaphore_signal(barrier, inc=1, device_id=left_id, device_id_type=MESH_ID)

    pl.semaphore_wait(barrier, jnp.where((pos == 0) | (pos == 3), 4, 5))

    def window(ref, spec, slab, lead):
        first, _, wide = spec
        local = slab - first
        rows = pl.ds(pl.multiple_of((local // wide) * SROWS, SROWS), SROWS)
        cols = pl.ds(pl.multiple_of((local % wide) * SCOLS, SCOLS), SCOLS)
        return ref.at[lead + (rows, cols)]

    def load(slab, start):
        slot = slab % SLOTS
        if not start:
            for side in range(2):
                pltpu.make_async_copy(
                    ins[0].at[:, side, pl.ds(0, SROWS), pl.ds(0, SCOLS)],
                    part.at[slot, side],
                    load_sem.at[slot, side],
                ).wait()
            return
        for ref, spec in zip(ins, plan):

            @pl.when((slab >= spec[0]) & (slab < spec[0] + spec[1]))
            def _():
                for side in range(2):
                    pltpu.make_async_copy(
                        window(ref, spec, slab, (slice(None), side)),
                        part.at[slot, side],
                        load_sem.at[slot, side],
                    ).start()

    def send(kind, slot, source, target, device):
        return pltpu.make_async_remote_copy(
            src_ref=source,
            dst_ref=target,
            send_sem=send_sem.at[kind, slot],
            recv_sem=recv_sem.at[kind, slot],
            device_id=device,
            device_id_type=MESH_ID,
        )

    def core_copy(slot):
        return send(0, slot, part.at[slot, 1 - core], recv_c.at[slot], core_id)

    def col_copy_a(slot):
        return send(1, slot, half_a.at[slot, 1 - col], recv_xa.at[slot], col_id)

    def utt_copy_b(slot):
        return send(2, slot, half_b.at[slot, 1 - utt], recv_yb.at[slot], utt_id)

    def col_copy_b(slot):
        return send(3, slot, sum_b.at[slot, 1 - col], recv_xb.at[slot], col_id)

    def utt_copy_a(slot, deep):
        return send(4, slot, sum_a.at[deep, pos], recv_ya.at[slot], utt_id)

    def utt_copy_b2(slot, deep):
        return send(5, slot, line_b.at[deep, pos], recv_yb2.at[slot], utt_id)

    def line_right(kind, slot, deep, step, source, target):
        dest = jnp.minimum(4 - step + pos, 3)
        return send(kind + step - 1, slot, source.at[deep, dest], target.at[slot, step - 1], right_id)

    def line_left(kind, slot, deep, step, source, target):
        dest = jnp.maximum(pos - 4 + step, 0)
        return send(kind + step - 1, slot, source.at[deep, dest], target.at[slot, step - 1], left_id)

    def line_start(slot, deep, step, source, right, left, kind):
        @pl.when((pos <= step - 1) & (pos < 3))
        def _():
            line_right(kind, slot, deep, step, source, right).start()

        @pl.when((pos >= 4 - step) & (pos > 0))
        def _():
            line_left(kind + 3, slot, deep, step, source, left).start()

    def line_finish(slot, deep, step, source, right, left, kind):
        @pl.when((pos <= step - 1) & (pos < 3))
        def _():
            line_right(kind, slot, deep, step, source, right).wait_send()

        @pl.when((pos >= 4 - step) & (pos > 0))
        def _():
            line_left(kind + 3, slot, deep, step, source, left).wait_send()

        @pl.when((pos >= 1) & (pos <= step))
        def _():
            line_right(kind, slot, deep, step, source, right).wait_recv()
            dest = 3 - step + pos
            source[deep, dest] = (
                source[deep, dest].astype(f32) + right[slot, step - 1].astype(f32)
            ).astype(low)

        @pl.when((pos <= 2) & (pos >= 3 - step))
        def _():
            line_left(kind + 3, slot, deep, step, source, left).wait_recv()
            dest = pos + step - 3
            source[deep, dest] = (
                source[deep, dest].astype(f32) + left[slot, step - 1].astype(f32)
            ).astype(low)

    line_a = (sum_a, right_a, left_a, 6)
    line_bb = (line_b, right_b, left_b, 12)

    load(0, True)

    @pl.loop(0, total + 8)
    def _(tick):
        def stage(offset):
            slab = tick - offset
            return slab, lax.rem(slab + SLOTS * 4, SLOTS), pl.when((slab >= 0) & (slab < total))

        slab, slot, guard = stage(0)

        @pl.when(slab + 1 < total)
        def _():
            load(slab + 1, True)

        @guard
        def _():
            load(slab, False)
            core_copy(slot).start()

        slab1, slot1, guard = stage(1)

        @guard
        def _():
            core_copy(slot1).wait()
            for line in range(4):
                for side in range(2):
                    both = part[slot1, core, 2 * line + side].astype(f32) + recv_c[
                        slot1, 2 * line + side
                    ].astype(f32)
                    both = both.astype(low)
                    half_a[slot1, side, line] = both[:32]
                    half_b[slot1, 0, side, line] = both[32:48]
                    half_b[slot1, 1, side, line] = both[48:]
            col_copy_a(slot1).start()
            utt_copy_b(slot1).start()

        slab2, slot2, guard = stage(2)
        deep2 = lax.rem(slab2 + DEEP, DEEP)

        @guard
        def _():
            col_copy_a(slot2).wait()
            sum_a[deep2] = (
                half_a[slot2, col].astype(f32) + recv_xa[slot2].astype(f32)
            ).astype(low)
            line_start(slot2, deep2, 1, *line_a)
            utt_copy_b(slot2).wait()
            sum_b[slot2] = (
                half_b[slot2, utt].astype(f32) + recv_yb[slot2].astype(f32)
            ).astype(low)
            col_copy_b(slot2).start()

        slab3, slot3, guard = stage(3)
        deep3 = lax.rem(slab3 + DEEP, DEEP)

        @guard
        def _():
            line_finish(slot3, deep3, 1, *line_a)
            line_start(slot3, deep3, 2, *line_a)
            col_copy_b(slot3).wait()
            line_b[deep3] = (
                sum_b[slot3, col].astype(f32) + recv_xb[slot3].astype(f32)
            ).astype(low)
            line_start(slot3, deep3, 1, *line_bb)

        slab4, slot4, guard = stage(4)
        deep4 = lax.rem(slab4 + DEEP, DEEP)

        @guard
        def _():
            line_finish(slot4, deep4, 2, *line_a)
            line_start(slot4, deep4, 3, *line_a)
            line_finish(slot4, deep4, 1, *line_bb)
            line_start(slot4, deep4, 2, *line_bb)

        slab5, slot5, guard = stage(5)
        deep5 = lax.rem(slab5 + DEEP, DEEP)

        @guard
        def _():
            line_finish(slot5, deep5, 3, *line_a)
            utt_copy_a(slot5, deep5).start()
            line_finish(slot5, deep5, 2, *line_bb)
            line_start(slot5, deep5, 3, *line_bb)

        slab6, slot6, guard = stage(6)
        deep6 = lax.rem(slab6 + DEEP, DEEP)

        @guard
        def _():
            utt_copy_a(slot6, deep6).wait()
            staged[slot6, 0:32] = sum_a[deep6, pos].astype(f32) + recv_ya[slot6].astype(f32)
            line_finish(slot6, deep6, 3, *line_bb)
            utt_copy_b2(slot6, deep6).start()

        slab7, slot7, guard = stage(7)
        deep7 = lax.rem(slab7 + DEEP, DEEP)

        @guard
        def _():
            utt_copy_b2(slot7, deep7).wait()
            mine = line_b[deep7, pos].astype(f32)
            theirs = recv_yb2[slot7].astype(f32)
            staged[slot7, 32:48] = jnp.where(utt == 0, mine, theirs)
            staged[slot7, 48:64] = jnp.where(utt == 0, theirs, mine)
            for ref, spec in zip(outs, plan):

                @pl.when((slab7 >= spec[0]) & (slab7 < spec[0] + spec[1]))
                def _():
                    pltpu.make_async_copy(
                        staged.at[slot7], window(ref, spec, slab7, ()), out_sem.at[slot7]
                    ).start()

        slab8, slot8, guard = stage(8)

        @guard
        def _():
            pltpu.make_async_copy(
                staged.at[slot8], outs[0].at[pl.ds(0, SROWS), pl.ds(0, SCOLS)], out_sem.at[slot8]
            ).wait()


def reduce_grads(arrays):
    views, plan, shapes, total = [], [], [], 0
    for item in arrays:
        rows, cols = item.shape[0] // 16, item.shape[1]
        views.append(item.reshape(8, 2, rows, cols))
        slabs = (rows // SROWS) * (cols // SCOLS)
        plan.append((total, slabs, cols // SCOLS))
        shapes.append(jax.ShapeDtypeStruct((rows, cols), jnp.float32))
        total += slabs
    low = jnp.bfloat16
    hbm = pl.BlockSpec(memory_space=pl.ANY)
    return pl.pallas_call(
        functools.partial(reduce_kernel, tuple(plan), total),
        out_shape=tuple(shapes),
        in_specs=[hbm] * len(views),
        out_specs=tuple([hbm] * len(views)),
        scratch_shapes=[
            pltpu.VMEM((SLOTS, 2, 8, 64, SCOLS), low),
            pltpu.VMEM((SLOTS, 8, 64, SCOLS), low),
            pltpu.VMEM((SLOTS, 2, 4, 32, SCOLS), low),
            pltpu.VMEM((SLOTS, 2, 2, 4, 16, SCOLS), low),
            pltpu.VMEM((SLOTS, 4, 32, SCOLS), low),
            pltpu.VMEM((SLOTS, 2, 4, 16, SCOLS), low),
            pltpu.VMEM((DEEP, 4, 32, SCOLS), low),
            pltpu.VMEM((SLOTS, 2, 4, 16, SCOLS), low),
            pltpu.VMEM((SLOTS, 4, 16, SCOLS), low),
            pltpu.VMEM((DEEP, 4, 16, SCOLS), low),
            pltpu.VMEM((SLOTS, 3, 32, SCOLS), low),
            pltpu.VMEM((SLOTS, 3, 32, SCOLS), low),
            pltpu.VMEM((SLOTS, 3, 16, SCOLS), low),
            pltpu.VMEM((SLOTS, 3, 16, SCOLS), low),
            pltpu.VMEM((SLOTS, 32, SCOLS), low),
            pltpu.VMEM((SLOTS, 16, SCOLS), low),
            pltpu.VMEM((SLOTS, 64, SCOLS), jnp.float32),
            pltpu.SemaphoreType.DMA((SLOTS, 2)),
            pltpu.SemaphoreType.DMA((SLOTS,)),
            pltpu.SemaphoreType.DMA((18, SLOTS)),
            pltpu.SemaphoreType.DMA((18, SLOTS)),
        ],
        compiler_params=pltpu.CompilerParams(
            collective_id=1, has_side_effects=True, vmem_limit_bytes=40 << 20
        ),
    )(*views)


def reduce_all(grads):
    low = [item.astype(jnp.bfloat16) for item in grads]
    if lax.axis_size("seq") != 16 or lax.axis_size("utt") != 2:
        return tuple(
            lax.psum(
                lax.psum_scatter(item, "seq", scatter_dimension=0, tiled=True), "utt"
            ).astype(jnp.float32)
            for item in low
        )
    wide = [index for index, item in enumerate(low) if item.ndim == 2]
    flat = [index for index, item in enumerate(low) if item.ndim == 1]
    small = jnp.concatenate([low[index].reshape(16, -1) for index in flat], axis=1)
    small = jnp.pad(small, ((0, 0), (0, SROWS * SCOLS - small.shape[1])))
    sums = reduce_grads([low[index] for index in wide] + [small.reshape(16 * SROWS, SCOLS)])
    out = [None] * len(low)
    for index, total in zip(wide, sums):
        out[index] = total
    first = 0
    rest = sums[-1].reshape(-1)
    for index in flat:
        size = low[index].shape[0] // 16
        out[index] = rest[first : first + size]
        first += size
    return tuple(out)


def mul(left_side, right_side):
    return jnp.dot(left_side, right_side, preferred_element_type=F32)


def mul_t(left_side, right_side):
    return lax.dot_general(
        left_side, right_side, (((1,), (1,)), ((), ())), preferred_element_type=F32
    )


def t_mul(left_side, right_side):
    return lax.dot_general(
        left_side, right_side, (((0,), (0,)), ((), ())), preferred_element_type=F32
    )


def scale_of(values):
    return lax.rsqrt(jnp.mean(values * values, axis=-1, keepdims=True) + EPSILON)


def scale_back(values, gain, grad):
    scale = scale_of(values)
    inner = grad * gain
    shared = jnp.mean(values * inner, axis=-1, keepdims=True) * (scale * scale * scale)
    return inner * scale - values * shared, grad * values * scale


def head_sums(width):
    rows = lax.broadcasted_iota(jnp.int32, (width, 128), 0) // HD
    cols = lax.broadcasted_iota(jnp.int32, (width, 128), 1)
    return (rows == cols).astype(LOW)


def head_spread(width):
    rows = lax.broadcasted_iota(jnp.int32, (128, width), 0)
    cols = lax.broadcasted_iota(jnp.int32, (128, width), 1) // HD
    return (rows == cols).astype(LOW)


def sum_heads(product, sums):
    high = product.astype(LOW)
    rest = (product - high.astype(F32)).astype(LOW)
    return mul(high, sums) + mul(rest, sums)


def front_kernel(
    x_ref, n1_ref, wq_ref, wk_ref, wv_ref, wo_ref, n2_ref,
    normed_ref, q_ref, k_ref, v_ref, probs_ref, mixed_ref, mid_ref, mid_norm_ref,
):
    places, frames, width = x_ref.shape
    rows = places * frames
    x = x_ref[...].astype(F32).reshape(rows, width)
    normed = (x * scale_of(x) * n1_ref[...]).astype(LOW)
    normed_ref[...] = normed.reshape(places, frames, width)
    q_ref[...] = mul(normed, wq_ref[...]).astype(LOW).reshape(places, frames, width)
    k_ref[...] = mul(normed, wk_ref[...]).astype(LOW).reshape(places, frames, width)
    v_ref[...] = mul(normed, wv_ref[...]).astype(LOW).reshape(places, frames, width)
    sums, spread = head_sums(width), head_spread(width)
    pair = 0
    for i in range(places):
        query = q_ref[i].astype(F32)
        scores = [
            sum_heads(query * k_ref[j].astype(F32), sums) * HD ** (-0.5) for j in range(i + 1)
        ]
        peak = scores[0]
        for item in scores[1:]:
            peak = jnp.maximum(peak, item)
        raised = [jnp.exp(item - peak) for item in scores]
        total = raised[0]
        for item in raised[1:]:
            total = total + item
        mixed = None
        for j in range(i + 1):
            probs = raised[j] / total
            probs_ref[pair] = probs
            pair += 1
            term = mul(probs.astype(LOW), spread) * v_ref[j].astype(F32)
            mixed = term if mixed is None else mixed + term
        mixed_ref[i] = mixed.astype(LOW)
    mid = x + mul(mixed_ref[...].reshape(rows, width), wo_ref[...])
    mid_ref[...] = mid.reshape(places, frames, width)
    mid_norm_ref[...] = (
        (mid * scale_of(mid) * n2_ref[...]).astype(LOW).reshape(places, frames, width)
    )


def local_front(x, params):
    places, frames, width = x.shape
    pairs = places * (places + 1) // 2
    step = 64
    rows = pl.BlockSpec((places, step, width), lambda i: (0, i, 0))
    whole = lambda item: pl.BlockSpec(item.shape, lambda i: (0, 0), pipeline_mode=pl.Buffered(1))
    n1, n2 = params[0].reshape(1, -1), params[5].reshape(1, -1)
    operands = (x, n1, params[1], params[2], params[3], params[4], n2)
    like = lambda kind: jax.ShapeDtypeStruct((places, frames, width), kind)
    return pl.pallas_call(
        front_kernel,
        grid=(frames // step,),
        in_specs=[rows] + [whole(item) for item in operands[1:]],
        out_specs=[rows] * 4
        + [pl.BlockSpec((pairs, step, 128), lambda i: (0, i, 0))]
        + [rows] * 3,
        out_shape=[
            like(LOW), like(LOW), like(LOW), like(LOW),
            jax.ShapeDtypeStruct((pairs, frames, 128), F32),
            like(LOW), like(F32), like(LOW),
        ],
        compiler_params=pltpu.CompilerParams(vmem_limit_bytes=56 << 20),
    )(*operands)


def gelu_parts(u):
    scale = 0.7978845608028654
    inner = jnp.tanh(scale * (u + 0.044715 * u * u * u))
    half = 0.5 * (1.0 + inner)
    slope = half + 0.5 * u * (1.0 - inner * inner) * scale * (1.0 + 3 * 0.044715 * u * u)
    return u * half, slope


def ffn_kernel(
    hn_ref, dout_ref, mid_ref, w1_ref, b1_ref, w2_ref, b2_ref,
    y_ref, dhn_ref, dw1_ref, dw2_ref, db1_ref, acc_ref, hn_t_ref,
):
    at = pl.program_id(0)
    last = pl.num_programs(0) - 1

    @pl.when(at == 0)
    def _():
        hn_t_ref[...] = hn_ref[...].T
        acc_ref[...] = mid_ref[...] + b2_ref[...]
        dhn_ref[...] = jnp.zeros_like(dhn_ref)

    hn, dout = hn_ref[...], dout_ref[...]
    u = mul(hn, w1_ref[...]) + b1_ref[...]
    act, slope = gelu_parts(u)
    act = act.astype(LOW)
    acc_ref[...] += mul(act, w2_ref[...])
    du = (mul_t(dout, w2_ref[...]) * slope).astype(LOW)
    db1_ref[...] = jnp.sum(du.astype(F32), axis=0, keepdims=True)
    dhn_ref[...] += mul_t(du, w1_ref[...])
    dw1_ref[...] = mul(hn_t_ref[...], du).astype(LOW)
    dw2_ref[...] = t_mul(act, dout).astype(LOW)

    @pl.when(at == last)
    def _():
        y_ref[...] = acc_ref[...].astype(LOW)


def local_ffn(hn, dout, mid, params):
    rows, width = hn.shape
    wide = params[6].shape[1]
    step = 512
    whole = pl.BlockSpec((rows, width), lambda i: (0, 0), pipeline_mode=pl.Buffered(1))
    out_whole = pl.BlockSpec((rows, width), lambda i: (0, 0))
    return pl.pallas_call(
        ffn_kernel,
        grid=(wide // step,),
        in_specs=[
            whole, whole, whole,
            pl.BlockSpec((width, step), lambda i: (0, i)),
            pl.BlockSpec((1, step), lambda i: (0, i)),
            pl.BlockSpec((step, width), lambda i: (i, 0)),
            pl.BlockSpec((1, width), lambda i: (0, 0)),
        ],
        out_specs=[
            out_whole, out_whole,
            pl.BlockSpec((width, step), lambda i: (0, i)),
            pl.BlockSpec((step, width), lambda i: (i, 0)),
            pl.BlockSpec((1, step), lambda i: (0, i)),
        ],
        out_shape=[
            jax.ShapeDtypeStruct((rows, width), LOW),
            jax.ShapeDtypeStruct((rows, width), F32),
            jax.ShapeDtypeStruct((width, wide), LOW),
            jax.ShapeDtypeStruct((wide, width), LOW),
            jax.ShapeDtypeStruct((1, wide), F32),
        ],
        scratch_shapes=[pltpu.VMEM((rows, width), F32), pltpu.VMEM((width, rows), LOW)],
        compiler_params=pltpu.CompilerParams(vmem_limit_bytes=56 << 20),
    )(hn, dout, mid, params[6], params[7].reshape(1, -1), params[8], params[9].reshape(1, -1))


def back_kernel(
    x_ref, mid_ref, dhn_ref, dout_ref, q_ref, k_ref, v_ref, probs_ref,
    n1_ref, n2_ref, wq_ref, wk_ref, wv_ref, wo_ref,
    dattn_ref, dq_ref, dk_ref, dv_ref, first_ref, rest_ref, dn1_ref, dn2_ref,
    dmid_ref,
):
    places, frames, width = x_ref.shape
    rows = places * frames

    @pl.when(pl.program_id(0) == 0)
    def _():
        dn1_ref[...] = jnp.zeros_like(dn1_ref)
        dn2_ref[...] = jnp.zeros_like(dn2_ref)

    mid = mid_ref[...].reshape(rows, width)
    dmid, gain = scale_back(mid, n2_ref[...], dhn_ref[...].reshape(rows, width))
    dn2_ref[...] += jnp.sum(gain, axis=0, keepdims=True)
    dmid = dmid + dout_ref[...].astype(F32).reshape(rows, width)
    dmid_ref[...] = dmid
    dattn = dmid.astype(LOW)
    dattn_ref[...] = dattn.reshape(places, frames, width)
    dmixed = mul_t(dattn, wo_ref[...]).astype(LOW).reshape(places, frames, width)
    sums, spread = head_sums(width), head_spread(width)
    pair = 0
    dk, dv = [None] * places, [None] * places
    add = lambda old, term: term if old is None else old + term
    for i in range(places):
        grad = dmixed[i].astype(F32)
        query = q_ref[i].astype(F32)
        dp = [sum_heads(grad * v_ref[j].astype(F32), sums) for j in range(i + 1)]
        delta = None
        for j in range(i + 1):
            delta = add(delta, probs_ref[pair + j] * dp[j])
        dq = None
        for j in range(i + 1):
            probs = probs_ref[pair + j]
            ds = (probs * (dp[j] - delta)).astype(LOW)
            ds = mul(ds, spread)
            dq = add(dq, ds * k_ref[j].astype(F32))
            dk[j] = add(dk[j], ds * query)
            dv[j] = add(dv[j], mul(probs.astype(LOW), spread) * grad)
        pair += i + 1
        dq_ref[i] = (dq * HD ** (-0.5)).astype(LOW)
    for j in range(places):
        dk_ref[j] = (dk[j] * HD ** (-0.5)).astype(LOW)
        dv_ref[j] = dv[j].astype(LOW)
    dnormed = (
        mul_t(dq_ref[...].reshape(rows, width), wq_ref[...])
        + mul_t(dk_ref[...].reshape(rows, width), wk_ref[...])
        + mul_t(dv_ref[...].reshape(rows, width), wv_ref[...])
    )
    x = x_ref[...].astype(F32).reshape(rows, width)
    dx, gain = scale_back(x, n1_ref[...], dnormed)
    dn1_ref[...] += jnp.sum(gain, axis=0, keepdims=True)
    dx = (dx + dmid_ref[...]).reshape(places, frames, width)
    first_ref[...] = dx[0]
    rest_ref[...] = dx[1:].astype(LOW)


def local_back(x, mid, dhn, dout, q, k, v, probs, params):
    places, frames, width = x.shape
    pairs = probs.shape[0]
    step = 64
    rows = pl.BlockSpec((places, step, width), lambda i: (0, i, 0))
    whole = lambda item: pl.BlockSpec(item.shape, lambda i: (0, 0), pipeline_mode=pl.Buffered(1))
    like = lambda kind: jax.ShapeDtypeStruct((places, frames, width), kind)
    fixed = (params[0].reshape(1, -1), params[5].reshape(1, -1)) + tuple(params[1:5])
    vector = pl.BlockSpec((1, width), lambda i: (0, 0))
    return pl.pallas_call(
        back_kernel,
        grid=(frames // step,),
        in_specs=[rows] * 7
        + [pl.BlockSpec((pairs, step, 128), lambda i: (0, i, 0))]
        + [whole(item) for item in fixed],
        out_specs=[rows] * 4
        + [
            pl.BlockSpec((step, width), lambda i: (i, 0)),
            pl.BlockSpec((places - 1, step, width), lambda i: (0, i, 0)),
            vector, vector,
        ],
        out_shape=[
            like(LOW), like(LOW), like(LOW), like(LOW),
            jax.ShapeDtypeStruct((frames, width), F32),
            jax.ShapeDtypeStruct((places - 1, frames, width), LOW),
            jax.ShapeDtypeStruct((1, width), F32),
            jax.ShapeDtypeStruct((1, width), F32),
        ],
        scratch_shapes=[pltpu.VMEM((places * step, width), F32)],
        compiler_params=pltpu.CompilerParams(vmem_limit_bytes=60 << 20),
    )(x, mid, dhn, dout, q, k, v, probs, *fixed)


def normalize(values, gain_vec):
    return (
        values * lax.rsqrt(jnp.mean(values * values, axis=-1, keepdims=True) + EPSILON) * gain_vec
    )


def gelu_fn(values):
    return jax.nn.gelu(values, approximate=True)


def softmax_rows(scores):
    row_peak = jnp.max(scores, axis=-1, keepdims=True)
    raised = jnp.exp(scores - row_peak)
    return raised / jnp.sum(raised, axis=-1, keepdims=True)


def project(left_side, weight):
    return jnp.dot(left_side, weight, preferred_element_type=jnp.float32)


def project_back(gradient, weight):
    return lax.dot_general(
        gradient, weight, (((1,), (1,)), ((), ())), preferred_element_type=jnp.float32
    )


def weight_grad(left_side, gradient):
    return lax.dot_general(
        left_side, gradient, (((0,), (0,)), ((), ())), preferred_element_type=jnp.float32
    )


def head_split(matrix):
    return matrix.reshape(matrix.shape[0], matrix.shape[1], H, HD)


def block_inputs(inputs, params):
    normed = normalize(inputs, params[0]).astype(jnp.bfloat16)
    queries = project(normed, params[1]).astype(jnp.bfloat16)
    key_rows = project(normed, params[2]).astype(jnp.bfloat16)
    value_rows = project(normed, params[3]).astype(jnp.bfloat16)
    return (normed, queries, key_rows, value_rows)


def block_outputs(inputs, mixed_rows, params):
    middle = inputs + project(mixed_rows, params[4])
    middle_norm = normalize(middle, params[5]).astype(jnp.bfloat16)
    pre_active = project(middle_norm, params[6]) + params[7]
    active = gelu_fn(pre_active).astype(jnp.bfloat16)
    result = middle + project(active, params[8]) + params[9]
    return (result, (middle, middle_norm, pre_active, active))


def block_back(inputs, front_parts, mixed_rows, kept_parts, params, grad_out, attention_back):
    normed, queries, key_rows, value_rows = front_parts
    middle, middle_norm, pre_active, active = kept_parts
    grad_branch = grad_out.astype(jnp.bfloat16)
    grad_b_down = jnp.sum(grad_branch.astype(jnp.float32), axis=0)
    grad_w_down = weight_grad(active, grad_branch)
    grad_active = project_back(grad_branch, params[8])
    grad_pre = jax.vjp(gelu_fn, pre_active)[1](grad_active)[0].astype(jnp.bfloat16)
    grad_b_up = jnp.sum(grad_pre.astype(jnp.float32), axis=0)
    grad_w_up = weight_grad(middle_norm, grad_pre)
    middle_back = jax.vjp(normalize, middle, params[5])[1]
    grad_middle, grad_norm_two = middle_back(project_back(grad_pre, params[6]))
    grad_middle = grad_middle + grad_out
    grad_attn = grad_middle.astype(jnp.bfloat16)
    grad_w_output = weight_grad(mixed_rows, grad_attn)
    grad_mixed = project_back(grad_attn, params[4]).astype(jnp.bfloat16)
    grad_query, grad_key, grad_value = attention_back(grad_mixed)
    grad_normed = (
        project_back(grad_query, params[1])
        + project_back(grad_key, params[2])
        + project_back(grad_value, params[3])
    )
    input_back = jax.vjp(normalize, inputs, params[0])[1]
    grad_inputs, grad_norm_one = input_back(grad_normed)
    weight_grads = (
        grad_norm_one,
        weight_grad(normed, grad_query),
        weight_grad(normed, grad_key),
        weight_grad(normed, grad_value),
        grad_w_output,
        grad_norm_two,
        grad_w_up,
        grad_b_up,
        grad_w_down,
        grad_b_down,
    )
    return (grad_inputs + grad_middle, weight_grads)


def permitted(row_ids, col_ids, usable_cols):
    causal = col_ids[None, :] <= row_ids[:, None]
    itself = col_ids[None, :] == row_ids[:, None]
    return (causal[None] & ((usable_cols[:, None, :] > 0) | itself[None]))[:, None]


def probs_from(query_heads, key_heads, allowed, log_total):
    scores = jnp.einsum(
        "uqhd,ukhd->uhqk", query_heads, key_heads, preferred_element_type=jnp.float32
    ) * HD ** (-0.5)
    return jnp.where(allowed, jnp.exp(scores - log_total[..., None]), 0.0)


def score_grads(probs, grad_heads, value_heads, delta_rows):
    grad_probs = jnp.einsum(
        "uqhd,ukhd->uhqk", grad_heads, value_heads, preferred_element_type=jnp.float32
    )
    return (probs * (grad_probs - delta_rows[..., None])).astype(jnp.bfloat16)


def on_device(
    frames,
    codes,
    lengths,
    frame_mask,
    table,
    glob_norm_one,
    glob_w_query,
    glob_w_key,
    glob_w_value,
    glob_w_output,
    glob_norm_two,
    glob_w_up,
    glob_b_up,
    glob_w_down,
    glob_b_down,
    local_norm_one,
    local_w_query,
    local_w_key,
    local_w_value,
    local_w_output,
    local_norm_two,
    local_w_up,
    local_b_up,
    local_w_down,
    local_b_down,
    cotan_global,
    cotan_local,
):
    utter_count, frame_count, model_width = frames.shape
    row_count = utter_count * frame_count
    local_len = CB + 1
    positions = lax.axis_index("seq") * frame_count + jnp.arange(frame_count, dtype=jnp.int32)
    valid = positions[None, :] < lengths[:, None]
    usable = frame_mask.astype(jnp.bfloat16)
    glob_params = (
        glob_norm_one,
        glob_w_query,
        glob_w_key,
        glob_w_value,
        glob_w_output,
        glob_norm_two,
        glob_w_up,
        glob_b_up,
        glob_w_down,
        glob_b_down,
    )
    local_params = (
        local_norm_one,
        local_w_query,
        local_w_key,
        local_w_value,
        local_w_output,
        local_norm_two,
        local_w_up,
        local_b_up,
        local_w_down,
        local_b_down,
    )
    global_in = frames.astype(jnp.float32).reshape(row_count, model_width)
    glob_front = block_inputs(global_in, glob_params)
    query_block = glob_front[1].reshape(utter_count, frame_count, model_width)
    key_block = glob_front[2].reshape(utter_count, frame_count, model_width)
    value_block = glob_front[3].reshape(utter_count, frame_count, model_width)
    query_heads = head_split(query_block)
    run_max = jnp.full((utter_count, H, frame_count), NEGATIVE, jnp.float32)
    part_keys = lax.all_gather(key_block, "seq", axis=1, tiled=True)
    part_values = lax.all_gather(value_block, "seq", axis=1, tiled=True)
    part_usable = lax.all_gather(usable, "seq", axis=1, tiled=True)
    span = part_keys.shape[1]
    allowed = permitted(positions, jnp.arange(span, dtype=jnp.int32), part_usable)
    scores = jnp.einsum(
        "uqhd,ukhd->uhqk", query_heads, head_split(part_keys), preferred_element_type=jnp.float32
    ) * HD ** (-0.5)
    scores = jnp.where(allowed, scores, NEGATIVE)
    new_max = jnp.maximum(run_max, jnp.max(scores, axis=-1))
    weights = jnp.where(allowed, jnp.exp(scores - new_max[..., None]), 0.0)
    new_sum = jnp.sum(weights, axis=-1)
    new_accum = jnp.einsum(
        "uhqk,ukhd->uqhd",
        weights.astype(jnp.bfloat16),
        head_split(part_values),
        preferred_element_type=jnp.float32,
    )
    log_total = new_max + jnp.log(new_sum)
    attn_heads = new_accum / new_sum.transpose(0, 2, 1)[..., None]
    glob_mixed = attn_heads.reshape(row_count, model_width).astype(jnp.bfloat16)
    glob_result, glob_kept = block_outputs(global_in, glob_mixed, glob_params)
    global_rows = jnp.where(valid.reshape(row_count, 1), glob_result, 0.0).astype(jnp.bfloat16)
    code_rows = codes.transpose(2, 0, 1).reshape(CB, row_count)
    table_ids = code_rows + VOCAB * jnp.arange(CB, dtype=jnp.int32)[:, None]
    embedded = table.at[table_ids].get(mode="promise_in_bounds")
    local_in = jnp.concatenate([global_rows[None], embedded], axis=0)
    local_shape = (local_len, row_count, model_width)
    flat_shape = (local_len * row_count, model_width)
    normed, local_q, local_k, local_v, local_probs, mixed, middle, middle_norm = local_front(
        local_in, local_params
    )
    row_valid = valid.reshape(1, row_count, 1)
    local_cotan = cotan_local.transpose(2, 0, 1, 3).reshape(local_shape)
    local_cotan = jnp.where(row_valid, local_cotan, 0)
    local_result, grad_hidden, grad_w_up, grad_w_down, grad_b_up = local_ffn(
        middle_norm.reshape(flat_shape),
        local_cotan.reshape(flat_shape),
        middle.reshape(flat_shape),
        local_params,
    )
    local_rows = jnp.where(row_valid, local_result.reshape(local_shape), 0)
    local_rows = local_rows.reshape(local_len, utter_count, frame_count, model_width)
    local_rows = local_rows.transpose(1, 2, 0, 3)
    grad_attn, grad_q, grad_k, grad_v, grad_first, grad_rest, grad_n1, grad_n2 = local_back(
        local_in,
        middle,
        grad_hidden.reshape(local_shape),
        local_cotan,
        local_q,
        local_k,
        local_v,
        local_probs,
        local_params,
    )
    normed = normed.reshape(flat_shape)
    local_grads = (
        grad_n1[0],
        weight_grad(normed, grad_q.reshape(flat_shape)),
        weight_grad(normed, grad_k.reshape(flat_shape)),
        weight_grad(normed, grad_v.reshape(flat_shape)),
        weight_grad(mixed.reshape(flat_shape), grad_attn.reshape(flat_shape)),
        grad_n2[0],
        grad_w_up,
        grad_b_up[0],
        grad_w_down,
        jnp.sum(local_cotan.astype(F32), axis=(0, 1)),
    )
    picked = code_rows[:, None, :] == jnp.arange(VOCAB, dtype=jnp.int32)[None, :, None]
    grad_tab = jnp.einsum(
        "cvn,cnd->cvd", picked.astype(LOW), grad_rest, preferred_element_type=F32
    ).reshape(CB * VOCAB, model_width)
    grad_first = grad_first.reshape(utter_count, frame_count, model_width)
    glob_cotan = jnp.where(
        valid[:, :, None], cotan_global.astype(jnp.float32) + grad_first, 0.0
    )
    glob_cotan = glob_cotan.reshape(row_count, model_width)

    def global_back(grad_mixed):
        grad_block = grad_mixed.reshape(utter_count, frame_count, model_width)
        grad_heads = head_split(grad_block)
        delta_rows = jnp.sum(grad_heads.astype(jnp.float32) * attn_heads, axis=-1).transpose(
            0, 2, 1
        )
        all_keys, all_values, all_usable = (
            lax.all_gather(key_block, "seq", axis=1, tiled=True),
            lax.all_gather(value_block, "seq", axis=1, tiled=True),
            lax.all_gather(usable, "seq", axis=1, tiled=True),
        )
        every_col = jnp.arange(all_keys.shape[1], dtype=jnp.int32)
        probs = probs_from(
            query_heads,
            head_split(all_keys),
            permitted(positions, every_col, all_usable),
            log_total,
        )
        grads_s = score_grads(probs, grad_heads, head_split(all_values), delta_rows)
        grad_query = jnp.einsum(
            "uhqk,ukhd->uqhd", grads_s, head_split(all_keys), preferred_element_type=jnp.float32
        ) * HD ** (-0.5)
        span = frame_count * lax.axis_size("seq")
        col_ids = jnp.arange(span, dtype=jnp.int32)
        part_probs = probs_from(
            query_heads, head_split(all_keys), permitted(positions, col_ids, all_usable), log_total
        )
        part_grads = score_grads(part_probs, grad_heads, head_split(all_values), delta_rows)
        term_keys = jnp.einsum(
            "uhqk,uqhd->ukhd", part_grads, query_heads, preferred_element_type=jnp.float32
        ) * HD ** (-0.5)
        term_values = jnp.einsum(
            "uhqk,uqhd->ukhd",
            part_probs.astype(jnp.bfloat16),
            grad_heads,
            preferred_element_type=jnp.float32,
        )
        joined = jnp.concatenate(
            [
                term_keys.reshape(utter_count, span, model_width),
                term_values.reshape(utter_count, span, model_width),
            ],
            axis=-1,
        )
        summed = (
            lax.psum_scatter(
                joined.transpose(1, 0, 2).astype(jnp.bfloat16),
                "seq",
                scatter_dimension=0,
                tiled=True,
            )
            .astype(jnp.float32)
            .transpose(1, 0, 2)
        )
        grad_key = summed[:, :, :model_width]
        grad_value = summed[:, :, model_width:]
        return (
            grad_query.reshape(row_count, model_width).astype(jnp.bfloat16),
            grad_key.reshape(row_count, model_width).astype(jnp.bfloat16),
            grad_value.reshape(row_count, model_width).astype(jnp.bfloat16),
        )

    grad_inputs, glob_grads = block_back(
        global_in, glob_front, glob_mixed, glob_kept, glob_params, glob_cotan, global_back
    )
    reduced = reduce_all((grad_tab,) + glob_grads + local_grads)
    return (
        global_rows.reshape(utter_count, frame_count, model_width),
        local_rows,
        grad_inputs.reshape(utter_count, frame_count, model_width),
    ) + reduced


def solution(mesh):
    return jax.shard_map(
        on_device,
        mesh=mesh,
        in_specs=(
            P("utt", "seq", None),
            P("utt", "seq", None),
            P("utt"),
            P("utt", "seq"),
            P(),
            P(),
            P(),
            P(),
            P(),
            P(),
            P(),
            P(),
            P(),
            P(),
            P(),
            P(),
            P(),
            P(),
            P(),
            P(),
            P(),
            P(),
            P(),
            P(),
            P(),
            P("utt", "seq", None),
            P("utt", "seq", None, None),
        ),
        out_specs=(
            P("utt", "seq", None),
            P("utt", "seq", None, None),
            P("utt", "seq", None),
            P("seq", None),
            P("seq"),
            P("seq", None),
            P("seq", None),
            P("seq", None),
            P("seq", None),
            P("seq"),
            P("seq", None),
            P("seq"),
            P("seq", None),
            P("seq"),
            P("seq"),
            P("seq", None),
            P("seq", None),
            P("seq", None),
            P("seq", None),
            P("seq"),
            P("seq", None),
            P("seq"),
            P("seq", None),
            P("seq"),
        ),
        check_vma=False,
    )
```

```python
import functools

import jax
import jax.numpy as jnp
from jax import lax
from jax.experimental import pallas as pl
from jax.experimental.pallas import tpu as pltpu
from jax.sharding import PartitionSpec as P

H = 16
HD = 64
CB = 3
VOCAB = 1024


EPSILON = 1e-05
NEGATIVE = -1e30
F32 = jnp.float32
LOW = jnp.bfloat16
LANES = 128
MESH_ID = pl.DeviceIdType.MESH
SLOTS = 4
SROWS = 64
SCOLS = 512
DEEP = 8


def reduce_kernel(plan, total, *refs):
    count = len(plan)
    ins = refs[:count]
    outs = refs[count : 2 * count]
    (
        part, recv_c, half_a, half_b, recv_xa, recv_yb, sum_a, sum_b, recv_xb, line_b,
        right_a, left_a, right_b, left_b, recv_ya, recv_yb2, staged,
        load_sem, out_sem, send_sem, recv_sem,
    ) = refs[2 * count :]
    f32 = jnp.float32
    low = jnp.bfloat16
    utt = lax.axis_index("utt")
    seq = lax.axis_index("seq")
    pos = seq // 4
    col = (seq // 2) % 2
    core = seq % 2
    base = pos * 4 + col * 2
    core_id = (utt, base + 1 - core)
    col_id = (utt, pos * 4 + (1 - col) * 2 + core)
    utt_id = (1 - utt, seq)
    right_id = (utt, lax.rem(seq + 4, 16))
    left_id = (utt, lax.rem(seq + 12, 16))

    barrier = pltpu.get_barrier_semaphore()
    for target in (core_id, col_id, utt_id):
        pl.semaphore_signal(barrier, inc=1, device_id=target, device_id_type=MESH_ID)

    @pl.when(pos < 3)
    def _():
        pl.semaphore_signal(barrier, inc=1, device_id=right_id, device_id_type=MESH_ID)

    @pl.when(pos > 0)
    def _():
        pl.semaphore_signal(barrier, inc=1, device_id=left_id, device_id_type=MESH_ID)

    pl.semaphore_wait(barrier, jnp.where((pos == 0) | (pos == 3), 4, 5))

    def window(ref, spec, slab, lead):
        first, _, wide = spec
        local = slab - first
        rows = pl.ds(pl.multiple_of((local // wide) * SROWS, SROWS), SROWS)
        cols = pl.ds(pl.multiple_of((local % wide) * SCOLS, SCOLS), SCOLS)
        return ref.at[lead + (rows, cols)]

    def load(slab, start):
        slot = slab % SLOTS
        if not start:
            for side in range(2):
                pltpu.make_async_copy(
                    ins[0].at[:, side, pl.ds(0, SROWS), pl.ds(0, SCOLS)],
                    part.at[slot, side],
                    load_sem.at[slot, side],
                ).wait()
            return
        for ref, spec in zip(ins, plan):

            @pl.when((slab >= spec[0]) & (slab < spec[0] + spec[1]))
            def _():
                for side in range(2):
                    pltpu.make_async_copy(
                        window(ref, spec, slab, (slice(None), side)),
                        part.at[slot, side],
                        load_sem.at[slot, side],
                    ).start()

    def send(kind, slot, source, target, device):
        return pltpu.make_async_remote_copy(
            src_ref=source,
            dst_ref=target,
            send_sem=send_sem.at[kind, slot],
            recv_sem=recv_sem.at[kind, slot],
            device_id=device,
            device_id_type=MESH_ID,
        )

    def core_copy(slot):
        return send(0, slot, part.at[slot, 1 - core], recv_c.at[slot], core_id)

    def col_copy_a(slot):
        return send(1, slot, half_a.at[slot, 1 - col], recv_xa.at[slot], col_id)

    def utt_copy_b(slot):
        return send(2, slot, half_b.at[slot, 1 - utt], recv_yb.at[slot], utt_id)

    def col_copy_b(slot):
        return send(3, slot, sum_b.at[slot, 1 - col], recv_xb.at[slot], col_id)

    def utt_copy_a(slot, deep):
        return send(4, slot, sum_a.at[deep, pos], recv_ya.at[slot], utt_id)

    def utt_copy_b2(slot, deep):
        return send(5, slot, line_b.at[deep, pos], recv_yb2.at[slot], utt_id)

    def line_right(kind, slot, deep, step, source, target):
        dest = jnp.minimum(4 - step + pos, 3)
        return send(kind + step - 1, slot, source.at[deep, dest], target.at[slot, step - 1], right_id)

    def line_left(kind, slot, deep, step, source, target):
        dest = jnp.maximum(pos - 4 + step, 0)
        return send(kind + step - 1, slot, source.at[deep, dest], target.at[slot, step - 1], left_id)

    def line_start(slot, deep, step, source, right, left, kind):
        @pl.when((pos <= step - 1) & (pos < 3))
        def _():
            line_right(kind, slot, deep, step, source, right).start()

        @pl.when((pos >= 4 - step) & (pos > 0))
        def _():
            line_left(kind + 3, slot, deep, step, source, left).start()

    def line_finish(slot, deep, step, source, right, left, kind):
        @pl.when((pos <= step - 1) & (pos < 3))
        def _():
            line_right(kind, slot, deep, step, source, right).wait_send()

        @pl.when((pos >= 4 - step) & (pos > 0))
        def _():
            line_left(kind + 3, slot, deep, step, source, left).wait_send()

        @pl.when((pos >= 1) & (pos <= step))
        def _():
            line_right(kind, slot, deep, step, source, right).wait_recv()
            dest = 3 - step + pos
            source[deep, dest] = (
                source[deep, dest].astype(f32) + right[slot, step - 1].astype(f32)
            ).astype(low)

        @pl.when((pos <= 2) & (pos >= 3 - step))
        def _():
            line_left(kind + 3, slot, deep, step, source, left).wait_recv()
            dest = pos + step - 3
            source[deep, dest] = (
                source[deep, dest].astype(f32) + left[slot, step - 1].astype(f32)
            ).astype(low)

    line_a = (sum_a, right_a, left_a, 6)
    line_bb = (line_b, right_b, left_b, 12)

    load(0, True)

    @pl.loop(0, total + 8)
    def _(tick):
        def stage(offset):
            slab = tick - offset
            return slab, lax.rem(slab + SLOTS * 4, SLOTS), pl.when((slab >= 0) & (slab < total))

        slab, slot, guard = stage(0)

        @pl.when(slab + 1 < total)
        def _():
            load(slab + 1, True)

        @guard
        def _():
            load(slab, False)
            core_copy(slot).start()

        slab1, slot1, guard = stage(1)

        @guard
        def _():
            core_copy(slot1).wait()
            for line in range(4):
                for side in range(2):
                    both = part[slot1, core, 2 * line + side].astype(f32) + recv_c[
                        slot1, 2 * line + side
                    ].astype(f32)
                    both = both.astype(low)
                    half_a[slot1, side, line] = both[:32]
                    half_b[slot1, 0, side, line] = both[32:48]
                    half_b[slot1, 1, side, line] = both[48:]
            col_copy_a(slot1).start()
            utt_copy_b(slot1).start()

        slab2, slot2, guard = stage(2)
        deep2 = lax.rem(slab2 + DEEP, DEEP)

        @guard
        def _():
            col_copy_a(slot2).wait()
            sum_a[deep2] = (
                half_a[slot2, col].astype(f32) + recv_xa[slot2].astype(f32)
            ).astype(low)
            line_start(slot2, deep2, 1, *line_a)
            utt_copy_b(slot2).wait()
            sum_b[slot2] = (
                half_b[slot2, utt].astype(f32) + recv_yb[slot2].astype(f32)
            ).astype(low)
            col_copy_b(slot2).start()

        slab3, slot3, guard = stage(3)
        deep3 = lax.rem(slab3 + DEEP, DEEP)

        @guard
        def _():
            line_finish(slot3, deep3, 1, *line_a)
            line_start(slot3, deep3, 2, *line_a)
            col_copy_b(slot3).wait()
            line_b[deep3] = (
                sum_b[slot3, col].astype(f32) + recv_xb[slot3].astype(f32)
            ).astype(low)
            line_start(slot3, deep3, 1, *line_bb)

        slab4, slot4, guard = stage(4)
        deep4 = lax.rem(slab4 + DEEP, DEEP)

        @guard
        def _():
            line_finish(slot4, deep4, 2, *line_a)
            line_start(slot4, deep4, 3, *line_a)
            line_finish(slot4, deep4, 1, *line_bb)
            line_start(slot4, deep4, 2, *line_bb)

        slab5, slot5, guard = stage(5)
        deep5 = lax.rem(slab5 + DEEP, DEEP)

        @guard
        def _():
            line_finish(slot5, deep5, 3, *line_a)
            utt_copy_a(slot5, deep5).start()
            line_finish(slot5, deep5, 2, *line_bb)
            line_start(slot5, deep5, 3, *line_bb)

        slab6, slot6, guard = stage(6)
        deep6 = lax.rem(slab6 + DEEP, DEEP)

        @guard
        def _():
            utt_copy_a(slot6, deep6).wait()
            staged[slot6, 0:32] = sum_a[deep6, pos].astype(f32) + recv_ya[slot6].astype(f32)
            line_finish(slot6, deep6, 3, *line_bb)
            utt_copy_b2(slot6, deep6).start()

        slab7, slot7, guard = stage(7)
        deep7 = lax.rem(slab7 + DEEP, DEEP)

        @guard
        def _():
            utt_copy_b2(slot7, deep7).wait()
            mine = line_b[deep7, pos].astype(f32)
            theirs = recv_yb2[slot7].astype(f32)
            staged[slot7, 32:48] = jnp.where(utt == 0, mine, theirs)
            staged[slot7, 48:64] = jnp.where(utt == 0, theirs, mine)
            for ref, spec in zip(outs, plan):

                @pl.when((slab7 >= spec[0]) & (slab7 < spec[0] + spec[1]))
                def _():
                    pltpu.make_async_copy(
                        staged.at[slot7], window(ref, spec, slab7, ()), out_sem.at[slot7]
                    ).start()

        slab8, slot8, guard = stage(8)

        @guard
        def _():
            pltpu.make_async_copy(
                staged.at[slot8], outs[0].at[pl.ds(0, SROWS), pl.ds(0, SCOLS)], out_sem.at[slot8]
            ).wait()


def reduce_grads(arrays):
    views, plan, shapes, total = [], [], [], 0
    for item in arrays:
        rows, cols = item.shape[0] // 16, item.shape[1]
        views.append(item.reshape(8, 2, rows, cols))
        slabs = (rows // SROWS) * (cols // SCOLS)
        plan.append((total, slabs, cols // SCOLS))
        shapes.append(jax.ShapeDtypeStruct((rows, cols), jnp.float32))
        total += slabs
    low = jnp.bfloat16
    hbm = pl.BlockSpec(memory_space=pl.ANY)
    return pl.pallas_call(
        functools.partial(reduce_kernel, tuple(plan), total),
        out_shape=tuple(shapes),
        in_specs=[hbm] * len(views),
        out_specs=tuple([hbm] * len(views)),
        scratch_shapes=[
            pltpu.VMEM((SLOTS, 2, 8, 64, SCOLS), low),
            pltpu.VMEM((SLOTS, 8, 64, SCOLS), low),
            pltpu.VMEM((SLOTS, 2, 4, 32, SCOLS), low),
            pltpu.VMEM((SLOTS, 2, 2, 4, 16, SCOLS), low),
            pltpu.VMEM((SLOTS, 4, 32, SCOLS), low),
            pltpu.VMEM((SLOTS, 2, 4, 16, SCOLS), low),
            pltpu.VMEM((DEEP, 4, 32, SCOLS), low),
            pltpu.VMEM((SLOTS, 2, 4, 16, SCOLS), low),
            pltpu.VMEM((SLOTS, 4, 16, SCOLS), low),
            pltpu.VMEM((DEEP, 4, 16, SCOLS), low),
            pltpu.VMEM((SLOTS, 3, 32, SCOLS), low),
            pltpu.VMEM((SLOTS, 3, 32, SCOLS), low),
            pltpu.VMEM((SLOTS, 3, 16, SCOLS), low),
            pltpu.VMEM((SLOTS, 3, 16, SCOLS), low),
            pltpu.VMEM((SLOTS, 32, SCOLS), low),
            pltpu.VMEM((SLOTS, 16, SCOLS), low),
            pltpu.VMEM((SLOTS, 64, SCOLS), jnp.float32),
            pltpu.SemaphoreType.DMA((SLOTS, 2)),
            pltpu.SemaphoreType.DMA((SLOTS,)),
            pltpu.SemaphoreType.DMA((18, SLOTS)),
            pltpu.SemaphoreType.DMA((18, SLOTS)),
        ],
        compiler_params=pltpu.CompilerParams(
            collective_id=1, has_side_effects=True, vmem_limit_bytes=40 << 20
        ),
    )(*views)


def reduce_all(grads):
    low = [item.astype(jnp.bfloat16) for item in grads]
    if lax.axis_size("seq") != 16 or lax.axis_size("utt") != 2:
        return tuple(
            lax.psum(
                lax.psum_scatter(item, "seq", scatter_dimension=0, tiled=True), "utt"
            ).astype(jnp.float32)
            for item in low
        )
    wide = [index for index, item in enumerate(low) if item.ndim == 2]
    flat = [index for index, item in enumerate(low) if item.ndim == 1]
    small = jnp.concatenate([low[index].reshape(16, -1) for index in flat], axis=1)
    small = jnp.pad(small, ((0, 0), (0, SROWS * SCOLS - small.shape[1])))
    sums = reduce_grads([low[index] for index in wide] + [small.reshape(16 * SROWS, SCOLS)])
    out = [None] * len(low)
    for index, total in zip(wide, sums):
        out[index] = total
    first = 0
    rest = sums[-1].reshape(-1)
    for index in flat:
        size = low[index].shape[0] // 16
        out[index] = rest[first : first + size]
        first += size
    return tuple(out)


def mul(left_side, right_side):
    return jnp.dot(left_side, right_side, preferred_element_type=F32)


def mul_t(left_side, right_side):
    return lax.dot_general(
        left_side, right_side, (((1,), (1,)), ((), ())), preferred_element_type=F32
    )


def t_mul(left_side, right_side):
    return lax.dot_general(
        left_side, right_side, (((0,), (0,)), ((), ())), preferred_element_type=F32
    )


def scale_of(values):
    return lax.rsqrt(jnp.mean(values * values, axis=-1, keepdims=True) + EPSILON)


def scale_back(values, gain, grad):
    scale = scale_of(values)
    inner = grad * gain
    shared = jnp.mean(values * inner, axis=-1, keepdims=True) * (scale * scale * scale)
    return inner * scale - values * shared, grad * values * scale


def head_sums(width):
    rows = lax.broadcasted_iota(jnp.int32, (width, 128), 0) // HD
    cols = lax.broadcasted_iota(jnp.int32, (width, 128), 1)
    return (rows == cols).astype(LOW)


def head_spread(width):
    rows = lax.broadcasted_iota(jnp.int32, (128, width), 0)
    cols = lax.broadcasted_iota(jnp.int32, (128, width), 1) // HD
    return (rows == cols).astype(LOW)


def sum_heads(product, sums):
    high = product.astype(LOW)
    rest = (product - high.astype(F32)).astype(LOW)
    return mul(high, sums) + mul(rest, sums)


def front_kernel(
    x_ref, n1_ref, wq_ref, wk_ref, wv_ref, wo_ref, n2_ref,
    normed_ref, q_ref, k_ref, v_ref, probs_ref, mixed_ref, mid_ref, mid_norm_ref,
):
    places, frames, width = x_ref.shape
    rows = places * frames
    x = x_ref[...].astype(F32).reshape(rows, width)
    normed = (x * scale_of(x) * n1_ref[...]).astype(LOW)
    normed_ref[...] = normed.reshape(places, frames, width)
    q_ref[...] = mul(normed, wq_ref[...]).astype(LOW).reshape(places, frames, width)
    k_ref[...] = mul(normed, wk_ref[...]).astype(LOW).reshape(places, frames, width)
    v_ref[...] = mul(normed, wv_ref[...]).astype(LOW).reshape(places, frames, width)
    sums, spread = head_sums(width), head_spread(width)
    pair = 0
    for i in range(places):
        query = q_ref[i].astype(F32)
        scores = [
            sum_heads(query * k_ref[j].astype(F32), sums) * HD ** (-0.5) for j in range(i + 1)
        ]
        peak = scores[0]
        for item in scores[1:]:
            peak = jnp.maximum(peak, item)
        raised = [jnp.exp(item - peak) for item in scores]
        total = raised[0]
        for item in raised[1:]:
            total = total + item
        mixed = None
        for j in range(i + 1):
            probs = raised[j] / total
            probs_ref[pair] = probs
            pair += 1
            term = mul(probs.astype(LOW), spread) * v_ref[j].astype(F32)
            mixed = term if mixed is None else mixed + term
        mixed_ref[i] = mixed.astype(LOW)
    mid = x + mul(mixed_ref[...].reshape(rows, width), wo_ref[...])
    mid_ref[...] = mid.reshape(places, frames, width)
    mid_norm_ref[...] = (
        (mid * scale_of(mid) * n2_ref[...]).astype(LOW).reshape(places, frames, width)
    )


def local_front(x, params):
    places, frames, width = x.shape
    pairs = places * (places + 1) // 2
    step = 64
    rows = pl.BlockSpec((places, step, width), lambda i: (0, i, 0))
    whole = lambda item: pl.BlockSpec(item.shape, lambda i: (0, 0), pipeline_mode=pl.Buffered(1))
    n1, n2 = params[0].reshape(1, -1), params[5].reshape(1, -1)
    operands = (x, n1, params[1], params[2], params[3], params[4], n2)
    like = lambda kind: jax.ShapeDtypeStruct((places, frames, width), kind)
    return pl.pallas_call(
        front_kernel,
        grid=(frames // step,),
        in_specs=[rows] + [whole(item) for item in operands[1:]],
        out_specs=[rows] * 4
        + [pl.BlockSpec((pairs, step, 128), lambda i: (0, i, 0))]
        + [rows] * 3,
        out_shape=[
            like(LOW), like(LOW), like(LOW), like(LOW),
            jax.ShapeDtypeStruct((pairs, frames, 128), F32),
            like(LOW), like(F32), like(LOW),
        ],
        compiler_params=pltpu.CompilerParams(vmem_limit_bytes=56 << 20),
    )(*operands)


def gelu_parts(u):
    scale = 0.7978845608028654
    inner = jnp.tanh(scale * (u + 0.044715 * u * u * u))
    half = 0.5 * (1.0 + inner)
    slope = half + 0.5 * u * (1.0 - inner * inner) * scale * (1.0 + 3 * 0.044715 * u * u)
    return u * half, slope


def ffn_kernel(
    hn_ref, dout_ref, mid_ref, w1_ref, b1_ref, w2_ref, b2_ref,
    y_ref, dhn_ref, dw1_ref, dw2_ref, db1_ref, acc_ref, hn_t_ref,
):
    at = pl.program_id(0)
    last = pl.num_programs(0) - 1

    @pl.when(at == 0)
    def _():
        hn_t_ref[...] = hn_ref[...].T
        acc_ref[...] = mid_ref[...] + b2_ref[...]
        dhn_ref[...] = jnp.zeros_like(dhn_ref)

    hn, dout = hn_ref[...], dout_ref[...]
    u = mul(hn, w1_ref[...]) + b1_ref[...]
    act, slope = gelu_parts(u)
    act = act.astype(LOW)
    acc_ref[...] += mul(act, w2_ref[...])
    du = (mul_t(dout, w2_ref[...]) * slope).astype(LOW)
    db1_ref[...] = jnp.sum(du.astype(F32), axis=0, keepdims=True)
    dhn_ref[...] += mul_t(du, w1_ref[...])
    dw1_ref[...] = mul(hn_t_ref[...], du).astype(LOW)
    dw2_ref[...] = t_mul(act, dout).astype(LOW)

    @pl.when(at == last)
    def _():
        y_ref[...] = acc_ref[...].astype(LOW)


def local_ffn(hn, dout, mid, params):
    rows, width = hn.shape
    wide = params[6].shape[1]
    step = 512
    whole = pl.BlockSpec((rows, width), lambda i: (0, 0), pipeline_mode=pl.Buffered(1))
    out_whole = pl.BlockSpec((rows, width), lambda i: (0, 0))
    return pl.pallas_call(
        ffn_kernel,
        grid=(wide // step,),
        in_specs=[
            whole, whole, whole,
            pl.BlockSpec((width, step), lambda i: (0, i)),
            pl.BlockSpec((1, step), lambda i: (0, i)),
            pl.BlockSpec((step, width), lambda i: (i, 0)),
            pl.BlockSpec((1, width), lambda i: (0, 0)),
        ],
        out_specs=[
            out_whole, out_whole,
            pl.BlockSpec((width, step), lambda i: (0, i)),
            pl.BlockSpec((step, width), lambda i: (i, 0)),
            pl.BlockSpec((1, step), lambda i: (0, i)),
        ],
        out_shape=[
            jax.ShapeDtypeStruct((rows, width), LOW),
            jax.ShapeDtypeStruct((rows, width), F32),
            jax.ShapeDtypeStruct((width, wide), LOW),
            jax.ShapeDtypeStruct((wide, width), LOW),
            jax.ShapeDtypeStruct((1, wide), F32),
        ],
        scratch_shapes=[pltpu.VMEM((rows, width), F32), pltpu.VMEM((width, rows), LOW)],
        compiler_params=pltpu.CompilerParams(vmem_limit_bytes=56 << 20),
    )(hn, dout, mid, params[6], params[7].reshape(1, -1), params[8], params[9].reshape(1, -1))


def back_kernel(
    x_ref, mid_ref, dhn_ref, dout_ref, q_ref, k_ref, v_ref, probs_ref,
    n1_ref, n2_ref, wq_ref, wk_ref, wv_ref, wo_ref,
    dattn_ref, dq_ref, dk_ref, dv_ref, first_ref, rest_ref, dn1_ref, dn2_ref,
    dmid_ref,
):
    places, frames, width = x_ref.shape
    rows = places * frames

    @pl.when(pl.program_id(0) == 0)
    def _():
        dn1_ref[...] = jnp.zeros_like(dn1_ref)
        dn2_ref[...] = jnp.zeros_like(dn2_ref)

    mid = mid_ref[...].reshape(rows, width)
    dmid, gain = scale_back(mid, n2_ref[...], dhn_ref[...].reshape(rows, width))
    dn2_ref[...] += jnp.sum(gain, axis=0, keepdims=True)
    dmid = dmid + dout_ref[...].astype(F32).reshape(rows, width)
    dmid_ref[...] = dmid
    dattn = dmid.astype(LOW)
    dattn_ref[...] = dattn.reshape(places, frames, width)
    dmixed = mul_t(dattn, wo_ref[...]).astype(LOW).reshape(places, frames, width)
    sums, spread = head_sums(width), head_spread(width)
    pair = 0
    dk, dv = [None] * places, [None] * places
    add = lambda old, term: term if old is None else old + term
    for i in range(places):
        grad = dmixed[i].astype(F32)
        query = q_ref[i].astype(F32)
        dp = [sum_heads(grad * v_ref[j].astype(F32), sums) for j in range(i + 1)]
        delta = None
        for j in range(i + 1):
            delta = add(delta, probs_ref[pair + j] * dp[j])
        dq = None
        for j in range(i + 1):
            probs = probs_ref[pair + j]
            ds = (probs * (dp[j] - delta)).astype(LOW)
            ds = mul(ds, spread)
            dq = add(dq, ds * k_ref[j].astype(F32))
            dk[j] = add(dk[j], ds * query)
            dv[j] = add(dv[j], mul(probs.astype(LOW), spread) * grad)
        pair += i + 1
        dq_ref[i] = (dq * HD ** (-0.5)).astype(LOW)
    for j in range(places):
        dk_ref[j] = (dk[j] * HD ** (-0.5)).astype(LOW)
        dv_ref[j] = dv[j].astype(LOW)
    dnormed = (
        mul_t(dq_ref[...].reshape(rows, width), wq_ref[...])
        + mul_t(dk_ref[...].reshape(rows, width), wk_ref[...])
        + mul_t(dv_ref[...].reshape(rows, width), wv_ref[...])
    )
    x = x_ref[...].astype(F32).reshape(rows, width)
    dx, gain = scale_back(x, n1_ref[...], dnormed)
    dn1_ref[...] += jnp.sum(gain, axis=0, keepdims=True)
    dx = (dx + dmid_ref[...]).reshape(places, frames, width)
    first_ref[...] = dx[0]
    rest_ref[...] = dx[1:].astype(LOW)


def local_back(x, mid, dhn, dout, q, k, v, probs, params):
    places, frames, width = x.shape
    pairs = probs.shape[0]
    step = 64
    rows = pl.BlockSpec((places, step, width), lambda i: (0, i, 0))
    whole = lambda item: pl.BlockSpec(item.shape, lambda i: (0, 0), pipeline_mode=pl.Buffered(1))
    like = lambda kind: jax.ShapeDtypeStruct((places, frames, width), kind)
    fixed = (params[0].reshape(1, -1), params[5].reshape(1, -1)) + tuple(params[1:5])
    vector = pl.BlockSpec((1, width), lambda i: (0, 0))
    return pl.pallas_call(
        back_kernel,
        grid=(frames // step,),
        in_specs=[rows] * 7
        + [pl.BlockSpec((pairs, step, 128), lambda i: (0, i, 0))]
        + [whole(item) for item in fixed],
        out_specs=[rows] * 4
        + [
            pl.BlockSpec((step, width), lambda i: (i, 0)),
            pl.BlockSpec((places - 1, step, width), lambda i: (0, i, 0)),
            vector, vector,
        ],
        out_shape=[
            like(LOW), like(LOW), like(LOW), like(LOW),
            jax.ShapeDtypeStruct((frames, width), F32),
            jax.ShapeDtypeStruct((places - 1, frames, width), LOW),
            jax.ShapeDtypeStruct((1, width), F32),
            jax.ShapeDtypeStruct((1, width), F32),
        ],
        scratch_shapes=[pltpu.VMEM((places * step, width), F32)],
        compiler_params=pltpu.CompilerParams(vmem_limit_bytes=60 << 20),
    )(x, mid, dhn, dout, q, k, v, probs, *fixed)


def greet(count):
    utt, me = lax.axis_index("utt"), lax.axis_index("seq")
    barrier = pltpu.get_barrier_semaphore()

    @pl.loop(1, count)
    def _(step):
        pl.semaphore_signal(
            barrier, inc=1, device_id=(utt, lax.rem(me + step, count)), device_id_type=MESH_ID
        )

    return barrier


def remote(source, target, send_sem, recv_sem, place):
    return pltpu.make_async_remote_copy(
        src_ref=source,
        dst_ref=target,
        send_sem=send_sem,
        recv_sem=recv_sem,
        device_id=(lax.axis_index("utt"), place),
        device_id_type=MESH_ID,
    )


def two_heads(rows):
    lane = lax.broadcasted_iota(jnp.int32, rows.shape, 1)
    zero = jnp.zeros_like(rows)
    return jnp.concatenate([jnp.where(lane < HD, rows, zero), jnp.where(lane < HD, zero, rows)], axis=0)


def join_heads(tall):
    rows = tall.T
    lane = lax.broadcasted_iota(jnp.int32, (HD, LANES), 1)
    return jnp.where(lane < HD, rows[:HD], rows[HD:])


def masked_scores(scores, bias, first, block):
    key = first + lax.broadcasted_iota(jnp.int32, scores.shape, 0)
    query = block * HD + lax.rem(lax.broadcasted_iota(jnp.int32, scores.shape, 1), HD)
    return jnp.where(key < query, scores + bias, jnp.where(key == query, scores, NEGATIVE))


def fill_bias(bias_ref, mask):
    for block in range(mask.shape[0]):
        row = lax.broadcasted_iota(jnp.int32, (HD, LANES), 0)
        lane = lax.broadcasted_iota(jnp.int32, (HD, LANES), 1)
        flags = jnp.broadcast_to(mask[block, 0:1, :], (HD, LANES))
        diagonal = jnp.where(row == lane, flags.astype(F32), 0.0).astype(LOW)
        usable = mul(diagonal, jnp.ones((LANES, LANES), LOW))
        bias_ref[block * HD : (block + 1) * HD, :] = (usable - 1.0) * 1e30


def attend_kernel(
    count, x_ref, mask_ref, n1_ref, wq_ref, wk_ref, wv_ref,
    normed_ref, mixed_ref, saved_ref, log_ref,
    packed, held, mixed_all, pieces, bias, v_t, send_sem, recv_sem, send_two, recv_two, save_sem,
):
    share = count // 16
    me = lax.axis_index("seq")
    unit, part = me // share, me % share
    own_utt, own_pair = unit // 8, unit % 8
    own_cols = pl.ds(pl.multiple_of(own_pair * LANES, LANES), LANES)
    utts, frames, width = x_ref.shape
    barrier = greet(count)

    x = x_ref[...].astype(F32).reshape(utts * frames, width)
    normed = (x * scale_of(x) * n1_ref[...]).astype(LOW)
    normed_ref[...] = normed
    packed[:, 0:64] = (mul(normed, wq_ref[...]).astype(LOW)).reshape(utts, frames, width)
    packed[:, 64:128] = mul(normed, wk_ref[...]).astype(LOW).reshape(utts, frames, width)
    packed[:, 128:192] = mul(normed, wv_ref[...]).astype(LOW).reshape(utts, frames, width)
    for pair in range(8):
        packed[:, 192:208, pair * LANES : (pair + 1) * LANES] = jnp.broadcast_to(
            mask_ref[...], (utts, 16, LANES)
        )
    pl.semaphore_wait(barrier, count - 1)

    def outgoing(step):
        place = lax.rem(me + step, count)
        target = place // share
        cols = pl.ds(pl.multiple_of((target % 8) * LANES, LANES), LANES)
        return remote(
            packed.at[target // 8, :, cols], held.at[me], send_sem.at[step], recv_sem.at[step], place
        )

    @pl.loop(1, count)
    def _(step):
        outgoing(step).start()

    held[me] = packed[own_utt, :, own_cols]

    @pl.loop(1, count)
    def _(step):
        place = lax.rem(me + count - step, count)
        remote(held.at[place], held.at[place], send_sem.at[step], recv_sem.at[step], place).wait_recv()

    save = pltpu.make_async_copy(held, saved_ref, save_sem)
    save.start()
    v_t[...] = held[:, 128:192].reshape(count * HD, LANES).T
    fill_bias(bias, held[:, 192:208])

    def returning(block):
        return remote(
            pieces.at[block],
            mixed_all.at[own_utt, :, own_cols],
            send_two.at[block],
            recv_two.at[unit],
            block,
        )

    for group in range(count // 4):
        below = group * 256
        here = below + 256

        @pl.loop(0, 4 // share)
        def _(index):
            block = 4 * group + share * index + part
            query = two_heads(held[block, 0:64] * LOW(HD ** (-0.5)))
            keys = held[4 * group : 4 * group + 4, 64:128].reshape(256, LANES)
            near = masked_scores(mul_t(keys, query), bias[below:here], below, block)
            peak = jnp.max(near, axis=0, keepdims=True)
            if group:
                keys = held[0 : 4 * group, 64:128].reshape(below, LANES)
                far = mul_t(keys, query) + bias[0:below]
                peak = jnp.maximum(peak, jnp.max(far, axis=0, keepdims=True))
                far = jnp.exp(far - peak)
            near = jnp.exp(near - peak)
            total = jnp.sum(near, axis=0, keepdims=True)
            if group:
                total = total + jnp.sum(far, axis=0, keepdims=True)
            inverse = 1.0 / total
            mixed = mul(v_t[:, below:here], (near * inverse).astype(LOW))
            if group:
                mixed = mixed + mul(v_t[:, 0:below], (far * inverse).astype(LOW))
            log_ref[block] = jnp.broadcast_to(peak + jnp.log(total), (8, LANES))
            pieces[block] = join_heads(mixed).astype(LOW)

            @pl.when(block != me)
            def _():
                returning(block).start()

            @pl.when(block == me)
            def _():
                mixed_all[own_utt, :, own_cols] = pieces[block]

    @pl.loop(0, 16)
    def _(other):
        place = other * share + me % share
        cols = pl.ds(pl.multiple_of((other % 8) * LANES, LANES), LANES)

        @pl.when(place != me)
        def _():
            here = mixed_all.at[other // 8, :, cols]
            remote(here, here, send_two.at[0], recv_two.at[other], place).wait_recv()

    @pl.loop(1, count)
    def _(step):
        outgoing(step).wait_send()

    @pl.loop(0, count // share)
    def _(index):
        block = share * index + part

        @pl.when(block != me)
        def _():
            returning(block).wait_send()

    mixed_ref[...] = mixed_all[...]
    save.wait()


def global_attend(x, mask, params):
    count = lax.axis_size("seq")
    utts, frames, width = x.shape
    vmem = pl.BlockSpec(memory_space=pltpu.VMEM)
    hbm = pl.BlockSpec(memory_space=pl.ANY)
    return pl.pallas_call(
        functools.partial(attend_kernel, count),
        in_specs=[vmem] * 6,
        out_specs=[vmem, vmem, hbm, vmem],
        out_shape=[
            jax.ShapeDtypeStruct((utts * frames, width), LOW),
            jax.ShapeDtypeStruct((utts, frames, width), LOW),
            jax.ShapeDtypeStruct((count, 208, LANES), LOW),
            jax.ShapeDtypeStruct((count, 8, LANES), F32),
        ],
        scratch_shapes=[
            pltpu.VMEM((utts, 208, width), LOW),
            pltpu.VMEM((count, 208, LANES), LOW),
            pltpu.VMEM((utts, frames, width), LOW),
            pltpu.VMEM((count, HD, LANES), LOW),
            pltpu.VMEM((count * HD, LANES), F32),
            pltpu.VMEM((LANES, count * HD), LOW),
            pltpu.SemaphoreType.DMA((count,)),
            pltpu.SemaphoreType.DMA((count,)),
            pltpu.SemaphoreType.DMA((count,)),
            pltpu.SemaphoreType.DMA((16,)),
            pltpu.SemaphoreType.DMA,
        ],
        compiler_params=pltpu.CompilerParams(
            collective_id=2, has_side_effects=True, vmem_limit_bytes=48 << 20
        ),
    )(x, mask, params[0].reshape(1, -1), params[1], params[2], params[3])


def attend_back_kernel(
    count, grad_ref, held, log_ref,
    dqkv_ref,
    grads, landed, pieces, dk_acc, dv_acc, bias, k_t, send_sem, recv_sem, send_two, recv_two,
):
    share = count // 16
    me = lax.axis_index("seq")
    unit, part = me // share, me % share
    own_utt, own_pair = unit // 8, unit % 8
    own_cols = pl.ds(pl.multiple_of(own_pair * LANES, LANES), LANES)
    barrier = greet(count)
    k_t[...] = held[:, 64:128].reshape(count * HD, LANES).T
    fill_bias(bias, held[:, 192:208])
    dk_acc[...] = jnp.zeros_like(dk_acc)
    dv_acc[...] = jnp.zeros_like(dv_acc)
    pl.semaphore_wait(barrier, count - 1)

    def outgoing(other):
        cols = pl.ds(pl.multiple_of((other % 8) * LANES, LANES), LANES)
        place = other * share + part
        return place, remote(
            grad_ref.at[other // 8, :, cols], grads.at[me // share], send_sem.at[other],
            recv_sem.at[me // share], place,
        )

    @pl.loop(1, 16)
    def _(step):
        _, copy = outgoing(lax.rem(unit + step, 16))
        copy.start()

    grads[unit] = grad_ref[own_utt, :, own_cols]

    @pl.loop(1, 16)
    def _(step):
        other = lax.rem(unit + step, 16)
        here = grads.at[other]
        remote(here, here, send_sem.at[other], recv_sem.at[other], other * share + part).wait_recv()

    def returning(block):
        return remote(
            pieces.at[block],
            landed.at[part, :, own_utt, :, own_cols],
            send_two.at[block],
            recv_two.at[me],
            block,
        )

    for group in reversed(range(count // 4)):
        below = group * 256
        here = below + 256

        @pl.loop(0, 4 // share)
        def _(index):
            block = 4 * group + share * index + part
            query = two_heads(held[block, 0:64] * LOW(HD ** (-0.5)))
            grad = two_heads(grads[block // share])
            log_total = log_ref[block][0:1]
            near_v = held[4 * group : 4 * group + 4, 128:192].reshape(256, LANES)
            near_k = held[4 * group : 4 * group + 4, 64:128].reshape(256, LANES)
            near = masked_scores(mul_t(near_k, query), bias[below:here], below, block)
            near = jnp.exp(near - log_total)
            near_dp = mul_t(near_v, grad)
            delta = jnp.sum(near * near_dp, axis=0, keepdims=True)
            if group:
                far_v = held[0 : 4 * group, 128:192].reshape(below, LANES)
                far_k = held[0 : 4 * group, 64:128].reshape(below, LANES)
                far = jnp.exp(mul_t(far_k, query) + bias[0:below] - log_total)
                far_dp = mul_t(far_v, grad)
                delta = delta + jnp.sum(far * far_dp, axis=0, keepdims=True)
                far_ds = (far * (far_dp - delta)).astype(LOW)
                dk_acc[0:below] += mul(far_ds, query)
                dv_acc[0:below] += mul(far.astype(LOW), grad)
            near_ds = (near * (near_dp - delta)).astype(LOW)
            dk_acc[below:here] += mul(near_ds, query)
            dv_acc[below:here] += mul(near.astype(LOW), grad)
            dq = mul(k_t[:, below:here], near_ds)
            if group:
                dq = dq + mul(k_t[:, 0:below], far_ds)
            pieces[block, 0] = (join_heads(dq) * HD ** (-0.5)).astype(LOW)

        for block in range(4 * group, 4 * group + 4):
            rows = slice(block * HD, (block + 1) * HD)
            pieces[block, 1] = dk_acc[rows].astype(LOW)
            pieces[block, 2] = dv_acc[rows].astype(LOW)
            if share > 1:

                @pl.when(block % share != part)
                def _():
                    pieces[block, 0] = jnp.zeros((HD, LANES), LOW)

            @pl.when(block != me)
            def _():
                returning(block).start()

            @pl.when(block == me)
            def _():
                landed[part, :, own_utt, :, own_cols] = pieces[block]

    @pl.loop(1, count)
    def _(step):
        place = lax.rem(me + step, count)
        other, other_part = place // share, place % share
        cols = pl.ds(pl.multiple_of((other % 8) * LANES, LANES), LANES)
        here = landed.at[other_part, :, other // 8, :, cols]
        remote(here, here, send_two.at[place], recv_two.at[place], place).wait_recv()

    @pl.loop(1, 16)
    def _(step):
        _, copy = outgoing(lax.rem(unit + step, 16))
        copy.wait_send()

    @pl.loop(1, count)
    def _(step):
        returning(lax.rem(me + step, count)).wait_send()

    total = landed[0]
    for other_part in range(1, share):
        total = (total.astype(F32) + landed[other_part].astype(F32)).astype(LOW)
    dqkv_ref[...] = total


def global_attend_back(grad_mixed, saved, log_total):
    count = lax.axis_size("seq")
    utts, frames, width = grad_mixed.shape
    vmem = pl.BlockSpec(memory_space=pltpu.VMEM)
    return pl.pallas_call(
        functools.partial(attend_back_kernel, count),
        in_specs=[vmem] * 3,
        out_specs=vmem,
        out_shape=jax.ShapeDtypeStruct((3, utts, frames, width), LOW),
        scratch_shapes=[
            pltpu.VMEM((16, HD, LANES), LOW),
            pltpu.VMEM((count // 16, 3, utts, frames, width), LOW),
            pltpu.VMEM((count, 3, HD, LANES), LOW),
            pltpu.VMEM((count * HD, LANES), F32),
            pltpu.VMEM((count * HD, LANES), F32),
            pltpu.VMEM((count * HD, LANES), F32),
            pltpu.VMEM((LANES, count * HD), LOW),
            pltpu.SemaphoreType.DMA((16,)),
            pltpu.SemaphoreType.DMA((16,)),
            pltpu.SemaphoreType.DMA((count,)),
            pltpu.SemaphoreType.DMA((count,)),
        ],
        compiler_params=pltpu.CompilerParams(
            collective_id=3, has_side_effects=True, vmem_limit_bytes=48 << 20
        ),
    )(grad_mixed, saved, log_total)


def normalize(values, gain_vec):
    return (
        values * lax.rsqrt(jnp.mean(values * values, axis=-1, keepdims=True) + EPSILON) * gain_vec
    )


def gelu_fn(values):
    return jax.nn.gelu(values, approximate=True)


def project(left_side, weight):
    return jnp.dot(left_side, weight, preferred_element_type=jnp.float32)


def project_back(gradient, weight):
    return lax.dot_general(
        gradient, weight, (((1,), (1,)), ((), ())), preferred_element_type=jnp.float32
    )


def weight_grad(left_side, gradient):
    return lax.dot_general(
        left_side, gradient, (((0,), (0,)), ((), ())), preferred_element_type=jnp.float32
    )


def block_outputs(inputs, mixed_rows, params):
    middle = inputs + project(mixed_rows, params[4])
    middle_norm = normalize(middle, params[5]).astype(jnp.bfloat16)
    pre_active = project(middle_norm, params[6]) + params[7]
    active = gelu_fn(pre_active).astype(jnp.bfloat16)
    result = middle + project(active, params[8]) + params[9]
    return (result, (middle, middle_norm, pre_active, active))


def block_back(inputs, normed, mixed_rows, kept_parts, params, grad_out, attention_back):
    middle, middle_norm, pre_active, active = kept_parts
    grad_branch = grad_out.astype(jnp.bfloat16)
    grad_b_down = jnp.sum(grad_branch.astype(jnp.float32), axis=0)
    grad_w_down = weight_grad(active, grad_branch)
    grad_active = project_back(grad_branch, params[8])
    grad_pre = jax.vjp(gelu_fn, pre_active)[1](grad_active)[0].astype(jnp.bfloat16)
    grad_b_up = jnp.sum(grad_pre.astype(jnp.float32), axis=0)
    grad_w_up = weight_grad(middle_norm, grad_pre)
    middle_back = jax.vjp(normalize, middle, params[5])[1]
    grad_middle, grad_norm_two = middle_back(project_back(grad_pre, params[6]))
    grad_middle = grad_middle + grad_out
    grad_attn = grad_middle.astype(jnp.bfloat16)
    grad_w_output = weight_grad(mixed_rows, grad_attn)
    grad_mixed = project_back(grad_attn, params[4]).astype(jnp.bfloat16)
    grad_query, grad_key, grad_value = attention_back(grad_mixed)
    grad_normed = (
        project_back(grad_query, params[1])
        + project_back(grad_key, params[2])
        + project_back(grad_value, params[3])
    )
    input_back = jax.vjp(normalize, inputs, params[0])[1]
    grad_inputs, grad_norm_one = input_back(grad_normed)
    weight_grads = (
        grad_norm_one,
        weight_grad(normed, grad_query),
        weight_grad(normed, grad_key),
        weight_grad(normed, grad_value),
        grad_w_output,
        grad_norm_two,
        grad_w_up,
        grad_b_up,
        grad_w_down,
        grad_b_down,
    )
    return (grad_inputs + grad_middle, weight_grads)


def on_device(
    frames,
    codes,
    lengths,
    frame_mask,
    table,
    glob_norm_one,
    glob_w_query,
    glob_w_key,
    glob_w_value,
    glob_w_output,
    glob_norm_two,
    glob_w_up,
    glob_b_up,
    glob_w_down,
    glob_b_down,
    local_norm_one,
    local_w_query,
    local_w_key,
    local_w_value,
    local_w_output,
    local_norm_two,
    local_w_up,
    local_b_up,
    local_w_down,
    local_b_down,
    cotan_global,
    cotan_local,
):
    utter_count, frame_count, model_width = frames.shape
    row_count = utter_count * frame_count
    local_len = CB + 1
    positions = lax.axis_index("seq") * frame_count + jnp.arange(frame_count, dtype=jnp.int32)
    valid = positions[None, :] < lengths[:, None]
    usable = jnp.pad(frame_mask.astype(LOW), ((0, 0), (0, LANES - frame_count)))
    usable = jnp.broadcast_to(usable[:, None, :], (utter_count, 16, LANES))
    glob_params = (
        glob_norm_one,
        glob_w_query,
        glob_w_key,
        glob_w_value,
        glob_w_output,
        glob_norm_two,
        glob_w_up,
        glob_b_up,
        glob_w_down,
        glob_b_down,
    )
    local_params = (
        local_norm_one,
        local_w_query,
        local_w_key,
        local_w_value,
        local_w_output,
        local_norm_two,
        local_w_up,
        local_b_up,
        local_w_down,
        local_b_down,
    )
    global_in = frames.astype(jnp.float32).reshape(row_count, model_width)
    glob_normed, glob_mixed, saved, log_total = global_attend(frames, usable, glob_params)
    glob_mixed = glob_mixed.reshape(row_count, model_width)
    glob_result, glob_kept = block_outputs(global_in, glob_mixed, glob_params)
    global_rows = jnp.where(valid.reshape(row_count, 1), glob_result, 0.0).astype(jnp.bfloat16)
    code_rows = codes.transpose(2, 0, 1).reshape(CB, row_count)
    table_ids = code_rows + VOCAB * jnp.arange(CB, dtype=jnp.int32)[:, None]
    embedded = table.at[table_ids].get(mode="promise_in_bounds")
    local_in = jnp.concatenate([global_rows[None], embedded], axis=0)
    local_shape = (local_len, row_count, model_width)
    flat_shape = (local_len * row_count, model_width)
    normed, local_q, local_k, local_v, local_probs, mixed, middle, middle_norm = local_front(
        local_in, local_params
    )
    row_valid = valid.reshape(1, row_count, 1)
    local_cotan = cotan_local.transpose(2, 0, 1, 3).reshape(local_shape)
    local_cotan = jnp.where(row_valid, local_cotan, 0)
    local_result, grad_hidden, grad_w_up, grad_w_down, grad_b_up = local_ffn(
        middle_norm.reshape(flat_shape),
        local_cotan.reshape(flat_shape),
        middle.reshape(flat_shape),
        local_params,
    )
    local_rows = jnp.where(row_valid, local_result.reshape(local_shape), 0)
    local_rows = local_rows.reshape(local_len, utter_count, frame_count, model_width)
    local_rows = local_rows.transpose(1, 2, 0, 3)
    grad_attn, grad_q, grad_k, grad_v, grad_first, grad_rest, grad_n1, grad_n2 = local_back(
        local_in,
        middle,
        grad_hidden.reshape(local_shape),
        local_cotan,
        local_q,
        local_k,
        local_v,
        local_probs,
        local_params,
    )
    normed = normed.reshape(flat_shape)
    local_grads = (
        grad_n1[0],
        weight_grad(normed, grad_q.reshape(flat_shape)),
        weight_grad(normed, grad_k.reshape(flat_shape)),
        weight_grad(normed, grad_v.reshape(flat_shape)),
        weight_grad(mixed.reshape(flat_shape), grad_attn.reshape(flat_shape)),
        grad_n2[0],
        grad_w_up,
        grad_b_up[0],
        grad_w_down,
        jnp.sum(local_cotan.astype(F32), axis=(0, 1)),
    )
    picked = code_rows[:, None, :] == jnp.arange(VOCAB, dtype=jnp.int32)[None, :, None]
    grad_tab = jnp.einsum(
        "cvn,cnd->cvd", picked.astype(LOW), grad_rest, preferred_element_type=F32
    ).reshape(CB * VOCAB, model_width)
    grad_first = grad_first.reshape(utter_count, frame_count, model_width)
    glob_cotan = jnp.where(
        valid[:, :, None], cotan_global.astype(jnp.float32) + grad_first, 0.0
    )
    glob_cotan = glob_cotan.reshape(row_count, model_width)

    def global_back(grad_mixed):
        grads = global_attend_back(
            grad_mixed.reshape(utter_count, frame_count, model_width), saved, log_total
        )
        return tuple(grads.reshape(3, row_count, model_width))

    grad_inputs, glob_grads = block_back(
        global_in, glob_normed, glob_mixed, glob_kept, glob_params, glob_cotan, global_back
    )
    reduced = reduce_all((grad_tab,) + glob_grads + local_grads)
    return (
        global_rows.reshape(utter_count, frame_count, model_width),
        local_rows,
        grad_inputs.reshape(utter_count, frame_count, model_width),
    ) + reduced


def solution(mesh):
    return jax.shard_map(
        on_device,
        mesh=mesh,
        in_specs=(
            P("utt", "seq", None),
            P("utt", "seq", None),
            P("utt"),
            P("utt", "seq"),
            P(),
            P(),
            P(),
            P(),
            P(),
            P(),
            P(),
            P(),
            P(),
            P(),
            P(),
            P(),
            P(),
            P(),
            P(),
            P(),
            P(),
            P(),
            P(),
            P(),
            P(),
            P("utt", "seq", None),
            P("utt", "seq", None, None),
        ),
        out_specs=(
            P("utt", "seq", None),
            P("utt", "seq", None, None),
            P("utt", "seq", None),
            P("seq", None),
            P("seq"),
            P("seq", None),
            P("seq", None),
            P("seq", None),
            P("seq", None),
            P("seq"),
            P("seq", None),
            P("seq"),
            P("seq", None),
            P("seq"),
            P("seq"),
            P("seq", None),
            P("seq", None),
            P("seq", None),
            P("seq", None),
            P("seq"),
            P("seq", None),
            P("seq"),
            P("seq", None),
            P("seq"),
        ),
        check_vma=False,
    )
```

```python
import functools
import types

import jax
import jax.numpy as jnp
from jax import lax
from jax.experimental import pallas as pl
from jax.experimental.pallas import tpu as pltpu
from jax.sharding import PartitionSpec as P

H = 16
HD = 64
CB = 3
VOCAB = 1024


EPSILON = 1e-05
NEGATIVE = -1e30
F32 = jnp.float32
LOW = jnp.bfloat16
LANES = 128
MESH_ID = pl.DeviceIdType.MESH


def reduce_all(grads):
    return tuple(
        lax.psum(
            lax.psum_scatter(item.astype(LOW), "seq", scatter_dimension=0, tiled=True), "utt"
        ).astype(F32)
        for item in grads
    )


def mul(left_side, right_side):
    return jnp.dot(left_side, right_side, preferred_element_type=F32)


def mul_t(left_side, right_side):
    return lax.dot_general(
        left_side, right_side, (((1,), (1,)), ((), ())), preferred_element_type=F32
    )


def t_mul(left_side, right_side):
    return lax.dot_general(
        left_side, right_side, (((0,), (0,)), ((), ())), preferred_element_type=F32
    )


def scale_of(values):
    return lax.rsqrt(jnp.mean(values * values, axis=-1, keepdims=True) + EPSILON)


def scale_back(values, gain, grad):
    scale = scale_of(values)
    inner = grad * gain
    shared = jnp.mean(values * inner, axis=-1, keepdims=True) * (scale * scale * scale)
    return inner * scale - values * shared, grad * values * scale


def head_sums(width):
    rows = lax.broadcasted_iota(jnp.int32, (width, 128), 0) // HD
    cols = lax.broadcasted_iota(jnp.int32, (width, 128), 1)
    return (rows == cols).astype(LOW)


def head_spread(width):
    rows = lax.broadcasted_iota(jnp.int32, (128, width), 0)
    cols = lax.broadcasted_iota(jnp.int32, (128, width), 1) // HD
    return (rows == cols).astype(LOW)


def sum_heads(product, sums):
    high = product.astype(LOW)
    rest = (product - high.astype(F32)).astype(LOW)
    return mul(high, sums) + mul(rest, sums)


def front_kernel(
    x_ref, n1_ref, wq_ref, wk_ref, wv_ref, wo_ref, n2_ref,
    normed_ref, q_ref, k_ref, v_ref, probs_ref, mixed_ref, mid_ref, mid_norm_ref,
):
    places, frames, width = x_ref.shape
    rows = places * frames
    x = x_ref[...].astype(F32).reshape(rows, width)
    normed = (x * scale_of(x) * n1_ref[...]).astype(LOW)
    normed_ref[...] = normed.reshape(places, frames, width)
    q_ref[...] = mul(normed, wq_ref[...]).astype(LOW).reshape(places, frames, width)
    k_ref[...] = mul(normed, wk_ref[...]).astype(LOW).reshape(places, frames, width)
    v_ref[...] = mul(normed, wv_ref[...]).astype(LOW).reshape(places, frames, width)
    sums, spread = head_sums(width), head_spread(width)
    pair = 0
    for i in range(places):
        query = q_ref[i].astype(F32)
        scores = [
            sum_heads(query * k_ref[j].astype(F32), sums) * HD ** (-0.5) for j in range(i + 1)
        ]
        peak = scores[0]
        for item in scores[1:]:
            peak = jnp.maximum(peak, item)
        raised = [jnp.exp(item - peak) for item in scores]
        total = raised[0]
        for item in raised[1:]:
            total = total + item
        mixed = None
        for j in range(i + 1):
            probs = raised[j] / total
            probs_ref[pair] = probs
            pair += 1
            term = mul(probs.astype(LOW), spread) * v_ref[j].astype(F32)
            mixed = term if mixed is None else mixed + term
        mixed_ref[i] = mixed.astype(LOW)
    mid = x + mul(mixed_ref[...].reshape(rows, width), wo_ref[...])
    mid_ref[...] = mid.reshape(places, frames, width)
    mid_norm_ref[...] = (
        (mid * scale_of(mid) * n2_ref[...]).astype(LOW).reshape(places, frames, width)
    )


def local_front(x, params):
    places, frames, width = x.shape
    pairs = places * (places + 1) // 2
    step = 64
    rows = pl.BlockSpec((places, step, width), lambda i: (0, i, 0))
    whole = lambda item: pl.BlockSpec(item.shape, lambda i: (0, 0), pipeline_mode=pl.Buffered(1))
    n1, n2 = params[0].reshape(1, -1), params[5].reshape(1, -1)
    operands = (x, n1, params[1], params[2], params[3], params[4], n2)
    like = lambda kind: jax.ShapeDtypeStruct((places, frames, width), kind)
    return pl.pallas_call(
        front_kernel,
        grid=(frames // step,),
        in_specs=[rows] + [whole(item) for item in operands[1:]],
        out_specs=[rows] * 4
        + [pl.BlockSpec((pairs, step, 128), lambda i: (0, i, 0))]
        + [rows] * 3,
        out_shape=[
            like(LOW), like(LOW), like(LOW), like(LOW),
            jax.ShapeDtypeStruct((pairs, frames, 128), F32),
            like(LOW), like(F32), like(LOW),
        ],
        compiler_params=pltpu.CompilerParams(vmem_limit_bytes=56 << 20),
    )(*operands)


def gelu_parts(u):
    scale = 0.7978845608028654
    inner = jnp.tanh(scale * (u + 0.044715 * u * u * u))
    half = 0.5 * (1.0 + inner)
    slope = half + 0.5 * u * (1.0 - inner * inner) * scale * (1.0 + 3 * 0.044715 * u * u)
    return u * half, slope


def ffn_kernel(
    hn_ref, dout_ref, mid_ref, w1_ref, b1_ref, w2_ref, b2_ref,
    y_ref, dhn_ref, dw1_ref, dw2_ref, db1_ref, acc_ref, hn_t_ref,
):
    at = pl.program_id(0)
    last = pl.num_programs(0) - 1

    @pl.when(at == 0)
    def _():
        hn_t_ref[...] = hn_ref[...].T
        acc_ref[...] = mid_ref[...] + b2_ref[...]
        dhn_ref[...] = jnp.zeros_like(dhn_ref)

    hn, dout = hn_ref[...], dout_ref[...]
    u = mul(hn, w1_ref[...]) + b1_ref[...]
    act, slope = gelu_parts(u)
    act = act.astype(LOW)
    acc_ref[...] += mul(act, w2_ref[...])
    du = (mul_t(dout, w2_ref[...]) * slope).astype(LOW)
    db1_ref[...] = jnp.sum(du.astype(F32), axis=0, keepdims=True)
    dhn_ref[...] += mul_t(du, w1_ref[...])
    dw1_ref[...] = mul(hn_t_ref[...], du).astype(LOW)
    dw2_ref[...] = t_mul(act, dout).astype(LOW)

    @pl.when(at == last)
    def _():
        y_ref[...] = acc_ref[...].astype(LOW)


def local_ffn(hn, dout, mid, params):
    rows, width = hn.shape
    wide = params[6].shape[1]
    step = 512
    whole = pl.BlockSpec((rows, width), lambda i: (0, 0), pipeline_mode=pl.Buffered(1))
    out_whole = pl.BlockSpec((rows, width), lambda i: (0, 0))
    return pl.pallas_call(
        ffn_kernel,
        grid=(wide // step,),
        in_specs=[
            whole, whole, whole,
            pl.BlockSpec((width, step), lambda i: (0, i)),
            pl.BlockSpec((1, step), lambda i: (0, i)),
            pl.BlockSpec((step, width), lambda i: (i, 0)),
            pl.BlockSpec((1, width), lambda i: (0, 0)),
        ],
        out_specs=[
            out_whole, out_whole,
            pl.BlockSpec((width, step), lambda i: (0, i)),
            pl.BlockSpec((step, width), lambda i: (i, 0)),
            pl.BlockSpec((1, step), lambda i: (0, i)),
        ],
        out_shape=[
            jax.ShapeDtypeStruct((rows, width), LOW),
            jax.ShapeDtypeStruct((rows, width), F32),
            jax.ShapeDtypeStruct((width, wide), LOW),
            jax.ShapeDtypeStruct((wide, width), LOW),
            jax.ShapeDtypeStruct((1, wide), F32),
        ],
        scratch_shapes=[pltpu.VMEM((rows, width), F32), pltpu.VMEM((width, rows), LOW)],
        compiler_params=pltpu.CompilerParams(vmem_limit_bytes=56 << 20),
    )(hn, dout, mid, params[6], params[7].reshape(1, -1), params[8], params[9].reshape(1, -1))


def back_kernel(
    x_ref, mid_ref, dhn_ref, dout_ref, q_ref, k_ref, v_ref, probs_ref,
    n1_ref, n2_ref, wq_ref, wk_ref, wv_ref, wo_ref,
    dattn_ref, dq_ref, dk_ref, dv_ref, first_ref, rest_ref, dn1_ref, dn2_ref,
    dmid_ref,
):
    places, frames, width = x_ref.shape
    rows = places * frames

    @pl.when(pl.program_id(0) == 0)
    def _():
        dn1_ref[...] = jnp.zeros_like(dn1_ref)
        dn2_ref[...] = jnp.zeros_like(dn2_ref)

    mid = mid_ref[...].reshape(rows, width)
    dmid, gain = scale_back(mid, n2_ref[...], dhn_ref[...].reshape(rows, width))
    dn2_ref[...] += jnp.sum(gain, axis=0, keepdims=True)
    dmid = dmid + dout_ref[...].astype(F32).reshape(rows, width)
    dmid_ref[...] = dmid
    dattn = dmid.astype(LOW)
    dattn_ref[...] = dattn.reshape(places, frames, width)
    dmixed = mul_t(dattn, wo_ref[...]).astype(LOW).reshape(places, frames, width)
    sums, spread = head_sums(width), head_spread(width)
    pair = 0
    dk, dv = [None] * places, [None] * places
    add = lambda old, term: term if old is None else old + term
    for i in range(places):
        grad = dmixed[i].astype(F32)
        query = q_ref[i].astype(F32)
        dp = [sum_heads(grad * v_ref[j].astype(F32), sums) for j in range(i + 1)]
        delta = None
        for j in range(i + 1):
            delta = add(delta, probs_ref[pair + j] * dp[j])
        dq = None
        for j in range(i + 1):
            probs = probs_ref[pair + j]
            ds = (probs * (dp[j] - delta)).astype(LOW)
            ds = mul(ds, spread)
            dq = add(dq, ds * k_ref[j].astype(F32))
            dk[j] = add(dk[j], ds * query)
            dv[j] = add(dv[j], mul(probs.astype(LOW), spread) * grad)
        pair += i + 1
        dq_ref[i] = (dq * HD ** (-0.5)).astype(LOW)
    for j in range(places):
        dk_ref[j] = (dk[j] * HD ** (-0.5)).astype(LOW)
        dv_ref[j] = dv[j].astype(LOW)
    dnormed = (
        mul_t(dq_ref[...].reshape(rows, width), wq_ref[...])
        + mul_t(dk_ref[...].reshape(rows, width), wk_ref[...])
        + mul_t(dv_ref[...].reshape(rows, width), wv_ref[...])
    )
    x = x_ref[...].astype(F32).reshape(rows, width)
    dx, gain = scale_back(x, n1_ref[...], dnormed)
    dn1_ref[...] += jnp.sum(gain, axis=0, keepdims=True)
    dx = (dx + dmid_ref[...]).reshape(places, frames, width)
    first_ref[...] = dx[0]
    rest_ref[...] = dx[1:].astype(LOW)


def local_back(x, mid, dhn, dout, q, k, v, probs, params):
    places, frames, width = x.shape
    pairs = probs.shape[0]
    step = 64
    rows = pl.BlockSpec((places, step, width), lambda i: (0, i, 0))
    whole = lambda item: pl.BlockSpec(item.shape, lambda i: (0, 0), pipeline_mode=pl.Buffered(1))
    like = lambda kind: jax.ShapeDtypeStruct((places, frames, width), kind)
    fixed = (params[0].reshape(1, -1), params[5].reshape(1, -1)) + tuple(params[1:5])
    vector = pl.BlockSpec((1, width), lambda i: (0, 0))
    return pl.pallas_call(
        back_kernel,
        grid=(frames // step,),
        in_specs=[rows] * 7
        + [pl.BlockSpec((pairs, step, 128), lambda i: (0, i, 0))]
        + [whole(item) for item in fixed],
        out_specs=[rows] * 4
        + [
            pl.BlockSpec((step, width), lambda i: (i, 0)),
            pl.BlockSpec((places - 1, step, width), lambda i: (0, i, 0)),
            vector, vector,
        ],
        out_shape=[
            like(LOW), like(LOW), like(LOW), like(LOW),
            jax.ShapeDtypeStruct((frames, width), F32),
            jax.ShapeDtypeStruct((places - 1, frames, width), LOW),
            jax.ShapeDtypeStruct((1, width), F32),
            jax.ShapeDtypeStruct((1, width), F32),
        ],
        scratch_shapes=[pltpu.VMEM((places * step, width), F32)],
        compiler_params=pltpu.CompilerParams(vmem_limit_bytes=60 << 20),
    )(x, mid, dhn, dout, q, k, v, probs, *fixed)


def greet(count):
    utt, me = lax.axis_index("utt"), lax.axis_index("seq")
    barrier = pltpu.get_barrier_semaphore()

    @pl.loop(1, count)
    def _(step):
        pl.semaphore_signal(
            barrier, inc=1, device_id=(utt, lax.rem(me + step, count)), device_id_type=MESH_ID
        )

    return barrier


def remote(source, target, send_sem, recv_sem, place):
    return pltpu.make_async_remote_copy(
        src_ref=source,
        dst_ref=target,
        send_sem=send_sem,
        recv_sem=recv_sem,
        device_id=(lax.axis_index("utt"), place),
        device_id_type=MESH_ID,
    )


def two_heads(rows):
    lane = lax.broadcasted_iota(jnp.int32, rows.shape, 1)
    zero = jnp.zeros_like(rows)
    return jnp.concatenate([jnp.where(lane < HD, rows, zero), jnp.where(lane < HD, zero, rows)], axis=0)


def join_heads(tall):
    rows = tall.T
    lane = lax.broadcasted_iota(jnp.int32, (HD, LANES), 1)
    return jnp.where(lane < HD, rows[:HD], rows[HD:])


def masked_scores(scores, bias, first, block):
    key = first + lax.broadcasted_iota(jnp.int32, scores.shape, 0)
    query = block * HD + lax.rem(lax.broadcasted_iota(jnp.int32, scores.shape, 1), HD)
    return jnp.where(key < query, scores + bias, jnp.where(key == query, scores, NEGATIVE))


def fill_bias(bias_ref, mask):
    for block in range(mask.shape[0]):
        row = lax.broadcasted_iota(jnp.int32, (HD, LANES), 0)
        lane = lax.broadcasted_iota(jnp.int32, (HD, LANES), 1)
        flags = jnp.broadcast_to(mask[block, 0:1, :], (HD, LANES))
        diagonal = jnp.where(row == lane, flags.astype(F32), 0.0).astype(LOW)
        usable = mul(diagonal, jnp.ones((LANES, LANES), LOW))
        bias_ref[block * HD : (block + 1) * HD, :] = (usable - 1.0) * 1e30


def attend_kernel(
    count, x_ref, mask_ref, n1_ref, wq_ref, wk_ref, wv_ref,
    normed_ref, mixed_ref, saved_ref, log_ref,
    packed, held, mixed_all, pieces, bias, v_t, send_sem, recv_sem, send_two, recv_two, save_sem,
):
    share = count // 16
    me = lax.axis_index("seq")
    unit, part = me // share, me % share
    own_utt, own_pair = unit // 8, unit % 8
    own_cols = pl.ds(pl.multiple_of(own_pair * LANES, LANES), LANES)
    utts, frames, width = x_ref.shape
    barrier = greet(count)

    x = x_ref[...].astype(F32).reshape(utts * frames, width)
    normed = (x * scale_of(x) * n1_ref[...]).astype(LOW)
    normed_ref[...] = normed
    packed[:, 0:64] = (mul(normed, wq_ref[...]).astype(LOW)).reshape(utts, frames, width)
    packed[:, 64:128] = mul(normed, wk_ref[...]).astype(LOW).reshape(utts, frames, width)
    packed[:, 128:192] = mul(normed, wv_ref[...]).astype(LOW).reshape(utts, frames, width)
    for pair in range(8):
        packed[:, 192:208, pair * LANES : (pair + 1) * LANES] = jnp.broadcast_to(
            mask_ref[...], (utts, 16, LANES)
        )
    pl.semaphore_wait(barrier, count - 1)

    def outgoing(step):
        place = lax.rem(me + step, count)
        target = place // share
        cols = pl.ds(pl.multiple_of((target % 8) * LANES, LANES), LANES)
        return remote(
            packed.at[target // 8, :, cols], held.at[me], send_sem.at[step], recv_sem.at[step], place
        )

    @pl.loop(1, count)
    def _(step):
        outgoing(step).start()

    held[me] = packed[own_utt, :, own_cols]

    @pl.loop(1, count)
    def _(step):
        place = lax.rem(me + count - step, count)
        remote(held.at[place], held.at[place], send_sem.at[step], recv_sem.at[step], place).wait_recv()

    save = pltpu.make_async_copy(held, saved_ref, save_sem)
    save.start()
    v_t[...] = held[:, 128:192].reshape(count * HD, LANES).T
    fill_bias(bias, held[:, 192:208])

    def returning(block):
        return remote(
            pieces.at[block],
            mixed_all.at[own_utt, :, own_cols],
            send_two.at[block],
            recv_two.at[unit],
            block,
        )

    for group in range(count // 4):
        below = group * 256
        here = below + 256

        @pl.loop(0, 4 // share)
        def _(index):
            block = 4 * group + share * index + part
            query = two_heads(held[block, 0:64] * LOW(HD ** (-0.5)))
            keys = held[4 * group : 4 * group + 4, 64:128].reshape(256, LANES)
            near = masked_scores(mul_t(keys, query), bias[below:here], below, block)
            peak = jnp.max(near, axis=0, keepdims=True)
            if group:
                keys = held[0 : 4 * group, 64:128].reshape(below, LANES)
                far = mul_t(keys, query) + bias[0:below]
                peak = jnp.maximum(peak, jnp.max(far, axis=0, keepdims=True))
                far = jnp.exp(far - peak)
            near = jnp.exp(near - peak)
            total = jnp.sum(near, axis=0, keepdims=True)
            if group:
                total = total + jnp.sum(far, axis=0, keepdims=True)
            inverse = 1.0 / total
            mixed = mul(v_t[:, below:here], (near * inverse).astype(LOW))
            if group:
                mixed = mixed + mul(v_t[:, 0:below], (far * inverse).astype(LOW))
            log_ref[block] = jnp.broadcast_to(peak + jnp.log(total), (8, LANES))
            pieces[block] = join_heads(mixed).astype(LOW)

            @pl.when(block != me)
            def _():
                returning(block).start()

            @pl.when(block == me)
            def _():
                mixed_all[own_utt, :, own_cols] = pieces[block]

    @pl.loop(0, 16)
    def _(other):
        place = other * share + me % share
        cols = pl.ds(pl.multiple_of((other % 8) * LANES, LANES), LANES)

        @pl.when(place != me)
        def _():
            here = mixed_all.at[other // 8, :, cols]
            remote(here, here, send_two.at[0], recv_two.at[other], place).wait_recv()

    @pl.loop(1, count)
    def _(step):
        outgoing(step).wait_send()

    @pl.loop(0, count // share)
    def _(index):
        block = share * index + part

        @pl.when(block != me)
        def _():
            returning(block).wait_send()

    mixed_ref[...] = mixed_all[...]
    save.wait()


def global_attend(x, mask, params):
    count = lax.axis_size("seq")
    utts, frames, width = x.shape
    vmem = pl.BlockSpec(memory_space=pltpu.VMEM)
    hbm = pl.BlockSpec(memory_space=pl.ANY)
    return pl.pallas_call(
        functools.partial(attend_kernel, count),
        in_specs=[vmem] * 6,
        out_specs=[vmem, vmem, hbm, vmem],
        out_shape=[
            jax.ShapeDtypeStruct((utts * frames, width), LOW),
            jax.ShapeDtypeStruct((utts, frames, width), LOW),
            jax.ShapeDtypeStruct((count, 208, LANES), LOW),
            jax.ShapeDtypeStruct((count, 8, LANES), F32),
        ],
        scratch_shapes=[
            pltpu.VMEM((utts, 208, width), LOW),
            pltpu.VMEM((count, 208, LANES), LOW),
            pltpu.VMEM((utts, frames, width), LOW),
            pltpu.VMEM((count, HD, LANES), LOW),
            pltpu.VMEM((count * HD, LANES), F32),
            pltpu.VMEM((LANES, count * HD), LOW),
            pltpu.SemaphoreType.DMA((count,)),
            pltpu.SemaphoreType.DMA((count,)),
            pltpu.SemaphoreType.DMA((count,)),
            pltpu.SemaphoreType.DMA((16,)),
            pltpu.SemaphoreType.DMA,
        ],
        compiler_params=pltpu.CompilerParams(
            collective_id=2, has_side_effects=True, vmem_limit_bytes=48 << 20
        ),
    )(x, mask, params[0].reshape(1, -1), params[1], params[2], params[3])


def attend_back_kernel(
    count, grad_ref, held, log_ref,
    dqkv_ref,
    grads, landed, pieces, dk_acc, dv_acc, bias, k_t, send_sem, recv_sem, send_two, recv_two,
):
    share = count // 16
    me = lax.axis_index("seq")
    unit, part = me // share, me % share
    own_utt, own_pair = unit // 8, unit % 8
    own_cols = pl.ds(pl.multiple_of(own_pair * LANES, LANES), LANES)
    barrier = greet(count)
    k_t[...] = held[:, 64:128].reshape(count * HD, LANES).T
    fill_bias(bias, held[:, 192:208])
    dk_acc[...] = jnp.zeros_like(dk_acc)
    dv_acc[...] = jnp.zeros_like(dv_acc)
    pl.semaphore_wait(barrier, count - 1)

    def outgoing(other):
        cols = pl.ds(pl.multiple_of((other % 8) * LANES, LANES), LANES)
        place = other * share + part
        return place, remote(
            grad_ref.at[other // 8, :, cols], grads.at[me // share], send_sem.at[other],
            recv_sem.at[me // share], place,
        )

    @pl.loop(1, 16)
    def _(step):
        _, copy = outgoing(lax.rem(unit + step, 16))
        copy.start()

    grads[unit] = grad_ref[own_utt, :, own_cols]

    @pl.loop(1, 16)
    def _(step):
        other = lax.rem(unit + step, 16)
        here = grads.at[other]
        remote(here, here, send_sem.at[other], recv_sem.at[other], other * share + part).wait_recv()

    def returning(block):
        return remote(
            pieces.at[block],
            landed.at[part, :, own_utt, :, own_cols],
            send_two.at[block],
            recv_two.at[me],
            block,
        )

    for group in reversed(range(count // 4)):
        below = group * 256
        here = below + 256

        @pl.loop(0, 4 // share)
        def _(index):
            block = 4 * group + share * index + part
            query = two_heads(held[block, 0:64] * LOW(HD ** (-0.5)))
            grad = two_heads(grads[block // share])
            log_total = log_ref[block][0:1]
            near_v = held[4 * group : 4 * group + 4, 128:192].reshape(256, LANES)
            near_k = held[4 * group : 4 * group + 4, 64:128].reshape(256, LANES)
            near = masked_scores(mul_t(near_k, query), bias[below:here], below, block)
            near = jnp.exp(near - log_total)
            near_dp = mul_t(near_v, grad)
            delta = jnp.sum(near * near_dp, axis=0, keepdims=True)
            if group:
                far_v = held[0 : 4 * group, 128:192].reshape(below, LANES)
                far_k = held[0 : 4 * group, 64:128].reshape(below, LANES)
                far = jnp.exp(mul_t(far_k, query) + bias[0:below] - log_total)
                far_dp = mul_t(far_v, grad)
                delta = delta + jnp.sum(far * far_dp, axis=0, keepdims=True)
                far_ds = (far * (far_dp - delta)).astype(LOW)
                dk_acc[0:below] += mul(far_ds, query)
                dv_acc[0:below] += mul(far.astype(LOW), grad)
            near_ds = (near * (near_dp - delta)).astype(LOW)
            dk_acc[below:here] += mul(near_ds, query)
            dv_acc[below:here] += mul(near.astype(LOW), grad)
            dq = mul(k_t[:, below:here], near_ds)
            if group:
                dq = dq + mul(k_t[:, 0:below], far_ds)
            pieces[block, 0] = (join_heads(dq) * HD ** (-0.5)).astype(LOW)

        for block in range(4 * group, 4 * group + 4):
            rows = slice(block * HD, (block + 1) * HD)
            pieces[block, 1] = dk_acc[rows].astype(LOW)
            pieces[block, 2] = dv_acc[rows].astype(LOW)
            if share > 1:

                @pl.when(block % share != part)
                def _():
                    pieces[block, 0] = jnp.zeros((HD, LANES), LOW)

            @pl.when(block != me)
            def _():
                returning(block).start()

            @pl.when(block == me)
            def _():
                landed[part, :, own_utt, :, own_cols] = pieces[block]

    @pl.loop(1, count)
    def _(step):
        place = lax.rem(me + step, count)
        other, other_part = place // share, place % share
        cols = pl.ds(pl.multiple_of((other % 8) * LANES, LANES), LANES)
        here = landed.at[other_part, :, other // 8, :, cols]
        remote(here, here, send_two.at[place], recv_two.at[place], place).wait_recv()

    @pl.loop(1, 16)
    def _(step):
        _, copy = outgoing(lax.rem(unit + step, 16))
        copy.wait_send()

    @pl.loop(1, count)
    def _(step):
        returning(lax.rem(me + step, count)).wait_send()

    total = landed[0]
    for other_part in range(1, share):
        total = (total.astype(F32) + landed[other_part].astype(F32)).astype(LOW)
    dqkv_ref[...] = total


def global_attend_back(grad_mixed, saved, log_total):
    count = lax.axis_size("seq")
    utts, frames, width = grad_mixed.shape
    vmem = pl.BlockSpec(memory_space=pltpu.VMEM)
    return pl.pallas_call(
        functools.partial(attend_back_kernel, count),
        in_specs=[vmem] * 3,
        out_specs=vmem,
        out_shape=jax.ShapeDtypeStruct((3, utts, frames, width), LOW),
        scratch_shapes=[
            pltpu.VMEM((16, HD, LANES), LOW),
            pltpu.VMEM((count // 16, 3, utts, frames, width), LOW),
            pltpu.VMEM((count, 3, HD, LANES), LOW),
            pltpu.VMEM((count * HD, LANES), F32),
            pltpu.VMEM((count * HD, LANES), F32),
            pltpu.VMEM((count * HD, LANES), F32),
            pltpu.VMEM((LANES, count * HD), LOW),
            pltpu.SemaphoreType.DMA((16,)),
            pltpu.SemaphoreType.DMA((16,)),
            pltpu.SemaphoreType.DMA((count,)),
            pltpu.SemaphoreType.DMA((count,)),
        ],
        compiler_params=pltpu.CompilerParams(
            collective_id=3, has_side_effects=True, vmem_limit_bytes=48 << 20
        ),
    )(grad_mixed, saved, log_total)


SLOTS = 4
DEEP = 8
SROWS = 64
SCOLS = 512
DRAIN = 8
PLAN = (
    (0, 8, 8), (8, 8, 2), (16, 2, 2), (18, 2, 2), (20, 2, 2), (22, 2, 2), (24, 6, 2),
    (30, 8, 2), (38, 8, 8), (46, 2, 2), (48, 2, 2), (50, 2, 2), (52, 2, 2), (54, 1, 1),
)
SLABS = 55
LOADED = 16
AT_BACK = 8
AT_ATTEND = 10
AT_LANDED = 20


def tail_kernel(names, out_count, *refs):
    r = types.SimpleNamespace(**dict(zip(names, refs)))
    outs = refs[names.index("out_0") : names.index("out_0") + out_count]
    utt = lax.axis_index("utt")
    seq = lax.axis_index("seq")
    count = 16
    pos = seq // 4
    col = (seq // 2) % 2
    core = seq % 2
    core_id = (utt, pos * 4 + col * 2 + 1 - core)
    col_id = (utt, pos * 4 + (1 - col) * 2 + core)
    utt_id = (1 - utt, seq)
    right_id = (utt, lax.rem(seq + 4, 16))
    left_id = (utt, lax.rem(seq + 12, 16))

    barrier = greet(count)
    pl.semaphore_signal(barrier, inc=1, device_id=utt_id, device_id_type=MESH_ID)

    def window(ref, spec, slab, lead):
        local = slab - spec[0]
        rows = pl.ds(pl.multiple_of((local // spec[2]) * SROWS, SROWS), SROWS)
        cols = pl.ds(pl.multiple_of((local % spec[2]) * SCOLS, SCOLS), SCOLS)
        return ref.at[lead + (rows, cols)]

    def load_start(slab):
        slot = slab % SLOTS
        for ref, spec in ((r.l_up, PLAN[0]), (r.l_down, PLAN[1])):

            @pl.when((slab >= spec[0]) & (slab < spec[0] + spec[1]))
            def _():
                for side in range(2):
                    pltpu.make_async_copy(
                        window(ref, spec, slab, (slice(None), side)),
                        r.part.at[slot, side],
                        r.load_sem.at[slot, side],
                    ).start()

    def load_wait(slot):
        for side in range(2):
            pltpu.make_async_copy(
                r.l_up.at[:, side, pl.ds(0, SROWS), pl.ds(0, SCOLS)],
                r.part.at[slot, side],
                r.load_sem.at[slot, side],
            ).wait()

    def weights(block, slot):
        start = block * SCOLS if isinstance(block, int) else pl.multiple_of(block * SCOLS, SCOLS)
        return (
            pltpu.make_async_copy(
                r.g_w_up.at[:, pl.ds(start, SCOLS)], r.up_buf.at[slot], r.weight_sem.at[slot, 0]
            ),
            pltpu.make_async_copy(
                r.g_w_down.at[pl.ds(start, SCOLS)], r.down_buf.at[slot], r.weight_sem.at[slot, 1]
            ),
        )

    fetches = (
        (r.g_w_o, r.square.at[0]), (r.g_w_q, r.square.at[1]), (r.g_w_k, r.square.at[2]),
        (r.g_w_v, r.square.at[3]), (r.saved, r.held), (r.l_normed, r.l_x.at[0]),
        (r.l_mixed, r.l_x.at[1]), (r.l_dq, r.l_g.at[0]), (r.l_dk, r.l_g.at[1]),
        (r.l_dv, r.l_g.at[2]), (r.l_dattn, r.l_g.at[3]), (r.rest, r.table_g),
        (r.g_act, r.act_buf), (r.g_mixed, r.g_x.at[0]), (r.g_normed, r.g_x.at[1]),
    )

    def fetch(*which):
        return [
            pltpu.make_async_copy(*fetches[index], r.fetch_sem.at[index]) for index in which
        ]

    for copy in weights(0, 0) + tuple(fetch(0)):
        copy.start()
    load_start(0)

    def send(kind, slot, source, target, device):
        return pltpu.make_async_remote_copy(
            src_ref=source,
            dst_ref=target,
            send_sem=r.send_sem.at[kind, slot],
            recv_sem=r.recv_sem.at[kind, slot],
            device_id=device,
            device_id_type=MESH_ID,
        )

    def core_copy(slot):
        return send(0, slot, r.part.at[slot, 1 - core], r.recv_c.at[slot], core_id)

    def col_copy_a(slot):
        return send(1, slot, r.half_a.at[slot, 1 - col], r.recv_xa.at[slot], col_id)

    def utt_copy_b(slot):
        return send(2, slot, r.half_b.at[slot, 1 - utt], r.recv_yb.at[slot], utt_id)

    def col_copy_b(slot):
        return send(3, slot, r.sum_b.at[slot, 1 - col], r.recv_xb.at[slot], col_id)

    def utt_copy_a(slot, deep):
        return send(4, slot, r.sum_a.at[deep, pos], r.recv_ya.at[slot], utt_id)

    def utt_copy_b2(slot, deep):
        return send(5, slot, r.line_b.at[deep, pos], r.recv_yb2.at[slot], utt_id)

    def line_right(kind, slot, deep, step, source, target):
        dest = jnp.minimum(4 - step + pos, 3)
        return send(kind + step - 1, slot, source.at[deep, dest], target.at[slot, step - 1], right_id)

    def line_left(kind, slot, deep, step, source, target):
        dest = jnp.maximum(pos - 4 + step, 0)
        return send(kind + step - 1, slot, source.at[deep, dest], target.at[slot, step - 1], left_id)

    def line_start(slot, deep, step, source, right, left, kind):
        @pl.when((pos <= step - 1) & (pos < 3))
        def _():
            line_right(kind, slot, deep, step, source, right).start()

        @pl.when((pos >= 4 - step) & (pos > 0))
        def _():
            line_left(kind + 3, slot, deep, step, source, left).start()

    def line_finish(slot, deep, step, source, right, left, kind):
        @pl.when((pos <= step - 1) & (pos < 3))
        def _():
            line_right(kind, slot, deep, step, source, right).wait_send()

        @pl.when((pos >= 4 - step) & (pos > 0))
        def _():
            line_left(kind + 3, slot, deep, step, source, left).wait_send()

        @pl.when((pos >= 1) & (pos <= step))
        def _():
            line_right(kind, slot, deep, step, source, right).wait_recv()
            dest = 3 - step + pos
            source[deep, dest] = (
                source[deep, dest].astype(F32) + right[slot, step - 1].astype(F32)
            ).astype(LOW)

        @pl.when((pos <= 2) & (pos >= 3 - step))
        def _():
            line_left(kind + 3, slot, deep, step, source, left).wait_recv()
            dest = pos + step - 3
            source[deep, dest] = (
                source[deep, dest].astype(F32) + left[slot, step - 1].astype(F32)
            ).astype(LOW)

    line_a = (r.sum_a, r.right_a, r.left_a, 6)
    line_bb = (r.line_b, r.right_b, r.left_b, 12)

    def advance(tick):
        def stage(offset):
            slab = tick - offset
            return (
                slab,
                lax.rem(slab + SLOTS * 4, SLOTS),
                lax.rem(slab + DEEP, DEEP),
                pl.when((slab >= 0) & (slab < SLABS)),
            )

        slab, slot, _, guard = stage(0)
        load_start(slab + 1)

        @pl.when(slab < LOADED)
        def _():
            load_wait(slot)

        @guard
        def _():
            core_copy(slot).start()

        _, slot1, _, guard = stage(1)

        @guard
        def _():
            core_copy(slot1).wait()
            for line in range(4):
                for side in range(2):
                    both = r.part[slot1, core, 2 * line + side].astype(F32) + r.recv_c[
                        slot1, 2 * line + side
                    ].astype(F32)
                    both = both.astype(LOW)
                    r.half_a[slot1, side, line] = both[:32]
                    r.half_b[slot1, 0, side, line] = both[32:48]
                    r.half_b[slot1, 1, side, line] = both[48:]
            col_copy_a(slot1).start()
            utt_copy_b(slot1).start()

        _, slot2, deep2, guard = stage(2)

        @guard
        def _():
            col_copy_a(slot2).wait()
            r.sum_a[deep2] = (
                r.half_a[slot2, col].astype(F32) + r.recv_xa[slot2].astype(F32)
            ).astype(LOW)
            line_start(slot2, deep2, 1, *line_a)
            utt_copy_b(slot2).wait()
            r.sum_b[slot2] = (
                r.half_b[slot2, utt].astype(F32) + r.recv_yb[slot2].astype(F32)
            ).astype(LOW)
            col_copy_b(slot2).start()

        _, slot3, deep3, guard = stage(3)

        @guard
        def _():
            line_finish(slot3, deep3, 1, *line_a)
            line_start(slot3, deep3, 2, *line_a)
            col_copy_b(slot3).wait()
            r.line_b[deep3] = (
                r.sum_b[slot3, col].astype(F32) + r.recv_xb[slot3].astype(F32)
            ).astype(LOW)
            line_start(slot3, deep3, 1, *line_bb)

        _, slot4, deep4, guard = stage(4)

        @guard
        def _():
            line_finish(slot4, deep4, 2, *line_a)
            line_start(slot4, deep4, 3, *line_a)
            line_finish(slot4, deep4, 1, *line_bb)
            line_start(slot4, deep4, 2, *line_bb)

        _, slot5, deep5, guard = stage(5)

        @guard
        def _():
            line_finish(slot5, deep5, 3, *line_a)
            utt_copy_a(slot5, deep5).start()
            line_finish(slot5, deep5, 2, *line_bb)
            line_start(slot5, deep5, 3, *line_bb)

        _, slot6, deep6, guard = stage(6)

        @guard
        def _():
            utt_copy_a(slot6, deep6).wait()
            r.staged[slot6, 0:32] = r.sum_a[deep6, pos].astype(F32) + r.recv_ya[slot6].astype(F32)
            line_finish(slot6, deep6, 3, *line_bb)
            utt_copy_b2(slot6, deep6).start()

        slab7, slot7, deep7, guard = stage(7)

        @guard
        def _():
            utt_copy_b2(slot7, deep7).wait()
            mine = r.line_b[deep7, pos].astype(F32)
            theirs = r.recv_yb2[slot7].astype(F32)
            r.staged[slot7, 32:48] = jnp.where(utt == 0, mine, theirs)
            r.staged[slot7, 48:64] = jnp.where(utt == 0, theirs, mine)
            for ref, spec in zip(outs, PLAN):

                @pl.when((slab7 >= spec[0]) & (slab7 < spec[0] + spec[1]))
                def _():
                    pltpu.make_async_copy(
                        r.staged.at[slot7], window(ref, spec, slab7, ()), r.out_sem.at[slot7]
                    ).start()

        _, slot8, _, guard = stage(8)

        @guard
        def _():
            pltpu.make_async_copy(
                r.staged.at[slot8], outs[0].at[pl.ds(0, SROWS), pl.ds(0, SCOLS)], r.out_sem.at[slot8]
            ).wait()

    def cols_of(index):
        return pl.ds(pl.multiple_of(index * SCOLS, SCOLS), SCOLS)

    def put(slot, dest, rows):
        r.part[slot, dest % 2, dest // 2] = rows.astype(LOW)

    def put_product(slot, left_of, right):
        for quarter in range(4):
            rows = mul(left_of(quarter), right)
            for index in range(4):
                put(slot, 4 * quarter + index, rows[64 * index : 64 * index + 64])

    def quarter_rows(ref, lead=()):
        return lambda quarter: ref[lead + (slice(256 * quarter, 256 * quarter + 256),)]

    def produce(slab):
        slot = slab % SLOTS

        def among(first, number):
            return pl.when((slab >= first) & (slab < first + number))

        @among(16, 8)
        def _():
            local = slab - 16
            put_product(slot, quarter_rows(r.l_x_t), r.l_g[local // 2, :, cols_of(local % 2)])

        @among(24, 6)
        def _():
            local = slab - 24
            for dest in range(16):
                place = 3 * dest + local // 2
                book = place // 16
                first = (place % 16) * SROWS
                ids = first + lax.broadcasted_iota(jnp.int32, (SROWS, LANES), 0)
                picked = (ids == r.codes[book][0:1]).astype(LOW)
                put(slot, dest, mul(picked, r.table_g[book, :, cols_of(local % 2)]))

        @among(30, 8)
        def _():
            local = slab - 30
            inner = local // 2

            def rows(quarter):
                return jnp.concatenate(
                    [
                        r.act_t[pl.ds(pl.multiple_of(256 * dest + 64 * inner, 64), 64)]
                        for dest in range(4 * quarter, 4 * quarter + 4)
                    ],
                    axis=0,
                )

            put_product(slot, rows, r.dout_low[:, cols_of(local % 2)])

        @among(38, 8)
        def _():
            put_product(slot, quarter_rows(r.g_hn_t), r.du[:, cols_of(slab - 38)])

        @among(46, 8)
        def _():
            local = slab - 46
            kind = local // 2
            put_product(
                slot,
                quarter_rows(r.g_x_t, (jnp.minimum(kind, 1),)),
                r.g_g[kind, :, cols_of(local % 2)],
            )

        @pl.when(slab == 54)
        def _():
            b_down = jnp.sum(r.dout_low[...].astype(F32), axis=0, keepdims=True)
            for dest in range(16):
                shared = slice(LANES * (dest // 2), LANES * (dest // 2) + LANES)
                rows = [r.dn1[:, shared], r.dn2[:, shared], b_down[:, shared]]
                for index in range(2):
                    first = 256 * (dest % 2) + LANES * index
                    rows.append(r.db1[dest // 2 : dest // 2 + 1, first : first + LANES])
                rows += [r.l_dn1[:, shared], r.l_dn2[:, shared], r.l_db2[:, shared]]
                for index in range(2):
                    first = 256 * dest + LANES * index
                    rows.append(r.l_db1[:, first : first + LANES])
                rows.append(jnp.zeros((6, LANES), F32))
                r.part[slot, dest % 2, dest // 2, 0:16, 0:LANES] = jnp.concatenate(
                    rows, axis=0
                ).astype(LOW)

    own_utt, own_pair = seq // 8, seq % 8
    own_cols = pl.ds(pl.multiple_of(own_pair * LANES, LANES), LANES)

    def pair_cols(other):
        return pl.ds(pl.multiple_of((other % 8) * LANES, LANES), LANES)

    def hand_out(other):
        return remote(
            r.dmix.at[other // 8, :, pair_cols(other)], r.grads.at[seq], r.send_one.at[other],
            r.recv_one.at[seq], other,
        )

    def hand_back(block):
        return remote(
            r.pieces.at[block], r.landed.at[:, own_utt, :, own_cols], r.send_two.at[block],
            r.recv_two.at[seq], block,
        )

    def others(body):
        @pl.loop(1, count)
        def _(step):
            body(lax.rem(seq + step, count))

    def compute(tick):
        def at(*ticks):
            hit = tick == ticks[0]
            for item in ticks[1:]:
                hit = hit | (tick == item)
            return pl.when(hit)

        @pl.when(tick < 8)
        def _():
            slot = tick % 2
            for copy in weights(tick, slot):
                copy.wait()

            @pl.when(tick < 7)
            def _():
                for copy in weights(tick + 1, 1 - slot):
                    copy.start()

            @pl.when(tick == 0)
            def _():
                r.dout_low[...] = r.dout[...].astype(LOW)
                r.dhn[...] = jnp.zeros_like(r.dhn)

            cols = cols_of(tick)
            _, slope = gelu_parts(r.u[:, cols])
            du = (mul_t(r.dout_low[...], r.down_buf[slot]) * slope).astype(LOW)
            r.du[:, cols] = du
            r.db1[pl.ds(tick, 1), :] = jnp.sum(du.astype(F32), axis=0, keepdims=True)
            r.dhn[...] += mul_t(du, r.up_buf[slot])

        @at(3)
        def _():
            for copy in fetch(4, 5, 6, 7, 8, 9, 10):
                copy.start()

        @at(12)
        def _():
            for copy in fetch(1, 2, 3, 11, 12, 13, 14):
                copy.start()

        @at(AT_BACK)
        def _():
            for copy in fetch(0):
                copy.wait()
            dmid, gain = scale_back(r.mid[...], r.n2[...], r.dhn[...])
            r.dn2[...] = jnp.sum(gain, axis=0, keepdims=True)
            dmid = dmid + r.dout[...]
            r.dmid[...] = dmid
            dattn = dmid.astype(LOW)
            r.g_g[0] = dattn
            r.dmix[...] = mul_t(dattn, r.square[0]).astype(LOW).reshape(r.dmix.shape)
            others(lambda other: hand_out(other).start())
            r.grads[seq] = r.dmix[own_utt, :, own_cols]

        @at(AT_BACK + 1)
        def _():
            for copy in fetch(4, 5, 6, 7, 8, 9, 10):
                copy.wait()
            r.k_t[...] = r.held[:, 64:128].reshape(count * HD, LANES).T
            fill_bias(r.bias, r.held[:, 192:208])
            r.dk_acc[...] = jnp.zeros_like(r.dk_acc)
            r.dv_acc[...] = jnp.zeros_like(r.dv_acc)
            r.l_x_t[...] = r.l_x[0].T

        @at(AT_ATTEND)
        def _():
            def arrived(other):
                here = r.grads.at[other]
                remote(here, here, r.send_one.at[other], r.recv_one.at[other], other).wait_recv()

            others(arrived)

        for order, group in enumerate(reversed(range(4))):
            below = group * 256
            here = below + 256
            begin = AT_ATTEND + 2 * order

            @at(begin, begin + 1)
            def _():
                @pl.loop(0, 2)
                def _(index):
                    block = 4 * group + 2 * (tick - begin) + index
                    attend_back_block(r, group, below, here, block)

            @at(begin + 1)
            def _():
                for block in range(4 * group, 4 * group + 4):
                    rows = slice(block * HD, (block + 1) * HD)
                    r.pieces[block, 1] = r.dk_acc[rows].astype(LOW)
                    r.pieces[block, 2] = r.dv_acc[rows].astype(LOW)

                    @pl.when(block != seq)
                    def _():
                        hand_back(block).start()

                    @pl.when(block == seq)
                    def _():
                        r.landed[:, own_utt, :, own_cols] = r.pieces[block]

        @at(AT_LANDED)
        def _():
            def arrived(other):
                here = r.landed.at[:, other // 8, :, pair_cols(other)]
                remote(here, here, r.send_two.at[other], r.recv_two.at[other], other).wait_recv()

            others(arrived)
            others(lambda other: hand_out(other).wait_send())
            others(lambda other: hand_back(other).wait_send())
            for index in range(3):
                r.g_g[1 + index] = r.landed[index].reshape(r.g_g.shape[1:])

        @at(AT_LANDED + 1)
        def _():
            for copy in fetch(1, 2, 3, 11, 12, 13, 14):
                copy.wait()
            r.l_x_t[...] = r.l_x[1].T
            r.dhn[...] = mul_t(r.g_g[1], r.square[1])

        @at(AT_LANDED + 2)
        def _():
            r.dhn[...] += mul_t(r.g_g[2], r.square[2])

        @at(AT_LANDED + 3)
        def _():
            dnormed = r.dhn[...] + mul_t(r.g_g[3], r.square[3])
            dx, gain = scale_back(r.x[...].astype(F32), r.n1[...], dnormed)
            r.dn1[...] = jnp.sum(gain, axis=0, keepdims=True)
            r.dx[...] = dx + r.dmid[...]

        @at(AT_LANDED + 4)
        def _():
            r.act_t[...] = r.act_buf[...].T

        @at(AT_LANDED + 5)
        def _():
            r.g_hn_t[...] = r.hn[...].T
            r.g_x_t[0] = r.g_x[0].T
            r.g_x_t[1] = r.g_x[1].T

    pl.semaphore_wait(barrier, count)

    @pl.loop(0, SLABS + DRAIN)
    def _(tick):
        advance(tick)
        compute(tick)
        produce(tick + 1)


def attend_back_block(r, group, below, here, block):
    query = two_heads(r.held[block, 0:64] * LOW(HD ** (-0.5)))
    grad = two_heads(r.grads[block])
    log_total = r.log_total[block][0:1]
    near_v = r.held[4 * group : 4 * group + 4, 128:192].reshape(256, LANES)
    near_k = r.held[4 * group : 4 * group + 4, 64:128].reshape(256, LANES)
    near = masked_scores(mul_t(near_k, query), r.bias[below:here], below, block)
    near = jnp.exp(near - log_total)
    near_dp = mul_t(near_v, grad)
    delta = jnp.sum(near * near_dp, axis=0, keepdims=True)
    if group:
        far_v = r.held[0 : 4 * group, 128:192].reshape(below, LANES)
        far_k = r.held[0 : 4 * group, 64:128].reshape(below, LANES)
        far = jnp.exp(mul_t(far_k, query) + r.bias[0:below] - log_total)
        far_dp = mul_t(far_v, grad)
        delta = delta + jnp.sum(far * far_dp, axis=0, keepdims=True)
        far_ds = (far * (far_dp - delta)).astype(LOW)
        r.dk_acc[0:below] += mul(far_ds, query)
        r.dv_acc[0:below] += mul(far.astype(LOW), grad)
    near_ds = (near * (near_dp - delta)).astype(LOW)
    r.dk_acc[below:here] += mul(near_ds, query)
    r.dv_acc[below:here] += mul(near.astype(LOW), grad)
    dq = mul(r.k_t[:, below:here], near_ds)
    if group:
        dq = dq + mul(r.k_t[:, 0:below], far_ds)
    r.pieces[block, 0] = (join_heads(dq) * HD ** (-0.5)).astype(LOW)


def finish_on_slice(far, near):
    vmem = pl.BlockSpec(memory_space=pltpu.VMEM)
    hbm = pl.BlockSpec(memory_space=pl.ANY)
    rows, width = near["x"].shape
    wide = near["u"].shape[1]
    utts = rows // HD
    shapes = [
        (width // 16, wide), (wide // 16, width), (width // 16, width), (width // 16, width),
        (width // 16, width), (width // 16, width), (3 * 1024 // 16, width), (wide // 16, width),
        (width // 16, wide), (width // 16, width), (width // 16, width), (width // 16, width),
        (width // 16, width), (SROWS, SCOLS),
    ]
    out_names = ["dx"] + ["out_%d" % index for index in range(len(shapes))]
    rows_l = far["l_normed"].shape[0]
    buffers = dict(
        part=((SLOTS, 2, 8, 64, SCOLS), LOW),
        recv_c=((SLOTS, 8, 64, SCOLS), LOW),
        half_a=((SLOTS, 2, 4, 32, SCOLS), LOW),
        half_b=((SLOTS, 2, 2, 4, 16, SCOLS), LOW),
        recv_xa=((SLOTS, 4, 32, SCOLS), LOW),
        recv_yb=((SLOTS, 2, 4, 16, SCOLS), LOW),
        sum_a=((DEEP, 4, 32, SCOLS), LOW),
        sum_b=((SLOTS, 2, 4, 16, SCOLS), LOW),
        recv_xb=((SLOTS, 4, 16, SCOLS), LOW),
        line_b=((DEEP, 4, 16, SCOLS), LOW),
        right_a=((SLOTS, 3, 32, SCOLS), LOW),
        left_a=((SLOTS, 3, 32, SCOLS), LOW),
        right_b=((SLOTS, 3, 16, SCOLS), LOW),
        left_b=((SLOTS, 3, 16, SCOLS), LOW),
        recv_ya=((SLOTS, 32, SCOLS), LOW),
        recv_yb2=((SLOTS, 16, SCOLS), LOW),
        staged=((SLOTS, 64, SCOLS), F32),
        up_buf=((2, width, SCOLS), LOW),
        down_buf=((2, SCOLS, width), LOW),
        square=((4, width, width), LOW),
        held=(far["saved"].shape, LOW),
        l_x=((2, rows_l, width), LOW),
        l_g=((4, rows_l, width), LOW),
        l_x_t=((width, rows_l), LOW),
        table_g=(far["rest"].shape, LOW),
        act_buf=((rows, wide), LOW),
        act_t=((wide, rows), LOW),
        g_x=((2, rows, width), LOW),
        g_x_t=((2, width, rows), LOW),
        g_hn_t=((width, rows), LOW),
        g_g=((4, rows, width), LOW),
        dout_low=((rows, width), LOW),
        du=((rows, wide), LOW),
        db1=((8, SCOLS), F32),
        dn1=((1, width), F32),
        dn2=((1, width), F32),
        dhn=((rows, width), F32),
        dmid=((rows, width), F32),
        dmix=((utts, HD, width), LOW),
        grads=((16, HD, LANES), LOW),
        landed=((3, utts, HD, width), LOW),
        pieces=((16, 3, HD, LANES), LOW),
        dk_acc=((16 * HD, LANES), F32),
        dv_acc=((16 * HD, LANES), F32),
        bias=((16 * HD, LANES), F32),
        k_t=((LANES, 16 * HD), LOW),
    )
    semaphores = dict(
        load_sem=(SLOTS, 2), out_sem=(SLOTS,), send_sem=(18, SLOTS), recv_sem=(18, SLOTS),
        weight_sem=(2, 2), fetch_sem=(15,), send_one=(16,), recv_one=(16,), send_two=(16,),
        recv_two=(16,),
    )
    names = list(far) + list(near) + out_names + list(buffers) + list(semaphores)
    return pl.pallas_call(
        functools.partial(tail_kernel, names, len(shapes)),
        in_specs=[hbm] * len(far) + [vmem] * len(near),
        out_specs=[vmem] + [hbm] * len(shapes),
        out_shape=[jax.ShapeDtypeStruct((rows, width), F32)]
        + [jax.ShapeDtypeStruct(shape, F32) for shape in shapes],
        scratch_shapes=[pltpu.VMEM(*item) for item in buffers.values()]
        + [pltpu.SemaphoreType.DMA(item) for item in semaphores.values()],
        compiler_params=pltpu.CompilerParams(
            collective_id=1, has_side_effects=True, vmem_limit_bytes=60 << 20
        ),
    )(*far.values(), *near.values())


def normalize(values, gain_vec):
    return (
        values * lax.rsqrt(jnp.mean(values * values, axis=-1, keepdims=True) + EPSILON) * gain_vec
    )


def gelu_fn(values):
    return jax.nn.gelu(values, approximate=True)


def project(left_side, weight):
    return jnp.dot(left_side, weight, preferred_element_type=jnp.float32)


def project_back(gradient, weight):
    return lax.dot_general(
        gradient, weight, (((1,), (1,)), ((), ())), preferred_element_type=jnp.float32
    )


def weight_grad(left_side, gradient):
    return lax.dot_general(
        left_side, gradient, (((0,), (0,)), ((), ())), preferred_element_type=jnp.float32
    )


def block_outputs(inputs, mixed_rows, params):
    middle = inputs + project(mixed_rows, params[4])
    middle_norm = normalize(middle, params[5]).astype(jnp.bfloat16)
    pre_active = project(middle_norm, params[6]) + params[7]
    active = gelu_fn(pre_active).astype(jnp.bfloat16)
    result = middle + project(active, params[8]) + params[9]
    return (result, (middle, middle_norm, pre_active, active))


def block_back(inputs, normed, mixed_rows, kept_parts, params, grad_out, attention_back):
    middle, middle_norm, pre_active, active = kept_parts
    grad_branch = grad_out.astype(jnp.bfloat16)
    grad_b_down = jnp.sum(grad_branch.astype(jnp.float32), axis=0)
    grad_w_down = weight_grad(active, grad_branch)
    grad_active = project_back(grad_branch, params[8])
    grad_pre = jax.vjp(gelu_fn, pre_active)[1](grad_active)[0].astype(jnp.bfloat16)
    grad_b_up = jnp.sum(grad_pre.astype(jnp.float32), axis=0)
    grad_w_up = weight_grad(middle_norm, grad_pre)
    middle_back = jax.vjp(normalize, middle, params[5])[1]
    grad_middle, grad_norm_two = middle_back(project_back(grad_pre, params[6]))
    grad_middle = grad_middle + grad_out
    grad_attn = grad_middle.astype(jnp.bfloat16)
    grad_w_output = weight_grad(mixed_rows, grad_attn)
    grad_mixed = project_back(grad_attn, params[4]).astype(jnp.bfloat16)
    grad_query, grad_key, grad_value = attention_back(grad_mixed)
    grad_normed = (
        project_back(grad_query, params[1])
        + project_back(grad_key, params[2])
        + project_back(grad_value, params[3])
    )
    input_back = jax.vjp(normalize, inputs, params[0])[1]
    grad_inputs, grad_norm_one = input_back(grad_normed)
    weight_grads = (
        grad_norm_one,
        weight_grad(normed, grad_query),
        weight_grad(normed, grad_key),
        weight_grad(normed, grad_value),
        grad_w_output,
        grad_norm_two,
        grad_w_up,
        grad_b_up,
        grad_w_down,
        grad_b_down,
    )
    return (grad_inputs + grad_middle, weight_grads)


def on_device(
    frames,
    codes,
    lengths,
    frame_mask,
    table,
    glob_norm_one,
    glob_w_query,
    glob_w_key,
    glob_w_value,
    glob_w_output,
    glob_norm_two,
    glob_w_up,
    glob_b_up,
    glob_w_down,
    glob_b_down,
    local_norm_one,
    local_w_query,
    local_w_key,
    local_w_value,
    local_w_output,
    local_norm_two,
    local_w_up,
    local_b_up,
    local_w_down,
    local_b_down,
    cotan_global,
    cotan_local,
):
    utter_count, frame_count, model_width = frames.shape
    row_count = utter_count * frame_count
    local_len = CB + 1
    positions = lax.axis_index("seq") * frame_count + jnp.arange(frame_count, dtype=jnp.int32)
    valid = positions[None, :] < lengths[:, None]
    usable = jnp.pad(frame_mask.astype(LOW), ((0, 0), (0, LANES - frame_count)))
    usable = jnp.broadcast_to(usable[:, None, :], (utter_count, 16, LANES))
    glob_params = (
        glob_norm_one,
        glob_w_query,
        glob_w_key,
        glob_w_value,
        glob_w_output,
        glob_norm_two,
        glob_w_up,
        glob_b_up,
        glob_w_down,
        glob_b_down,
    )
    local_params = (
        local_norm_one,
        local_w_query,
        local_w_key,
        local_w_value,
        local_w_output,
        local_norm_two,
        local_w_up,
        local_b_up,
        local_w_down,
        local_b_down,
    )
    global_in = frames.astype(jnp.float32).reshape(row_count, model_width)
    glob_normed, glob_mixed, saved, log_total = global_attend(frames, usable, glob_params)
    glob_mixed = glob_mixed.reshape(row_count, model_width)
    glob_result, glob_kept = block_outputs(global_in, glob_mixed, glob_params)
    global_rows = jnp.where(valid.reshape(row_count, 1), glob_result, 0.0).astype(jnp.bfloat16)
    code_rows = codes.transpose(2, 0, 1).reshape(CB, row_count)
    table_ids = code_rows + VOCAB * jnp.arange(CB, dtype=jnp.int32)[:, None]
    embedded = table.at[table_ids].get(mode="promise_in_bounds")
    local_in = jnp.concatenate([global_rows[None], embedded], axis=0)
    local_shape = (local_len, row_count, model_width)
    flat_shape = (local_len * row_count, model_width)
    normed, local_q, local_k, local_v, local_probs, mixed, middle, middle_norm = local_front(
        local_in, local_params
    )
    row_valid = valid.reshape(1, row_count, 1)
    local_cotan = cotan_local.transpose(2, 0, 1, 3).reshape(local_shape)
    local_cotan = jnp.where(row_valid, local_cotan, 0)
    local_result, grad_hidden, grad_w_up, grad_w_down, grad_b_up = local_ffn(
        middle_norm.reshape(flat_shape),
        local_cotan.reshape(flat_shape),
        middle.reshape(flat_shape),
        local_params,
    )
    local_rows = jnp.where(row_valid, local_result.reshape(local_shape), 0)
    local_rows = local_rows.reshape(local_len, utter_count, frame_count, model_width)
    local_rows = local_rows.transpose(1, 2, 0, 3)
    grad_attn, grad_q, grad_k, grad_v, grad_first, grad_rest, grad_n1, grad_n2 = local_back(
        local_in,
        middle,
        grad_hidden.reshape(local_shape),
        local_cotan,
        local_q,
        local_k,
        local_v,
        local_probs,
        local_params,
    )
    normed = normed.reshape(flat_shape)
    mixed = mixed.reshape(flat_shape)
    grad_b_down = jnp.sum(local_cotan.astype(F32), axis=(0, 1))
    grad_first = grad_first.reshape(utter_count, frame_count, model_width)
    glob_cotan = jnp.where(
        valid[:, :, None], cotan_global.astype(jnp.float32) + grad_first, 0.0
    )
    glob_cotan = glob_cotan.reshape(row_count, model_width)
    outputs = (global_rows.reshape(utter_count, frame_count, model_width), local_rows)

    if lax.axis_size("seq") == 16 and lax.axis_size("utt") == 2:
        glob_middle, glob_middle_norm, pre_active, active = glob_kept
        far = dict(
            l_up=grad_w_up.reshape(8, 2, -1, grad_w_up.shape[1]),
            l_down=grad_w_down.reshape(8, 2, -1, grad_w_down.shape[1]),
            g_w_up=glob_w_up,
            g_w_down=glob_w_down,
            g_w_o=glob_w_output,
            g_w_q=glob_w_query,
            g_w_k=glob_w_key,
            g_w_v=glob_w_value,
            saved=saved,
            l_normed=normed,
            l_mixed=mixed,
            l_dq=grad_q.reshape(flat_shape),
            l_dk=grad_k.reshape(flat_shape),
            l_dv=grad_v.reshape(flat_shape),
            l_dattn=grad_attn.reshape(flat_shape),
            rest=grad_rest,
            g_act=active,
            g_mixed=glob_mixed,
            g_normed=glob_normed,
        )
        near = dict(
            u=pre_active,
            dout=glob_cotan,
            mid=glob_middle,
            hn=glob_middle_norm,
            x=frames.reshape(row_count, model_width),
            n1=glob_norm_one.reshape(1, -1),
            n2=glob_norm_two.reshape(1, -1),
            log_total=log_total,
            codes=jnp.broadcast_to(code_rows[:, None, :], (CB, 8, row_count)),
            l_dn1=grad_n1,
            l_dn2=grad_n2,
            l_db1=grad_b_up,
            l_db2=grad_b_down.reshape(1, -1),
        )
        grad_inputs, *sums = finish_on_slice(far, near)
        wide = dict(zip("12qkvot76pabc", sums[:-1]))
        half = lax.axis_index("seq") % 2
        rest = sums[-1]

        def piece(row):
            return jnp.where(half == 0, rest[row, : LANES // 2], rest[row, LANES // 2 : LANES])

        def piece_wide(row):
            return rest[row : row + 2, :LANES].reshape(-1)

        return outputs + (
            grad_inputs.reshape(utter_count, frame_count, model_width),
            wide["t"],
            piece(0),
            wide["a"],
            wide["b"],
            wide["c"],
            wide["p"],
            piece(1),
            wide["6"],
            piece_wide(3),
            wide["7"],
            piece(2),
            piece(5),
            wide["q"],
            wide["k"],
            wide["v"],
            wide["o"],
            piece(6),
            wide["1"],
            piece_wide(8),
            wide["2"],
            piece(7),
        )

    local_grads = (
        grad_n1[0],
        weight_grad(normed, grad_q.reshape(flat_shape)),
        weight_grad(normed, grad_k.reshape(flat_shape)),
        weight_grad(normed, grad_v.reshape(flat_shape)),
        weight_grad(mixed, grad_attn.reshape(flat_shape)),
        grad_n2[0],
        grad_w_up,
        grad_b_up[0],
        grad_w_down,
        grad_b_down,
    )
    picked = code_rows[:, None, :] == jnp.arange(VOCAB, dtype=jnp.int32)[None, :, None]
    grad_tab = jnp.einsum(
        "cvn,cnd->cvd", picked.astype(LOW), grad_rest, preferred_element_type=F32
    ).reshape(CB * VOCAB, model_width)

    def global_back(grad_mixed):
        grads = global_attend_back(
            grad_mixed.reshape(utter_count, frame_count, model_width), saved, log_total
        )
        return tuple(grads.reshape(3, row_count, model_width))

    grad_inputs, glob_grads = block_back(
        global_in, glob_normed, glob_mixed, glob_kept, glob_params, glob_cotan, global_back
    )
    reduced = reduce_all((grad_tab,) + glob_grads + local_grads)
    return outputs + (grad_inputs.reshape(utter_count, frame_count, model_width),) + reduced


def solution(mesh):
    return jax.shard_map(
        on_device,
        mesh=mesh,
        in_specs=(
            P("utt", "seq", None),
            P("utt", "seq", None),
            P("utt"),
            P("utt", "seq"),
            P(),
            P(),
            P(),
            P(),
            P(),
            P(),
            P(),
            P(),
            P(),
            P(),
            P(),
            P(),
            P(),
            P(),
            P(),
            P(),
            P(),
            P(),
            P(),
            P(),
            P(),
            P("utt", "seq", None),
            P("utt", "seq", None, None),
        ),
        out_specs=(
            P("utt", "seq", None),
            P("utt", "seq", None, None),
            P("utt", "seq", None),
            P("seq", None),
            P("seq"),
            P("seq", None),
            P("seq", None),
            P("seq", None),
            P("seq", None),
            P("seq"),
            P("seq", None),
            P("seq"),
            P("seq", None),
            P("seq"),
            P("seq"),
            P("seq", None),
            P("seq", None),
            P("seq", None),
            P("seq", None),
            P("seq"),
            P("seq", None),
            P("seq"),
            P("seq", None),
            P("seq"),
        ),
        check_vma=False,
    )
```

```python
import functools
import types

import jax
import jax.numpy as jnp
from jax import lax
from jax.experimental import pallas as pl
from jax.experimental.pallas import tpu as pltpu
from jax.sharding import PartitionSpec as P

H = 16
HD = 64
CB = 3
VOCAB = 1024


EPSILON = 1e-05
NEGATIVE = -1e30
F32 = jnp.float32
LOW = jnp.bfloat16
LANES = 128
MESH_ID = pl.DeviceIdType.MESH


def reduce_all(grads):
    return tuple(
        lax.psum(
            lax.psum_scatter(item.astype(LOW), "seq", scatter_dimension=0, tiled=True), "utt"
        ).astype(F32)
        for item in grads
    )


def mul(left_side, right_side):
    return jnp.dot(left_side, right_side, preferred_element_type=F32)


def mul_t(left_side, right_side):
    return lax.dot_general(
        left_side, right_side, (((1,), (1,)), ((), ())), preferred_element_type=F32
    )


def t_mul(left_side, right_side):
    return lax.dot_general(
        left_side, right_side, (((0,), (0,)), ((), ())), preferred_element_type=F32
    )


def scale_of(values):
    return lax.rsqrt(jnp.mean(values * values, axis=-1, keepdims=True) + EPSILON)


def scale_back(values, gain, grad):
    scale = scale_of(values)
    inner = grad * gain
    shared = jnp.mean(values * inner, axis=-1, keepdims=True) * (scale * scale * scale)
    return inner * scale - values * shared, grad * values * scale


def head_sums(width):
    rows = lax.broadcasted_iota(jnp.int32, (width, 128), 0) // HD
    cols = lax.broadcasted_iota(jnp.int32, (width, 128), 1)
    return (rows == cols).astype(LOW)


def head_spread(width):
    rows = lax.broadcasted_iota(jnp.int32, (128, width), 0)
    cols = lax.broadcasted_iota(jnp.int32, (128, width), 1) // HD
    return (rows == cols).astype(LOW)


def sum_heads(product, sums):
    high = product.astype(LOW)
    rest = (product - high.astype(F32)).astype(LOW)
    return mul(high, sums) + mul(rest, sums)


def front_kernel(
    x_ref, n1_ref, wq_ref, wk_ref, wv_ref, wo_ref, n2_ref,
    normed_ref, q_ref, k_ref, v_ref, probs_ref, mixed_ref, mid_ref, mid_norm_ref,
):
    places, frames, width = x_ref.shape
    rows = places * frames
    x = x_ref[...].astype(F32).reshape(rows, width)
    normed = (x * scale_of(x) * n1_ref[...]).astype(LOW)
    normed_ref[...] = normed.reshape(places, frames, width)
    q_ref[...] = mul(normed, wq_ref[...]).astype(LOW).reshape(places, frames, width)
    k_ref[...] = mul(normed, wk_ref[...]).astype(LOW).reshape(places, frames, width)
    v_ref[...] = mul(normed, wv_ref[...]).astype(LOW).reshape(places, frames, width)
    sums, spread = head_sums(width), head_spread(width)
    pair = 0
    for i in range(places):
        query = q_ref[i].astype(F32)
        scores = [
            sum_heads(query * k_ref[j].astype(F32), sums) * HD ** (-0.5) for j in range(i + 1)
        ]
        peak = scores[0]
        for item in scores[1:]:
            peak = jnp.maximum(peak, item)
        raised = [jnp.exp(item - peak) for item in scores]
        total = raised[0]
        for item in raised[1:]:
            total = total + item
        mixed = None
        for j in range(i + 1):
            probs = raised[j] / total
            probs_ref[pair] = probs
            pair += 1
            term = mul(probs.astype(LOW), spread) * v_ref[j].astype(F32)
            mixed = term if mixed is None else mixed + term
        mixed_ref[i] = mixed.astype(LOW)
    mid = x + mul(mixed_ref[...].reshape(rows, width), wo_ref[...])
    mid_ref[...] = mid.reshape(places, frames, width)
    mid_norm_ref[...] = (
        (mid * scale_of(mid) * n2_ref[...]).astype(LOW).reshape(places, frames, width)
    )


def local_front(x, params):
    places, frames, width = x.shape
    pairs = places * (places + 1) // 2
    step = 64
    rows = pl.BlockSpec((places, step, width), lambda i: (0, i, 0))
    whole = lambda item: pl.BlockSpec(item.shape, lambda i: (0, 0), pipeline_mode=pl.Buffered(1))
    n1, n2 = params[0].reshape(1, -1), params[5].reshape(1, -1)
    operands = (x, n1, params[1], params[2], params[3], params[4], n2)
    like = lambda kind: jax.ShapeDtypeStruct((places, frames, width), kind)
    return pl.pallas_call(
        front_kernel,
        grid=(frames // step,),
        in_specs=[rows] + [whole(item) for item in operands[1:]],
        out_specs=[rows] * 4
        + [pl.BlockSpec((pairs, step, 128), lambda i: (0, i, 0))]
        + [rows] * 3,
        out_shape=[
            like(LOW), like(LOW), like(LOW), like(LOW),
            jax.ShapeDtypeStruct((pairs, frames, 128), F32),
            like(LOW), like(F32), like(LOW),
        ],
        compiler_params=pltpu.CompilerParams(vmem_limit_bytes=56 << 20),
    )(*operands)


def gelu_parts(u):
    scale = 0.7978845608028654
    inner = jnp.tanh(scale * (u + 0.044715 * u * u * u))
    half = 0.5 * (1.0 + inner)
    slope = half + 0.5 * u * (1.0 - inner * inner) * scale * (1.0 + 3 * 0.044715 * u * u)
    return u * half, slope


def ffn_kernel(
    hn_ref, dout_ref, mid_ref, w1_ref, b1_ref, w2_ref, b2_ref,
    y_ref, dhn_ref, dw1_ref, dw2_ref, db1_ref, acc_ref, hn_t_ref,
):
    at = pl.program_id(0)
    last = pl.num_programs(0) - 1

    @pl.when(at == 0)
    def _():
        hn_t_ref[...] = hn_ref[...].T
        acc_ref[...] = mid_ref[...] + b2_ref[...]
        dhn_ref[...] = jnp.zeros_like(dhn_ref)

    hn, dout = hn_ref[...], dout_ref[...]
    u = mul(hn, w1_ref[...]) + b1_ref[...]
    act, slope = gelu_parts(u)
    act = act.astype(LOW)
    acc_ref[...] += mul(act, w2_ref[...])
    du = (mul_t(dout, w2_ref[...]) * slope).astype(LOW)
    db1_ref[...] = jnp.sum(du.astype(F32), axis=0, keepdims=True)
    dhn_ref[...] += mul_t(du, w1_ref[...])
    dw1_ref[...] = mul(hn_t_ref[...], du).astype(LOW)
    dw2_ref[...] = t_mul(act, dout).astype(LOW)

    @pl.when(at == last)
    def _():
        y_ref[...] = acc_ref[...].astype(LOW)


def local_ffn(hn, dout, mid, params):
    rows, width = hn.shape
    wide = params[6].shape[1]
    step = 512
    whole = pl.BlockSpec((rows, width), lambda i: (0, 0), pipeline_mode=pl.Buffered(1))
    out_whole = pl.BlockSpec((rows, width), lambda i: (0, 0))
    return pl.pallas_call(
        ffn_kernel,
        grid=(wide // step,),
        in_specs=[
            whole, whole, whole,
            pl.BlockSpec((width, step), lambda i: (0, i)),
            pl.BlockSpec((1, step), lambda i: (0, i)),
            pl.BlockSpec((step, width), lambda i: (i, 0)),
            pl.BlockSpec((1, width), lambda i: (0, 0)),
        ],
        out_specs=[
            out_whole, out_whole,
            pl.BlockSpec((width, step), lambda i: (0, i)),
            pl.BlockSpec((step, width), lambda i: (i, 0)),
            pl.BlockSpec((1, step), lambda i: (0, i)),
        ],
        out_shape=[
            jax.ShapeDtypeStruct((rows, width), LOW),
            jax.ShapeDtypeStruct((rows, width), F32),
            jax.ShapeDtypeStruct((width, wide), LOW),
            jax.ShapeDtypeStruct((wide, width), LOW),
            jax.ShapeDtypeStruct((1, wide), F32),
        ],
        scratch_shapes=[pltpu.VMEM((rows, width), F32), pltpu.VMEM((width, rows), LOW)],
        compiler_params=pltpu.CompilerParams(vmem_limit_bytes=56 << 20),
    )(hn, dout, mid, params[6], params[7].reshape(1, -1), params[8], params[9].reshape(1, -1))


def back_kernel(
    x_ref, mid_ref, dhn_ref, dout_ref, q_ref, k_ref, v_ref, probs_ref,
    n1_ref, n2_ref, wq_ref, wk_ref, wv_ref, wo_ref,
    dattn_ref, dq_ref, dk_ref, dv_ref, first_ref, rest_ref, dn1_ref, dn2_ref,
    dmid_ref,
):
    places, frames, width = x_ref.shape
    rows = places * frames

    @pl.when(pl.program_id(0) == 0)
    def _():
        dn1_ref[...] = jnp.zeros_like(dn1_ref)
        dn2_ref[...] = jnp.zeros_like(dn2_ref)

    mid = mid_ref[...].reshape(rows, width)
    dmid, gain = scale_back(mid, n2_ref[...], dhn_ref[...].reshape(rows, width))
    dn2_ref[...] += jnp.sum(gain, axis=0, keepdims=True)
    dmid = dmid + dout_ref[...].astype(F32).reshape(rows, width)
    dmid_ref[...] = dmid
    dattn = dmid.astype(LOW)
    dattn_ref[...] = dattn.reshape(places, frames, width)
    dmixed = mul_t(dattn, wo_ref[...]).astype(LOW).reshape(places, frames, width)
    sums, spread = head_sums(width), head_spread(width)
    pair = 0
    dk, dv = [None] * places, [None] * places
    add = lambda old, term: term if old is None else old + term
    for i in range(places):
        grad = dmixed[i].astype(F32)
        query = q_ref[i].astype(F32)
        dp = [sum_heads(grad * v_ref[j].astype(F32), sums) for j in range(i + 1)]
        delta = None
        for j in range(i + 1):
            delta = add(delta, probs_ref[pair + j] * dp[j])
        dq = None
        for j in range(i + 1):
            probs = probs_ref[pair + j]
            ds = (probs * (dp[j] - delta)).astype(LOW)
            ds = mul(ds, spread)
            dq = add(dq, ds * k_ref[j].astype(F32))
            dk[j] = add(dk[j], ds * query)
            dv[j] = add(dv[j], mul(probs.astype(LOW), spread) * grad)
        pair += i + 1
        dq_ref[i] = (dq * HD ** (-0.5)).astype(LOW)
    for j in range(places):
        dk_ref[j] = (dk[j] * HD ** (-0.5)).astype(LOW)
        dv_ref[j] = dv[j].astype(LOW)
    dnormed = (
        mul_t(dq_ref[...].reshape(rows, width), wq_ref[...])
        + mul_t(dk_ref[...].reshape(rows, width), wk_ref[...])
        + mul_t(dv_ref[...].reshape(rows, width), wv_ref[...])
    )
    x = x_ref[...].astype(F32).reshape(rows, width)
    dx, gain = scale_back(x, n1_ref[...], dnormed)
    dn1_ref[...] += jnp.sum(gain, axis=0, keepdims=True)
    dx = (dx + dmid_ref[...]).reshape(places, frames, width)
    first_ref[...] = dx[0]
    rest_ref[...] = dx[1:].astype(LOW)


def local_back(x, mid, dhn, dout, q, k, v, probs, params):
    places, frames, width = x.shape
    pairs = probs.shape[0]
    step = 64
    rows = pl.BlockSpec((places, step, width), lambda i: (0, i, 0))
    whole = lambda item: pl.BlockSpec(item.shape, lambda i: (0, 0), pipeline_mode=pl.Buffered(1))
    like = lambda kind: jax.ShapeDtypeStruct((places, frames, width), kind)
    fixed = (params[0].reshape(1, -1), params[5].reshape(1, -1)) + tuple(params[1:5])
    vector = pl.BlockSpec((1, width), lambda i: (0, 0))
    return pl.pallas_call(
        back_kernel,
        grid=(frames // step,),
        in_specs=[rows] * 7
        + [pl.BlockSpec((pairs, step, 128), lambda i: (0, i, 0))]
        + [whole(item) for item in fixed],
        out_specs=[rows] * 4
        + [
            pl.BlockSpec((step, width), lambda i: (i, 0)),
            pl.BlockSpec((places - 1, step, width), lambda i: (0, i, 0)),
            vector, vector,
        ],
        out_shape=[
            like(LOW), like(LOW), like(LOW), like(LOW),
            jax.ShapeDtypeStruct((frames, width), F32),
            jax.ShapeDtypeStruct((places - 1, frames, width), LOW),
            jax.ShapeDtypeStruct((1, width), F32),
            jax.ShapeDtypeStruct((1, width), F32),
        ],
        scratch_shapes=[pltpu.VMEM((places * step, width), F32)],
        compiler_params=pltpu.CompilerParams(vmem_limit_bytes=60 << 20),
    )(x, mid, dhn, dout, q, k, v, probs, *fixed)


def greet(count):
    utt, me = lax.axis_index("utt"), lax.axis_index("seq")
    barrier = pltpu.get_barrier_semaphore()

    @pl.loop(1, count)
    def _(step):
        pl.semaphore_signal(
            barrier, inc=1, device_id=(utt, lax.rem(me + step, count)), device_id_type=MESH_ID
        )

    return barrier


def remote(source, target, send_sem, recv_sem, place):
    return pltpu.make_async_remote_copy(
        src_ref=source,
        dst_ref=target,
        send_sem=send_sem,
        recv_sem=recv_sem,
        device_id=(lax.axis_index("utt"), place),
        device_id_type=MESH_ID,
    )


def two_heads(rows):
    lane = lax.broadcasted_iota(jnp.int32, rows.shape, 1)
    zero = jnp.zeros_like(rows)
    return jnp.concatenate([jnp.where(lane < HD, rows, zero), jnp.where(lane < HD, zero, rows)], axis=0)


def join_heads(tall):
    rows = tall.T
    lane = lax.broadcasted_iota(jnp.int32, (HD, LANES), 1)
    return jnp.where(lane < HD, rows[:HD], rows[HD:])


def masked_scores(scores, bias, first, block):
    key = first + lax.broadcasted_iota(jnp.int32, scores.shape, 0)
    query = block * HD + lax.rem(lax.broadcasted_iota(jnp.int32, scores.shape, 1), HD)
    return jnp.where(key < query, scores + bias, jnp.where(key == query, scores, NEGATIVE))


def fill_bias(bias_ref, mask):
    for block in range(mask.shape[0]):
        row = lax.broadcasted_iota(jnp.int32, (HD, LANES), 0)
        lane = lax.broadcasted_iota(jnp.int32, (HD, LANES), 1)
        flags = jnp.broadcast_to(mask[block, 0:1, :], (HD, LANES))
        diagonal = jnp.where(row == lane, flags.astype(F32), 0.0).astype(LOW)
        usable = mul(diagonal, jnp.ones((LANES, LANES), LOW))
        bias_ref[block * HD : (block + 1) * HD, :] = (usable - 1.0) * 1e30


def attend_kernel(
    count, x_ref, mask_ref, n1_ref, wq_ref, wk_ref, wv_ref,
    normed_ref, mixed_ref, saved_ref, log_ref,
    packed, held, mixed_all, pieces, bias, v_t, send_sem, recv_sem, send_two, recv_two, save_sem,
):
    share = count // 16
    me = lax.axis_index("seq")
    unit, part = me // share, me % share
    own_utt, own_pair = unit // 8, unit % 8
    own_cols = pl.ds(pl.multiple_of(own_pair * LANES, LANES), LANES)
    utts, frames, width = x_ref.shape
    barrier = greet(count)

    x = x_ref[...].astype(F32).reshape(utts * frames, width)
    normed = (x * scale_of(x) * n1_ref[...]).astype(LOW)
    normed_ref[...] = normed
    packed[:, 0:64] = (mul(normed, wq_ref[...]).astype(LOW)).reshape(utts, frames, width)
    packed[:, 64:128] = mul(normed, wk_ref[...]).astype(LOW).reshape(utts, frames, width)
    packed[:, 128:192] = mul(normed, wv_ref[...]).astype(LOW).reshape(utts, frames, width)
    for pair in range(8):
        packed[:, 192:208, pair * LANES : (pair + 1) * LANES] = jnp.broadcast_to(
            mask_ref[...], (utts, 16, LANES)
        )
    pl.semaphore_wait(barrier, count - 1)

    def outgoing(step):
        place = lax.rem(me + step, count)
        target = place // share
        cols = pl.ds(pl.multiple_of((target % 8) * LANES, LANES), LANES)
        return remote(
            packed.at[target // 8, :, cols], held.at[me], send_sem.at[step], recv_sem.at[step], place
        )

    @pl.loop(1, count)
    def _(step):
        outgoing(step).start()

    held[me] = packed[own_utt, :, own_cols]

    @pl.loop(1, count)
    def _(step):
        place = lax.rem(me + count - step, count)
        remote(held.at[place], held.at[place], send_sem.at[step], recv_sem.at[step], place).wait_recv()

    save = pltpu.make_async_copy(held, saved_ref, save_sem)
    save.start()
    v_t[...] = held[:, 128:192].reshape(count * HD, LANES).T
    fill_bias(bias, held[:, 192:208])

    def returning(block):
        return remote(
            pieces.at[block],
            mixed_all.at[own_utt, :, own_cols],
            send_two.at[block],
            recv_two.at[unit],
            block,
        )

    for group in range(count // 4):
        below = group * 256
        here = below + 256

        @pl.loop(0, 4 // share)
        def _(index):
            block = 4 * group + share * index + part
            query = two_heads(held[block, 0:64] * LOW(HD ** (-0.5)))
            keys = held[4 * group : 4 * group + 4, 64:128].reshape(256, LANES)
            near = masked_scores(mul_t(keys, query), bias[below:here], below, block)
            peak = jnp.max(near, axis=0, keepdims=True)
            if group:
                keys = held[0 : 4 * group, 64:128].reshape(below, LANES)
                far = mul_t(keys, query) + bias[0:below]
                peak = jnp.maximum(peak, jnp.max(far, axis=0, keepdims=True))
                far = jnp.exp(far - peak)
            near = jnp.exp(near - peak)
            total = jnp.sum(near, axis=0, keepdims=True)
            if group:
                total = total + jnp.sum(far, axis=0, keepdims=True)
            inverse = 1.0 / total
            mixed = mul(v_t[:, below:here], (near * inverse).astype(LOW))
            if group:
                mixed = mixed + mul(v_t[:, 0:below], (far * inverse).astype(LOW))
            log_ref[block] = jnp.broadcast_to(peak + jnp.log(total), (8, LANES))
            pieces[block] = join_heads(mixed).astype(LOW)

            @pl.when(block != me)
            def _():
                returning(block).start()

            @pl.when(block == me)
            def _():
                mixed_all[own_utt, :, own_cols] = pieces[block]

    @pl.loop(0, 16)
    def _(other):
        place = other * share + me % share
        cols = pl.ds(pl.multiple_of((other % 8) * LANES, LANES), LANES)

        @pl.when(place != me)
        def _():
            here = mixed_all.at[other // 8, :, cols]
            remote(here, here, send_two.at[0], recv_two.at[other], place).wait_recv()

    @pl.loop(1, count)
    def _(step):
        outgoing(step).wait_send()

    @pl.loop(0, count // share)
    def _(index):
        block = share * index + part

        @pl.when(block != me)
        def _():
            returning(block).wait_send()

    mixed_ref[...] = mixed_all[...]
    save.wait()


def global_attend(x, mask, params):
    count = lax.axis_size("seq")
    utts, frames, width = x.shape
    vmem = pl.BlockSpec(memory_space=pltpu.VMEM)
    hbm = pl.BlockSpec(memory_space=pl.ANY)
    return pl.pallas_call(
        functools.partial(attend_kernel, count),
        in_specs=[vmem] * 6,
        out_specs=[vmem, vmem, hbm, vmem],
        out_shape=[
            jax.ShapeDtypeStruct((utts * frames, width), LOW),
            jax.ShapeDtypeStruct((utts, frames, width), LOW),
            jax.ShapeDtypeStruct((count, 208, LANES), LOW),
            jax.ShapeDtypeStruct((count, 8, LANES), F32),
        ],
        scratch_shapes=[
            pltpu.VMEM((utts, 208, width), LOW),
            pltpu.VMEM((count, 208, LANES), LOW),
            pltpu.VMEM((utts, frames, width), LOW),
            pltpu.VMEM((count, HD, LANES), LOW),
            pltpu.VMEM((count * HD, LANES), F32),
            pltpu.VMEM((LANES, count * HD), LOW),
            pltpu.SemaphoreType.DMA((count,)),
            pltpu.SemaphoreType.DMA((count,)),
            pltpu.SemaphoreType.DMA((count,)),
            pltpu.SemaphoreType.DMA((16,)),
            pltpu.SemaphoreType.DMA,
        ],
        compiler_params=pltpu.CompilerParams(
            collective_id=2, has_side_effects=True, vmem_limit_bytes=48 << 20
        ),
    )(x, mask, params[0].reshape(1, -1), params[1], params[2], params[3])


def attend_back_kernel(
    count, grad_ref, held, log_ref,
    dqkv_ref,
    grads, landed, pieces, dk_acc, dv_acc, bias, k_t, send_sem, recv_sem, send_two, recv_two,
):
    share = count // 16
    me = lax.axis_index("seq")
    unit, part = me // share, me % share
    own_utt, own_pair = unit // 8, unit % 8
    own_cols = pl.ds(pl.multiple_of(own_pair * LANES, LANES), LANES)
    barrier = greet(count)
    k_t[...] = held[:, 64:128].reshape(count * HD, LANES).T
    fill_bias(bias, held[:, 192:208])
    dk_acc[...] = jnp.zeros_like(dk_acc)
    dv_acc[...] = jnp.zeros_like(dv_acc)
    pl.semaphore_wait(barrier, count - 1)

    def outgoing(other):
        cols = pl.ds(pl.multiple_of((other % 8) * LANES, LANES), LANES)
        place = other * share + part
        return place, remote(
            grad_ref.at[other // 8, :, cols], grads.at[me // share], send_sem.at[other],
            recv_sem.at[me // share], place,
        )

    @pl.loop(1, 16)
    def _(step):
        _, copy = outgoing(lax.rem(unit + step, 16))
        copy.start()

    grads[unit] = grad_ref[own_utt, :, own_cols]

    @pl.loop(1, 16)
    def _(step):
        other = lax.rem(unit + step, 16)
        here = grads.at[other]
        remote(here, here, send_sem.at[other], recv_sem.at[other], other * share + part).wait_recv()

    def returning(block):
        return remote(
            pieces.at[block],
            landed.at[part, :, own_utt, :, own_cols],
            send_two.at[block],
            recv_two.at[me],
            block,
        )

    for group in reversed(range(count // 4)):
        below = group * 256
        here = below + 256

        @pl.loop(0, 4 // share)
        def _(index):
            block = 4 * group + share * index + part
            query = two_heads(held[block, 0:64] * LOW(HD ** (-0.5)))
            grad = two_heads(grads[block // share])
            log_total = log_ref[block][0:1]
            near_v = held[4 * group : 4 * group + 4, 128:192].reshape(256, LANES)
            near_k = held[4 * group : 4 * group + 4, 64:128].reshape(256, LANES)
            near = masked_scores(mul_t(near_k, query), bias[below:here], below, block)
            near = jnp.exp(near - log_total)
            near_dp = mul_t(near_v, grad)
            delta = jnp.sum(near * near_dp, axis=0, keepdims=True)
            if group:
                far_v = held[0 : 4 * group, 128:192].reshape(below, LANES)
                far_k = held[0 : 4 * group, 64:128].reshape(below, LANES)
                far = jnp.exp(mul_t(far_k, query) + bias[0:below] - log_total)
                far_dp = mul_t(far_v, grad)
                delta = delta + jnp.sum(far * far_dp, axis=0, keepdims=True)
                far_ds = (far * (far_dp - delta)).astype(LOW)
                dk_acc[0:below] += mul(far_ds, query)
                dv_acc[0:below] += mul(far.astype(LOW), grad)
            near_ds = (near * (near_dp - delta)).astype(LOW)
            dk_acc[below:here] += mul(near_ds, query)
            dv_acc[below:here] += mul(near.astype(LOW), grad)
            dq = mul(k_t[:, below:here], near_ds)
            if group:
                dq = dq + mul(k_t[:, 0:below], far_ds)
            pieces[block, 0] = (join_heads(dq) * HD ** (-0.5)).astype(LOW)

        for block in range(4 * group, 4 * group + 4):
            rows = slice(block * HD, (block + 1) * HD)
            pieces[block, 1] = dk_acc[rows].astype(LOW)
            pieces[block, 2] = dv_acc[rows].astype(LOW)
            if share > 1:

                @pl.when(block % share != part)
                def _():
                    pieces[block, 0] = jnp.zeros((HD, LANES), LOW)

            @pl.when(block != me)
            def _():
                returning(block).start()

            @pl.when(block == me)
            def _():
                landed[part, :, own_utt, :, own_cols] = pieces[block]

    @pl.loop(1, count)
    def _(step):
        place = lax.rem(me + step, count)
        other, other_part = place // share, place % share
        cols = pl.ds(pl.multiple_of((other % 8) * LANES, LANES), LANES)
        here = landed.at[other_part, :, other // 8, :, cols]
        remote(here, here, send_two.at[place], recv_two.at[place], place).wait_recv()

    @pl.loop(1, 16)
    def _(step):
        _, copy = outgoing(lax.rem(unit + step, 16))
        copy.wait_send()

    @pl.loop(1, count)
    def _(step):
        returning(lax.rem(me + step, count)).wait_send()

    total = landed[0]
    for other_part in range(1, share):
        total = (total.astype(F32) + landed[other_part].astype(F32)).astype(LOW)
    dqkv_ref[...] = total


def global_attend_back(grad_mixed, saved, log_total):
    count = lax.axis_size("seq")
    utts, frames, width = grad_mixed.shape
    vmem = pl.BlockSpec(memory_space=pltpu.VMEM)
    return pl.pallas_call(
        functools.partial(attend_back_kernel, count),
        in_specs=[vmem] * 3,
        out_specs=vmem,
        out_shape=jax.ShapeDtypeStruct((3, utts, frames, width), LOW),
        scratch_shapes=[
            pltpu.VMEM((16, HD, LANES), LOW),
            pltpu.VMEM((count // 16, 3, utts, frames, width), LOW),
            pltpu.VMEM((count, 3, HD, LANES), LOW),
            pltpu.VMEM((count * HD, LANES), F32),
            pltpu.VMEM((count * HD, LANES), F32),
            pltpu.VMEM((count * HD, LANES), F32),
            pltpu.VMEM((LANES, count * HD), LOW),
            pltpu.SemaphoreType.DMA((16,)),
            pltpu.SemaphoreType.DMA((16,)),
            pltpu.SemaphoreType.DMA((count,)),
            pltpu.SemaphoreType.DMA((count,)),
        ],
        compiler_params=pltpu.CompilerParams(
            collective_id=3, has_side_effects=True, vmem_limit_bytes=48 << 20
        ),
    )(grad_mixed, saved, log_total)


SLOTS = 4
DEEP = 8
SROWS = 64
SCOLS = 512
ACOLS = 384
DRAIN = 8
PLAN = (
    (0, 8, 8), (8, 8, 2), (16, 2, 2), (18, 2, 2), (20, 2, 2), (22, 2, 2), (24, 6, 2),
    (30, 8, 2), (38, 8, 8), (46, 2, 2), (48, 2, 2), (50, 2, 2), (52, 2, 2), (54, 1, 1),
)
SLABS = 55
LOADED = 16
AT_BACK = 8
AT_ATTEND = 15
AT_RETURN = 23
AT_LANDED = 40


def tail_kernel(names, out_count, *refs):
    r = types.SimpleNamespace(**dict(zip(names, refs)))
    outs = refs[names.index("out_0") : names.index("out_0") + out_count]
    utt = lax.axis_index("utt")
    seq = lax.axis_index("seq")
    count = 16
    pos = seq // 4
    col = (seq // 2) % 2
    core = seq % 2
    core_id = (utt, pos * 4 + col * 2 + 1 - core)
    col_id = (utt, pos * 4 + (1 - col) * 2 + core)
    utt_id = (1 - utt, seq)
    right_id = (utt, lax.rem(seq + 4, 16))
    left_id = (utt, lax.rem(seq + 12, 16))

    barrier = greet(count)
    pl.semaphore_signal(barrier, inc=1, device_id=utt_id, device_id_type=MESH_ID)

    def window(ref, spec, slab, lead):
        local = slab - spec[0]
        rows = pl.ds(pl.multiple_of((local // spec[2]) * SROWS, SROWS), SROWS)
        cols = pl.ds(pl.multiple_of((local % spec[2]) * SCOLS, SCOLS), SCOLS)
        return ref.at[lead + (rows, cols)]

    def load_start(slab):
        slot = slab % SLOTS
        for ref, spec in ((r.l_up, PLAN[0]), (r.l_down, PLAN[1])):

            @pl.when((slab >= spec[0]) & (slab < spec[0] + spec[1]))
            def _():
                for side in range(2):
                    pltpu.make_async_copy(
                        window(ref, spec, slab, (slice(None), side)),
                        r.part.at[slot, side],
                        r.load_sem.at[slot, side],
                    ).start()

    def load_wait(slot):
        for side in range(2):
            pltpu.make_async_copy(
                r.l_up.at[:, side, pl.ds(0, SROWS), pl.ds(0, SCOLS)],
                r.part.at[slot, side],
                r.load_sem.at[slot, side],
            ).wait()

    def weights(block, slot):
        start = block * SCOLS if isinstance(block, int) else pl.multiple_of(block * SCOLS, SCOLS)
        return (
            pltpu.make_async_copy(
                r.g_w_up.at[:, pl.ds(start, SCOLS)], r.up_buf.at[slot], r.weight_sem.at[slot, 0]
            ),
            pltpu.make_async_copy(
                r.g_w_down.at[pl.ds(start, SCOLS)], r.down_buf.at[slot], r.weight_sem.at[slot, 1]
            ),
        )

    fetches = (
        (r.g_w_o, r.square.at[0]), (r.g_w_q, r.square.at[1]), (r.g_w_k, r.square.at[2]),
        (r.g_w_v, r.square.at[3]), (r.saved, r.held), (r.l_normed, r.l_x.at[0]),
        (r.l_mixed, r.l_x.at[1]), (r.l_dq, r.l_g.at[0]), (r.l_dk, r.l_g.at[1]),
        (r.l_dv, r.l_g.at[2]), (r.l_dattn, r.l_g.at[3]), (r.rest, r.table_g),
        (r.g_act, r.act_buf), (r.g_mixed, r.g_x.at[0]), (r.g_normed, r.g_x.at[1]),
    )

    def fetch(*which):
        return [
            pltpu.make_async_copy(*fetches[index], r.fetch_sem.at[index]) for index in which
        ]

    for copy in weights(0, 0) + tuple(fetch(0)):
        copy.start()
    load_start(0)

    def send(kind, slot, source, target, device):
        return pltpu.make_async_remote_copy(
            src_ref=source,
            dst_ref=target,
            send_sem=r.send_sem.at[kind, slot],
            recv_sem=r.recv_sem.at[kind, slot],
            device_id=device,
            device_id_type=MESH_ID,
        )

    def core_copy(slot):
        return send(0, slot, r.part.at[slot, 1 - core], r.recv_c.at[slot], core_id)

    def col_copy_a(slot):
        return send(1, slot, r.half_a.at[slot, 1 - col], r.recv_xa.at[slot], col_id)

    def utt_copy_b(slot):
        return send(2, slot, r.half_b.at[slot, 1 - utt], r.recv_yb.at[slot], utt_id)

    def col_copy_b(slot):
        return send(3, slot, r.sum_b.at[slot, 1 - col], r.recv_xb.at[slot], col_id)

    def utt_copy_a(slot, deep):
        return send(4, slot, r.sum_a.at[deep, pos], r.recv_ya.at[slot], utt_id)

    def utt_copy_b2(slot, deep):
        return send(5, slot, r.line_b.at[deep, pos], r.recv_yb2.at[slot], utt_id)

    def col_copy_c(slot, deep):
        return send(24, slot, r.line_c.at[deep, pos, 1 - col], r.recv_xc.at[slot], col_id)

    def utt_copy_c(slot):
        return send(25, slot, r.sum_c.at[slot], r.recv_yc.at[slot], utt_id)

    def line_right(kind, slot, deep, step, source, target):
        dest = jnp.minimum(4 - step + pos, 3)
        return send(kind + step - 1, slot, source.at[deep, dest], target.at[slot, step - 1], right_id)

    def line_left(kind, slot, deep, step, source, target):
        dest = jnp.maximum(pos - 4 + step, 0)
        return send(kind + step - 1, slot, source.at[deep, dest], target.at[slot, step - 1], left_id)

    def line_start(slot, deep, step, source, right, left, kind):
        @pl.when((pos <= step - 1) & (pos < 3))
        def _():
            line_right(kind, slot, deep, step, source, right).start()

        @pl.when((pos >= 4 - step) & (pos > 0))
        def _():
            line_left(kind + 3, slot, deep, step, source, left).start()

    def line_finish(slot, deep, step, source, right, left, kind):
        @pl.when((pos <= step - 1) & (pos < 3))
        def _():
            line_right(kind, slot, deep, step, source, right).wait_send()

        @pl.when((pos >= 4 - step) & (pos > 0))
        def _():
            line_left(kind + 3, slot, deep, step, source, left).wait_send()

        @pl.when((pos >= 1) & (pos <= step))
        def _():
            line_right(kind, slot, deep, step, source, right).wait_recv()
            dest = 3 - step + pos
            source[deep, dest] = (
                source[deep, dest].astype(F32) + right[slot, step - 1].astype(F32)
            ).astype(LOW)

        @pl.when((pos <= 2) & (pos >= 3 - step))
        def _():
            line_left(kind + 3, slot, deep, step, source, left).wait_recv()
            dest = pos + step - 3
            source[deep, dest] = (
                source[deep, dest].astype(F32) + left[slot, step - 1].astype(F32)
            ).astype(LOW)

    line_a = (r.sum_a, r.right_a, r.left_a, 6)
    line_bb = (r.line_b, r.right_b, r.left_b, 12)
    line_cc = (r.line_c, r.right_c, r.left_c, 18)

    def advance(tick):
        def stage(offset):
            slab = tick - offset
            return (
                slab,
                lax.rem(slab + SLOTS * 4, SLOTS),
                lax.rem(slab + DEEP, DEEP),
                pl.when((slab >= 0) & (slab < SLABS)),
                pl.when((slab >= 0) & (slab < SLABS - 1)),
            )

        slab, slot, _, guard, _ = stage(0)
        load_start(slab + 1)

        @pl.when(slab < LOADED)
        def _():
            load_wait(slot)

        @guard
        def _():
            core_copy(slot).start()

        _, slot1, deep1, guard, most = stage(1)

        @guard
        def _():
            core_copy(slot1).wait()
            for line in range(4):
                for side in range(2):
                    both = r.part[slot1, core, 2 * line + side].astype(F32) + r.recv_c[
                        slot1, 2 * line + side
                    ].astype(F32)
                    both = both.astype(LOW)
                    r.half_a[slot1, side, line] = both[:32, :ACOLS]
                    r.line_c[deep1, line, side] = both[:32, ACOLS:]
                    r.half_b[slot1, 0, side, line] = both[32:48]
                    r.half_b[slot1, 1, side, line] = both[48:]
            line_start(slot1, deep1, 1, *line_cc)

        @most
        def _():
            col_copy_a(slot1).start()
            utt_copy_b(slot1).start()

        _, slot2, deep2, guard, most = stage(2)

        @guard
        def _():
            line_finish(slot2, deep2, 1, *line_cc)
            line_start(slot2, deep2, 2, *line_cc)

        @most
        def _():
            col_copy_a(slot2).wait()
            r.sum_a[deep2] = (
                r.half_a[slot2, col].astype(F32) + r.recv_xa[slot2].astype(F32)
            ).astype(LOW)
            line_start(slot2, deep2, 1, *line_a)
            utt_copy_b(slot2).wait()
            r.sum_b[slot2] = (
                r.half_b[slot2, utt].astype(F32) + r.recv_yb[slot2].astype(F32)
            ).astype(LOW)
            col_copy_b(slot2).start()

        _, slot3, deep3, guard, most = stage(3)

        @guard
        def _():
            line_finish(slot3, deep3, 2, *line_cc)
            line_start(slot3, deep3, 3, *line_cc)

        @most
        def _():
            line_finish(slot3, deep3, 1, *line_a)
            line_start(slot3, deep3, 2, *line_a)
            col_copy_b(slot3).wait()
            r.line_b[deep3] = (
                r.sum_b[slot3, col].astype(F32) + r.recv_xb[slot3].astype(F32)
            ).astype(LOW)
            line_start(slot3, deep3, 1, *line_bb)

        _, slot4, deep4, guard, most = stage(4)

        @guard
        def _():
            line_finish(slot4, deep4, 3, *line_cc)
            col_copy_c(slot4, deep4).start()

        @most
        def _():
            line_finish(slot4, deep4, 2, *line_a)
            line_start(slot4, deep4, 3, *line_a)
            line_finish(slot4, deep4, 1, *line_bb)
            line_start(slot4, deep4, 2, *line_bb)

        _, slot5, deep5, guard, most = stage(5)

        @guard
        def _():
            col_copy_c(slot5, deep5).wait()
            r.sum_c[slot5] = (
                r.line_c[deep5, pos, col].astype(F32) + r.recv_xc[slot5].astype(F32)
            ).astype(LOW)
            utt_copy_c(slot5).start()

        @most
        def _():
            line_finish(slot5, deep5, 3, *line_a)
            utt_copy_a(slot5, deep5).start()
            line_finish(slot5, deep5, 2, *line_bb)
            line_start(slot5, deep5, 3, *line_bb)

        _, slot6, deep6, guard, most = stage(6)

        @guard
        def _():
            utt_copy_c(slot6).wait()
            r.staged[slot6, 0:32, ACOLS:] = r.sum_c[slot6].astype(F32) + r.recv_yc[slot6].astype(F32)

        @most
        def _():
            utt_copy_a(slot6, deep6).wait()
            r.staged[slot6, 0:32, :ACOLS] = r.sum_a[deep6, pos].astype(F32) + r.recv_ya[
                slot6
            ].astype(F32)
            line_finish(slot6, deep6, 3, *line_bb)
            utt_copy_b2(slot6, deep6).start()

        slab7, slot7, deep7, guard, most = stage(7)

        @most
        def _():
            utt_copy_b2(slot7, deep7).wait()
            mine = r.line_b[deep7, pos].astype(F32)
            theirs = r.recv_yb2[slot7].astype(F32)
            r.staged[slot7, 32:48] = jnp.where(utt == 0, mine, theirs)
            r.staged[slot7, 48:64] = jnp.where(utt == 0, theirs, mine)

        for ref, spec in zip(outs, PLAN):

            @pl.when((slab7 >= spec[0]) & (slab7 < spec[0] + spec[1]))
            def _():
                pltpu.make_async_copy(
                    r.staged.at[slot7], window(ref, spec, slab7, ()), r.out_sem.at[slot7]
                ).start()

        _, slot8, _, guard, _ = stage(8)

        @guard
        def _():
            pltpu.make_async_copy(
                r.staged.at[slot8], outs[0].at[pl.ds(0, SROWS), pl.ds(0, SCOLS)], r.out_sem.at[slot8]
            ).wait()

    def cols_of(index):
        return pl.ds(pl.multiple_of(index * SCOLS, SCOLS), SCOLS)

    def put(slot, dest, rows):
        r.part[slot, dest % 2, dest // 2] = rows.astype(LOW)

    def put_product(slot, left_of, right):
        for quarter in range(4):
            rows = mul(left_of(quarter), right)
            for index in range(4):
                put(slot, 4 * quarter + index, rows[64 * index : 64 * index + 64])

    def quarter_rows(ref, lead=()):
        return lambda quarter: ref[lead + (slice(256 * quarter, 256 * quarter + 256),)]

    def produce(slab):
        slot = slab % SLOTS

        def among(first, number):
            return pl.when((slab >= first) & (slab < first + number))

        @among(16, 8)
        def _():
            local = slab - 16
            put_product(slot, quarter_rows(r.l_x_t), r.l_g[local // 2, :, cols_of(local % 2)])

        @among(24, 6)
        def _():
            local = slab - 24
            for dest in range(16):
                place = 3 * dest + local // 2
                book = place // 16
                first = (place % 16) * SROWS
                ids = first + lax.broadcasted_iota(jnp.int32, (SROWS, LANES), 0)
                picked = (ids == r.codes[book][0:1]).astype(LOW)
                put(slot, dest, mul(picked, r.table_g[book, :, cols_of(local % 2)]))

        @among(30, 8)
        def _():
            local = slab - 30
            inner = local // 2

            def rows(quarter):
                return jnp.concatenate(
                    [
                        r.act_t[pl.ds(pl.multiple_of(256 * dest + 64 * inner, 64), 64)]
                        for dest in range(4 * quarter, 4 * quarter + 4)
                    ],
                    axis=0,
                )

            put_product(slot, rows, r.dout_low[:, cols_of(local % 2)])

        @among(38, 8)
        def _():
            put_product(slot, quarter_rows(r.g_hn_t), r.du[:, cols_of(slab - 38)])

        @among(46, 8)
        def _():
            local = slab - 46
            kind = local // 2
            put_product(
                slot,
                quarter_rows(r.g_x_t, (jnp.minimum(kind, 1),)),
                r.g_g[kind, :, cols_of(local % 2)],
            )

        @pl.when(slab == 54)
        def _():
            b_down = jnp.sum(r.dout_low[...].astype(F32), axis=0, keepdims=True)
            for dest in range(16):
                shared = slice(LANES * (dest // 2), LANES * (dest // 2) + LANES)
                rows = [r.dn1[:, shared], r.dn2[:, shared], b_down[:, shared]]
                for index in range(2):
                    first = 256 * (dest % 2) + LANES * index
                    rows.append(r.db1[dest // 2 : dest // 2 + 1, first : first + LANES])
                rows += [r.l_dn1[:, shared], r.l_dn2[:, shared], r.l_db2[:, shared]]
                for index in range(2):
                    first = 256 * dest + LANES * index
                    rows.append(r.l_db1[:, first : first + LANES])
                rows.append(jnp.zeros((6, LANES), F32))
                r.part[slot, dest % 2, dest // 2, 0:16, ACOLS:] = jnp.concatenate(
                    rows, axis=0
                ).astype(LOW)

    own_utt, own_pair = seq // 8, seq % 8
    own_cols = pl.ds(pl.multiple_of(own_pair * LANES, LANES), LANES)

    def pair_cols(other):
        return pl.ds(pl.multiple_of((other % 8) * LANES, LANES), LANES)

    def hand_out(other):
        return remote(
            r.dmix.at[other // 8, :, pair_cols(other)], r.grads.at[seq], r.send_one.at[other],
            r.recv_one.at[seq], other,
        )

    def hand_back(block):
        return remote(
            r.pieces.at[block], r.landed.at[:, own_utt, :, own_cols], r.send_two.at[block],
            r.recv_two.at[seq], block,
        )

    def others(body):
        @pl.loop(1, count)
        def _(step):
            body(lax.rem(seq + step, count))

    def compute(tick):
        def at(*ticks):
            hit = tick == ticks[0]
            for item in ticks[1:]:
                hit = hit | (tick == item)
            return pl.when(hit)

        @pl.when(tick < 8)
        def _():
            slot = tick % 2
            for copy in weights(tick, slot):
                copy.wait()

            @pl.when(tick < 7)
            def _():
                for copy in weights(tick + 1, 1 - slot):
                    copy.start()

            @pl.when(tick == 0)
            def _():
                r.dout_low[...] = r.dout[...].astype(LOW)
                r.dhn[...] = jnp.zeros_like(r.dhn)

            cols = cols_of(tick)
            _, slope = gelu_parts(r.u[:, cols])
            du = (mul_t(r.dout_low[...], r.down_buf[slot]) * slope).astype(LOW)
            r.du[:, cols] = du
            r.db1[pl.ds(tick, 1), :] = jnp.sum(du.astype(F32), axis=0, keepdims=True)
            r.dhn[...] += mul_t(du, r.up_buf[slot])

        @at(3)
        def _():
            for copy in fetch(4, 5, 6, 7, 8, 9, 10):
                copy.start()

        @at(12)
        def _():
            for copy in fetch(1, 2, 3, 11, 12, 13, 14):
                copy.start()

        @at(AT_BACK)
        def _():
            for copy in fetch(0):
                copy.wait()
            dmid, gain = scale_back(r.mid[...], r.n2[...], r.dhn[...])
            r.dn2[...] = jnp.sum(gain, axis=0, keepdims=True)
            dmid = dmid + r.dout[...]
            r.dmid[...] = dmid
            dattn = dmid.astype(LOW)
            r.g_g[0] = dattn
            r.dmix[...] = mul_t(dattn, r.square[0]).astype(LOW).reshape(r.dmix.shape)
            r.grads[seq] = r.dmix[own_utt, :, own_cols]

        @pl.when((tick >= AT_BACK) & (tick < AT_BACK + 5))
        def _():
            @pl.loop(0, 3)
            def _(index):
                hand_out(lax.rem(seq + 3 * (tick - AT_BACK) + index + 1, count)).start()

        @at(AT_BACK + 1)
        def _():
            for copy in fetch(4, 5, 6, 7, 8, 9, 10):
                copy.wait()
            r.k_t[...] = r.held[:, 64:128].reshape(count * HD, LANES).T
            fill_bias(r.bias, r.held[:, 192:208])
            r.dk_acc[...] = jnp.zeros_like(r.dk_acc)
            r.dv_acc[...] = jnp.zeros_like(r.dv_acc)
            r.l_x_t[...] = r.l_x[0].T

        @at(AT_ATTEND)
        def _():
            def arrived(other):
                here = r.grads.at[other]
                remote(here, here, r.send_one.at[other], r.recv_one.at[other], other).wait_recv()

            others(arrived)

        for order, group in enumerate(reversed(range(4))):
            below = group * 256
            here = below + 256
            begin = AT_ATTEND + 2 * order

            @at(begin, begin + 1)
            def _():
                @pl.loop(0, 2)
                def _(index):
                    attend_back_block(
                        r, group, below, here, 4 * group + 2 * (tick - begin) + index
                    )

            @at(begin + 1)
            def _():
                for block in range(4 * group, 4 * group + 4):
                    rows = slice(block * HD, (block + 1) * HD)
                    r.pieces[block, 1] = r.dk_acc[rows].astype(LOW)
                    r.pieces[block, 2] = r.dv_acc[rows].astype(LOW)

        @at(AT_RETURN)
        def _():
            r.landed[:, own_utt, :, own_cols] = r.pieces[seq]

        @pl.when((tick >= AT_RETURN) & (tick < AT_RETURN + 15))
        def _():
            hand_back(lax.rem(seq + tick - AT_RETURN + 1, count)).start()

        @at(AT_LANDED)
        def _():
            def arrived(other):
                here = r.landed.at[:, other // 8, :, pair_cols(other)]
                remote(here, here, r.send_two.at[other], r.recv_two.at[other], other).wait_recv()

            others(arrived)
            others(lambda other: hand_out(other).wait_send())
            others(lambda other: hand_back(other).wait_send())
            for index in range(3):
                r.g_g[1 + index] = r.landed[index].reshape(r.g_g.shape[1:])

        @at(AT_LANDED + 1)
        def _():
            for copy in fetch(1, 2, 3):
                copy.wait()
            r.dhn[...] = mul_t(r.g_g[1], r.square[1])

        @at(AT_LANDED + 2)
        def _():
            r.dhn[...] += mul_t(r.g_g[2], r.square[2])

        @at(AT_LANDED + 3)
        def _():
            dnormed = r.dhn[...] + mul_t(r.g_g[3], r.square[3])
            dx, gain = scale_back(r.x[...].astype(F32), r.n1[...], dnormed)
            r.dn1[...] = jnp.sum(gain, axis=0, keepdims=True)
            r.dx[...] = dx + r.dmid[...]

        @at(21)
        def _():
            r.l_x_t[...] = r.l_x[1].T

        @at(22)
        def _():
            for copy in fetch(11, 12, 13, 14):
                copy.wait()

        @pl.when((tick >= 24) & (tick < 28))
        def _():
            cols = pl.ds(pl.multiple_of((tick - 24) * 1024, 1024), 1024)
            r.act_t[cols] = r.act_buf[:, cols].T

        @at(29)
        def _():
            r.g_hn_t[...] = r.hn[...].T

        @at(31, 32)
        def _():
            r.g_x_t[tick - 31] = r.g_x[tick - 31].T

    pl.semaphore_wait(barrier, count)

    @pl.loop(0, SLABS + DRAIN)
    def _(tick):
        advance(tick)
        compute(tick)
        produce(tick + 1)


def attend_back_block(r, group, below, here, block):
    query = two_heads(r.held[block, 0:64] * LOW(HD ** (-0.5)))
    grad = two_heads(r.grads[block])
    log_total = r.log_total[block][0:1]
    near_v = r.held[4 * group : 4 * group + 4, 128:192].reshape(256, LANES)
    near_k = r.held[4 * group : 4 * group + 4, 64:128].reshape(256, LANES)
    near = masked_scores(mul_t(near_k, query), r.bias[below:here], below, block)
    near = jnp.exp(near - log_total)
    near_dp = mul_t(near_v, grad)
    delta = jnp.sum(near * near_dp, axis=0, keepdims=True)
    if group:
        far_v = r.held[0 : 4 * group, 128:192].reshape(below, LANES)
        far_k = r.held[0 : 4 * group, 64:128].reshape(below, LANES)
        far = jnp.exp(mul_t(far_k, query) + r.bias[0:below] - log_total)
        far_dp = mul_t(far_v, grad)
        delta = delta + jnp.sum(far * far_dp, axis=0, keepdims=True)
        far_ds = (far * (far_dp - delta)).astype(LOW)
        r.dk_acc[0:below] += mul(far_ds, query)
        r.dv_acc[0:below] += mul(far.astype(LOW), grad)
    near_ds = (near * (near_dp - delta)).astype(LOW)
    r.dk_acc[below:here] += mul(near_ds, query)
    r.dv_acc[below:here] += mul(near.astype(LOW), grad)
    dq = mul(r.k_t[:, below:here], near_ds)
    if group:
        dq = dq + mul(r.k_t[:, 0:below], far_ds)
    r.pieces[block, 0] = (join_heads(dq) * HD ** (-0.5)).astype(LOW)


def finish_on_slice(far, near):
    vmem = pl.BlockSpec(memory_space=pltpu.VMEM)
    hbm = pl.BlockSpec(memory_space=pl.ANY)
    rows, width = near["x"].shape
    wide = near["u"].shape[1]
    utts = rows // HD
    shapes = [
        (width // 16, wide), (wide // 16, width), (width // 16, width), (width // 16, width),
        (width // 16, width), (width // 16, width), (3 * 1024 // 16, width), (wide // 16, width),
        (width // 16, wide), (width // 16, width), (width // 16, width), (width // 16, width),
        (width // 16, width), (SROWS, SCOLS),
    ]
    out_names = ["dx"] + ["out_%d" % index for index in range(len(shapes))]
    rows_l = far["l_normed"].shape[0]
    buffers = dict(
        part=((SLOTS, 2, 8, 64, SCOLS), LOW),
        recv_c=((SLOTS, 8, 64, SCOLS), LOW),
        half_a=((SLOTS, 2, 4, 32, ACOLS), LOW),
        half_b=((SLOTS, 2, 2, 4, 16, SCOLS), LOW),
        recv_xa=((SLOTS, 4, 32, ACOLS), LOW),
        recv_yb=((SLOTS, 2, 4, 16, SCOLS), LOW),
        sum_a=((DEEP, 4, 32, ACOLS), LOW),
        sum_b=((SLOTS, 2, 4, 16, SCOLS), LOW),
        recv_xb=((SLOTS, 4, 16, SCOLS), LOW),
        line_b=((DEEP, 4, 16, SCOLS), LOW),
        right_a=((SLOTS, 3, 32, ACOLS), LOW),
        left_a=((SLOTS, 3, 32, ACOLS), LOW),
        right_b=((SLOTS, 3, 16, SCOLS), LOW),
        left_b=((SLOTS, 3, 16, SCOLS), LOW),
        recv_ya=((SLOTS, 32, ACOLS), LOW),
        recv_yb2=((SLOTS, 16, SCOLS), LOW),
        line_c=((DEEP, 4, 2, 32, LANES), LOW),
        right_c=((SLOTS, 3, 2, 32, LANES), LOW),
        left_c=((SLOTS, 3, 2, 32, LANES), LOW),
        recv_xc=((SLOTS, 32, LANES), LOW),
        sum_c=((SLOTS, 32, LANES), LOW),
        recv_yc=((SLOTS, 32, LANES), LOW),
        staged=((SLOTS, 64, SCOLS), F32),
        up_buf=((2, width, SCOLS), LOW),
        down_buf=((2, SCOLS, width), LOW),
        square=((4, width, width), LOW),
        held=(far["saved"].shape, LOW),
        l_x=((2, rows_l, width), LOW),
        l_g=((4, rows_l, width), LOW),
        l_x_t=((width, rows_l), LOW),
        table_g=(far["rest"].shape, LOW),
        act_buf=((rows, wide), LOW),
        act_t=((wide, rows), LOW),
        g_x=((2, rows, width), LOW),
        g_x_t=((2, width, rows), LOW),
        g_hn_t=((width, rows), LOW),
        g_g=((4, rows, width), LOW),
        dout_low=((rows, width), LOW),
        du=((rows, wide), LOW),
        db1=((8, SCOLS), F32),
        dn1=((1, width), F32),
        dn2=((1, width), F32),
        dhn=((rows, width), F32),
        dmid=((rows, width), F32),
        dmix=((utts, HD, width), LOW),
        grads=((16, HD, LANES), LOW),
        landed=((3, utts, HD, width), LOW),
        pieces=((16, 3, HD, LANES), LOW),
        dk_acc=((16 * HD, LANES), F32),
        dv_acc=((16 * HD, LANES), F32),
        bias=((16 * HD, LANES), F32),
        k_t=((LANES, 16 * HD), LOW),
    )
    semaphores = dict(
        load_sem=(SLOTS, 2), out_sem=(SLOTS,), send_sem=(26, SLOTS), recv_sem=(26, SLOTS),
        weight_sem=(2, 2), fetch_sem=(15,), send_one=(16,), recv_one=(16,), send_two=(16,),
        recv_two=(16,),
    )
    names = list(far) + list(near) + out_names + list(buffers) + list(semaphores)
    return pl.pallas_call(
        functools.partial(tail_kernel, names, len(shapes)),
        in_specs=[hbm] * len(far) + [vmem] * len(near),
        out_specs=[vmem] + [hbm] * len(shapes),
        out_shape=[jax.ShapeDtypeStruct((rows, width), F32)]
        + [jax.ShapeDtypeStruct(shape, F32) for shape in shapes],
        scratch_shapes=[pltpu.VMEM(*item) for item in buffers.values()]
        + [pltpu.SemaphoreType.DMA(item) for item in semaphores.values()],
        compiler_params=pltpu.CompilerParams(
            collective_id=1, has_side_effects=True, vmem_limit_bytes=60 << 20
        ),
    )(*far.values(), *near.values())


def normalize(values, gain_vec):
    return (
        values * lax.rsqrt(jnp.mean(values * values, axis=-1, keepdims=True) + EPSILON) * gain_vec
    )


def gelu_fn(values):
    return jax.nn.gelu(values, approximate=True)


def project(left_side, weight):
    return jnp.dot(left_side, weight, preferred_element_type=jnp.float32)


def project_back(gradient, weight):
    return lax.dot_general(
        gradient, weight, (((1,), (1,)), ((), ())), preferred_element_type=jnp.float32
    )


def weight_grad(left_side, gradient):
    return lax.dot_general(
        left_side, gradient, (((0,), (0,)), ((), ())), preferred_element_type=jnp.float32
    )


def block_outputs(inputs, mixed_rows, params):
    middle = inputs + project(mixed_rows, params[4])
    middle_norm = normalize(middle, params[5]).astype(jnp.bfloat16)
    pre_active = project(middle_norm, params[6]) + params[7]
    active = gelu_fn(pre_active).astype(jnp.bfloat16)
    result = middle + project(active, params[8]) + params[9]
    return (result, (middle, middle_norm, pre_active, active))


def block_back(inputs, normed, mixed_rows, kept_parts, params, grad_out, attention_back):
    middle, middle_norm, pre_active, active = kept_parts
    grad_branch = grad_out.astype(jnp.bfloat16)
    grad_b_down = jnp.sum(grad_branch.astype(jnp.float32), axis=0)
    grad_w_down = weight_grad(active, grad_branch)
    grad_active = project_back(grad_branch, params[8])
    grad_pre = jax.vjp(gelu_fn, pre_active)[1](grad_active)[0].astype(jnp.bfloat16)
    grad_b_up = jnp.sum(grad_pre.astype(jnp.float32), axis=0)
    grad_w_up = weight_grad(middle_norm, grad_pre)
    middle_back = jax.vjp(normalize, middle, params[5])[1]
    grad_middle, grad_norm_two = middle_back(project_back(grad_pre, params[6]))
    grad_middle = grad_middle + grad_out
    grad_attn = grad_middle.astype(jnp.bfloat16)
    grad_w_output = weight_grad(mixed_rows, grad_attn)
    grad_mixed = project_back(grad_attn, params[4]).astype(jnp.bfloat16)
    grad_query, grad_key, grad_value = attention_back(grad_mixed)
    grad_normed = (
        project_back(grad_query, params[1])
        + project_back(grad_key, params[2])
        + project_back(grad_value, params[3])
    )
    input_back = jax.vjp(normalize, inputs, params[0])[1]
    grad_inputs, grad_norm_one = input_back(grad_normed)
    weight_grads = (
        grad_norm_one,
        weight_grad(normed, grad_query),
        weight_grad(normed, grad_key),
        weight_grad(normed, grad_value),
        grad_w_output,
        grad_norm_two,
        grad_w_up,
        grad_b_up,
        grad_w_down,
        grad_b_down,
    )
    return (grad_inputs + grad_middle, weight_grads)


def on_device(
    frames,
    codes,
    lengths,
    frame_mask,
    table,
    glob_norm_one,
    glob_w_query,
    glob_w_key,
    glob_w_value,
    glob_w_output,
    glob_norm_two,
    glob_w_up,
    glob_b_up,
    glob_w_down,
    glob_b_down,
    local_norm_one,
    local_w_query,
    local_w_key,
    local_w_value,
    local_w_output,
    local_norm_two,
    local_w_up,
    local_b_up,
    local_w_down,
    local_b_down,
    cotan_global,
    cotan_local,
):
    utter_count, frame_count, model_width = frames.shape
    row_count = utter_count * frame_count
    local_len = CB + 1
    positions = lax.axis_index("seq") * frame_count + jnp.arange(frame_count, dtype=jnp.int32)
    valid = positions[None, :] < lengths[:, None]
    usable = jnp.pad(frame_mask.astype(LOW), ((0, 0), (0, LANES - frame_count)))
    usable = jnp.broadcast_to(usable[:, None, :], (utter_count, 16, LANES))
    glob_params = (
        glob_norm_one,
        glob_w_query,
        glob_w_key,
        glob_w_value,
        glob_w_output,
        glob_norm_two,
        glob_w_up,
        glob_b_up,
        glob_w_down,
        glob_b_down,
    )
    local_params = (
        local_norm_one,
        local_w_query,
        local_w_key,
        local_w_value,
        local_w_output,
        local_norm_two,
        local_w_up,
        local_b_up,
        local_w_down,
        local_b_down,
    )
    global_in = frames.astype(jnp.float32).reshape(row_count, model_width)
    glob_normed, glob_mixed, saved, log_total = global_attend(frames, usable, glob_params)
    glob_mixed = glob_mixed.reshape(row_count, model_width)
    glob_result, glob_kept = block_outputs(global_in, glob_mixed, glob_params)
    global_rows = jnp.where(valid.reshape(row_count, 1), glob_result, 0.0).astype(jnp.bfloat16)
    code_rows = codes.transpose(2, 0, 1).reshape(CB, row_count)
    table_ids = code_rows + VOCAB * jnp.arange(CB, dtype=jnp.int32)[:, None]
    embedded = table.at[table_ids].get(mode="promise_in_bounds")
    local_in = jnp.concatenate([global_rows[None], embedded], axis=0)
    local_shape = (local_len, row_count, model_width)
    flat_shape = (local_len * row_count, model_width)
    normed, local_q, local_k, local_v, local_probs, mixed, middle, middle_norm = local_front(
        local_in, local_params
    )
    row_valid = valid.reshape(1, row_count, 1)
    local_cotan = cotan_local.transpose(2, 0, 1, 3).reshape(local_shape)
    local_cotan = jnp.where(row_valid, local_cotan, 0)
    local_result, grad_hidden, grad_w_up, grad_w_down, grad_b_up = local_ffn(
        middle_norm.reshape(flat_shape),
        local_cotan.reshape(flat_shape),
        middle.reshape(flat_shape),
        local_params,
    )
    local_rows = jnp.where(row_valid, local_result.reshape(local_shape), 0)
    local_rows = local_rows.reshape(local_len, utter_count, frame_count, model_width)
    local_rows = local_rows.transpose(1, 2, 0, 3)
    grad_attn, grad_q, grad_k, grad_v, grad_first, grad_rest, grad_n1, grad_n2 = local_back(
        local_in,
        middle,
        grad_hidden.reshape(local_shape),
        local_cotan,
        local_q,
        local_k,
        local_v,
        local_probs,
        local_params,
    )
    normed = normed.reshape(flat_shape)
    mixed = mixed.reshape(flat_shape)
    grad_b_down = jnp.sum(local_cotan.astype(F32), axis=(0, 1))
    grad_first = grad_first.reshape(utter_count, frame_count, model_width)
    glob_cotan = jnp.where(
        valid[:, :, None], cotan_global.astype(jnp.float32) + grad_first, 0.0
    )
    glob_cotan = glob_cotan.reshape(row_count, model_width)
    outputs = (global_rows.reshape(utter_count, frame_count, model_width), local_rows)

    if lax.axis_size("seq") == 16 and lax.axis_size("utt") == 2:
        glob_middle, glob_middle_norm, pre_active, active = glob_kept
        far = dict(
            l_up=grad_w_up.reshape(8, 2, -1, grad_w_up.shape[1]),
            l_down=grad_w_down.reshape(8, 2, -1, grad_w_down.shape[1]),
            g_w_up=glob_w_up,
            g_w_down=glob_w_down,
            g_w_o=glob_w_output,
            g_w_q=glob_w_query,
            g_w_k=glob_w_key,
            g_w_v=glob_w_value,
            saved=saved,
            l_normed=normed,
            l_mixed=mixed,
            l_dq=grad_q.reshape(flat_shape),
            l_dk=grad_k.reshape(flat_shape),
            l_dv=grad_v.reshape(flat_shape),
            l_dattn=grad_attn.reshape(flat_shape),
            rest=grad_rest,
            g_act=active,
            g_mixed=glob_mixed,
            g_normed=glob_normed,
        )
        near = dict(
            u=pre_active,
            dout=glob_cotan,
            mid=glob_middle,
            hn=glob_middle_norm,
            x=frames.reshape(row_count, model_width),
            n1=glob_norm_one.reshape(1, -1),
            n2=glob_norm_two.reshape(1, -1),
            log_total=log_total,
            codes=jnp.broadcast_to(code_rows[:, None, :], (CB, 8, row_count)),
            l_dn1=grad_n1,
            l_dn2=grad_n2,
            l_db1=grad_b_up,
            l_db2=grad_b_down.reshape(1, -1),
        )
        grad_inputs, *sums = finish_on_slice(far, near)
        wide = dict(zip("12qkvot76pabc", sums[:-1]))
        half = lax.axis_index("seq") % 2
        rest = sums[-1]

        def piece(row):
            return jnp.where(half == 0, rest[row, ACOLS : ACOLS + LANES // 2], rest[row, ACOLS + LANES // 2 :])

        def piece_wide(row):
            return rest[row : row + 2, ACOLS:].reshape(-1)

        return outputs + (
            grad_inputs.reshape(utter_count, frame_count, model_width),
            wide["t"],
            piece(0),
            wide["a"],
            wide["b"],
            wide["c"],
            wide["p"],
            piece(1),
            wide["6"],
            piece_wide(3),
            wide["7"],
            piece(2),
            piece(5),
            wide["q"],
            wide["k"],
            wide["v"],
            wide["o"],
            piece(6),
            wide["1"],
            piece_wide(8),
            wide["2"],
            piece(7),
        )

    local_grads = (
        grad_n1[0],
        weight_grad(normed, grad_q.reshape(flat_shape)),
        weight_grad(normed, grad_k.reshape(flat_shape)),
        weight_grad(normed, grad_v.reshape(flat_shape)),
        weight_grad(mixed, grad_attn.reshape(flat_shape)),
        grad_n2[0],
        grad_w_up,
        grad_b_up[0],
        grad_w_down,
        grad_b_down,
    )
    picked = code_rows[:, None, :] == jnp.arange(VOCAB, dtype=jnp.int32)[None, :, None]
    grad_tab = jnp.einsum(
        "cvn,cnd->cvd", picked.astype(LOW), grad_rest, preferred_element_type=F32
    ).reshape(CB * VOCAB, model_width)

    def global_back(grad_mixed):
        grads = global_attend_back(
            grad_mixed.reshape(utter_count, frame_count, model_width), saved, log_total
        )
        return tuple(grads.reshape(3, row_count, model_width))

    grad_inputs, glob_grads = block_back(
        global_in, glob_normed, glob_mixed, glob_kept, glob_params, glob_cotan, global_back
    )
    reduced = reduce_all((grad_tab,) + glob_grads + local_grads)
    return outputs + (grad_inputs.reshape(utter_count, frame_count, model_width),) + reduced


def solution(mesh):
    return jax.shard_map(
        on_device,
        mesh=mesh,
        in_specs=(
            P("utt", "seq", None),
            P("utt", "seq", None),
            P("utt"),
            P("utt", "seq"),
            P(),
            P(),
            P(),
            P(),
            P(),
            P(),
            P(),
            P(),
            P(),
            P(),
            P(),
            P(),
            P(),
            P(),
            P(),
            P(),
            P(),
            P(),
            P(),
            P(),
            P(),
            P("utt", "seq", None),
            P("utt", "seq", None, None),
        ),
        out_specs=(
            P("utt", "seq", None),
            P("utt", "seq", None, None),
            P("utt", "seq", None),
            P("seq", None),
            P("seq"),
            P("seq", None),
            P("seq", None),
            P("seq", None),
            P("seq", None),
            P("seq"),
            P("seq", None),
            P("seq"),
            P("seq", None),
            P("seq"),
            P("seq"),
            P("seq", None),
            P("seq", None),
            P("seq", None),
            P("seq", None),
            P("seq"),
            P("seq", None),
            P("seq"),
            P("seq", None),
            P("seq"),
        ),
        check_vma=False,
    )
```

```python
import functools
import types

import jax
import jax.numpy as jnp
from jax import lax
from jax.experimental import pallas as pl
from jax.experimental.pallas import tpu as pltpu
from jax.sharding import PartitionSpec as P

H = 16
HD = 64
CB = 3
VOCAB = 1024


EPSILON = 1e-05
NEGATIVE = -1e30
F32 = jnp.float32
LOW = jnp.bfloat16
LANES = 128
MESH_ID = pl.DeviceIdType.MESH


def reduce_all(grads):
    return tuple(
        lax.psum(
            lax.psum_scatter(item.astype(LOW), "seq", scatter_dimension=0, tiled=True), "utt"
        ).astype(F32)
        for item in grads
    )


def mul(left_side, right_side):
    return jnp.dot(left_side, right_side, preferred_element_type=F32)


def mul_t(left_side, right_side):
    return lax.dot_general(
        left_side, right_side, (((1,), (1,)), ((), ())), preferred_element_type=F32
    )


def t_mul(left_side, right_side):
    return lax.dot_general(
        left_side, right_side, (((0,), (0,)), ((), ())), preferred_element_type=F32
    )


def scale_of(values):
    return lax.rsqrt(jnp.mean(values * values, axis=-1, keepdims=True) + EPSILON)


def scale_back(values, gain, grad):
    scale = scale_of(values)
    inner = grad * gain
    shared = jnp.mean(values * inner, axis=-1, keepdims=True) * (scale * scale * scale)
    return inner * scale - values * shared, grad * values * scale


def head_sums(width):
    rows = lax.broadcasted_iota(jnp.int32, (width, 128), 0) // HD
    cols = lax.broadcasted_iota(jnp.int32, (width, 128), 1)
    return (rows == cols).astype(LOW)


def head_spread(width):
    rows = lax.broadcasted_iota(jnp.int32, (128, width), 0)
    cols = lax.broadcasted_iota(jnp.int32, (128, width), 1) // HD
    return (rows == cols).astype(LOW)


def sum_heads(product, sums):
    high = product.astype(LOW)
    rest = (product - high.astype(F32)).astype(LOW)
    return mul(high, sums) + mul(rest, sums)


def front_kernel(
    x_ref, n1_ref, wq_ref, wk_ref, wv_ref, wo_ref, n2_ref,
    normed_ref, q_ref, k_ref, v_ref, probs_ref, mixed_ref, mid_ref, mid_norm_ref,
):
    places, frames, width = x_ref.shape
    rows = places * frames
    x = x_ref[...].astype(F32).reshape(rows, width)
    normed = (x * scale_of(x) * n1_ref[...]).astype(LOW)
    normed_ref[...] = normed.reshape(places, frames, width)
    q_ref[...] = mul(normed, wq_ref[...]).astype(LOW).reshape(places, frames, width)
    k_ref[...] = mul(normed, wk_ref[...]).astype(LOW).reshape(places, frames, width)
    v_ref[...] = mul(normed, wv_ref[...]).astype(LOW).reshape(places, frames, width)
    sums, spread = head_sums(width), head_spread(width)
    pair = 0
    for i in range(places):
        query = q_ref[i].astype(F32)
        scores = [
            sum_heads(query * k_ref[j].astype(F32), sums) * HD ** (-0.5) for j in range(i + 1)
        ]
        peak = scores[0]
        for item in scores[1:]:
            peak = jnp.maximum(peak, item)
        raised = [jnp.exp(item - peak) for item in scores]
        total = raised[0]
        for item in raised[1:]:
            total = total + item
        mixed = None
        for j in range(i + 1):
            probs = raised[j] / total
            probs_ref[pair] = probs
            pair += 1
            term = mul(probs.astype(LOW), spread) * v_ref[j].astype(F32)
            mixed = term if mixed is None else mixed + term
        mixed_ref[i] = mixed.astype(LOW)
    mid = x + mul(mixed_ref[...].reshape(rows, width), wo_ref[...])
    mid_ref[...] = mid.reshape(places, frames, width)
    mid_norm_ref[...] = (
        (mid * scale_of(mid) * n2_ref[...]).astype(LOW).reshape(places, frames, width)
    )


def local_front(x, params):
    places, frames, width = x.shape
    pairs = places * (places + 1) // 2
    step = 64
    rows = pl.BlockSpec((places, step, width), lambda i: (0, i, 0))
    whole = lambda item: pl.BlockSpec(item.shape, lambda i: (0, 0), pipeline_mode=pl.Buffered(1))
    n1, n2 = params[0].reshape(1, -1), params[5].reshape(1, -1)
    operands = (x, n1, params[1], params[2], params[3], params[4], n2)
    like = lambda kind: jax.ShapeDtypeStruct((places, frames, width), kind)
    return pl.pallas_call(
        front_kernel,
        grid=(frames // step,),
        in_specs=[rows] + [whole(item) for item in operands[1:]],
        out_specs=[rows] * 4
        + [pl.BlockSpec((pairs, step, 128), lambda i: (0, i, 0))]
        + [rows] * 3,
        out_shape=[
            like(LOW), like(LOW), like(LOW), like(LOW),
            jax.ShapeDtypeStruct((pairs, frames, 128), F32),
            like(LOW), like(F32), like(LOW),
        ],
        compiler_params=pltpu.CompilerParams(vmem_limit_bytes=56 << 20),
    )(*operands)


def gelu_parts(u):
    scale = 0.7978845608028654
    inner = jnp.tanh(scale * (u + 0.044715 * u * u * u))
    half = 0.5 * (1.0 + inner)
    slope = half + 0.5 * u * (1.0 - inner * inner) * scale * (1.0 + 3 * 0.044715 * u * u)
    return u * half, slope


def ffn_kernel(
    hn_ref, dout_ref, mid_ref, w1_ref, b1_ref, w2_ref, b2_ref,
    y_ref, dhn_ref, dw1_ref, dw2_ref, db1_ref, acc_ref, hn_t_ref,
):
    at = pl.program_id(0)
    last = pl.num_programs(0) - 1

    @pl.when(at == 0)
    def _():
        hn_t_ref[...] = hn_ref[...].T
        acc_ref[...] = mid_ref[...] + b2_ref[...]
        dhn_ref[...] = jnp.zeros_like(dhn_ref)

    hn, dout = hn_ref[...], dout_ref[...]
    u = mul(hn, w1_ref[...]) + b1_ref[...]
    act, slope = gelu_parts(u)
    act = act.astype(LOW)
    acc_ref[...] += mul(act, w2_ref[...])
    du = (mul_t(dout, w2_ref[...]) * slope).astype(LOW)
    db1_ref[...] = jnp.sum(du.astype(F32), axis=0, keepdims=True)
    dhn_ref[...] += mul_t(du, w1_ref[...])
    dw1_ref[...] = mul(hn_t_ref[...], du).astype(LOW)
    dw2_ref[...] = t_mul(act, dout).astype(LOW)

    @pl.when(at == last)
    def _():
        y_ref[...] = acc_ref[...].astype(LOW)


def local_ffn(hn, dout, mid, params):
    rows, width = hn.shape
    wide = params[6].shape[1]
    step = 512
    whole = pl.BlockSpec((rows, width), lambda i: (0, 0), pipeline_mode=pl.Buffered(1))
    out_whole = pl.BlockSpec((rows, width), lambda i: (0, 0))
    return pl.pallas_call(
        ffn_kernel,
        grid=(wide // step,),
        in_specs=[
            whole, whole, whole,
            pl.BlockSpec((width, step), lambda i: (0, i)),
            pl.BlockSpec((1, step), lambda i: (0, i)),
            pl.BlockSpec((step, width), lambda i: (i, 0)),
            pl.BlockSpec((1, width), lambda i: (0, 0)),
        ],
        out_specs=[
            out_whole, out_whole,
            pl.BlockSpec((width, step), lambda i: (0, i)),
            pl.BlockSpec((step, width), lambda i: (i, 0)),
            pl.BlockSpec((1, step), lambda i: (0, i)),
        ],
        out_shape=[
            jax.ShapeDtypeStruct((rows, width), LOW),
            jax.ShapeDtypeStruct((rows, width), F32),
            jax.ShapeDtypeStruct((width, wide), LOW),
            jax.ShapeDtypeStruct((wide, width), LOW),
            jax.ShapeDtypeStruct((1, wide), F32),
        ],
        scratch_shapes=[pltpu.VMEM((rows, width), F32), pltpu.VMEM((width, rows), LOW)],
        compiler_params=pltpu.CompilerParams(vmem_limit_bytes=56 << 20),
    )(hn, dout, mid, params[6], params[7].reshape(1, -1), params[8], params[9].reshape(1, -1))


def back_kernel(
    x_ref, mid_ref, dhn_ref, dout_ref, q_ref, k_ref, v_ref, probs_ref,
    n1_ref, n2_ref, wq_ref, wk_ref, wv_ref, wo_ref,
    dattn_ref, dq_ref, dk_ref, dv_ref, first_ref, rest_ref, dn1_ref, dn2_ref,
    dmid_ref,
):
    places, frames, width = x_ref.shape
    rows = places * frames

    @pl.when(pl.program_id(0) == 0)
    def _():
        dn1_ref[...] = jnp.zeros_like(dn1_ref)
        dn2_ref[...] = jnp.zeros_like(dn2_ref)

    mid = mid_ref[...].reshape(rows, width)
    dmid, gain = scale_back(mid, n2_ref[...], dhn_ref[...].reshape(rows, width))
    dn2_ref[...] += jnp.sum(gain, axis=0, keepdims=True)
    dmid = dmid + dout_ref[...].astype(F32).reshape(rows, width)
    dmid_ref[...] = dmid
    dattn = dmid.astype(LOW)
    dattn_ref[...] = dattn.reshape(places, frames, width)
    dmixed = mul_t(dattn, wo_ref[...]).astype(LOW).reshape(places, frames, width)
    sums, spread = head_sums(width), head_spread(width)
    pair = 0
    dk, dv = [None] * places, [None] * places
    add = lambda old, term: term if old is None else old + term
    for i in range(places):
        grad = dmixed[i].astype(F32)
        query = q_ref[i].astype(F32)
        dp = [sum_heads(grad * v_ref[j].astype(F32), sums) for j in range(i + 1)]
        delta = None
        for j in range(i + 1):
            delta = add(delta, probs_ref[pair + j] * dp[j])
        dq = None
        for j in range(i + 1):
            probs = probs_ref[pair + j]
            ds = (probs * (dp[j] - delta)).astype(LOW)
            ds = mul(ds, spread)
            dq = add(dq, ds * k_ref[j].astype(F32))
            dk[j] = add(dk[j], ds * query)
            dv[j] = add(dv[j], mul(probs.astype(LOW), spread) * grad)
        pair += i + 1
        dq_ref[i] = (dq * HD ** (-0.5)).astype(LOW)
    for j in range(places):
        dk_ref[j] = (dk[j] * HD ** (-0.5)).astype(LOW)
        dv_ref[j] = dv[j].astype(LOW)
    dnormed = (
        mul_t(dq_ref[...].reshape(rows, width), wq_ref[...])
        + mul_t(dk_ref[...].reshape(rows, width), wk_ref[...])
        + mul_t(dv_ref[...].reshape(rows, width), wv_ref[...])
    )
    x = x_ref[...].astype(F32).reshape(rows, width)
    dx, gain = scale_back(x, n1_ref[...], dnormed)
    dn1_ref[...] += jnp.sum(gain, axis=0, keepdims=True)
    dx = (dx + dmid_ref[...]).reshape(places, frames, width)
    first_ref[...] = dx[0]
    rest_ref[...] = dx[1:].astype(LOW)


def local_back(x, mid, dhn, dout, q, k, v, probs, params):
    places, frames, width = x.shape
    pairs = probs.shape[0]
    step = 64
    rows = pl.BlockSpec((places, step, width), lambda i: (0, i, 0))
    whole = lambda item: pl.BlockSpec(item.shape, lambda i: (0, 0), pipeline_mode=pl.Buffered(1))
    like = lambda kind: jax.ShapeDtypeStruct((places, frames, width), kind)
    fixed = (params[0].reshape(1, -1), params[5].reshape(1, -1)) + tuple(params[1:5])
    vector = pl.BlockSpec((1, width), lambda i: (0, 0))
    return pl.pallas_call(
        back_kernel,
        grid=(frames // step,),
        in_specs=[rows] * 7
        + [pl.BlockSpec((pairs, step, 128), lambda i: (0, i, 0))]
        + [whole(item) for item in fixed],
        out_specs=[rows] * 4
        + [
            pl.BlockSpec((step, width), lambda i: (i, 0)),
            pl.BlockSpec((places - 1, step, width), lambda i: (0, i, 0)),
            vector, vector,
        ],
        out_shape=[
            like(LOW), like(LOW), like(LOW), like(LOW),
            jax.ShapeDtypeStruct((frames, width), F32),
            jax.ShapeDtypeStruct((places - 1, frames, width), LOW),
            jax.ShapeDtypeStruct((1, width), F32),
            jax.ShapeDtypeStruct((1, width), F32),
        ],
        scratch_shapes=[pltpu.VMEM((places * step, width), F32)],
        compiler_params=pltpu.CompilerParams(vmem_limit_bytes=60 << 20),
    )(x, mid, dhn, dout, q, k, v, probs, *fixed)


def greet(count):
    utt, me = lax.axis_index("utt"), lax.axis_index("seq")
    barrier = pltpu.get_barrier_semaphore()

    @pl.loop(1, count)
    def _(step):
        pl.semaphore_signal(
            barrier, inc=1, device_id=(utt, lax.rem(me + step, count)), device_id_type=MESH_ID
        )

    return barrier


def remote(source, target, send_sem, recv_sem, place):
    return pltpu.make_async_remote_copy(
        src_ref=source,
        dst_ref=target,
        send_sem=send_sem,
        recv_sem=recv_sem,
        device_id=(lax.axis_index("utt"), place),
        device_id_type=MESH_ID,
    )


def two_heads(rows):
    lane = lax.broadcasted_iota(jnp.int32, rows.shape, 1)
    zero = jnp.zeros_like(rows)
    return jnp.concatenate([jnp.where(lane < HD, rows, zero), jnp.where(lane < HD, zero, rows)], axis=0)


def join_heads(tall):
    rows = tall.T
    lane = lax.broadcasted_iota(jnp.int32, (HD, LANES), 1)
    return jnp.where(lane < HD, rows[:HD], rows[HD:])


def masked_scores(scores, bias, first, block):
    key = first + lax.broadcasted_iota(jnp.int32, scores.shape, 0)
    query = block * HD + lax.rem(lax.broadcasted_iota(jnp.int32, scores.shape, 1), HD)
    return jnp.where(key < query, scores + bias, jnp.where(key == query, scores, NEGATIVE))


def fill_bias(bias_ref, mask):
    for block in range(mask.shape[0]):
        row = lax.broadcasted_iota(jnp.int32, (HD, LANES), 0)
        lane = lax.broadcasted_iota(jnp.int32, (HD, LANES), 1)
        flags = jnp.broadcast_to(mask[block, 0:1, :], (HD, LANES))
        diagonal = jnp.where(row == lane, flags.astype(F32), 0.0).astype(LOW)
        usable = mul(diagonal, jnp.ones((LANES, LANES), LOW))
        bias_ref[block * HD : (block + 1) * HD, :] = (usable - 1.0) * 1e30


def attend_kernel(
    count, x_ref, mask_ref, n1_ref, wq_ref, wk_ref, wv_ref, codes_ref, valid_ref, n2_ref, b1_ref,
    b2_ref, table_ref, wo_ref, w1_ref, w2_ref,
    normed_ref, mixed_ref, saved_ref, log_ref, local_ref, mid_ref, hn_ref, u_ref, act_ref,
    packed, held, mixed_all, pieces, bias, v_t, table, wo, w1, w2,
    send_sem, recv_sem, send_two, recv_two, save_sem, fetch_sem,
):
    share = count // 16
    me = lax.axis_index("seq")
    unit, part = me // share, me % share
    own_utt, own_pair = unit // 8, unit % 8
    own_cols = pl.ds(pl.multiple_of(own_pair * LANES, LANES), LANES)
    utts, frames, width = x_ref.shape
    rows = utts * frames
    barrier = greet(count)
    fetches = [
        pltpu.make_async_copy(source, target, fetch_sem.at[index])
        for index, (source, target) in enumerate(
            ((table_ref, table), (wo_ref, wo), (w1_ref, w1), (w2_ref, w2))
        )
    ]
    for copy in fetches:
        copy.start()

    x = x_ref[...].astype(F32).reshape(rows, width)
    normed = (x * scale_of(x) * n1_ref[...]).astype(LOW)
    normed_ref[...] = normed
    packed[:, 0:64] = (mul(normed, wq_ref[...]).astype(LOW)).reshape(utts, frames, width)
    packed[:, 64:128] = mul(normed, wk_ref[...]).astype(LOW).reshape(utts, frames, width)
    packed[:, 128:192] = mul(normed, wv_ref[...]).astype(LOW).reshape(utts, frames, width)
    for pair in range(8):
        packed[:, 192:208, pair * LANES : (pair + 1) * LANES] = jnp.broadcast_to(
            mask_ref[...], (utts, 16, LANES)
        )
    pl.semaphore_wait(barrier, count - 1)

    def outgoing(step):
        place = lax.rem(me + step, count)
        target = place // share
        cols = pl.ds(pl.multiple_of((target % 8) * LANES, LANES), LANES)
        return remote(
            packed.at[target // 8, :, cols], held.at[me], send_sem.at[step], recv_sem.at[step], place
        )

    @pl.loop(1, count)
    def _(step):
        outgoing(step).start()

    held[me] = packed[own_utt, :, own_cols]

    fetches[0].wait()
    vocab = table.shape[0] // CB
    for book in range(CB):
        ids = jnp.broadcast_to(codes_ref[book][:, 0:1], (rows, vocab))
        picked = (ids == lax.broadcasted_iota(jnp.int32, (rows, vocab), 1)).astype(LOW)
        local_ref[1 + book] = mul(picked, table[book * vocab : (book + 1) * vocab]).astype(LOW)

    save = pltpu.make_async_copy(held, saved_ref, save_sem)

    def returning(block):
        return remote(
            pieces.at[block],
            mixed_all.at[own_utt, :, own_cols],
            send_two.at[block],
            recv_two.at[unit],
            block,
        )

    for group in range(count // 4):
        below = group * 256
        here = below + 256
        for place in range(4 * group, 4 * group + 4):

            @pl.when(place != me)
            def _():
                step = lax.rem(me + count - place, count)
                remote(
                    held.at[place], held.at[place], send_sem.at[step], recv_sem.at[step], place
                ).wait_recv()

        v_t[:, below:here] = held[4 * group : 4 * group + 4, 128:192].reshape(256, LANES).T
        fill_bias(bias.at[below:here], held[4 * group : 4 * group + 4, 192:208])

        @pl.loop(0, 4 // share)
        def _(index):
            block = 4 * group + share * index + part
            query = two_heads(held[block, 0:64] * LOW(HD ** (-0.5)))
            keys = held[4 * group : 4 * group + 4, 64:128].reshape(256, LANES)
            near = masked_scores(mul_t(keys, query), bias[below:here], below, block)
            peak = jnp.max(near, axis=0, keepdims=True)
            if group:
                keys = held[0 : 4 * group, 64:128].reshape(below, LANES)
                far = mul_t(keys, query) + bias[0:below]
                peak = jnp.maximum(peak, jnp.max(far, axis=0, keepdims=True))
                far = jnp.exp(far - peak)
            near = jnp.exp(near - peak)
            total = jnp.sum(near, axis=0, keepdims=True)
            if group:
                total = total + jnp.sum(far, axis=0, keepdims=True)
            inverse = 1.0 / total
            mixed = mul(v_t[:, below:here], (near * inverse).astype(LOW))
            if group:
                mixed = mixed + mul(v_t[:, 0:below], (far * inverse).astype(LOW))
            log_ref[block] = jnp.broadcast_to(peak + jnp.log(total), (8, LANES))
            pieces[block] = join_heads(mixed).astype(LOW)

            @pl.when(block != me)
            def _():
                returning(block).start()

            @pl.when(block == me)
            def _():
                mixed_all[own_utt, :, own_cols] = pieces[block]

    save.start()

    @pl.loop(0, 16)
    def _(other):
        place = other * share + me % share
        cols = pl.ds(pl.multiple_of((other % 8) * LANES, LANES), LANES)

        @pl.when(place != me)
        def _():
            here = mixed_all.at[other // 8, :, cols]
            remote(here, here, send_two.at[0], recv_two.at[other], place).wait_recv()

    mixed = mixed_all[...].reshape(rows, width)
    mixed_ref[...] = mixed
    fetches[1].wait()
    mid = x_ref[...].astype(F32).reshape(rows, width) + mul(mixed, wo[...])
    hn = (mid * scale_of(mid) * n2_ref[...]).astype(LOW)
    mid_ref[...] = mid
    hn_ref[...] = hn
    fetches[2].wait()
    fetches[3].wait()
    result = mid + b2_ref[...]
    for first in range(0, u_ref.shape[1], 512):
        cols = slice(first, first + 512)
        u = mul(hn, w1[:, cols]) + b1_ref[:, cols]
        act = gelu_parts(u)[0].astype(LOW)
        u_ref[:, cols] = u
        act_ref[:, cols] = act
        result = result + mul(act, w2[cols])
    local_ref[0] = jnp.where(valid_ref[...] > 0, result, 0.0).astype(LOW)

    @pl.loop(1, count)
    def _(step):
        outgoing(step).wait_send()

    @pl.loop(0, count // share)
    def _(index):
        block = share * index + part

        @pl.when(block != me)
        def _():
            returning(block).wait_send()

    save.wait()


def global_forward(x, mask, codes, valid, table, params):
    count = lax.axis_size("seq")
    utts, frames, width = x.shape
    rows, wide = utts * frames, params[6].shape[1]
    vmem = pl.BlockSpec(memory_space=pltpu.VMEM)
    hbm = pl.BlockSpec(memory_space=pl.ANY)
    return pl.pallas_call(
        functools.partial(attend_kernel, count),
        in_specs=[vmem] * 11 + [hbm] * 4,
        out_specs=[vmem, vmem, hbm] + [vmem] * 6,
        out_shape=[
            jax.ShapeDtypeStruct((rows, width), LOW),
            jax.ShapeDtypeStruct((rows, width), LOW),
            jax.ShapeDtypeStruct((count, 208, LANES), LOW),
            jax.ShapeDtypeStruct((count, 8, LANES), F32),
            jax.ShapeDtypeStruct((1 + CB, rows, width), LOW),
            jax.ShapeDtypeStruct((rows, width), F32),
            jax.ShapeDtypeStruct((rows, width), LOW),
            jax.ShapeDtypeStruct((rows, wide), F32),
            jax.ShapeDtypeStruct((rows, wide), LOW),
        ],
        scratch_shapes=[
            pltpu.VMEM((utts, 208, width), LOW),
            pltpu.VMEM((count, 208, LANES), LOW),
            pltpu.VMEM((utts, frames, width), LOW),
            pltpu.VMEM((count, HD, LANES), LOW),
            pltpu.VMEM((count * HD, LANES), F32),
            pltpu.VMEM((LANES, count * HD), LOW),
            pltpu.VMEM(table.shape, LOW),
            pltpu.VMEM(params[4].shape, LOW),
            pltpu.VMEM(params[6].shape, LOW),
            pltpu.VMEM(params[8].shape, LOW),
            pltpu.SemaphoreType.DMA((count,)),
            pltpu.SemaphoreType.DMA((count,)),
            pltpu.SemaphoreType.DMA((count,)),
            pltpu.SemaphoreType.DMA((16,)),
            pltpu.SemaphoreType.DMA,
            pltpu.SemaphoreType.DMA((4,)),
        ],
        compiler_params=pltpu.CompilerParams(
            collective_id=2, has_side_effects=True, vmem_limit_bytes=58 << 20
        ),
    )(
        x, mask, params[0].reshape(1, -1), params[1], params[2], params[3], codes, valid,
        params[5].reshape(1, -1), params[7].reshape(1, -1), params[9].reshape(1, -1), table,
        params[4], params[6], params[8],
    )


def settle_kernel(number, *refs):
    sources, targets, held = (refs[index * number : (index + 1) * number] for index in range(3))
    into = [
        pltpu.make_async_copy(sources[index], held[index], refs[-1].at[0, index])
        for index in range(number)
    ]
    out = [
        pltpu.make_async_copy(held[index], targets[index], refs[-1].at[1, index])
        for index in range(number)
    ]
    for copy in into:
        copy.start()
    for first, second in zip(into, out):
        first.wait()
        second.start()
    for copy in out:
        copy.wait()


def settle(arrays):
    hbm = pl.BlockSpec(memory_space=pl.ANY)
    return pl.pallas_call(
        functools.partial(settle_kernel, len(arrays)),
        in_specs=[hbm] * len(arrays),
        out_specs=[hbm] * len(arrays),
        out_shape=[jax.ShapeDtypeStruct(item.shape, item.dtype) for item in arrays],
        scratch_shapes=[pltpu.VMEM(item.shape, item.dtype) for item in arrays]
        + [pltpu.SemaphoreType.DMA((2, len(arrays)))],
        compiler_params=pltpu.CompilerParams(vmem_limit_bytes=62 << 20),
    )(*arrays)


def attend_back_kernel(
    count, grad_ref, held, log_ref,
    dqkv_ref,
    grads, landed, pieces, dk_acc, dv_acc, bias, k_t, send_sem, recv_sem, send_two, recv_two,
):
    share = count // 16
    me = lax.axis_index("seq")
    unit, part = me // share, me % share
    own_utt, own_pair = unit // 8, unit % 8
    own_cols = pl.ds(pl.multiple_of(own_pair * LANES, LANES), LANES)
    barrier = greet(count)
    k_t[...] = held[:, 64:128].reshape(count * HD, LANES).T
    fill_bias(bias, held[:, 192:208])
    dk_acc[...] = jnp.zeros_like(dk_acc)
    dv_acc[...] = jnp.zeros_like(dv_acc)
    pl.semaphore_wait(barrier, count - 1)

    def outgoing(other):
        cols = pl.ds(pl.multiple_of((other % 8) * LANES, LANES), LANES)
        place = other * share + part
        return place, remote(
            grad_ref.at[other // 8, :, cols], grads.at[me // share], send_sem.at[other],
            recv_sem.at[me // share], place,
        )

    @pl.loop(1, 16)
    def _(step):
        _, copy = outgoing(lax.rem(unit + step, 16))
        copy.start()

    grads[unit] = grad_ref[own_utt, :, own_cols]

    @pl.loop(1, 16)
    def _(step):
        other = lax.rem(unit + step, 16)
        here = grads.at[other]
        remote(here, here, send_sem.at[other], recv_sem.at[other], other * share + part).wait_recv()

    def returning(block):
        return remote(
            pieces.at[block],
            landed.at[part, :, own_utt, :, own_cols],
            send_two.at[block],
            recv_two.at[me],
            block,
        )

    for group in reversed(range(count // 4)):
        below = group * 256
        here = below + 256

        @pl.loop(0, 4 // share)
        def _(index):
            block = 4 * group + share * index + part
            query = two_heads(held[block, 0:64] * LOW(HD ** (-0.5)))
            grad = two_heads(grads[block // share])
            log_total = log_ref[block][0:1]
            near_v = held[4 * group : 4 * group + 4, 128:192].reshape(256, LANES)
            near_k = held[4 * group : 4 * group + 4, 64:128].reshape(256, LANES)
            near = masked_scores(mul_t(near_k, query), bias[below:here], below, block)
            near = jnp.exp(near - log_total)
            near_dp = mul_t(near_v, grad)
            delta = jnp.sum(near * near_dp, axis=0, keepdims=True)
            if group:
                far_v = held[0 : 4 * group, 128:192].reshape(below, LANES)
                far_k = held[0 : 4 * group, 64:128].reshape(below, LANES)
                far = jnp.exp(mul_t(far_k, query) + bias[0:below] - log_total)
                far_dp = mul_t(far_v, grad)
                delta = delta + jnp.sum(far * far_dp, axis=0, keepdims=True)
                far_ds = (far * (far_dp - delta)).astype(LOW)
                dk_acc[0:below] += mul(far_ds, query)
                dv_acc[0:below] += mul(far.astype(LOW), grad)
            near_ds = (near * (near_dp - delta)).astype(LOW)
            dk_acc[below:here] += mul(near_ds, query)
            dv_acc[below:here] += mul(near.astype(LOW), grad)
            dq = mul(k_t[:, below:here], near_ds)
            if group:
                dq = dq + mul(k_t[:, 0:below], far_ds)
            pieces[block, 0] = (join_heads(dq) * HD ** (-0.5)).astype(LOW)

        for block in range(4 * group, 4 * group + 4):
            rows = slice(block * HD, (block + 1) * HD)
            pieces[block, 1] = dk_acc[rows].astype(LOW)
            pieces[block, 2] = dv_acc[rows].astype(LOW)
            if share > 1:

                @pl.when(block % share != part)
                def _():
                    pieces[block, 0] = jnp.zeros((HD, LANES), LOW)

            @pl.when(block != me)
            def _():
                returning(block).start()

            @pl.when(block == me)
            def _():
                landed[part, :, own_utt, :, own_cols] = pieces[block]

    @pl.loop(1, count)
    def _(step):
        place = lax.rem(me + step, count)
        other, other_part = place // share, place % share
        cols = pl.ds(pl.multiple_of((other % 8) * LANES, LANES), LANES)
        here = landed.at[other_part, :, other // 8, :, cols]
        remote(here, here, send_two.at[place], recv_two.at[place], place).wait_recv()

    @pl.loop(1, 16)
    def _(step):
        _, copy = outgoing(lax.rem(unit + step, 16))
        copy.wait_send()

    @pl.loop(1, count)
    def _(step):
        returning(lax.rem(me + step, count)).wait_send()

    total = landed[0]
    for other_part in range(1, share):
        total = (total.astype(F32) + landed[other_part].astype(F32)).astype(LOW)
    dqkv_ref[...] = total


def global_attend_back(grad_mixed, saved, log_total):
    count = lax.axis_size("seq")
    utts, frames, width = grad_mixed.shape
    vmem = pl.BlockSpec(memory_space=pltpu.VMEM)
    return pl.pallas_call(
        functools.partial(attend_back_kernel, count),
        in_specs=[vmem] * 3,
        out_specs=vmem,
        out_shape=jax.ShapeDtypeStruct((3, utts, frames, width), LOW),
        scratch_shapes=[
            pltpu.VMEM((16, HD, LANES), LOW),
            pltpu.VMEM((count // 16, 3, utts, frames, width), LOW),
            pltpu.VMEM((count, 3, HD, LANES), LOW),
            pltpu.VMEM((count * HD, LANES), F32),
            pltpu.VMEM((count * HD, LANES), F32),
            pltpu.VMEM((count * HD, LANES), F32),
            pltpu.VMEM((LANES, count * HD), LOW),
            pltpu.SemaphoreType.DMA((16,)),
            pltpu.SemaphoreType.DMA((16,)),
            pltpu.SemaphoreType.DMA((count,)),
            pltpu.SemaphoreType.DMA((count,)),
        ],
        compiler_params=pltpu.CompilerParams(
            collective_id=3, has_side_effects=True, vmem_limit_bytes=48 << 20
        ),
    )(grad_mixed, saved, log_total)


SLOTS = 4
DEEP = 8
SROWS = 64
SCOLS = 512
ACOLS = 384
DRAIN = 8
PLAN = (
    (0, 8, 8), (8, 8, 2), (16, 2, 2), (18, 2, 2), (20, 2, 2), (22, 2, 2), (24, 6, 2),
    (30, 8, 2), (38, 8, 8), (46, 2, 2), (48, 2, 2), (50, 2, 2), (52, 2, 2), (54, 1, 1),
)
SLABS = 55
LOADED = 16
AT_BACK = 8
AT_ATTEND = 15
AT_RETURN = 23
AT_LANDED = 40


def tail_kernel(names, out_count, *refs):
    r = types.SimpleNamespace(**dict(zip(names, refs)))
    outs = refs[names.index("out_0") : names.index("out_0") + out_count]
    utt = lax.axis_index("utt")
    seq = lax.axis_index("seq")
    count = 16
    pos = seq // 4
    col = (seq // 2) % 2
    core = seq % 2
    core_id = (utt, pos * 4 + col * 2 + 1 - core)
    col_id = (utt, pos * 4 + (1 - col) * 2 + core)
    utt_id = (1 - utt, seq)
    right_id = (utt, lax.rem(seq + 4, 16))
    left_id = (utt, lax.rem(seq + 12, 16))

    barrier = greet(count)
    pl.semaphore_signal(barrier, inc=1, device_id=utt_id, device_id_type=MESH_ID)

    def window(ref, spec, slab, lead):
        local = slab - spec[0]
        rows = pl.ds(pl.multiple_of((local // spec[2]) * SROWS, SROWS), SROWS)
        cols = pl.ds(pl.multiple_of((local % spec[2]) * SCOLS, SCOLS), SCOLS)
        return ref.at[lead + (rows, cols)]

    def load_start(slab):
        slot = slab % SLOTS
        for ref, spec in ((r.l_up, PLAN[0]), (r.l_down, PLAN[1])):

            @pl.when((slab >= spec[0]) & (slab < spec[0] + spec[1]))
            def _():
                for side in range(2):
                    pltpu.make_async_copy(
                        window(ref, spec, slab, (slice(None), side)),
                        r.part.at[slot, side],
                        r.load_sem.at[slot, side],
                    ).start()

    def load_wait(slot):
        for side in range(2):
            pltpu.make_async_copy(
                r.l_up.at[:, side, pl.ds(0, SROWS), pl.ds(0, SCOLS)],
                r.part.at[slot, side],
                r.load_sem.at[slot, side],
            ).wait()

    def weights(block, slot):
        start = block * SCOLS if isinstance(block, int) else pl.multiple_of(block * SCOLS, SCOLS)
        return (
            pltpu.make_async_copy(
                r.g_w_up.at[:, pl.ds(start, SCOLS)], r.up_buf.at[slot], r.weight_sem.at[slot, 0]
            ),
            pltpu.make_async_copy(
                r.g_w_down.at[pl.ds(start, SCOLS)], r.down_buf.at[slot], r.weight_sem.at[slot, 1]
            ),
        )

    fetches = (
        (r.g_w_o, r.square.at[0]), (r.g_w_q, r.square.at[1]), (r.g_w_k, r.square.at[2]),
        (r.g_w_v, r.square.at[3]), (r.saved, r.held), (r.l_normed, r.l_x.at[0]),
        (r.l_mixed, r.l_x.at[1]), (r.l_dq, r.l_g.at[0]), (r.l_dk, r.l_g.at[1]),
        (r.l_dv, r.l_g.at[2]), (r.l_dattn, r.l_g.at[3]), (r.rest, r.table_g),
        (r.g_act, r.act_buf), (r.g_mixed, r.g_x.at[0]), (r.g_normed, r.g_x.at[1]),
    )

    def fetch(*which):
        return [
            pltpu.make_async_copy(*fetches[index], r.fetch_sem.at[index]) for index in which
        ]

    for copy in weights(0, 0) + tuple(fetch(0)):
        copy.start()
    load_start(0)

    def send(kind, slot, source, target, device):
        return pltpu.make_async_remote_copy(
            src_ref=source,
            dst_ref=target,
            send_sem=r.send_sem.at[kind, slot],
            recv_sem=r.recv_sem.at[kind, slot],
            device_id=device,
            device_id_type=MESH_ID,
        )

    def core_copy(slot):
        return send(0, slot, r.part.at[slot, 1 - core], r.recv_c.at[slot], core_id)

    def col_copy_a(slot):
        return send(1, slot, r.half_a.at[slot, 1 - col], r.recv_xa.at[slot], col_id)

    def utt_copy_b(slot):
        return send(2, slot, r.half_b.at[slot, 1 - utt], r.recv_yb.at[slot], utt_id)

    def col_copy_b(slot):
        return send(3, slot, r.sum_b.at[slot, 1 - col], r.recv_xb.at[slot], col_id)

    def utt_copy_a(slot, deep):
        return send(4, slot, r.sum_a.at[deep, pos], r.recv_ya.at[slot], utt_id)

    def utt_copy_b2(slot, deep):
        return send(5, slot, r.line_b.at[deep, pos], r.recv_yb2.at[slot], utt_id)

    def col_copy_c(slot, deep):
        return send(24, slot, r.line_c.at[deep, pos, 1 - col], r.recv_xc.at[slot], col_id)

    def utt_copy_c(slot):
        return send(25, slot, r.sum_c.at[slot], r.recv_yc.at[slot], utt_id)

    def line_right(kind, slot, deep, step, source, target):
        dest = jnp.minimum(4 - step + pos, 3)
        return send(kind + step - 1, slot, source.at[deep, dest], target.at[slot, step - 1], right_id)

    def line_left(kind, slot, deep, step, source, target):
        dest = jnp.maximum(pos - 4 + step, 0)
        return send(kind + step - 1, slot, source.at[deep, dest], target.at[slot, step - 1], left_id)

    def line_start(slot, deep, step, source, right, left, kind):
        @pl.when((pos <= step - 1) & (pos < 3))
        def _():
            line_right(kind, slot, deep, step, source, right).start()

        @pl.when((pos >= 4 - step) & (pos > 0))
        def _():
            line_left(kind + 3, slot, deep, step, source, left).start()

    def line_finish(slot, deep, step, source, right, left, kind):
        @pl.when((pos <= step - 1) & (pos < 3))
        def _():
            line_right(kind, slot, deep, step, source, right).wait_send()

        @pl.when((pos >= 4 - step) & (pos > 0))
        def _():
            line_left(kind + 3, slot, deep, step, source, left).wait_send()

        @pl.when((pos >= 1) & (pos <= step))
        def _():
            line_right(kind, slot, deep, step, source, right).wait_recv()
            dest = 3 - step + pos
            source[deep, dest] = (
                source[deep, dest].astype(F32) + right[slot, step - 1].astype(F32)
            ).astype(LOW)

        @pl.when((pos <= 2) & (pos >= 3 - step))
        def _():
            line_left(kind + 3, slot, deep, step, source, left).wait_recv()
            dest = pos + step - 3
            source[deep, dest] = (
                source[deep, dest].astype(F32) + left[slot, step - 1].astype(F32)
            ).astype(LOW)

    line_a = (r.sum_a, r.right_a, r.left_a, 6)
    line_bb = (r.line_b, r.right_b, r.left_b, 12)
    line_cc = (r.line_c, r.right_c, r.left_c, 18)

    def advance(tick):
        def stage(offset):
            slab = tick - offset
            return (
                slab,
                lax.rem(slab + SLOTS * 4, SLOTS),
                lax.rem(slab + DEEP, DEEP),
                pl.when((slab >= 0) & (slab < SLABS)),
                pl.when((slab >= 0) & (slab < SLABS - 1)),
            )

        slab, slot, _, guard, _ = stage(0)
        load_start(slab + 1)

        @pl.when(slab < LOADED)
        def _():
            load_wait(slot)

        @guard
        def _():
            core_copy(slot).start()

        _, slot1, deep1, guard, most = stage(1)

        @guard
        def _():
            core_copy(slot1).wait()
            for line in range(4):
                for side in range(2):
                    both = r.part[slot1, core, 2 * line + side].astype(F32) + r.recv_c[
                        slot1, 2 * line + side
                    ].astype(F32)
                    both = both.astype(LOW)
                    r.half_a[slot1, side, line] = both[:32, :ACOLS]
                    r.line_c[deep1, line, side] = both[:32, ACOLS:]
                    r.half_b[slot1, 0, side, line] = both[32:48]
                    r.half_b[slot1, 1, side, line] = both[48:]
            line_start(slot1, deep1, 1, *line_cc)

        @most
        def _():
            col_copy_a(slot1).start()
            utt_copy_b(slot1).start()

        _, slot2, deep2, guard, most = stage(2)

        @guard
        def _():
            line_finish(slot2, deep2, 1, *line_cc)
            line_start(slot2, deep2, 2, *line_cc)

        @most
        def _():
            col_copy_a(slot2).wait()
            r.sum_a[deep2] = (
                r.half_a[slot2, col].astype(F32) + r.recv_xa[slot2].astype(F32)
            ).astype(LOW)
            line_start(slot2, deep2, 1, *line_a)
            utt_copy_b(slot2).wait()
            r.sum_b[slot2] = (
                r.half_b[slot2, utt].astype(F32) + r.recv_yb[slot2].astype(F32)
            ).astype(LOW)
            col_copy_b(slot2).start()

        _, slot3, deep3, guard, most = stage(3)

        @guard
        def _():
            line_finish(slot3, deep3, 2, *line_cc)
            line_start(slot3, deep3, 3, *line_cc)

        @most
        def _():
            line_finish(slot3, deep3, 1, *line_a)
            line_start(slot3, deep3, 2, *line_a)
            col_copy_b(slot3).wait()
            r.line_b[deep3] = (
                r.sum_b[slot3, col].astype(F32) + r.recv_xb[slot3].astype(F32)
            ).astype(LOW)
            line_start(slot3, deep3, 1, *line_bb)

        _, slot4, deep4, guard, most = stage(4)

        @guard
        def _():
            line_finish(slot4, deep4, 3, *line_cc)
            col_copy_c(slot4, deep4).start()

        @most
        def _():
            line_finish(slot4, deep4, 2, *line_a)
            line_start(slot4, deep4, 3, *line_a)
            line_finish(slot4, deep4, 1, *line_bb)
            line_start(slot4, deep4, 2, *line_bb)

        _, slot5, deep5, guard, most = stage(5)

        @guard
        def _():
            col_copy_c(slot5, deep5).wait()
            r.sum_c[slot5] = (
                r.line_c[deep5, pos, col].astype(F32) + r.recv_xc[slot5].astype(F32)
            ).astype(LOW)
            utt_copy_c(slot5).start()

        @most
        def _():
            line_finish(slot5, deep5, 3, *line_a)
            utt_copy_a(slot5, deep5).start()
            line_finish(slot5, deep5, 2, *line_bb)
            line_start(slot5, deep5, 3, *line_bb)

        _, slot6, deep6, guard, most = stage(6)

        @guard
        def _():
            utt_copy_c(slot6).wait()
            r.staged[slot6, 0:32, ACOLS:] = r.sum_c[slot6].astype(F32) + r.recv_yc[slot6].astype(F32)

        @most
        def _():
            utt_copy_a(slot6, deep6).wait()
            r.staged[slot6, 0:32, :ACOLS] = r.sum_a[deep6, pos].astype(F32) + r.recv_ya[
                slot6
            ].astype(F32)
            line_finish(slot6, deep6, 3, *line_bb)
            utt_copy_b2(slot6, deep6).start()

        slab7, slot7, deep7, guard, most = stage(7)

        @most
        def _():
            utt_copy_b2(slot7, deep7).wait()
            mine = r.line_b[deep7, pos].astype(F32)
            theirs = r.recv_yb2[slot7].astype(F32)
            r.staged[slot7, 32:48] = jnp.where(utt == 0, mine, theirs)
            r.staged[slot7, 48:64] = jnp.where(utt == 0, theirs, mine)

        for ref, spec in zip(outs, PLAN):

            @pl.when((slab7 >= spec[0]) & (slab7 < spec[0] + spec[1]))
            def _():
                pltpu.make_async_copy(
                    r.staged.at[slot7], window(ref, spec, slab7, ()), r.out_sem.at[slot7]
                ).start()

        _, slot8, _, guard, _ = stage(8)

        @guard
        def _():
            pltpu.make_async_copy(
                r.staged.at[slot8], outs[0].at[pl.ds(0, SROWS), pl.ds(0, SCOLS)], r.out_sem.at[slot8]
            ).wait()

    def cols_of(index):
        return pl.ds(pl.multiple_of(index * SCOLS, SCOLS), SCOLS)

    def put(slot, dest, rows):
        r.part[slot, dest % 2, dest // 2] = rows.astype(LOW)

    def put_product(slot, left_of, right):
        for quarter in range(4):
            rows = mul(left_of(quarter), right)
            for index in range(4):
                put(slot, 4 * quarter + index, rows[64 * index : 64 * index + 64])

    def quarter_rows(ref, lead=()):
        return lambda quarter: ref[lead + (slice(256 * quarter, 256 * quarter + 256),)]

    def produce(slab):
        slot = slab % SLOTS

        def among(first, number):
            return pl.when((slab >= first) & (slab < first + number))

        @among(16, 8)
        def _():
            local = slab - 16
            put_product(slot, quarter_rows(r.l_x_t), r.l_g[local // 2, :, cols_of(local % 2)])

        @among(24, 6)
        def _():
            local = slab - 24
            for dest in range(16):
                place = 3 * dest + local // 2
                book = place // 16
                first = (place % 16) * SROWS
                ids = first + lax.broadcasted_iota(jnp.int32, (SROWS, LANES), 0)
                picked = (ids == r.codes[book][0:1]).astype(LOW)
                put(slot, dest, mul(picked, r.table_g[book, :, cols_of(local % 2)]))

        @among(30, 8)
        def _():
            local = slab - 30
            inner = local // 2

            def rows(quarter):
                return jnp.concatenate(
                    [
                        r.act_t[pl.ds(pl.multiple_of(256 * dest + 64 * inner, 64), 64)]
                        for dest in range(4 * quarter, 4 * quarter + 4)
                    ],
                    axis=0,
                )

            put_product(slot, rows, r.dout_low[:, cols_of(local % 2)])

        @among(38, 8)
        def _():
            put_product(slot, quarter_rows(r.g_hn_t), r.du[:, cols_of(slab - 38)])

        @among(46, 8)
        def _():
            local = slab - 46
            kind = local // 2
            put_product(
                slot,
                quarter_rows(r.g_x_t, (jnp.minimum(kind, 1),)),
                r.g_g[kind, :, cols_of(local % 2)],
            )

        @pl.when(slab == 54)
        def _():
            b_down = jnp.sum(r.dout_low[...].astype(F32), axis=0, keepdims=True)
            for dest in range(16):
                shared = slice(LANES * (dest // 2), LANES * (dest // 2) + LANES)
                rows = [r.dn1[:, shared], r.dn2[:, shared], b_down[:, shared]]
                for index in range(2):
                    first = 256 * (dest % 2) + LANES * index
                    rows.append(r.db1[dest // 2 : dest // 2 + 1, first : first + LANES])
                rows += [r.l_dn1[:, shared], r.l_dn2[:, shared], r.l_db2[:, shared]]
                for index in range(2):
                    first = 256 * dest + LANES * index
                    rows.append(r.l_db1[:, first : first + LANES])
                rows.append(jnp.zeros((6, LANES), F32))
                r.part[slot, dest % 2, dest // 2, 0:16, ACOLS:] = jnp.concatenate(
                    rows, axis=0
                ).astype(LOW)

    own_utt, own_pair = seq // 8, seq % 8
    own_cols = pl.ds(pl.multiple_of(own_pair * LANES, LANES), LANES)

    def pair_cols(other):
        return pl.ds(pl.multiple_of((other % 8) * LANES, LANES), LANES)

    def hand_out(other):
        return remote(
            r.dmix.at[other // 8, :, pair_cols(other)], r.grads.at[seq], r.send_one.at[other],
            r.recv_one.at[seq], other,
        )

    def hand_back(block):
        return remote(
            r.pieces.at[block], r.landed.at[:, own_utt, :, own_cols], r.send_two.at[block],
            r.recv_two.at[seq], block,
        )

    def others(body):
        @pl.loop(1, count)
        def _(step):
            body(lax.rem(seq + step, count))

    def compute(tick):
        def at(*ticks):
            hit = tick == ticks[0]
            for item in ticks[1:]:
                hit = hit | (tick == item)
            return pl.when(hit)

        @pl.when(tick < 8)
        def _():
            slot = tick % 2
            for copy in weights(tick, slot):
                copy.wait()

            @pl.when(tick < 7)
            def _():
                for copy in weights(tick + 1, 1 - slot):
                    copy.start()

            @pl.when(tick == 0)
            def _():
                r.dout_low[...] = r.dout[...].astype(LOW)
                r.dhn[...] = jnp.zeros_like(r.dhn)

            cols = cols_of(tick)
            _, slope = gelu_parts(r.u[:, cols])
            du = (mul_t(r.dout_low[...], r.down_buf[slot]) * slope).astype(LOW)
            r.du[:, cols] = du
            r.db1[pl.ds(tick, 1), :] = jnp.sum(du.astype(F32), axis=0, keepdims=True)
            r.dhn[...] += mul_t(du, r.up_buf[slot])

        @at(3)
        def _():
            for copy in fetch(4, 5, 6, 7, 8, 9, 10):
                copy.start()

        @at(12)
        def _():
            for copy in fetch(1, 2, 3, 11, 12, 13, 14):
                copy.start()

        @at(AT_BACK)
        def _():
            for copy in fetch(0):
                copy.wait()
            dmid, gain = scale_back(r.mid[...], r.n2[...], r.dhn[...])
            r.dn2[...] = jnp.sum(gain, axis=0, keepdims=True)
            dmid = dmid + r.dout[...]
            r.dmid[...] = dmid
            dattn = dmid.astype(LOW)
            r.g_g[0] = dattn
            r.dmix[...] = mul_t(dattn, r.square[0]).astype(LOW).reshape(r.dmix.shape)
            r.grads[seq] = r.dmix[own_utt, :, own_cols]

        @pl.when((tick >= AT_BACK) & (tick < AT_BACK + 5))
        def _():
            @pl.loop(0, 3)
            def _(index):
                hand_out(lax.rem(seq + 3 * (tick - AT_BACK) + index + 1, count)).start()

        @at(AT_BACK + 1)
        def _():
            for copy in fetch(4, 5, 6, 7, 8, 9, 10):
                copy.wait()
            r.k_t[...] = r.held[:, 64:128].reshape(count * HD, LANES).T
            fill_bias(r.bias, r.held[:, 192:208])
            r.dk_acc[...] = jnp.zeros_like(r.dk_acc)
            r.dv_acc[...] = jnp.zeros_like(r.dv_acc)
            r.l_x_t[...] = r.l_x[0].T

        @at(AT_ATTEND)
        def _():
            def arrived(other):
                here = r.grads.at[other]
                remote(here, here, r.send_one.at[other], r.recv_one.at[other], other).wait_recv()

            others(arrived)

        for order, group in enumerate(reversed(range(4))):
            below = group * 256
            here = below + 256
            begin = AT_ATTEND + 2 * order

            @at(begin, begin + 1)
            def _():
                @pl.loop(0, 2)
                def _(index):
                    attend_back_block(
                        r, group, below, here, 4 * group + 2 * (tick - begin) + index
                    )

            @at(begin + 1)
            def _():
                for block in range(4 * group, 4 * group + 4):
                    rows = slice(block * HD, (block + 1) * HD)
                    r.pieces[block, 1] = r.dk_acc[rows].astype(LOW)
                    r.pieces[block, 2] = r.dv_acc[rows].astype(LOW)

        @at(AT_RETURN)
        def _():
            r.landed[:, own_utt, :, own_cols] = r.pieces[seq]

        @pl.when((tick >= AT_RETURN) & (tick < AT_RETURN + 15))
        def _():
            hand_back(lax.rem(seq + tick - AT_RETURN + 1, count)).start()

        @at(AT_LANDED)
        def _():
            def arrived(other):
                here = r.landed.at[:, other // 8, :, pair_cols(other)]
                remote(here, here, r.send_two.at[other], r.recv_two.at[other], other).wait_recv()

            others(arrived)
            others(lambda other: hand_out(other).wait_send())
            others(lambda other: hand_back(other).wait_send())
            for index in range(3):
                r.g_g[1 + index] = r.landed[index].reshape(r.g_g.shape[1:])

        @at(AT_LANDED + 1)
        def _():
            for copy in fetch(1, 2, 3):
                copy.wait()
            r.dhn[...] = mul_t(r.g_g[1], r.square[1])

        @at(AT_LANDED + 2)
        def _():
            r.dhn[...] += mul_t(r.g_g[2], r.square[2])

        @at(AT_LANDED + 3)
        def _():
            dnormed = r.dhn[...] + mul_t(r.g_g[3], r.square[3])
            dx, gain = scale_back(r.x[...].astype(F32), r.n1[...], dnormed)
            r.dn1[...] = jnp.sum(gain, axis=0, keepdims=True)
            r.dx[...] = dx + r.dmid[...]

        @at(21)
        def _():
            r.l_x_t[...] = r.l_x[1].T

        @at(22)
        def _():
            for copy in fetch(11, 12, 13, 14):
                copy.wait()

        @pl.when((tick >= 24) & (tick < 28))
        def _():
            cols = pl.ds(pl.multiple_of((tick - 24) * 1024, 1024), 1024)
            r.act_t[cols] = r.act_buf[:, cols].T

        @at(29)
        def _():
            r.g_hn_t[...] = r.hn[...].T

        @at(31, 32)
        def _():
            r.g_x_t[tick - 31] = r.g_x[tick - 31].T

    pl.semaphore_wait(barrier, count)

    @pl.loop(0, SLABS + DRAIN)
    def _(tick):
        advance(tick)
        compute(tick)
        produce(tick + 1)


def attend_back_block(r, group, below, here, block):
    query = two_heads(r.held[block, 0:64] * LOW(HD ** (-0.5)))
    grad = two_heads(r.grads[block])
    log_total = r.log_total[block][0:1]
    near_v = r.held[4 * group : 4 * group + 4, 128:192].reshape(256, LANES)
    near_k = r.held[4 * group : 4 * group + 4, 64:128].reshape(256, LANES)
    near = masked_scores(mul_t(near_k, query), r.bias[below:here], below, block)
    near = jnp.exp(near - log_total)
    near_dp = mul_t(near_v, grad)
    delta = jnp.sum(near * near_dp, axis=0, keepdims=True)
    if group:
        far_v = r.held[0 : 4 * group, 128:192].reshape(below, LANES)
        far_k = r.held[0 : 4 * group, 64:128].reshape(below, LANES)
        far = jnp.exp(mul_t(far_k, query) + r.bias[0:below] - log_total)
        far_dp = mul_t(far_v, grad)
        delta = delta + jnp.sum(far * far_dp, axis=0, keepdims=True)
        far_ds = (far * (far_dp - delta)).astype(LOW)
        r.dk_acc[0:below] += mul(far_ds, query)
        r.dv_acc[0:below] += mul(far.astype(LOW), grad)
    near_ds = (near * (near_dp - delta)).astype(LOW)
    r.dk_acc[below:here] += mul(near_ds, query)
    r.dv_acc[below:here] += mul(near.astype(LOW), grad)
    dq = mul(r.k_t[:, below:here], near_ds)
    if group:
        dq = dq + mul(r.k_t[:, 0:below], far_ds)
    r.pieces[block, 0] = (join_heads(dq) * HD ** (-0.5)).astype(LOW)


def finish_on_slice(far, near):
    vmem = pl.BlockSpec(memory_space=pltpu.VMEM)
    hbm = pl.BlockSpec(memory_space=pl.ANY)
    rows, width = near["x"].shape
    wide = near["u"].shape[1]
    utts = rows // HD
    shapes = [
        (width // 16, wide), (wide // 16, width), (width // 16, width), (width // 16, width),
        (width // 16, width), (width // 16, width), (3 * 1024 // 16, width), (wide // 16, width),
        (width // 16, wide), (width // 16, width), (width // 16, width), (width // 16, width),
        (width // 16, width), (SROWS, SCOLS),
    ]
    out_names = ["dx"] + ["out_%d" % index for index in range(len(shapes))]
    rows_l = far["l_normed"].shape[0]
    buffers = dict(
        part=((SLOTS, 2, 8, 64, SCOLS), LOW),
        recv_c=((SLOTS, 8, 64, SCOLS), LOW),
        half_a=((SLOTS, 2, 4, 32, ACOLS), LOW),
        half_b=((SLOTS, 2, 2, 4, 16, SCOLS), LOW),
        recv_xa=((SLOTS, 4, 32, ACOLS), LOW),
        recv_yb=((SLOTS, 2, 4, 16, SCOLS), LOW),
        sum_a=((DEEP, 4, 32, ACOLS), LOW),
        sum_b=((SLOTS, 2, 4, 16, SCOLS), LOW),
        recv_xb=((SLOTS, 4, 16, SCOLS), LOW),
        line_b=((DEEP, 4, 16, SCOLS), LOW),
        right_a=((SLOTS, 3, 32, ACOLS), LOW),
        left_a=((SLOTS, 3, 32, ACOLS), LOW),
        right_b=((SLOTS, 3, 16, SCOLS), LOW),
        left_b=((SLOTS, 3, 16, SCOLS), LOW),
        recv_ya=((SLOTS, 32, ACOLS), LOW),
        recv_yb2=((SLOTS, 16, SCOLS), LOW),
        line_c=((DEEP, 4, 2, 32, LANES), LOW),
        right_c=((SLOTS, 3, 2, 32, LANES), LOW),
        left_c=((SLOTS, 3, 2, 32, LANES), LOW),
        recv_xc=((SLOTS, 32, LANES), LOW),
        sum_c=((SLOTS, 32, LANES), LOW),
        recv_yc=((SLOTS, 32, LANES), LOW),
        staged=((SLOTS, 64, SCOLS), F32),
        up_buf=((2, width, SCOLS), LOW),
        down_buf=((2, SCOLS, width), LOW),
        square=((4, width, width), LOW),
        held=(far["saved"].shape, LOW),
        l_x=((2, rows_l, width), LOW),
        l_g=((4, rows_l, width), LOW),
        l_x_t=((width, rows_l), LOW),
        table_g=(far["rest"].shape, LOW),
        act_buf=((rows, wide), LOW),
        act_t=((wide, rows), LOW),
        g_x=((2, rows, width), LOW),
        g_x_t=((2, width, rows), LOW),
        g_hn_t=((width, rows), LOW),
        g_g=((4, rows, width), LOW),
        dout_low=((rows, width), LOW),
        du=((rows, wide), LOW),
        db1=((8, SCOLS), F32),
        dn1=((1, width), F32),
        dn2=((1, width), F32),
        dhn=((rows, width), F32),
        dmid=((rows, width), F32),
        dmix=((utts, HD, width), LOW),
        grads=((16, HD, LANES), LOW),
        landed=((3, utts, HD, width), LOW),
        pieces=((16, 3, HD, LANES), LOW),
        dk_acc=((16 * HD, LANES), F32),
        dv_acc=((16 * HD, LANES), F32),
        bias=((16 * HD, LANES), F32),
        k_t=((LANES, 16 * HD), LOW),
    )
    semaphores = dict(
        load_sem=(SLOTS, 2), out_sem=(SLOTS,), send_sem=(26, SLOTS), recv_sem=(26, SLOTS),
        weight_sem=(2, 2), fetch_sem=(15,), send_one=(16,), recv_one=(16,), send_two=(16,),
        recv_two=(16,),
    )
    names = list(far) + list(near) + out_names + list(buffers) + list(semaphores)
    return pl.pallas_call(
        functools.partial(tail_kernel, names, len(shapes)),
        in_specs=[hbm] * len(far) + [vmem] * len(near),
        out_specs=[vmem] + [hbm] * len(shapes),
        out_shape=[jax.ShapeDtypeStruct((rows, width), F32)]
        + [jax.ShapeDtypeStruct(shape, F32) for shape in shapes],
        scratch_shapes=[pltpu.VMEM(*item) for item in buffers.values()]
        + [pltpu.SemaphoreType.DMA(item) for item in semaphores.values()],
        compiler_params=pltpu.CompilerParams(
            collective_id=1, has_side_effects=True, vmem_limit_bytes=60 << 20
        ),
    )(*far.values(), *near.values())


def normalize(values, gain_vec):
    return (
        values * lax.rsqrt(jnp.mean(values * values, axis=-1, keepdims=True) + EPSILON) * gain_vec
    )


def gelu_fn(values):
    return jax.nn.gelu(values, approximate=True)


def project_back(gradient, weight):
    return lax.dot_general(
        gradient, weight, (((1,), (1,)), ((), ())), preferred_element_type=jnp.float32
    )


def weight_grad(left_side, gradient):
    return lax.dot_general(
        left_side, gradient, (((0,), (0,)), ((), ())), preferred_element_type=jnp.float32
    )


def block_back(inputs, normed, mixed_rows, kept_parts, params, grad_out, attention_back):
    middle, middle_norm, pre_active, active = kept_parts
    grad_branch = grad_out.astype(jnp.bfloat16)
    grad_b_down = jnp.sum(grad_branch.astype(jnp.float32), axis=0)
    grad_w_down = weight_grad(active, grad_branch)
    grad_active = project_back(grad_branch, params[8])
    grad_pre = jax.vjp(gelu_fn, pre_active)[1](grad_active)[0].astype(jnp.bfloat16)
    grad_b_up = jnp.sum(grad_pre.astype(jnp.float32), axis=0)
    grad_w_up = weight_grad(middle_norm, grad_pre)
    middle_back = jax.vjp(normalize, middle, params[5])[1]
    grad_middle, grad_norm_two = middle_back(project_back(grad_pre, params[6]))
    grad_middle = grad_middle + grad_out
    grad_attn = grad_middle.astype(jnp.bfloat16)
    grad_w_output = weight_grad(mixed_rows, grad_attn)
    grad_mixed = project_back(grad_attn, params[4]).astype(jnp.bfloat16)
    grad_query, grad_key, grad_value = attention_back(grad_mixed)
    grad_normed = (
        project_back(grad_query, params[1])
        + project_back(grad_key, params[2])
        + project_back(grad_value, params[3])
    )
    input_back = jax.vjp(normalize, inputs, params[0])[1]
    grad_inputs, grad_norm_one = input_back(grad_normed)
    weight_grads = (
        grad_norm_one,
        weight_grad(normed, grad_query),
        weight_grad(normed, grad_key),
        weight_grad(normed, grad_value),
        grad_w_output,
        grad_norm_two,
        grad_w_up,
        grad_b_up,
        grad_w_down,
        grad_b_down,
    )
    return (grad_inputs + grad_middle, weight_grads)


def on_device(
    frames,
    codes,
    lengths,
    frame_mask,
    table,
    glob_norm_one,
    glob_w_query,
    glob_w_key,
    glob_w_value,
    glob_w_output,
    glob_norm_two,
    glob_w_up,
    glob_b_up,
    glob_w_down,
    glob_b_down,
    local_norm_one,
    local_w_query,
    local_w_key,
    local_w_value,
    local_w_output,
    local_norm_two,
    local_w_up,
    local_b_up,
    local_w_down,
    local_b_down,
    cotan_global,
    cotan_local,
):
    utter_count, frame_count, model_width = frames.shape
    row_count = utter_count * frame_count
    local_len = CB + 1
    positions = lax.axis_index("seq") * frame_count + jnp.arange(frame_count, dtype=jnp.int32)
    valid = positions[None, :] < lengths[:, None]
    usable = jnp.pad(frame_mask.astype(LOW), ((0, 0), (0, LANES - frame_count)))
    usable = jnp.broadcast_to(usable[:, None, :], (utter_count, 16, LANES))
    glob_params = (
        glob_norm_one,
        glob_w_query,
        glob_w_key,
        glob_w_value,
        glob_w_output,
        glob_norm_two,
        glob_w_up,
        glob_b_up,
        glob_w_down,
        glob_b_down,
    )
    local_params = (
        local_norm_one,
        local_w_query,
        local_w_key,
        local_w_value,
        local_w_output,
        local_norm_two,
        local_w_up,
        local_b_up,
        local_w_down,
        local_b_down,
    )
    code_rows = codes.transpose(2, 0, 1).reshape(CB, row_count)
    (
        glob_normed, glob_mixed, saved, log_total, local_in,
        glob_middle, glob_middle_norm, pre_active, active,
    ) = global_forward(
        frames,
        usable,
        jnp.broadcast_to(code_rows[:, :, None], (CB, row_count, LANES)),
        valid.reshape(row_count, 1).astype(F32),
        table,
        glob_params,
    )
    global_rows = local_in[0]
    local_shape = (local_len, row_count, model_width)
    flat_shape = (local_len * row_count, model_width)
    normed, local_q, local_k, local_v, local_probs, mixed, middle, middle_norm = local_front(
        local_in, local_params
    )
    row_valid = valid.reshape(1, row_count, 1)
    local_cotan = cotan_local.transpose(2, 0, 1, 3).reshape(local_shape)
    local_cotan = jnp.where(row_valid, local_cotan, 0)
    local_result, grad_hidden, grad_w_up, grad_w_down, grad_b_up = local_ffn(
        middle_norm.reshape(flat_shape),
        local_cotan.reshape(flat_shape),
        middle.reshape(flat_shape),
        local_params,
    )
    local_rows = jnp.where(row_valid, local_result.reshape(local_shape), 0)
    local_rows = local_rows.reshape(local_len, utter_count, frame_count, model_width)
    local_rows = local_rows.transpose(1, 2, 0, 3)
    grad_attn, grad_q, grad_k, grad_v, grad_first, grad_rest, grad_n1, grad_n2 = local_back(
        local_in,
        middle,
        grad_hidden.reshape(local_shape),
        local_cotan,
        local_q,
        local_k,
        local_v,
        local_probs,
        local_params,
    )
    normed = normed.reshape(flat_shape)
    mixed = mixed.reshape(flat_shape)
    grad_b_down = jnp.sum(local_cotan.astype(F32), axis=(0, 1))
    grad_first = grad_first.reshape(utter_count, frame_count, model_width)
    glob_cotan = jnp.where(
        valid[:, :, None], cotan_global.astype(jnp.float32) + grad_first, 0.0
    )
    glob_cotan = glob_cotan.reshape(row_count, model_width)
    outputs = (global_rows.reshape(utter_count, frame_count, model_width), local_rows)

    if lax.axis_size("seq") == 16 and lax.axis_size("utt") == 2:
        far = dict(
            l_up=grad_w_up.reshape(8, 2, -1, grad_w_up.shape[1]),
            l_down=grad_w_down.reshape(8, 2, -1, grad_w_down.shape[1]),
            g_w_up=glob_w_up,
            g_w_down=glob_w_down,
            g_w_o=glob_w_output,
            g_w_q=glob_w_query,
            g_w_k=glob_w_key,
            g_w_v=glob_w_value,
            saved=saved,
            l_normed=normed,
            l_mixed=mixed,
            l_dq=grad_q.reshape(flat_shape),
            l_dk=grad_k.reshape(flat_shape),
            l_dv=grad_v.reshape(flat_shape),
            l_dattn=grad_attn.reshape(flat_shape),
            rest=grad_rest,
            g_act=active,
            g_mixed=glob_mixed,
            g_normed=glob_normed,
        )
        near = dict(
            u=pre_active,
            dout=glob_cotan,
            mid=glob_middle,
            hn=glob_middle_norm,
            x=frames.reshape(row_count, model_width),
            n1=glob_norm_one.reshape(1, -1),
            n2=glob_norm_two.reshape(1, -1),
            log_total=log_total,
            codes=jnp.broadcast_to(code_rows[:, None, :], (CB, 8, row_count)),
            l_dn1=grad_n1,
            l_dn2=grad_n2,
            l_db1=grad_b_up,
            l_db2=grad_b_down.reshape(1, -1),
        )
        grad_inputs, *sums = settle(finish_on_slice(far, near))
        wide = dict(zip("12qkvot76pabc", sums[:-1]))
        half = lax.axis_index("seq") % 2
        rest = sums[-1]

        def piece(row):
            return jnp.where(half == 0, rest[row, ACOLS : ACOLS + LANES // 2], rest[row, ACOLS + LANES // 2 :])

        def piece_wide(row):
            return rest[row : row + 2, ACOLS:].reshape(-1)

        return outputs + (
            grad_inputs.reshape(utter_count, frame_count, model_width),
            wide["t"],
            piece(0),
            wide["a"],
            wide["b"],
            wide["c"],
            wide["p"],
            piece(1),
            wide["6"],
            piece_wide(3),
            wide["7"],
            piece(2),
            piece(5),
            wide["q"],
            wide["k"],
            wide["v"],
            wide["o"],
            piece(6),
            wide["1"],
            piece_wide(8),
            wide["2"],
            piece(7),
        )

    local_grads = (
        grad_n1[0],
        weight_grad(normed, grad_q.reshape(flat_shape)),
        weight_grad(normed, grad_k.reshape(flat_shape)),
        weight_grad(normed, grad_v.reshape(flat_shape)),
        weight_grad(mixed, grad_attn.reshape(flat_shape)),
        grad_n2[0],
        grad_w_up,
        grad_b_up[0],
        grad_w_down,
        grad_b_down,
    )
    picked = code_rows[:, None, :] == jnp.arange(VOCAB, dtype=jnp.int32)[None, :, None]
    grad_tab = jnp.einsum(
        "cvn,cnd->cvd", picked.astype(LOW), grad_rest, preferred_element_type=F32
    ).reshape(CB * VOCAB, model_width)

    def global_back(grad_mixed):
        grads = global_attend_back(
            grad_mixed.reshape(utter_count, frame_count, model_width), saved, log_total
        )
        return tuple(grads.reshape(3, row_count, model_width))

    global_in = frames.astype(F32).reshape(row_count, model_width)
    glob_kept = (glob_middle, glob_middle_norm, pre_active, active)
    grad_inputs, glob_grads = block_back(
        global_in, glob_normed, glob_mixed, glob_kept, glob_params, glob_cotan, global_back
    )
    reduced = reduce_all((grad_tab,) + glob_grads + local_grads)
    return outputs + (grad_inputs.reshape(utter_count, frame_count, model_width),) + reduced


def solution(mesh):
    return jax.shard_map(
        on_device,
        mesh=mesh,
        in_specs=(
            P("utt", "seq", None),
            P("utt", "seq", None),
            P("utt"),
            P("utt", "seq"),
            P(),
            P(),
            P(),
            P(),
            P(),
            P(),
            P(),
            P(),
            P(),
            P(),
            P(),
            P(),
            P(),
            P(),
            P(),
            P(),
            P(),
            P(),
            P(),
            P(),
            P(),
            P("utt", "seq", None),
            P("utt", "seq", None, None),
        ),
        out_specs=(
            P("utt", "seq", None),
            P("utt", "seq", None, None),
            P("utt", "seq", None),
            P("seq", None),
            P("seq"),
            P("seq", None),
            P("seq", None),
            P("seq", None),
            P("seq", None),
            P("seq"),
            P("seq", None),
            P("seq"),
            P("seq", None),
            P("seq"),
            P("seq"),
            P("seq", None),
            P("seq", None),
            P("seq", None),
            P("seq", None),
            P("seq"),
            P("seq", None),
            P("seq"),
            P("seq", None),
            P("seq"),
        ),
        check_vma=False,
    )
```

```python
import functools
import types

import jax
import jax.numpy as jnp
from jax import lax
from jax.experimental import pallas as pl
from jax.experimental.pallas import tpu as pltpu
from jax.sharding import PartitionSpec as P

H = 16
HD = 64
CB = 3
VOCAB = 1024


EPSILON = 1e-05
NEGATIVE = -1e30
F32 = jnp.float32
LOW = jnp.bfloat16
LANES = 128
MESH_ID = pl.DeviceIdType.MESH


def reduce_all(grads):
    return tuple(
        lax.psum(
            lax.psum_scatter(item.astype(LOW), "seq", scatter_dimension=0, tiled=True), "utt"
        ).astype(F32)
        for item in grads
    )


def mul(left_side, right_side):
    return jnp.dot(left_side, right_side, preferred_element_type=F32)


def mul_t(left_side, right_side):
    return lax.dot_general(
        left_side, right_side, (((1,), (1,)), ((), ())), preferred_element_type=F32
    )


def t_mul(left_side, right_side):
    return lax.dot_general(
        left_side, right_side, (((0,), (0,)), ((), ())), preferred_element_type=F32
    )


def scale_of(values):
    return lax.rsqrt(jnp.mean(values * values, axis=-1, keepdims=True) + EPSILON)


def scale_back(values, gain, grad):
    scale = scale_of(values)
    inner = grad * gain
    shared = jnp.mean(values * inner, axis=-1, keepdims=True) * (scale * scale * scale)
    return inner * scale - values * shared, grad * values * scale


def head_sums(width):
    rows = lax.broadcasted_iota(jnp.int32, (width, 128), 0) // HD
    cols = lax.broadcasted_iota(jnp.int32, (width, 128), 1)
    return (rows == cols).astype(LOW)


def head_spread(width):
    rows = lax.broadcasted_iota(jnp.int32, (128, width), 0)
    cols = lax.broadcasted_iota(jnp.int32, (128, width), 1) // HD
    return (rows == cols).astype(LOW)


def sum_heads(product, sums):
    high = product.astype(LOW)
    rest = (product - high.astype(F32)).astype(LOW)
    return mul(high, sums) + mul(rest, sums)


def front_kernel(
    x_ref, n1_ref, wq_ref, wk_ref, wv_ref, wo_ref, n2_ref,
    normed_ref, q_ref, k_ref, v_ref, probs_ref, mixed_ref, mid_ref, mid_norm_ref,
):
    places, frames, width = x_ref.shape
    rows = places * frames
    x = x_ref[...].astype(F32).reshape(rows, width)
    normed = (x * scale_of(x) * n1_ref[...]).astype(LOW)
    normed_ref[...] = normed.reshape(places, frames, width)
    q_ref[...] = mul(normed, wq_ref[...]).astype(LOW).reshape(places, frames, width)
    k_ref[...] = mul(normed, wk_ref[...]).astype(LOW).reshape(places, frames, width)
    v_ref[...] = mul(normed, wv_ref[...]).astype(LOW).reshape(places, frames, width)
    sums, spread = head_sums(width), head_spread(width)
    pair = 0
    for i in range(places):
        query = q_ref[i].astype(F32)
        scores = [
            sum_heads(query * k_ref[j].astype(F32), sums) * HD ** (-0.5) for j in range(i + 1)
        ]
        peak = scores[0]
        for item in scores[1:]:
            peak = jnp.maximum(peak, item)
        raised = [jnp.exp(item - peak) for item in scores]
        total = raised[0]
        for item in raised[1:]:
            total = total + item
        mixed = None
        for j in range(i + 1):
            probs = raised[j] / total
            probs_ref[pair] = probs
            pair += 1
            term = mul(probs.astype(LOW), spread) * v_ref[j].astype(F32)
            mixed = term if mixed is None else mixed + term
        mixed_ref[i] = mixed.astype(LOW)
    mid = x + mul(mixed_ref[...].reshape(rows, width), wo_ref[...])
    mid_ref[...] = mid.reshape(places, frames, width)
    mid_norm_ref[...] = (
        (mid * scale_of(mid) * n2_ref[...]).astype(LOW).reshape(places, frames, width)
    )


def local_front(x, params):
    places, frames, width = x.shape
    pairs = places * (places + 1) // 2
    step = 64
    rows = pl.BlockSpec((places, step, width), lambda i: (0, i, 0))
    whole = lambda item: pl.BlockSpec(item.shape, lambda i: (0, 0), pipeline_mode=pl.Buffered(1))
    n1, n2 = params[0].reshape(1, -1), params[5].reshape(1, -1)
    operands = (x, n1, params[1], params[2], params[3], params[4], n2)
    like = lambda kind: jax.ShapeDtypeStruct((places, frames, width), kind)
    return pl.pallas_call(
        front_kernel,
        grid=(frames // step,),
        in_specs=[rows] + [whole(item) for item in operands[1:]],
        out_specs=[rows] * 4
        + [pl.BlockSpec((pairs, step, 128), lambda i: (0, i, 0))]
        + [rows] * 3,
        out_shape=[
            like(LOW), like(LOW), like(LOW), like(LOW),
            jax.ShapeDtypeStruct((pairs, frames, 128), F32),
            like(LOW), like(F32), like(LOW),
        ],
        compiler_params=pltpu.CompilerParams(vmem_limit_bytes=56 << 20),
    )(*operands)


def gelu_parts(u):
    scale = 0.7978845608028654
    inner = jnp.tanh(scale * (u + 0.044715 * u * u * u))
    half = 0.5 * (1.0 + inner)
    slope = half + 0.5 * u * (1.0 - inner * inner) * scale * (1.0 + 3 * 0.044715 * u * u)
    return u * half, slope


def ffn_kernel(
    hn_ref, dout_ref, mid_ref, w1_ref, b1_ref, w2_ref, b2_ref,
    y_ref, dhn_ref, dw1_ref, dw2_ref, db1_ref, db2_ref, acc_ref, hn_t_ref,
):
    at = pl.program_id(0)
    last = pl.num_programs(0) - 1

    @pl.when(at == 0)
    def _():
        hn_t_ref[...] = hn_ref[...].T
        acc_ref[...] = mid_ref[...] + b2_ref[...]
        dhn_ref[...] = jnp.zeros_like(dhn_ref)
        db2_ref[...] = jnp.sum(dout_ref[...].astype(F32), axis=0, keepdims=True)

    hn, dout = hn_ref[...], dout_ref[...]
    u = mul(hn, w1_ref[...]) + b1_ref[...]
    act, slope = gelu_parts(u)
    act = act.astype(LOW)
    acc_ref[...] += mul(act, w2_ref[...])
    du = (mul_t(dout, w2_ref[...]) * slope).astype(LOW)
    db1_ref[...] = jnp.sum(du.astype(F32), axis=0, keepdims=True)
    dhn_ref[...] += mul_t(du, w1_ref[...])
    dw1_ref[...] = mul(hn_t_ref[...], du).astype(LOW)
    dw2_ref[...] = t_mul(act, dout).astype(LOW)

    @pl.when(at == last)
    def _():
        y_ref[...] = acc_ref[...].astype(LOW)


def local_ffn(hn, dout, mid, params):
    rows, width = hn.shape
    wide = params[6].shape[1]
    step = 512
    whole = pl.BlockSpec((rows, width), lambda i: (0, 0), pipeline_mode=pl.Buffered(1))
    out_whole = pl.BlockSpec((rows, width), lambda i: (0, 0))
    return pl.pallas_call(
        ffn_kernel,
        grid=(wide // step,),
        in_specs=[
            whole, whole, whole,
            pl.BlockSpec((width, step), lambda i: (0, i)),
            pl.BlockSpec((1, step), lambda i: (0, i)),
            pl.BlockSpec((step, width), lambda i: (i, 0)),
            pl.BlockSpec((1, width), lambda i: (0, 0)),
        ],
        out_specs=[
            out_whole, out_whole,
            pl.BlockSpec((width, step), lambda i: (0, i)),
            pl.BlockSpec((step, width), lambda i: (i, 0)),
            pl.BlockSpec((1, step), lambda i: (0, i)),
            pl.BlockSpec((1, width), lambda i: (0, 0)),
        ],
        out_shape=[
            jax.ShapeDtypeStruct((rows, width), LOW),
            jax.ShapeDtypeStruct((rows, width), F32),
            jax.ShapeDtypeStruct((width, wide), LOW),
            jax.ShapeDtypeStruct((wide, width), LOW),
            jax.ShapeDtypeStruct((1, wide), F32),
            jax.ShapeDtypeStruct((1, width), F32),
        ],
        scratch_shapes=[pltpu.VMEM((rows, width), F32), pltpu.VMEM((width, rows), LOW)],
        compiler_params=pltpu.CompilerParams(vmem_limit_bytes=56 << 20),
    )(hn, dout, mid, params[6], params[7].reshape(1, -1), params[8], params[9].reshape(1, -1))


def back_kernel(
    x_ref, mid_ref, dhn_ref, dout_ref, q_ref, k_ref, v_ref, probs_ref,
    n1_ref, n2_ref, wq_ref, wk_ref, wv_ref, wo_ref,
    dattn_ref, dq_ref, dk_ref, dv_ref, first_ref, rest_ref, dn1_ref, dn2_ref,
    dmid_ref,
):
    places, frames, width = x_ref.shape
    rows = places * frames

    @pl.when(pl.program_id(0) == 0)
    def _():
        dn1_ref[...] = jnp.zeros_like(dn1_ref)
        dn2_ref[...] = jnp.zeros_like(dn2_ref)

    mid = mid_ref[...].reshape(rows, width)
    dmid, gain = scale_back(mid, n2_ref[...], dhn_ref[...].reshape(rows, width))
    dn2_ref[...] += jnp.sum(gain, axis=0, keepdims=True)
    dmid = dmid + dout_ref[...].astype(F32).reshape(rows, width)
    dmid_ref[...] = dmid
    dattn = dmid.astype(LOW)
    dattn_ref[...] = dattn.reshape(places, frames, width)
    dmixed = mul_t(dattn, wo_ref[...]).astype(LOW).reshape(places, frames, width)
    sums, spread = head_sums(width), head_spread(width)
    pair = 0
    dk, dv = [None] * places, [None] * places
    add = lambda old, term: term if old is None else old + term
    for i in range(places):
        grad = dmixed[i].astype(F32)
        query = q_ref[i].astype(F32)
        dp = [sum_heads(grad * v_ref[j].astype(F32), sums) for j in range(i + 1)]
        delta = None
        for j in range(i + 1):
            delta = add(delta, probs_ref[pair + j] * dp[j])
        dq = None
        for j in range(i + 1):
            probs = probs_ref[pair + j]
            ds = (probs * (dp[j] - delta)).astype(LOW)
            ds = mul(ds, spread)
            dq = add(dq, ds * k_ref[j].astype(F32))
            dk[j] = add(dk[j], ds * query)
            dv[j] = add(dv[j], mul(probs.astype(LOW), spread) * grad)
        pair += i + 1
        dq_ref[i] = (dq * HD ** (-0.5)).astype(LOW)
    for j in range(places):
        dk_ref[j] = (dk[j] * HD ** (-0.5)).astype(LOW)
        dv_ref[j] = dv[j].astype(LOW)
    dnormed = (
        mul_t(dq_ref[...].reshape(rows, width), wq_ref[...])
        + mul_t(dk_ref[...].reshape(rows, width), wk_ref[...])
        + mul_t(dv_ref[...].reshape(rows, width), wv_ref[...])
    )
    x = x_ref[...].astype(F32).reshape(rows, width)
    dx, gain = scale_back(x, n1_ref[...], dnormed)
    dn1_ref[...] += jnp.sum(gain, axis=0, keepdims=True)
    dx = (dx + dmid_ref[...]).reshape(places, frames, width)
    first_ref[...] = dx[0]
    rest_ref[...] = dx[1:].astype(LOW)


def local_back(x, mid, dhn, dout, q, k, v, probs, params):
    places, frames, width = x.shape
    pairs = probs.shape[0]
    step = 64
    rows = pl.BlockSpec((places, step, width), lambda i: (0, i, 0))
    whole = lambda item: pl.BlockSpec(item.shape, lambda i: (0, 0), pipeline_mode=pl.Buffered(1))
    like = lambda kind: jax.ShapeDtypeStruct((places, frames, width), kind)
    fixed = (params[0].reshape(1, -1), params[5].reshape(1, -1)) + tuple(params[1:5])
    vector = pl.BlockSpec((1, width), lambda i: (0, 0))
    return pl.pallas_call(
        back_kernel,
        grid=(frames // step,),
        in_specs=[rows] * 7
        + [pl.BlockSpec((pairs, step, 128), lambda i: (0, i, 0))]
        + [whole(item) for item in fixed],
        out_specs=[rows] * 4
        + [
            pl.BlockSpec((step, width), lambda i: (i, 0)),
            pl.BlockSpec((places - 1, step, width), lambda i: (0, i, 0)),
            vector, vector,
        ],
        out_shape=[
            like(LOW), like(LOW), like(LOW), like(LOW),
            jax.ShapeDtypeStruct((frames, width), F32),
            jax.ShapeDtypeStruct((places - 1, frames, width), LOW),
            jax.ShapeDtypeStruct((1, width), F32),
            jax.ShapeDtypeStruct((1, width), F32),
        ],
        scratch_shapes=[pltpu.VMEM((places * step, width), F32)],
        compiler_params=pltpu.CompilerParams(vmem_limit_bytes=60 << 20),
    )(x, mid, dhn, dout, q, k, v, probs, *fixed)


def greet(count):
    utt, me = lax.axis_index("utt"), lax.axis_index("seq")
    barrier = pltpu.get_barrier_semaphore()

    @pl.loop(1, count)
    def _(step):
        pl.semaphore_signal(
            barrier, inc=1, device_id=(utt, lax.rem(me + step, count)), device_id_type=MESH_ID
        )

    return barrier


def remote(source, target, send_sem, recv_sem, place):
    return pltpu.make_async_remote_copy(
        src_ref=source,
        dst_ref=target,
        send_sem=send_sem,
        recv_sem=recv_sem,
        device_id=(lax.axis_index("utt"), place),
        device_id_type=MESH_ID,
    )


def two_heads(rows):
    lane = lax.broadcasted_iota(jnp.int32, rows.shape, 1)
    zero = jnp.zeros_like(rows)
    return jnp.concatenate([jnp.where(lane < HD, rows, zero), jnp.where(lane < HD, zero, rows)], axis=0)


def join_heads(tall):
    rows = tall.T
    lane = lax.broadcasted_iota(jnp.int32, (HD, LANES), 1)
    return jnp.where(lane < HD, rows[:HD], rows[HD:])


def masked_scores(scores, bias, first, block):
    key = first + lax.broadcasted_iota(jnp.int32, scores.shape, 0)
    query = block * HD + lax.rem(lax.broadcasted_iota(jnp.int32, scores.shape, 1), HD)
    return jnp.where(key < query, scores + bias, jnp.where(key == query, scores, NEGATIVE))


def fill_bias(bias_ref, mask):
    for block in range(mask.shape[0]):
        row = lax.broadcasted_iota(jnp.int32, (HD, LANES), 0)
        lane = lax.broadcasted_iota(jnp.int32, (HD, LANES), 1)
        flags = jnp.broadcast_to(mask[block, 0:1, :], (HD, LANES))
        diagonal = jnp.where(row == lane, flags.astype(F32), 0.0).astype(LOW)
        usable = mul(diagonal, jnp.ones((LANES, LANES), LOW))
        bias_ref[block * HD : (block + 1) * HD, :] = (usable - 1.0) * 1e30


def attend_kernel(
    count, x_ref, mask_ref, n1_ref, wq_ref, wk_ref, wv_ref, codes_ref, valid_ref, n2_ref, b1_ref,
    b2_ref, table_ref, wo_ref, w1_ref, w2_ref,
    normed_ref, mixed_ref, saved_ref, log_ref, local_ref, mid_ref, hn_ref, u_ref, act_ref,
    packed, held, mixed_all, pieces, bias, v_t, table, wo, w1, w2,
    send_sem, recv_sem, send_two, recv_two, save_sem, fetch_sem,
):
    share = count // 16
    me = lax.axis_index("seq")
    unit, part = me // share, me % share
    own_utt, own_pair = unit // 8, unit % 8
    own_cols = pl.ds(pl.multiple_of(own_pair * LANES, LANES), LANES)
    utts, frames, width = x_ref.shape
    rows = utts * frames
    barrier = greet(count)
    fetches = [
        pltpu.make_async_copy(source, target, fetch_sem.at[index])
        for index, (source, target) in enumerate(
            ((table_ref, table), (wo_ref, wo), (w1_ref, w1), (w2_ref, w2))
        )
    ]
    for copy in fetches:
        copy.start()

    x = x_ref[...].astype(F32).reshape(rows, width)
    normed = (x * scale_of(x) * n1_ref[...]).astype(LOW)
    normed_ref[...] = normed
    packed[:, 0:64] = (mul(normed, wq_ref[...]).astype(LOW)).reshape(utts, frames, width)
    packed[:, 64:128] = mul(normed, wk_ref[...]).astype(LOW).reshape(utts, frames, width)
    packed[:, 128:192] = mul(normed, wv_ref[...]).astype(LOW).reshape(utts, frames, width)
    for pair in range(8):
        packed[:, 192:208, pair * LANES : (pair + 1) * LANES] = jnp.broadcast_to(
            mask_ref[...], (utts, 16, LANES)
        )
    pl.semaphore_wait(barrier, count - 1)

    def outgoing(step):
        place = lax.rem(me + step, count)
        target = place // share
        cols = pl.ds(pl.multiple_of((target % 8) * LANES, LANES), LANES)
        return remote(
            packed.at[target // 8, :, cols], held.at[me], send_sem.at[step], recv_sem.at[step], place
        )

    @pl.loop(1, count)
    def _(step):
        outgoing(step).start()

    held[me] = packed[own_utt, :, own_cols]

    fetches[0].wait()
    vocab = table.shape[0] // CB
    for book in range(CB):
        ids = jnp.broadcast_to(codes_ref[book][:, 0:1], (rows, vocab))
        picked = (ids == lax.broadcasted_iota(jnp.int32, (rows, vocab), 1)).astype(LOW)
        local_ref[1 + book] = mul(picked, table[book * vocab : (book + 1) * vocab]).astype(LOW)

    save = pltpu.make_async_copy(held, saved_ref, save_sem)

    def returning(block):
        return remote(
            pieces.at[block],
            mixed_all.at[own_utt, :, own_cols],
            send_two.at[block],
            recv_two.at[unit],
            block,
        )

    for group in range(count // 4):
        below = group * 256
        here = below + 256
        for place in range(4 * group, 4 * group + 4):

            @pl.when(place != me)
            def _():
                step = lax.rem(me + count - place, count)
                remote(
                    held.at[place], held.at[place], send_sem.at[step], recv_sem.at[step], place
                ).wait_recv()

        v_t[:, below:here] = held[4 * group : 4 * group + 4, 128:192].reshape(256, LANES).T
        fill_bias(bias.at[below:here], held[4 * group : 4 * group + 4, 192:208])

        @pl.loop(0, 4 // share)
        def _(index):
            block = 4 * group + share * index + part
            query = two_heads(held[block, 0:64] * LOW(HD ** (-0.5)))
            keys = held[4 * group : 4 * group + 4, 64:128].reshape(256, LANES)
            near = masked_scores(mul_t(keys, query), bias[below:here], below, block)
            peak = jnp.max(near, axis=0, keepdims=True)
            if group:
                keys = held[0 : 4 * group, 64:128].reshape(below, LANES)
                far = mul_t(keys, query) + bias[0:below]
                peak = jnp.maximum(peak, jnp.max(far, axis=0, keepdims=True))
                far = jnp.exp(far - peak)
            near = jnp.exp(near - peak)
            total = jnp.sum(near, axis=0, keepdims=True)
            if group:
                total = total + jnp.sum(far, axis=0, keepdims=True)
            inverse = 1.0 / total
            mixed = mul(v_t[:, below:here], (near * inverse).astype(LOW))
            if group:
                mixed = mixed + mul(v_t[:, 0:below], (far * inverse).astype(LOW))
            log_ref[block] = jnp.broadcast_to(peak + jnp.log(total), (8, LANES))
            pieces[block] = join_heads(mixed).astype(LOW)

            @pl.when(block != me)
            def _():
                returning(block).start()

            @pl.when(block == me)
            def _():
                mixed_all[own_utt, :, own_cols] = pieces[block]

    save.start()

    @pl.loop(0, 16)
    def _(other):
        place = other * share + me % share
        cols = pl.ds(pl.multiple_of((other % 8) * LANES, LANES), LANES)

        @pl.when(place != me)
        def _():
            here = mixed_all.at[other // 8, :, cols]
            remote(here, here, send_two.at[0], recv_two.at[other], place).wait_recv()

    mixed = mixed_all[...].reshape(rows, width)
    mixed_ref[...] = mixed
    fetches[1].wait()
    mid = x_ref[...].astype(F32).reshape(rows, width) + mul(mixed, wo[...])
    hn = (mid * scale_of(mid) * n2_ref[...]).astype(LOW)
    mid_ref[...] = mid
    hn_ref[...] = hn
    fetches[2].wait()
    fetches[3].wait()
    result = mid + b2_ref[...]
    for first in range(0, u_ref.shape[1], 512):
        cols = slice(first, first + 512)
        u = mul(hn, w1[:, cols]) + b1_ref[:, cols]
        act = gelu_parts(u)[0].astype(LOW)
        u_ref[:, cols] = u
        act_ref[:, cols] = act
        result = result + mul(act, w2[cols])
    local_ref[0] = jnp.where(valid_ref[...] > 0, result, 0.0).astype(LOW)

    @pl.loop(1, count)
    def _(step):
        outgoing(step).wait_send()

    @pl.loop(0, count // share)
    def _(index):
        block = share * index + part

        @pl.when(block != me)
        def _():
            returning(block).wait_send()

    save.wait()


def global_forward(x, mask, codes, valid, table, params):
    count = lax.axis_size("seq")
    utts, frames, width = x.shape
    rows, wide = utts * frames, params[6].shape[1]
    vmem = pl.BlockSpec(memory_space=pltpu.VMEM)
    hbm = pl.BlockSpec(memory_space=pl.ANY)
    return pl.pallas_call(
        functools.partial(attend_kernel, count),
        in_specs=[vmem] * 11 + [hbm] * 4,
        out_specs=[vmem, vmem, hbm] + [vmem] * 6,
        out_shape=[
            jax.ShapeDtypeStruct((rows, width), LOW),
            jax.ShapeDtypeStruct((rows, width), LOW),
            jax.ShapeDtypeStruct((count, 208, LANES), LOW),
            jax.ShapeDtypeStruct((count, 8, LANES), F32),
            jax.ShapeDtypeStruct((1 + CB, rows, width), LOW),
            jax.ShapeDtypeStruct((rows, width), F32),
            jax.ShapeDtypeStruct((rows, width), LOW),
            jax.ShapeDtypeStruct((rows, wide), F32),
            jax.ShapeDtypeStruct((rows, wide), LOW),
        ],
        scratch_shapes=[
            pltpu.VMEM((utts, 208, width), LOW),
            pltpu.VMEM((count, 208, LANES), LOW),
            pltpu.VMEM((utts, frames, width), LOW),
            pltpu.VMEM((count, HD, LANES), LOW),
            pltpu.VMEM((count * HD, LANES), F32),
            pltpu.VMEM((LANES, count * HD), LOW),
            pltpu.VMEM(table.shape, LOW),
            pltpu.VMEM(params[4].shape, LOW),
            pltpu.VMEM(params[6].shape, LOW),
            pltpu.VMEM(params[8].shape, LOW),
            pltpu.SemaphoreType.DMA((count,)),
            pltpu.SemaphoreType.DMA((count,)),
            pltpu.SemaphoreType.DMA((count,)),
            pltpu.SemaphoreType.DMA((16,)),
            pltpu.SemaphoreType.DMA,
            pltpu.SemaphoreType.DMA((4,)),
        ],
        compiler_params=pltpu.CompilerParams(
            collective_id=2, has_side_effects=True, vmem_limit_bytes=58 << 20
        ),
    )(
        x, mask, params[0].reshape(1, -1), params[1], params[2], params[3], codes, valid,
        params[5].reshape(1, -1), params[7].reshape(1, -1), params[9].reshape(1, -1), table,
        params[4], params[6], params[8],
    )


def settle_kernel(number, *refs):
    sources, targets, held = (refs[index * number : (index + 1) * number] for index in range(3))
    into = [
        pltpu.make_async_copy(sources[index], held[index], refs[-1].at[0, index])
        for index in range(number)
    ]
    out = [
        pltpu.make_async_copy(held[index], targets[index], refs[-1].at[1, index])
        for index in range(number)
    ]
    for copy in into:
        copy.start()
    for first, second in zip(into, out):
        first.wait()
        second.start()
    for copy in out:
        copy.wait()


def settle(arrays):
    hbm = pl.BlockSpec(memory_space=pl.ANY)
    return pl.pallas_call(
        functools.partial(settle_kernel, len(arrays)),
        in_specs=[hbm] * len(arrays),
        out_specs=[hbm] * len(arrays),
        out_shape=[jax.ShapeDtypeStruct(item.shape, item.dtype) for item in arrays],
        scratch_shapes=[pltpu.VMEM(item.shape, item.dtype) for item in arrays]
        + [pltpu.SemaphoreType.DMA((2, len(arrays)))],
        compiler_params=pltpu.CompilerParams(vmem_limit_bytes=62 << 20),
    )(*arrays)


def attend_back_kernel(
    count, grad_ref, held, log_ref,
    dqkv_ref,
    grads, landed, pieces, dk_acc, dv_acc, bias, k_t, send_sem, recv_sem, send_two, recv_two,
):
    share = count // 16
    me = lax.axis_index("seq")
    unit, part = me // share, me % share
    own_utt, own_pair = unit // 8, unit % 8
    own_cols = pl.ds(pl.multiple_of(own_pair * LANES, LANES), LANES)
    barrier = greet(count)
    k_t[...] = held[:, 64:128].reshape(count * HD, LANES).T
    fill_bias(bias, held[:, 192:208])
    dk_acc[...] = jnp.zeros_like(dk_acc)
    dv_acc[...] = jnp.zeros_like(dv_acc)
    pl.semaphore_wait(barrier, count - 1)

    def outgoing(other):
        cols = pl.ds(pl.multiple_of((other % 8) * LANES, LANES), LANES)
        place = other * share + part
        return place, remote(
            grad_ref.at[other // 8, :, cols], grads.at[me // share], send_sem.at[other],
            recv_sem.at[me // share], place,
        )

    @pl.loop(1, 16)
    def _(step):
        _, copy = outgoing(lax.rem(unit + step, 16))
        copy.start()

    grads[unit] = grad_ref[own_utt, :, own_cols]

    @pl.loop(1, 16)
    def _(step):
        other = lax.rem(unit + step, 16)
        here = grads.at[other]
        remote(here, here, send_sem.at[other], recv_sem.at[other], other * share + part).wait_recv()

    def returning(block):
        return remote(
            pieces.at[block],
            landed.at[part, :, own_utt, :, own_cols],
            send_two.at[block],
            recv_two.at[me],
            block,
        )

    for group in reversed(range(count // 4)):
        below = group * 256
        here = below + 256

        @pl.loop(0, 4 // share)
        def _(index):
            block = 4 * group + share * index + part
            query = two_heads(held[block, 0:64] * LOW(HD ** (-0.5)))
            grad = two_heads(grads[block // share])
            log_total = log_ref[block][0:1]
            near_v = held[4 * group : 4 * group + 4, 128:192].reshape(256, LANES)
            near_k = held[4 * group : 4 * group + 4, 64:128].reshape(256, LANES)
            near = masked_scores(mul_t(near_k, query), bias[below:here], below, block)
            near = jnp.exp(near - log_total)
            near_dp = mul_t(near_v, grad)
            delta = jnp.sum(near * near_dp, axis=0, keepdims=True)
            if group:
                far_v = held[0 : 4 * group, 128:192].reshape(below, LANES)
                far_k = held[0 : 4 * group, 64:128].reshape(below, LANES)
                far = jnp.exp(mul_t(far_k, query) + bias[0:below] - log_total)
                far_dp = mul_t(far_v, grad)
                delta = delta + jnp.sum(far * far_dp, axis=0, keepdims=True)
                far_ds = (far * (far_dp - delta)).astype(LOW)
                dk_acc[0:below] += mul(far_ds, query)
                dv_acc[0:below] += mul(far.astype(LOW), grad)
            near_ds = (near * (near_dp - delta)).astype(LOW)
            dk_acc[below:here] += mul(near_ds, query)
            dv_acc[below:here] += mul(near.astype(LOW), grad)
            dq = mul(k_t[:, below:here], near_ds)
            if group:
                dq = dq + mul(k_t[:, 0:below], far_ds)
            pieces[block, 0] = (join_heads(dq) * HD ** (-0.5)).astype(LOW)

        for block in range(4 * group, 4 * group + 4):
            rows = slice(block * HD, (block + 1) * HD)
            pieces[block, 1] = dk_acc[rows].astype(LOW)
            pieces[block, 2] = dv_acc[rows].astype(LOW)
            if share > 1:

                @pl.when(block % share != part)
                def _():
                    pieces[block, 0] = jnp.zeros((HD, LANES), LOW)

            @pl.when(block != me)
            def _():
                returning(block).start()

            @pl.when(block == me)
            def _():
                landed[part, :, own_utt, :, own_cols] = pieces[block]

    @pl.loop(1, count)
    def _(step):
        place = lax.rem(me + step, count)
        other, other_part = place // share, place % share
        cols = pl.ds(pl.multiple_of((other % 8) * LANES, LANES), LANES)
        here = landed.at[other_part, :, other // 8, :, cols]
        remote(here, here, send_two.at[place], recv_two.at[place], place).wait_recv()

    @pl.loop(1, 16)
    def _(step):
        _, copy = outgoing(lax.rem(unit + step, 16))
        copy.wait_send()

    @pl.loop(1, count)
    def _(step):
        returning(lax.rem(me + step, count)).wait_send()

    total = landed[0]
    for other_part in range(1, share):
        total = (total.astype(F32) + landed[other_part].astype(F32)).astype(LOW)
    dqkv_ref[...] = total


def global_attend_back(grad_mixed, saved, log_total):
    count = lax.axis_size("seq")
    utts, frames, width = grad_mixed.shape
    vmem = pl.BlockSpec(memory_space=pltpu.VMEM)
    return pl.pallas_call(
        functools.partial(attend_back_kernel, count),
        in_specs=[vmem] * 3,
        out_specs=vmem,
        out_shape=jax.ShapeDtypeStruct((3, utts, frames, width), LOW),
        scratch_shapes=[
            pltpu.VMEM((16, HD, LANES), LOW),
            pltpu.VMEM((count // 16, 3, utts, frames, width), LOW),
            pltpu.VMEM((count, 3, HD, LANES), LOW),
            pltpu.VMEM((count * HD, LANES), F32),
            pltpu.VMEM((count * HD, LANES), F32),
            pltpu.VMEM((count * HD, LANES), F32),
            pltpu.VMEM((LANES, count * HD), LOW),
            pltpu.SemaphoreType.DMA((16,)),
            pltpu.SemaphoreType.DMA((16,)),
            pltpu.SemaphoreType.DMA((count,)),
            pltpu.SemaphoreType.DMA((count,)),
        ],
        compiler_params=pltpu.CompilerParams(
            collective_id=3, has_side_effects=True, vmem_limit_bytes=48 << 20
        ),
    )(grad_mixed, saved, log_total)


SLOTS = 4
DEEP = 8
SROWS = 64
SCOLS = 512
ACOLS = 384
DRAIN = 8
PLAN = (
    (0, 8, 8), (8, 8, 2), (16, 2, 2), (18, 2, 2), (20, 2, 2), (22, 2, 2), (24, 6, 2),
    (30, 8, 2), (38, 8, 8), (46, 2, 2), (48, 2, 2), (50, 2, 2), (52, 2, 2), (54, 1, 1),
)
SLABS = 55
LOADED = 16
AT_HIDDEN = 8
AT_BACK = 16
AT_ATTEND = 23
AT_RETURN = 31
AT_LANDED = 47
PART = 32


def tail_kernel(names, out_count, *refs):
    r = types.SimpleNamespace(**dict(zip(names, refs)))
    outs = refs[names.index("out_0") : names.index("out_0") + out_count]
    utt = lax.axis_index("utt")
    seq = lax.axis_index("seq")
    count = 16
    pos = seq // 4
    col = (seq // 2) % 2
    core = seq % 2
    core_id = (utt, pos * 4 + col * 2 + 1 - core)
    col_id = (utt, pos * 4 + (1 - col) * 2 + core)
    utt_id = (1 - utt, seq)
    right_id = (utt, lax.rem(seq + 4, 16))
    left_id = (utt, lax.rem(seq + 12, 16))

    barrier = greet(count)
    pl.semaphore_signal(barrier, inc=1, device_id=utt_id, device_id_type=MESH_ID)

    def window(ref, spec, slab, lead):
        local = slab - spec[0]
        rows = pl.ds(pl.multiple_of((local // spec[2]) * SROWS, SROWS), SROWS)
        cols = pl.ds(pl.multiple_of((local % spec[2]) * SCOLS, SCOLS), SCOLS)
        return ref.at[lead + (rows, cols)]

    def load_start(slab):
        slot = slab % SLOTS
        for ref, spec in ((r.l_up, PLAN[0]), (r.l_down, PLAN[1])):

            @pl.when((slab >= spec[0]) & (slab < spec[0] + spec[1]))
            def _():
                for side in range(2):
                    pltpu.make_async_copy(
                        window(ref, spec, slab, (slice(None), side)),
                        r.part.at[slot, side],
                        r.load_sem.at[slot, side],
                    ).start()

    def load_wait(slot):
        for side in range(2):
            pltpu.make_async_copy(
                r.l_up.at[:, side, pl.ds(0, SROWS), pl.ds(0, SCOLS)],
                r.part.at[slot, side],
                r.load_sem.at[slot, side],
            ).wait()

    def weights(block, slot):
        start = block * SCOLS if isinstance(block, int) else pl.multiple_of(block * SCOLS, SCOLS)
        return (
            pltpu.make_async_copy(
                r.g_w_up.at[:, pl.ds(start, SCOLS)], r.up_buf.at[slot], r.weight_sem.at[slot, 0]
            ),
            pltpu.make_async_copy(
                r.g_w_down.at[pl.ds(start, SCOLS)], r.down_buf.at[slot], r.weight_sem.at[slot, 1]
            ),
        )

    fetches = (
        (r.g_w_o, r.square.at[0]), (r.g_w_q, r.square.at[1]), (r.g_w_k, r.square.at[2]),
        (r.g_w_v, r.square.at[3]), (r.saved, r.held), (r.l_normed, r.l_x.at[0]),
        (r.l_mixed, r.l_x.at[1]), (r.g_act, r.act_buf), (r.g_mixed, r.g_x.at[0]),
        (r.g_normed, r.g_x.at[1]), (r.l_w_o, r.square.at[0]), (r.l_w_q, r.square.at[1]),
        (r.l_w_k, r.square.at[2]), (r.l_w_v, r.square.at[3]),
    )

    def fetch(*which):
        return [
            pltpu.make_async_copy(*fetches[index], r.fetch_sem.at[index]) for index in which
        ]

    def local_rows(step, slot):
        rows = pl.ds(step * PART if isinstance(step, int) else pl.multiple_of(step * PART, PART), PART)
        pairs = (
            (r.l_in, r.l_in_buf), (r.l_mid, r.l_mid_buf), (r.l_dhn, r.l_dhn_buf),
            (r.l_dout, r.l_dout_buf), (r.l_q, r.l_q_buf), (r.l_k, r.l_k_buf), (r.l_v, r.l_v_buf),
            (r.l_probs, r.l_probs_buf),
        )
        return [
            pltpu.make_async_copy(ref.at[:, rows], buffer.at[slot], r.local_sem.at[slot, index])
            for index, (ref, buffer) in enumerate(pairs)
        ]

    load_start(0)
    for copy in local_rows(0, 0) + fetch(10, 11, 12, 13):
        copy.start()

    def send(kind, slot, source, target, device):
        return pltpu.make_async_remote_copy(
            src_ref=source,
            dst_ref=target,
            send_sem=r.send_sem.at[kind, slot],
            recv_sem=r.recv_sem.at[kind, slot],
            device_id=device,
            device_id_type=MESH_ID,
        )

    def core_copy(slot):
        return send(0, slot, r.part.at[slot, 1 - core], r.recv_c.at[slot], core_id)

    def col_copy_a(slot):
        return send(1, slot, r.half_a.at[slot, 1 - col], r.recv_xa.at[slot], col_id)

    def utt_copy_b(slot):
        return send(2, slot, r.half_b.at[slot, 1 - utt], r.recv_yb.at[slot], utt_id)

    def col_copy_b(slot):
        return send(3, slot, r.sum_b.at[slot, 1 - col], r.recv_xb.at[slot], col_id)

    def utt_copy_a(slot, deep):
        return send(4, slot, r.sum_a.at[deep, pos], r.recv_ya.at[slot], utt_id)

    def utt_copy_b2(slot, deep):
        return send(5, slot, r.line_b.at[deep, pos], r.recv_yb2.at[slot], utt_id)

    def col_copy_c(slot, deep):
        return send(24, slot, r.line_c.at[deep, pos, 1 - col], r.recv_xc.at[slot], col_id)

    def utt_copy_c(slot):
        return send(25, slot, r.sum_c.at[slot], r.recv_yc.at[slot], utt_id)

    def line_right(kind, slot, deep, step, source, target):
        dest = jnp.minimum(4 - step + pos, 3)
        return send(kind + step - 1, slot, source.at[deep, dest], target.at[slot, step - 1], right_id)

    def line_left(kind, slot, deep, step, source, target):
        dest = jnp.maximum(pos - 4 + step, 0)
        return send(kind + step - 1, slot, source.at[deep, dest], target.at[slot, step - 1], left_id)

    def line_start(slot, deep, step, source, right, left, kind):
        @pl.when((pos <= step - 1) & (pos < 3))
        def _():
            line_right(kind, slot, deep, step, source, right).start()

        @pl.when((pos >= 4 - step) & (pos > 0))
        def _():
            line_left(kind + 3, slot, deep, step, source, left).start()

    def line_finish(slot, deep, step, source, right, left, kind):
        @pl.when((pos <= step - 1) & (pos < 3))
        def _():
            line_right(kind, slot, deep, step, source, right).wait_send()

        @pl.when((pos >= 4 - step) & (pos > 0))
        def _():
            line_left(kind + 3, slot, deep, step, source, left).wait_send()

        @pl.when((pos >= 1) & (pos <= step))
        def _():
            line_right(kind, slot, deep, step, source, right).wait_recv()
            dest = 3 - step + pos
            source[deep, dest] = (
                source[deep, dest].astype(F32) + right[slot, step - 1].astype(F32)
            ).astype(LOW)

        @pl.when((pos <= 2) & (pos >= 3 - step))
        def _():
            line_left(kind + 3, slot, deep, step, source, left).wait_recv()
            dest = pos + step - 3
            source[deep, dest] = (
                source[deep, dest].astype(F32) + left[slot, step - 1].astype(F32)
            ).astype(LOW)

    line_a = (r.sum_a, r.right_a, r.left_a, 6)
    line_bb = (r.line_b, r.right_b, r.left_b, 12)
    line_cc = (r.line_c, r.right_c, r.left_c, 18)

    def advance(tick):
        def stage(offset):
            slab = tick - offset
            return (
                slab,
                lax.rem(slab + SLOTS * 4, SLOTS),
                lax.rem(slab + DEEP, DEEP),
                pl.when((slab >= 0) & (slab < SLABS)),
                pl.when((slab >= 0) & (slab < SLABS - 1)),
            )

        slab, slot, _, guard, _ = stage(0)
        load_start(slab + 1)

        @pl.when(slab < LOADED)
        def _():
            load_wait(slot)

        @guard
        def _():
            core_copy(slot).start()

        _, slot1, deep1, guard, most = stage(1)

        @guard
        def _():
            core_copy(slot1).wait()
            for line in range(4):
                for side in range(2):
                    both = r.part[slot1, core, 2 * line + side].astype(F32) + r.recv_c[
                        slot1, 2 * line + side
                    ].astype(F32)
                    both = both.astype(LOW)
                    r.half_a[slot1, side, line] = both[:32, :ACOLS]
                    r.line_c[deep1, line, side] = both[:32, ACOLS:]
                    r.half_b[slot1, 0, side, line] = both[32:48]
                    r.half_b[slot1, 1, side, line] = both[48:]
            line_start(slot1, deep1, 1, *line_cc)

        @most
        def _():
            col_copy_a(slot1).start()
            utt_copy_b(slot1).start()

        _, slot2, deep2, guard, most = stage(2)

        @guard
        def _():
            line_finish(slot2, deep2, 1, *line_cc)
            line_start(slot2, deep2, 2, *line_cc)

        @most
        def _():
            col_copy_a(slot2).wait()
            r.sum_a[deep2] = (
                r.half_a[slot2, col].astype(F32) + r.recv_xa[slot2].astype(F32)
            ).astype(LOW)
            line_start(slot2, deep2, 1, *line_a)
            utt_copy_b(slot2).wait()
            r.sum_b[slot2] = (
                r.half_b[slot2, utt].astype(F32) + r.recv_yb[slot2].astype(F32)
            ).astype(LOW)
            col_copy_b(slot2).start()

        _, slot3, deep3, guard, most = stage(3)

        @guard
        def _():
            line_finish(slot3, deep3, 2, *line_cc)
            line_start(slot3, deep3, 3, *line_cc)

        @most
        def _():
            line_finish(slot3, deep3, 1, *line_a)
            line_start(slot3, deep3, 2, *line_a)
            col_copy_b(slot3).wait()
            r.line_b[deep3] = (
                r.sum_b[slot3, col].astype(F32) + r.recv_xb[slot3].astype(F32)
            ).astype(LOW)
            line_start(slot3, deep3, 1, *line_bb)

        _, slot4, deep4, guard, most = stage(4)

        @guard
        def _():
            line_finish(slot4, deep4, 3, *line_cc)
            col_copy_c(slot4, deep4).start()

        @most
        def _():
            line_finish(slot4, deep4, 2, *line_a)
            line_start(slot4, deep4, 3, *line_a)
            line_finish(slot4, deep4, 1, *line_bb)
            line_start(slot4, deep4, 2, *line_bb)

        _, slot5, deep5, guard, most = stage(5)

        @guard
        def _():
            col_copy_c(slot5, deep5).wait()
            r.sum_c[slot5] = (
                r.line_c[deep5, pos, col].astype(F32) + r.recv_xc[slot5].astype(F32)
            ).astype(LOW)
            utt_copy_c(slot5).start()

        @most
        def _():
            line_finish(slot5, deep5, 3, *line_a)
            utt_copy_a(slot5, deep5).start()
            line_finish(slot5, deep5, 2, *line_bb)
            line_start(slot5, deep5, 3, *line_bb)

        _, slot6, deep6, guard, most = stage(6)

        @guard
        def _():
            utt_copy_c(slot6).wait()
            r.staged[slot6, 0:32, ACOLS:] = r.sum_c[slot6].astype(F32) + r.recv_yc[slot6].astype(F32)

        @most
        def _():
            utt_copy_a(slot6, deep6).wait()
            r.staged[slot6, 0:32, :ACOLS] = r.sum_a[deep6, pos].astype(F32) + r.recv_ya[
                slot6
            ].astype(F32)
            line_finish(slot6, deep6, 3, *line_bb)
            utt_copy_b2(slot6, deep6).start()

        slab7, slot7, deep7, guard, most = stage(7)

        @most
        def _():
            utt_copy_b2(slot7, deep7).wait()
            mine = r.line_b[deep7, pos].astype(F32)
            theirs = r.recv_yb2[slot7].astype(F32)
            r.staged[slot7, 32:48] = jnp.where(utt == 0, mine, theirs)
            r.staged[slot7, 48:64] = jnp.where(utt == 0, theirs, mine)

        for ref, spec in zip(outs, PLAN):

            @pl.when((slab7 >= spec[0]) & (slab7 < spec[0] + spec[1]))
            def _():
                pltpu.make_async_copy(
                    r.staged.at[slot7], window(ref, spec, slab7, ()), r.out_sem.at[slot7]
                ).start()

        _, slot8, _, guard, _ = stage(8)

        @guard
        def _():
            pltpu.make_async_copy(
                r.staged.at[slot8], outs[0].at[pl.ds(0, SROWS), pl.ds(0, SCOLS)], r.out_sem.at[slot8]
            ).wait()

    def cols_of(index):
        return pl.ds(pl.multiple_of(index * SCOLS, SCOLS), SCOLS)

    def put(slot, dest, rows):
        r.part[slot, dest % 2, dest // 2] = rows.astype(LOW)

    def put_product(slot, left_of, right):
        for quarter in range(4):
            rows = mul(left_of(quarter), right)
            for index in range(4):
                put(slot, 4 * quarter + index, rows[64 * index : 64 * index + 64])

    def quarter_rows(ref, lead=()):
        return lambda quarter: ref[lead + (slice(256 * quarter, 256 * quarter + 256),)]

    def produce(slab):
        slot = slab % SLOTS

        def among(first, number):
            return pl.when((slab >= first) & (slab < first + number))

        @among(16, 8)
        def _():
            local = slab - 16
            put_product(slot, quarter_rows(r.l_x_t), r.l_g[local // 2, :, cols_of(local % 2)])

        @among(24, 6)
        def _():
            local = slab - 24
            for dest in range(16):
                place = 3 * dest + local // 2
                book = place // 16
                first = (place % 16) * SROWS
                ids = first + lax.broadcasted_iota(jnp.int32, (SROWS, LANES), 0)
                picked = (ids == r.codes[book][0:1]).astype(LOW)
                put(slot, dest, mul(picked, r.table_g[book, :, cols_of(local % 2)]))

        @among(30, 8)
        def _():
            local = slab - 30
            inner = local // 2

            def rows(quarter):
                return jnp.concatenate(
                    [
                        r.act_t[pl.ds(pl.multiple_of(256 * dest + 64 * inner, 64), 64)]
                        for dest in range(4 * quarter, 4 * quarter + 4)
                    ],
                    axis=0,
                )

            put_product(slot, rows, r.dout_low[:, cols_of(local % 2)])

        @among(38, 8)
        def _():
            put_product(slot, quarter_rows(r.g_hn_t), r.du[:, cols_of(slab - 38)])

        @among(46, 8)
        def _():
            local = slab - 46
            kind = local // 2
            put_product(
                slot,
                quarter_rows(r.g_x_t, (jnp.minimum(kind, 1),)),
                r.g_g[kind, :, cols_of(local % 2)],
            )

        @pl.when(slab == 54)
        def _():
            b_down = jnp.sum(r.dout_low[...].astype(F32), axis=0, keepdims=True)
            for dest in range(16):
                shared = slice(LANES * (dest // 2), LANES * (dest // 2) + LANES)
                rows = [r.dn1[:, shared], r.dn2[:, shared], b_down[:, shared]]
                for index in range(2):
                    first = 256 * (dest % 2) + LANES * index
                    rows.append(r.db1[dest // 2 : dest // 2 + 1, first : first + LANES])
                rows += [r.l_dn1[:, shared], r.l_dn2[:, shared], r.l_db2[:, shared]]
                for index in range(2):
                    first = 256 * dest + LANES * index
                    rows.append(r.l_db1[:, first : first + LANES])
                rows.append(jnp.zeros((6, LANES), F32))
                r.part[slot, dest % 2, dest // 2, 0:16, ACOLS:] = jnp.concatenate(
                    rows, axis=0
                ).astype(LOW)

    own_utt, own_pair = seq // 8, seq % 8
    own_cols = pl.ds(pl.multiple_of(own_pair * LANES, LANES), LANES)

    def pair_cols(other):
        return pl.ds(pl.multiple_of((other % 8) * LANES, LANES), LANES)

    def hand_out(other):
        return remote(
            r.dmix.at[other // 8, :, pair_cols(other)], r.grads.at[seq], r.send_one.at[other],
            r.recv_one.at[seq], other,
        )

    def hand_back(block):
        return remote(
            r.pieces.at[block], r.landed.at[:, own_utt, :, own_cols], r.send_two.at[block],
            r.recv_two.at[seq], block,
        )

    def others(body):
        @pl.loop(1, count)
        def _(step):
            body(lax.rem(seq + step, count))

    def compute(tick):
        def at(*ticks):
            hit = tick == ticks[0]
            for item in ticks[1:]:
                hit = hit | (tick == item)
            return pl.when(hit)

        @pl.when((tick < 8) & (tick % 2 == 0))
        def _():
            step = tick // 2
            slot = step % 2
            for copy in local_rows(step, slot):
                copy.wait()

            @pl.when(tick == 0)
            def _():
                for copy in fetch(10):
                    copy.wait()
                r.l_dn1[...] = jnp.zeros_like(r.l_dn1)
                r.l_dn2[...] = jnp.zeros_like(r.l_dn2)

            @pl.when(step < 3)
            def _():
                for copy in local_rows(step + 1, 1 - slot):
                    copy.start()

            local_attend_back(r, step, slot)

        @pl.when((tick < 8) & (tick % 2 == 1))
        def _():
            @pl.when(tick == 1)
            def _():
                for copy in fetch(11, 12, 13):
                    copy.wait()

            local_project_back(r, tick // 2, (tick // 2) % 2)

        @at(6)
        def _():
            for copy in weights(0, 0) + tuple(fetch(4, 5, 6)):
                copy.start()

        @at(AT_HIDDEN)
        def _():
            for copy in fetch(0, 1, 2, 3):
                copy.start()
            r.dout_low[...] = r.dout[...].astype(LOW)
            r.dhn[...] = jnp.zeros_like(r.dhn)

        @pl.when((tick >= AT_HIDDEN) & (tick < AT_HIDDEN + 8))
        def _():
            block = tick - AT_HIDDEN
            slot = block % 2
            for copy in weights(block, slot):
                copy.wait()

            @pl.when(block < 7)
            def _():
                for copy in weights(block + 1, 1 - slot):
                    copy.start()

            cols = cols_of(block)
            _, slope = gelu_parts(r.u[:, cols])
            du = (mul_t(r.dout_low[...], r.down_buf[slot]) * slope).astype(LOW)
            r.du[:, cols] = du
            r.db1[pl.ds(block, 1), :] = jnp.sum(du.astype(F32), axis=0, keepdims=True)
            r.dhn[...] += mul_t(du, r.up_buf[slot])

        @at(13)
        def _():
            for copy in fetch(4, 5, 6):
                copy.wait()
            r.l_x_t[...] = r.l_x[0].T

        @at(18)
        def _():
            for copy in fetch(7, 8, 9):
                copy.start()

        @at(AT_BACK)
        def _():
            for copy in fetch(0):
                copy.wait()
            dmid, gain = scale_back(r.mid[...], r.n2[...], r.dhn[...])
            r.dn2[...] = jnp.sum(gain, axis=0, keepdims=True)
            dmid = dmid + r.dout[...]
            r.dmid[...] = dmid
            dattn = dmid.astype(LOW)
            r.g_g[0] = dattn
            r.dmix[...] = mul_t(dattn, r.square[0]).astype(LOW).reshape(r.dmix.shape)
            r.grads[seq] = r.dmix[own_utt, :, own_cols]

        @pl.when((tick >= AT_BACK) & (tick < AT_BACK + 5))
        def _():
            @pl.loop(0, 3)
            def _(index):
                hand_out(lax.rem(seq + 3 * (tick - AT_BACK) + index + 1, count)).start()

        @at(AT_BACK + 1)
        def _():
            r.k_t[...] = r.held[:, 64:128].reshape(count * HD, LANES).T
            fill_bias(r.bias, r.held[:, 192:208])
            r.dk_acc[...] = jnp.zeros_like(r.dk_acc)
            r.dv_acc[...] = jnp.zeros_like(r.dv_acc)

        @at(AT_ATTEND)
        def _():
            def arrived(other):
                here = r.grads.at[other]
                remote(here, here, r.send_one.at[other], r.recv_one.at[other], other).wait_recv()

            others(arrived)

        for order, group in enumerate(reversed(range(4))):
            below = group * 256
            here = below + 256
            begin = AT_ATTEND + 2 * order

            @at(begin, begin + 1)
            def _():
                @pl.loop(0, 2)
                def _(index):
                    attend_back_block(
                        r, group, below, here, 4 * group + 2 * (tick - begin) + index
                    )

            @at(begin + 1)
            def _():
                for block in range(4 * group, 4 * group + 4):
                    rows = slice(block * HD, (block + 1) * HD)
                    r.pieces[block, 1] = r.dk_acc[rows].astype(LOW)
                    r.pieces[block, 2] = r.dv_acc[rows].astype(LOW)

        @at(AT_RETURN)
        def _():
            r.landed[:, own_utt, :, own_cols] = r.pieces[seq]

        @pl.when((tick >= AT_RETURN) & (tick < AT_RETURN + 15))
        def _():
            hand_back(lax.rem(seq + tick - AT_RETURN + 1, count)).start()

        @at(AT_LANDED)
        def _():
            def arrived(other):
                here = r.landed.at[:, other // 8, :, pair_cols(other)]
                remote(here, here, r.send_two.at[other], r.recv_two.at[other], other).wait_recv()

            others(arrived)
            others(lambda other: hand_out(other).wait_send())
            others(lambda other: hand_back(other).wait_send())
            for index in range(3):
                r.g_g[1 + index] = r.landed[index].reshape(r.g_g.shape[1:])

        @at(AT_LANDED + 1)
        def _():
            for copy in fetch(1, 2, 3):
                copy.wait()
            r.dhn[...] = mul_t(r.g_g[1], r.square[1])

        @at(AT_LANDED + 2)
        def _():
            r.dhn[...] += mul_t(r.g_g[2], r.square[2])

        @at(AT_LANDED + 3)
        def _():
            dnormed = r.dhn[...] + mul_t(r.g_g[3], r.square[3])
            dx, gain = scale_back(r.x[...].astype(F32), r.n1[...], dnormed)
            r.dn1[...] = jnp.sum(gain, axis=0, keepdims=True)
            r.dx[...] = dx + r.dmid[...]

        @at(21)
        def _():
            r.l_x_t[...] = r.l_x[1].T

        @at(22)
        def _():
            for copy in fetch(7, 8, 9):
                copy.wait()

        @pl.when((tick >= 24) & (tick < 28))
        def _():
            cols = pl.ds(pl.multiple_of((tick - 24) * 1024, 1024), 1024)
            r.act_t[cols] = r.act_buf[:, cols].T

        @at(28)
        def _():
            r.g_hn_t[...] = r.hn[...].T

        @at(31, 32)
        def _():
            r.g_x_t[tick - 31] = r.g_x[tick - 31].T

    pl.semaphore_wait(barrier, count)

    @pl.loop(0, SLABS + DRAIN)
    def _(tick):
        advance(tick)
        compute(tick)
        produce(tick + 1)


def local_attend_back(r, step, slot):
    places, width = r.l_in_buf.shape[1], r.l_in_buf.shape[3]
    frames = r.l_in.shape[1]
    rows = places * PART

    def rows_of(place):
        return pl.ds(pl.multiple_of(place * frames + step * PART, PART), PART)

    mid = r.l_mid_buf[slot].reshape(rows, width)
    dmid, gain = scale_back(mid, r.l_n2[...], r.l_dhn_buf[slot].reshape(rows, width))
    r.l_dn2[...] += jnp.sum(gain, axis=0, keepdims=True)
    dmid = dmid + r.l_dout_buf[slot].astype(F32).reshape(rows, width)
    r.l_dmid[...] = dmid
    dattn = dmid.astype(LOW)
    for place in range(places):
        r.l_g[3, rows_of(place)] = dattn[place * PART : (place + 1) * PART]
    r.l_dmix[...] = mul_t(dattn, r.square[0]).astype(LOW).reshape(places, PART, width)
    sums, spread = head_sums(width), head_spread(width)
    add = lambda old, term: term if old is None else old + term
    pair = 0
    dk, dv = [None] * places, [None] * places
    for i in range(places):
        grad = r.l_dmix[i].astype(F32)
        query = r.l_q_buf[slot, i].astype(F32)
        dp = [sum_heads(grad * r.l_v_buf[slot, j].astype(F32), sums) for j in range(i + 1)]
        delta = None
        for j in range(i + 1):
            delta = add(delta, r.l_probs_buf[slot, pair + j] * dp[j])
        dq = None
        for j in range(i + 1):
            probs = r.l_probs_buf[slot, pair + j]
            ds = mul((probs * (dp[j] - delta)).astype(LOW), spread)
            dq = add(dq, ds * r.l_k_buf[slot, j].astype(F32))
            dk[j] = add(dk[j], ds * query)
            dv[j] = add(dv[j], mul(probs.astype(LOW), spread) * grad)
        pair += i + 1
        r.l_g[0, rows_of(i)] = (dq * HD ** (-0.5)).astype(LOW)
    for j in range(places):
        r.l_g[1, rows_of(j)] = (dk[j] * HD ** (-0.5)).astype(LOW)
        r.l_g[2, rows_of(j)] = dv[j].astype(LOW)


def local_project_back(r, step, slot):
    places, width = r.l_in_buf.shape[1], r.l_in_buf.shape[3]
    frames = r.l_in.shape[1]
    rows = places * PART
    dnormed = None
    for kind in range(3):
        grad = jnp.concatenate(
            [
                r.l_g[kind, pl.ds(pl.multiple_of(place * frames + step * PART, PART), PART)]
                for place in range(places)
            ],
            axis=0,
        )
        term = mul_t(grad, r.square[1 + kind])
        dnormed = term if dnormed is None else dnormed + term
    x = r.l_in_buf[slot].astype(F32).reshape(rows, width)
    dx, gain = scale_back(x, r.l_n1[...], dnormed)
    r.l_dn1[...] += jnp.sum(gain, axis=0, keepdims=True)
    dx = dx + r.l_dmid[...]
    here = pl.ds(pl.multiple_of(step * PART, PART), PART)
    total = r.cotan[here].astype(F32) + dx[:PART]
    r.dout[here] = jnp.where(r.valid[here] > 0, total, 0.0)
    for place in range(1, places):
        r.table_g[place - 1, here] = dx[place * PART : (place + 1) * PART].astype(LOW)


def attend_back_block(r, group, below, here, block):
    query = two_heads(r.held[block, 0:64] * LOW(HD ** (-0.5)))
    grad = two_heads(r.grads[block])
    log_total = r.log_total[block][0:1]
    near_v = r.held[4 * group : 4 * group + 4, 128:192].reshape(256, LANES)
    near_k = r.held[4 * group : 4 * group + 4, 64:128].reshape(256, LANES)
    near = masked_scores(mul_t(near_k, query), r.bias[below:here], below, block)
    near = jnp.exp(near - log_total)
    near_dp = mul_t(near_v, grad)
    delta = jnp.sum(near * near_dp, axis=0, keepdims=True)
    if group:
        far_v = r.held[0 : 4 * group, 128:192].reshape(below, LANES)
        far_k = r.held[0 : 4 * group, 64:128].reshape(below, LANES)
        far = jnp.exp(mul_t(far_k, query) + r.bias[0:below] - log_total)
        far_dp = mul_t(far_v, grad)
        delta = delta + jnp.sum(far * far_dp, axis=0, keepdims=True)
        far_ds = (far * (far_dp - delta)).astype(LOW)
        r.dk_acc[0:below] += mul(far_ds, query)
        r.dv_acc[0:below] += mul(far.astype(LOW), grad)
    near_ds = (near * (near_dp - delta)).astype(LOW)
    r.dk_acc[below:here] += mul(near_ds, query)
    r.dv_acc[below:here] += mul(near.astype(LOW), grad)
    dq = mul(r.k_t[:, below:here], near_ds)
    if group:
        dq = dq + mul(r.k_t[:, 0:below], far_ds)
    r.pieces[block, 0] = (join_heads(dq) * HD ** (-0.5)).astype(LOW)


def finish_on_slice(far, near):
    vmem = pl.BlockSpec(memory_space=pltpu.VMEM)
    hbm = pl.BlockSpec(memory_space=pl.ANY)
    rows, width = near["x"].shape
    wide = near["u"].shape[1]
    utts = rows // HD
    shapes = [
        (width // 16, wide), (wide // 16, width), (width // 16, width), (width // 16, width),
        (width // 16, width), (width // 16, width), (3 * 1024 // 16, width), (wide // 16, width),
        (width // 16, wide), (width // 16, width), (width // 16, width), (width // 16, width),
        (width // 16, width), (SROWS, SCOLS),
    ]
    out_names = ["dx"] + ["out_%d" % index for index in range(len(shapes))]
    rows_l = far["l_normed"].shape[0]
    places, pairs = far["l_in"].shape[0], far["l_probs"].shape[0]
    buffers = dict(
        part=((SLOTS, 2, 8, 64, SCOLS), LOW),
        recv_c=((SLOTS, 8, 64, SCOLS), LOW),
        half_a=((SLOTS, 2, 4, 32, ACOLS), LOW),
        half_b=((SLOTS, 2, 2, 4, 16, SCOLS), LOW),
        recv_xa=((SLOTS, 4, 32, ACOLS), LOW),
        recv_yb=((SLOTS, 2, 4, 16, SCOLS), LOW),
        sum_a=((DEEP, 4, 32, ACOLS), LOW),
        sum_b=((SLOTS, 2, 4, 16, SCOLS), LOW),
        recv_xb=((SLOTS, 4, 16, SCOLS), LOW),
        line_b=((DEEP, 4, 16, SCOLS), LOW),
        right_a=((SLOTS, 3, 32, ACOLS), LOW),
        left_a=((SLOTS, 3, 32, ACOLS), LOW),
        right_b=((SLOTS, 3, 16, SCOLS), LOW),
        left_b=((SLOTS, 3, 16, SCOLS), LOW),
        recv_ya=((SLOTS, 32, ACOLS), LOW),
        recv_yb2=((SLOTS, 16, SCOLS), LOW),
        line_c=((DEEP, 4, 2, 32, LANES), LOW),
        right_c=((SLOTS, 3, 2, 32, LANES), LOW),
        left_c=((SLOTS, 3, 2, 32, LANES), LOW),
        recv_xc=((SLOTS, 32, LANES), LOW),
        sum_c=((SLOTS, 32, LANES), LOW),
        recv_yc=((SLOTS, 32, LANES), LOW),
        staged=((SLOTS, 64, SCOLS), F32),
        up_buf=((2, width, SCOLS), LOW),
        down_buf=((2, SCOLS, width), LOW),
        square=((4, width, width), LOW),
        held=(far["saved"].shape, LOW),
        l_x=((2, rows_l, width), LOW),
        l_g=((4, rows_l, width), LOW),
        l_x_t=((width, rows_l), LOW),
        l_in_buf=((2, places, PART, width), LOW),
        l_mid_buf=((2, places, PART, width), F32),
        l_dhn_buf=((2, places, PART, width), F32),
        l_dout_buf=((2, places, PART, width), LOW),
        l_q_buf=((2, places, PART, width), LOW),
        l_k_buf=((2, places, PART, width), LOW),
        l_v_buf=((2, places, PART, width), LOW),
        l_probs_buf=((2, pairs, PART, LANES), F32),
        l_dmid=((places * PART, width), F32),
        l_dmix=((places, PART, width), LOW),
        l_dn1=((1, width), F32),
        l_dn2=((1, width), F32),
        dout=((rows, width), F32),
        table_g=((places - 1, rows, width), LOW),
        act_buf=((rows, wide), LOW),
        act_t=((wide, rows), LOW),
        g_x=((2, rows, width), LOW),
        g_x_t=((2, width, rows), LOW),
        g_hn_t=((width, rows), LOW),
        g_g=((4, rows, width), LOW),
        dout_low=((rows, width), LOW),
        du=((rows, wide), LOW),
        db1=((8, SCOLS), F32),
        dn1=((1, width), F32),
        dn2=((1, width), F32),
        dhn=((rows, width), F32),
        dmid=((rows, width), F32),
        dmix=((utts, HD, width), LOW),
        grads=((16, HD, LANES), LOW),
        landed=((3, utts, HD, width), LOW),
        pieces=((16, 3, HD, LANES), LOW),
        dk_acc=((16 * HD, LANES), F32),
        dv_acc=((16 * HD, LANES), F32),
        bias=((16 * HD, LANES), F32),
        k_t=((LANES, 16 * HD), LOW),
    )
    semaphores = dict(
        load_sem=(SLOTS, 2), out_sem=(SLOTS,), send_sem=(26, SLOTS), recv_sem=(26, SLOTS),
        weight_sem=(2, 2), fetch_sem=(14,), local_sem=(2, 8), send_one=(16,), recv_one=(16,), send_two=(16,),
        recv_two=(16,),
    )
    names = list(far) + list(near) + out_names + list(buffers) + list(semaphores)
    return pl.pallas_call(
        functools.partial(tail_kernel, names, len(shapes)),
        in_specs=[hbm] * len(far) + [vmem] * len(near),
        out_specs=[vmem] + [hbm] * len(shapes),
        out_shape=[jax.ShapeDtypeStruct((rows, width), F32)]
        + [jax.ShapeDtypeStruct(shape, F32) for shape in shapes],
        scratch_shapes=[pltpu.VMEM(*item) for item in buffers.values()]
        + [pltpu.SemaphoreType.DMA(item) for item in semaphores.values()],
        compiler_params=pltpu.CompilerParams(
            collective_id=1, has_side_effects=True, vmem_limit_bytes=62 << 20
        ),
    )(*far.values(), *near.values())


def normalize(values, gain_vec):
    return (
        values * lax.rsqrt(jnp.mean(values * values, axis=-1, keepdims=True) + EPSILON) * gain_vec
    )


def gelu_fn(values):
    return jax.nn.gelu(values, approximate=True)


def project_back(gradient, weight):
    return lax.dot_general(
        gradient, weight, (((1,), (1,)), ((), ())), preferred_element_type=jnp.float32
    )


def weight_grad(left_side, gradient):
    return lax.dot_general(
        left_side, gradient, (((0,), (0,)), ((), ())), preferred_element_type=jnp.float32
    )


def block_back(inputs, normed, mixed_rows, kept_parts, params, grad_out, attention_back):
    middle, middle_norm, pre_active, active = kept_parts
    grad_branch = grad_out.astype(jnp.bfloat16)
    grad_b_down = jnp.sum(grad_branch.astype(jnp.float32), axis=0)
    grad_w_down = weight_grad(active, grad_branch)
    grad_active = project_back(grad_branch, params[8])
    grad_pre = jax.vjp(gelu_fn, pre_active)[1](grad_active)[0].astype(jnp.bfloat16)
    grad_b_up = jnp.sum(grad_pre.astype(jnp.float32), axis=0)
    grad_w_up = weight_grad(middle_norm, grad_pre)
    middle_back = jax.vjp(normalize, middle, params[5])[1]
    grad_middle, grad_norm_two = middle_back(project_back(grad_pre, params[6]))
    grad_middle = grad_middle + grad_out
    grad_attn = grad_middle.astype(jnp.bfloat16)
    grad_w_output = weight_grad(mixed_rows, grad_attn)
    grad_mixed = project_back(grad_attn, params[4]).astype(jnp.bfloat16)
    grad_query, grad_key, grad_value = attention_back(grad_mixed)
    grad_normed = (
        project_back(grad_query, params[1])
        + project_back(grad_key, params[2])
        + project_back(grad_value, params[3])
    )
    input_back = jax.vjp(normalize, inputs, params[0])[1]
    grad_inputs, grad_norm_one = input_back(grad_normed)
    weight_grads = (
        grad_norm_one,
        weight_grad(normed, grad_query),
        weight_grad(normed, grad_key),
        weight_grad(normed, grad_value),
        grad_w_output,
        grad_norm_two,
        grad_w_up,
        grad_b_up,
        grad_w_down,
        grad_b_down,
    )
    return (grad_inputs + grad_middle, weight_grads)


def on_device(
    frames,
    codes,
    lengths,
    frame_mask,
    table,
    glob_norm_one,
    glob_w_query,
    glob_w_key,
    glob_w_value,
    glob_w_output,
    glob_norm_two,
    glob_w_up,
    glob_b_up,
    glob_w_down,
    glob_b_down,
    local_norm_one,
    local_w_query,
    local_w_key,
    local_w_value,
    local_w_output,
    local_norm_two,
    local_w_up,
    local_b_up,
    local_w_down,
    local_b_down,
    cotan_global,
    cotan_local,
):
    utter_count, frame_count, model_width = frames.shape
    row_count = utter_count * frame_count
    local_len = CB + 1
    positions = lax.axis_index("seq") * frame_count + jnp.arange(frame_count, dtype=jnp.int32)
    valid = positions[None, :] < lengths[:, None]
    usable = jnp.pad(frame_mask.astype(LOW), ((0, 0), (0, LANES - frame_count)))
    usable = jnp.broadcast_to(usable[:, None, :], (utter_count, 16, LANES))
    glob_params = (
        glob_norm_one,
        glob_w_query,
        glob_w_key,
        glob_w_value,
        glob_w_output,
        glob_norm_two,
        glob_w_up,
        glob_b_up,
        glob_w_down,
        glob_b_down,
    )
    local_params = (
        local_norm_one,
        local_w_query,
        local_w_key,
        local_w_value,
        local_w_output,
        local_norm_two,
        local_w_up,
        local_b_up,
        local_w_down,
        local_b_down,
    )
    code_rows = codes.transpose(2, 0, 1).reshape(CB, row_count)
    (
        glob_normed, glob_mixed, saved, log_total, local_in,
        glob_middle, glob_middle_norm, pre_active, active,
    ) = global_forward(
        frames,
        usable,
        jnp.broadcast_to(code_rows[:, :, None], (CB, row_count, LANES)),
        valid.reshape(row_count, 1).astype(F32),
        table,
        glob_params,
    )
    global_rows = local_in[0]
    local_shape = (local_len, row_count, model_width)
    flat_shape = (local_len * row_count, model_width)
    normed, local_q, local_k, local_v, local_probs, mixed, middle, middle_norm = local_front(
        local_in, local_params
    )
    row_valid = valid.reshape(1, row_count, 1)
    local_cotan = cotan_local.transpose(2, 0, 1, 3).reshape(local_shape)
    local_cotan = jnp.where(row_valid, local_cotan, 0)
    local_result, grad_hidden, grad_w_up, grad_w_down, grad_b_up, grad_b_down = local_ffn(
        middle_norm.reshape(flat_shape),
        local_cotan.reshape(flat_shape),
        middle.reshape(flat_shape),
        local_params,
    )
    local_rows = jnp.where(row_valid, local_result.reshape(local_shape), 0)
    local_rows = local_rows.reshape(local_len, utter_count, frame_count, model_width)
    local_rows = local_rows.transpose(1, 2, 0, 3)
    normed = normed.reshape(flat_shape)
    mixed = mixed.reshape(flat_shape)
    outputs = (global_rows.reshape(utter_count, frame_count, model_width), local_rows)

    if lax.axis_size("seq") == 16 and lax.axis_size("utt") == 2:
        far = dict(
            l_up=grad_w_up.reshape(8, 2, -1, grad_w_up.shape[1]),
            l_down=grad_w_down.reshape(8, 2, -1, grad_w_down.shape[1]),
            g_w_up=glob_w_up,
            g_w_down=glob_w_down,
            g_w_o=glob_w_output,
            g_w_q=glob_w_query,
            g_w_k=glob_w_key,
            g_w_v=glob_w_value,
            saved=saved,
            l_normed=normed,
            l_mixed=mixed,
            l_in=local_in,
            l_mid=middle,
            l_dhn=grad_hidden.reshape(local_shape),
            l_dout=local_cotan,
            l_q=local_q,
            l_k=local_k,
            l_v=local_v,
            l_probs=local_probs,
            l_w_o=local_w_output,
            l_w_q=local_w_query,
            l_w_k=local_w_key,
            l_w_v=local_w_value,
            g_act=active,
            g_mixed=glob_mixed,
            g_normed=glob_normed,
        )
        near = dict(
            u=pre_active,
            cotan=cotan_global.reshape(row_count, model_width),
            valid=valid.reshape(row_count, 1).astype(F32),
            mid=glob_middle,
            hn=glob_middle_norm,
            x=frames.reshape(row_count, model_width),
            n1=glob_norm_one.reshape(1, -1),
            n2=glob_norm_two.reshape(1, -1),
            log_total=log_total,
            codes=jnp.broadcast_to(code_rows[:, None, :], (CB, 8, row_count)),
            l_n1=local_norm_one.reshape(1, -1),
            l_n2=local_norm_two.reshape(1, -1),
            l_db1=grad_b_up,
            l_db2=grad_b_down,
        )
        grad_inputs, *sums = settle(finish_on_slice(far, near))
        wide = dict(zip("12qkvot76pabc", sums[:-1]))
        half = lax.axis_index("seq") % 2
        rest = sums[-1]

        def piece(row):
            return jnp.where(half == 0, rest[row, ACOLS : ACOLS + LANES // 2], rest[row, ACOLS + LANES // 2 :])

        def piece_wide(row):
            return rest[row : row + 2, ACOLS:].reshape(-1)

        return outputs + (
            grad_inputs.reshape(utter_count, frame_count, model_width),
            wide["t"],
            piece(0),
            wide["a"],
            wide["b"],
            wide["c"],
            wide["p"],
            piece(1),
            wide["6"],
            piece_wide(3),
            wide["7"],
            piece(2),
            piece(5),
            wide["q"],
            wide["k"],
            wide["v"],
            wide["o"],
            piece(6),
            wide["1"],
            piece_wide(8),
            wide["2"],
            piece(7),
        )

    grad_attn, grad_q, grad_k, grad_v, grad_first, grad_rest, grad_n1, grad_n2 = local_back(
        local_in,
        middle,
        grad_hidden.reshape(local_shape),
        local_cotan,
        local_q,
        local_k,
        local_v,
        local_probs,
        local_params,
    )
    grad_first = grad_first.reshape(utter_count, frame_count, model_width)
    glob_cotan = jnp.where(
        valid[:, :, None], cotan_global.astype(jnp.float32) + grad_first, 0.0
    )
    glob_cotan = glob_cotan.reshape(row_count, model_width)
    local_grads = (
        grad_n1[0],
        weight_grad(normed, grad_q.reshape(flat_shape)),
        weight_grad(normed, grad_k.reshape(flat_shape)),
        weight_grad(normed, grad_v.reshape(flat_shape)),
        weight_grad(mixed, grad_attn.reshape(flat_shape)),
        grad_n2[0],
        grad_w_up,
        grad_b_up[0],
        grad_w_down,
        grad_b_down[0],
    )
    picked = code_rows[:, None, :] == jnp.arange(VOCAB, dtype=jnp.int32)[None, :, None]
    grad_tab = jnp.einsum(
        "cvn,cnd->cvd", picked.astype(LOW), grad_rest, preferred_element_type=F32
    ).reshape(CB * VOCAB, model_width)

    def global_back(grad_mixed):
        grads = global_attend_back(
            grad_mixed.reshape(utter_count, frame_count, model_width), saved, log_total
        )
        return tuple(grads.reshape(3, row_count, model_width))

    global_in = frames.astype(F32).reshape(row_count, model_width)
    glob_kept = (glob_middle, glob_middle_norm, pre_active, active)
    grad_inputs, glob_grads = block_back(
        global_in, glob_normed, glob_mixed, glob_kept, glob_params, glob_cotan, global_back
    )
    reduced = reduce_all((grad_tab,) + glob_grads + local_grads)
    return outputs + (grad_inputs.reshape(utter_count, frame_count, model_width),) + reduced


def solution(mesh):
    return jax.shard_map(
        on_device,
        mesh=mesh,
        in_specs=(
            P("utt", "seq", None),
            P("utt", "seq", None),
            P("utt"),
            P("utt", "seq"),
            P(),
            P(),
            P(),
            P(),
            P(),
            P(),
            P(),
            P(),
            P(),
            P(),
            P(),
            P(),
            P(),
            P(),
            P(),
            P(),
            P(),
            P(),
            P(),
            P(),
            P(),
            P("utt", "seq", None),
            P("utt", "seq", None, None),
        ),
        out_specs=(
            P("utt", "seq", None),
            P("utt", "seq", None, None),
            P("utt", "seq", None),
            P("seq", None),
            P("seq"),
            P("seq", None),
            P("seq", None),
            P("seq", None),
            P("seq", None),
            P("seq"),
            P("seq", None),
            P("seq"),
            P("seq", None),
            P("seq"),
            P("seq"),
            P("seq", None),
            P("seq", None),
            P("seq", None),
            P("seq", None),
            P("seq"),
            P("seq", None),
            P("seq"),
            P("seq", None),
            P("seq"),
        ),
        check_vma=False,
    )
```

```python
import functools
import types

import jax
import jax.numpy as jnp
from jax import lax
from jax.experimental import pallas as pl
from jax.experimental.pallas import tpu as pltpu
from jax.sharding import PartitionSpec as P

H = 16
HD = 64
CB = 3
VOCAB = 1024


EPSILON = 1e-05
NEGATIVE = -1e30
F32 = jnp.float32
LOW = jnp.bfloat16
LANES = 128
MESH_ID = pl.DeviceIdType.MESH


def reduce_all(grads):
    return tuple(
        lax.psum(
            lax.psum_scatter(item.astype(LOW), "seq", scatter_dimension=0, tiled=True), "utt"
        ).astype(F32)
        for item in grads
    )


def mul(left_side, right_side):
    return jnp.dot(left_side, right_side, preferred_element_type=F32)


def mul_t(left_side, right_side):
    return lax.dot_general(
        left_side, right_side, (((1,), (1,)), ((), ())), preferred_element_type=F32
    )


def t_mul(left_side, right_side):
    return lax.dot_general(
        left_side, right_side, (((0,), (0,)), ((), ())), preferred_element_type=F32
    )


def scale_of(values):
    return lax.rsqrt(jnp.mean(values * values, axis=-1, keepdims=True) + EPSILON)


def scale_back(values, gain, grad):
    scale = scale_of(values)
    inner = grad * gain
    shared = jnp.mean(values * inner, axis=-1, keepdims=True) * (scale * scale * scale)
    return inner * scale - values * shared, grad * values * scale


def head_sums(width):
    rows = lax.broadcasted_iota(jnp.int32, (width, 128), 0) // HD
    cols = lax.broadcasted_iota(jnp.int32, (width, 128), 1)
    return (rows == cols).astype(LOW)


def head_spread(width):
    rows = lax.broadcasted_iota(jnp.int32, (128, width), 0)
    cols = lax.broadcasted_iota(jnp.int32, (128, width), 1) // HD
    return (rows == cols).astype(LOW)


def sum_heads(product, sums):
    high = product.astype(LOW)
    rest = (product - high.astype(F32)).astype(LOW)
    return mul(high, sums) + mul(rest, sums)


def front_kernel(
    x_ref, n1_ref, wq_ref, wk_ref, wv_ref, wo_ref, n2_ref,
    normed_ref, q_ref, k_ref, v_ref, probs_ref, mixed_ref, mid_ref, mid_norm_ref,
):
    places, frames, width = x_ref.shape
    rows = places * frames
    x = x_ref[...].astype(F32).reshape(rows, width)
    normed = (x * scale_of(x) * n1_ref[...]).astype(LOW)
    normed_ref[...] = normed.reshape(places, frames, width)
    q_ref[...] = mul(normed, wq_ref[...]).astype(LOW).reshape(places, frames, width)
    k_ref[...] = mul(normed, wk_ref[...]).astype(LOW).reshape(places, frames, width)
    v_ref[...] = mul(normed, wv_ref[...]).astype(LOW).reshape(places, frames, width)
    sums, spread = head_sums(width), head_spread(width)
    pair = 0
    for i in range(places):
        query = q_ref[i].astype(F32)
        scores = [
            sum_heads(query * k_ref[j].astype(F32), sums) * HD ** (-0.5) for j in range(i + 1)
        ]
        peak = scores[0]
        for item in scores[1:]:
            peak = jnp.maximum(peak, item)
        raised = [jnp.exp(item - peak) for item in scores]
        total = raised[0]
        for item in raised[1:]:
            total = total + item
        mixed = None
        for j in range(i + 1):
            probs = raised[j] / total
            probs_ref[pair] = probs
            pair += 1
            term = mul(probs.astype(LOW), spread) * v_ref[j].astype(F32)
            mixed = term if mixed is None else mixed + term
        mixed_ref[i] = mixed.astype(LOW)
    mid = x + mul(mixed_ref[...].reshape(rows, width), wo_ref[...])
    mid_ref[...] = mid.reshape(places, frames, width)
    mid_norm_ref[...] = (
        (mid * scale_of(mid) * n2_ref[...]).astype(LOW).reshape(places, frames, width)
    )


def local_front(x, params):
    places, frames, width = x.shape
    pairs = places * (places + 1) // 2
    step = frames
    rows = pl.BlockSpec((places, step, width), lambda i: (0, i, 0))
    whole = lambda item: pl.BlockSpec(item.shape, lambda i: (0, 0), pipeline_mode=pl.Buffered(1))
    n1, n2 = params[0].reshape(1, -1), params[5].reshape(1, -1)
    operands = (x, n1, params[1], params[2], params[3], params[4], n2)
    like = lambda kind: jax.ShapeDtypeStruct((places, frames, width), kind)
    return pl.pallas_call(
        front_kernel,
        grid=(frames // step,),
        in_specs=[rows] + [whole(item) for item in operands[1:]],
        out_specs=[rows] * 4
        + [pl.BlockSpec((pairs, step, 128), lambda i: (0, i, 0))]
        + [rows] * 3,
        out_shape=[
            like(LOW), like(LOW), like(LOW), like(LOW),
            jax.ShapeDtypeStruct((pairs, frames, 128), F32),
            like(LOW), like(F32), like(LOW),
        ],
        compiler_params=pltpu.CompilerParams(vmem_limit_bytes=56 << 20),
    )(*operands)


def gelu_parts(u):
    scale = 0.7978845608028654
    inner = jnp.tanh(scale * (u + 0.044715 * u * u * u))
    half = 0.5 * (1.0 + inner)
    slope = half + 0.5 * u * (1.0 - inner * inner) * scale * (1.0 + 3 * 0.044715 * u * u)
    return u * half, slope


def ffn_kernel(
    hn_ref, dout_ref, mid_ref, w1_ref, b1_ref, w2_ref, b2_ref,
    y_ref, dhn_ref, dw1_ref, dw2_ref, db1_ref, db2_ref, acc_ref, hn_t_ref,
):
    at = pl.program_id(0)
    last = pl.num_programs(0) - 1

    @pl.when(at == 0)
    def _():
        hn_t_ref[...] = hn_ref[...].T
        acc_ref[...] = mid_ref[...] + b2_ref[...]
        dhn_ref[...] = jnp.zeros_like(dhn_ref)
        db2_ref[...] = jnp.sum(dout_ref[...].astype(F32), axis=0, keepdims=True)

    hn, dout = hn_ref[...], dout_ref[...]
    u = mul(hn, w1_ref[...]) + b1_ref[...]
    act, slope = gelu_parts(u)
    act = act.astype(LOW)
    acc_ref[...] += mul(act, w2_ref[...])
    du = (mul_t(dout, w2_ref[...]) * slope).astype(LOW)
    db1_ref[...] = jnp.sum(du.astype(F32), axis=0, keepdims=True)
    dhn_ref[...] += mul_t(du, w1_ref[...])
    dw1_ref[...] = mul(hn_t_ref[...], du).astype(LOW)
    dw2_ref[...] = t_mul(act, dout).astype(LOW)

    @pl.when(at == last)
    def _():
        y_ref[...] = acc_ref[...].astype(LOW)


def local_ffn(hn, dout, mid, params):
    rows, width = hn.shape
    wide = params[6].shape[1]
    step = 512
    whole = pl.BlockSpec((rows, width), lambda i: (0, 0), pipeline_mode=pl.Buffered(1))
    out_whole = pl.BlockSpec((rows, width), lambda i: (0, 0))
    return pl.pallas_call(
        ffn_kernel,
        grid=(wide // step,),
        in_specs=[
            whole, whole, whole,
            pl.BlockSpec((width, step), lambda i: (0, i)),
            pl.BlockSpec((1, step), lambda i: (0, i)),
            pl.BlockSpec((step, width), lambda i: (i, 0)),
            pl.BlockSpec((1, width), lambda i: (0, 0)),
        ],
        out_specs=[
            out_whole, out_whole,
            pl.BlockSpec((width, step), lambda i: (0, i)),
            pl.BlockSpec((step, width), lambda i: (i, 0)),
            pl.BlockSpec((1, step), lambda i: (0, i)),
            pl.BlockSpec((1, width), lambda i: (0, 0)),
        ],
        out_shape=[
            jax.ShapeDtypeStruct((rows, width), LOW),
            jax.ShapeDtypeStruct((rows, width), F32),
            jax.ShapeDtypeStruct((width, wide), LOW),
            jax.ShapeDtypeStruct((wide, width), LOW),
            jax.ShapeDtypeStruct((1, wide), F32),
            jax.ShapeDtypeStruct((1, width), F32),
        ],
        scratch_shapes=[pltpu.VMEM((rows, width), F32), pltpu.VMEM((width, rows), LOW)],
        compiler_params=pltpu.CompilerParams(vmem_limit_bytes=56 << 20),
    )(hn, dout, mid, params[6], params[7].reshape(1, -1), params[8], params[9].reshape(1, -1))


def back_kernel(
    x_ref, mid_ref, dhn_ref, dout_ref, q_ref, k_ref, v_ref, probs_ref,
    n1_ref, n2_ref, wq_ref, wk_ref, wv_ref, wo_ref,
    dattn_ref, dq_ref, dk_ref, dv_ref, first_ref, rest_ref, dn1_ref, dn2_ref,
    dmid_ref,
):
    places, frames, width = x_ref.shape
    rows = places * frames

    @pl.when(pl.program_id(0) == 0)
    def _():
        dn1_ref[...] = jnp.zeros_like(dn1_ref)
        dn2_ref[...] = jnp.zeros_like(dn2_ref)

    mid = mid_ref[...].reshape(rows, width)
    dmid, gain = scale_back(mid, n2_ref[...], dhn_ref[...].reshape(rows, width))
    dn2_ref[...] += jnp.sum(gain, axis=0, keepdims=True)
    dmid = dmid + dout_ref[...].astype(F32).reshape(rows, width)
    dmid_ref[...] = dmid
    dattn = dmid.astype(LOW)
    dattn_ref[...] = dattn.reshape(places, frames, width)
    dmixed = mul_t(dattn, wo_ref[...]).astype(LOW).reshape(places, frames, width)
    sums, spread = head_sums(width), head_spread(width)
    pair = 0
    dk, dv = [None] * places, [None] * places
    add = lambda old, term: term if old is None else old + term
    for i in range(places):
        grad = dmixed[i].astype(F32)
        query = q_ref[i].astype(F32)
        dp = [sum_heads(grad * v_ref[j].astype(F32), sums) for j in range(i + 1)]
        delta = None
        for j in range(i + 1):
            delta = add(delta, probs_ref[pair + j] * dp[j])
        dq = None
        for j in range(i + 1):
            probs = probs_ref[pair + j]
            ds = (probs * (dp[j] - delta)).astype(LOW)
            ds = mul(ds, spread)
            dq = add(dq, ds * k_ref[j].astype(F32))
            dk[j] = add(dk[j], ds * query)
            dv[j] = add(dv[j], mul(probs.astype(LOW), spread) * grad)
        pair += i + 1
        dq_ref[i] = (dq * HD ** (-0.5)).astype(LOW)
    for j in range(places):
        dk_ref[j] = (dk[j] * HD ** (-0.5)).astype(LOW)
        dv_ref[j] = dv[j].astype(LOW)
    dnormed = (
        mul_t(dq_ref[...].reshape(rows, width), wq_ref[...])
        + mul_t(dk_ref[...].reshape(rows, width), wk_ref[...])
        + mul_t(dv_ref[...].reshape(rows, width), wv_ref[...])
    )
    x = x_ref[...].astype(F32).reshape(rows, width)
    dx, gain = scale_back(x, n1_ref[...], dnormed)
    dn1_ref[...] += jnp.sum(gain, axis=0, keepdims=True)
    dx = (dx + dmid_ref[...]).reshape(places, frames, width)
    first_ref[...] = dx[0]
    rest_ref[...] = dx[1:].astype(LOW)


def local_back(x, mid, dhn, dout, q, k, v, probs, params):
    places, frames, width = x.shape
    pairs = probs.shape[0]
    step = 64
    rows = pl.BlockSpec((places, step, width), lambda i: (0, i, 0))
    whole = lambda item: pl.BlockSpec(item.shape, lambda i: (0, 0), pipeline_mode=pl.Buffered(1))
    like = lambda kind: jax.ShapeDtypeStruct((places, frames, width), kind)
    fixed = (params[0].reshape(1, -1), params[5].reshape(1, -1)) + tuple(params[1:5])
    vector = pl.BlockSpec((1, width), lambda i: (0, 0))
    return pl.pallas_call(
        back_kernel,
        grid=(frames // step,),
        in_specs=[rows] * 7
        + [pl.BlockSpec((pairs, step, 128), lambda i: (0, i, 0))]
        + [whole(item) for item in fixed],
        out_specs=[rows] * 4
        + [
            pl.BlockSpec((step, width), lambda i: (i, 0)),
            pl.BlockSpec((places - 1, step, width), lambda i: (0, i, 0)),
            vector, vector,
        ],
        out_shape=[
            like(LOW), like(LOW), like(LOW), like(LOW),
            jax.ShapeDtypeStruct((frames, width), F32),
            jax.ShapeDtypeStruct((places - 1, frames, width), LOW),
            jax.ShapeDtypeStruct((1, width), F32),
            jax.ShapeDtypeStruct((1, width), F32),
        ],
        scratch_shapes=[pltpu.VMEM((places * step, width), F32)],
        compiler_params=pltpu.CompilerParams(vmem_limit_bytes=60 << 20),
    )(x, mid, dhn, dout, q, k, v, probs, *fixed)


def greet(count):
    utt, me = lax.axis_index("utt"), lax.axis_index("seq")
    barrier = pltpu.get_barrier_semaphore()

    @pl.loop(1, count)
    def _(step):
        pl.semaphore_signal(
            barrier, inc=1, device_id=(utt, lax.rem(me + step, count)), device_id_type=MESH_ID
        )

    return barrier


def remote(source, target, send_sem, recv_sem, place):
    return pltpu.make_async_remote_copy(
        src_ref=source,
        dst_ref=target,
        send_sem=send_sem,
        recv_sem=recv_sem,
        device_id=(lax.axis_index("utt"), place),
        device_id_type=MESH_ID,
    )


def two_heads(rows):
    lane = lax.broadcasted_iota(jnp.int32, rows.shape, 1)
    zero = jnp.zeros_like(rows)
    return jnp.concatenate([jnp.where(lane < HD, rows, zero), jnp.where(lane < HD, zero, rows)], axis=0)


def join_heads(tall):
    rows = tall.T
    lane = lax.broadcasted_iota(jnp.int32, (HD, LANES), 1)
    return jnp.where(lane < HD, rows[:HD], rows[HD:])


def masked_scores(scores, bias, first, block):
    key = first + lax.broadcasted_iota(jnp.int32, scores.shape, 0)
    query = block * HD + lax.rem(lax.broadcasted_iota(jnp.int32, scores.shape, 1), HD)
    return jnp.where(key < query, scores + bias, jnp.where(key == query, scores, NEGATIVE))


def fill_bias(bias_ref, mask):
    for block in range(mask.shape[0]):
        row = lax.broadcasted_iota(jnp.int32, (HD, LANES), 0)
        lane = lax.broadcasted_iota(jnp.int32, (HD, LANES), 1)
        flags = jnp.broadcast_to(mask[block, 0:1, :], (HD, LANES))
        diagonal = jnp.where(row == lane, flags.astype(F32), 0.0).astype(LOW)
        usable = mul(diagonal, jnp.ones((LANES, LANES), LOW))
        bias_ref[block * HD : (block + 1) * HD, :] = (usable - 1.0) * 1e30


def attend_kernel(
    count, x_ref, mask_ref, n1_ref, wq_ref, wk_ref, wv_ref, codes_ref, valid_ref, n2_ref, b1_ref,
    b2_ref, table_ref, wo_ref, w1_ref, w2_ref,
    normed_ref, mixed_ref, saved_ref, log_ref, local_ref, mid_ref, hn_ref, u_ref, act_ref, out_ref,
    packed, held, mixed_all, pieces, bias, v_t, table, wo, w1, w2,
    send_sem, recv_sem, send_two, recv_two, save_sem, fetch_sem,
):
    share = count // 16
    me = lax.axis_index("seq")
    unit, part = me // share, me % share
    own_utt, own_pair = unit // 8, unit % 8
    own_cols = pl.ds(pl.multiple_of(own_pair * LANES, LANES), LANES)
    utts, frames, width = x_ref.shape
    rows = utts * frames
    barrier = greet(count)
    fetches = [
        pltpu.make_async_copy(source, target, fetch_sem.at[index])
        for index, (source, target) in enumerate(
            ((table_ref, table), (wo_ref, wo), (w1_ref, w1), (w2_ref, w2))
        )
    ]
    for copy in fetches:
        copy.start()

    x = x_ref[...].astype(F32).reshape(rows, width)
    normed = (x * scale_of(x) * n1_ref[...]).astype(LOW)
    normed_ref[...] = normed
    packed[:, 0:64] = (mul(normed, wq_ref[...]).astype(LOW)).reshape(utts, frames, width)
    packed[:, 64:128] = mul(normed, wk_ref[...]).astype(LOW).reshape(utts, frames, width)
    packed[:, 128:192] = mul(normed, wv_ref[...]).astype(LOW).reshape(utts, frames, width)
    for pair in range(8):
        packed[:, 192:208, pair * LANES : (pair + 1) * LANES] = jnp.broadcast_to(
            mask_ref[...], (utts, 16, LANES)
        )
    pl.semaphore_wait(barrier, count - 1)

    def outgoing(step):
        place = lax.rem(me + step, count)
        target = place // share
        cols = pl.ds(pl.multiple_of((target % 8) * LANES, LANES), LANES)
        return remote(
            packed.at[target // 8, :, cols], held.at[me], send_sem.at[step], recv_sem.at[step], place
        )

    @pl.loop(1, count)
    def _(step):
        outgoing(step).start()

    held[me] = packed[own_utt, :, own_cols]

    fetches[0].wait()
    vocab = table.shape[0] // CB
    for book in range(CB):
        ids = jnp.broadcast_to(codes_ref[:, book : book + 1], (rows, vocab))
        picked = (ids == lax.broadcasted_iota(jnp.int32, (rows, vocab), 1)).astype(LOW)
        local_ref[1 + book] = mul(picked, table[book * vocab : (book + 1) * vocab]).astype(LOW)

    save = pltpu.make_async_copy(held, saved_ref, save_sem)

    def returning(block):
        return remote(
            pieces.at[block],
            mixed_all.at[own_utt, :, own_cols],
            send_two.at[block],
            recv_two.at[unit],
            block,
        )

    for group in range(count // 4):
        below = group * 256
        here = below + 256
        for place in range(4 * group, 4 * group + 4):

            @pl.when(place != me)
            def _():
                step = lax.rem(me + count - place, count)
                remote(
                    held.at[place], held.at[place], send_sem.at[step], recv_sem.at[step], place
                ).wait_recv()

        v_t[:, below:here] = held[4 * group : 4 * group + 4, 128:192].reshape(256, LANES).T
        fill_bias(bias.at[below:here], held[4 * group : 4 * group + 4, 192:208])

        @pl.loop(0, 4 // share)
        def _(index):
            block = 4 * group + share * index + part
            query = two_heads(held[block, 0:64] * LOW(HD ** (-0.5)))
            keys = held[4 * group : 4 * group + 4, 64:128].reshape(256, LANES)
            near = masked_scores(mul_t(keys, query), bias[below:here], below, block)
            peak = jnp.max(near, axis=0, keepdims=True)
            if group:
                keys = held[0 : 4 * group, 64:128].reshape(below, LANES)
                far = mul_t(keys, query) + bias[0:below]
                peak = jnp.maximum(peak, jnp.max(far, axis=0, keepdims=True))
                far = jnp.exp(far - peak)
            near = jnp.exp(near - peak)
            total = jnp.sum(near, axis=0, keepdims=True)
            if group:
                total = total + jnp.sum(far, axis=0, keepdims=True)
            inverse = 1.0 / total
            mixed = mul(v_t[:, below:here], (near * inverse).astype(LOW))
            if group:
                mixed = mixed + mul(v_t[:, 0:below], (far * inverse).astype(LOW))
            log_ref[block] = jnp.broadcast_to(peak + jnp.log(total), (8, LANES))
            pieces[block] = join_heads(mixed).astype(LOW)

            @pl.when(block != me)
            def _():
                returning(block).start()

            @pl.when(block == me)
            def _():
                mixed_all[own_utt, :, own_cols] = pieces[block]

    save.start()

    @pl.loop(0, 16)
    def _(other):
        place = other * share + me % share
        cols = pl.ds(pl.multiple_of((other % 8) * LANES, LANES), LANES)

        @pl.when(place != me)
        def _():
            here = mixed_all.at[other // 8, :, cols]
            remote(here, here, send_two.at[0], recv_two.at[other], place).wait_recv()

    mixed = mixed_all[...].reshape(rows, width)
    mixed_ref[...] = mixed
    fetches[1].wait()
    mid = x_ref[...].astype(F32).reshape(rows, width) + mul(mixed, wo[...])
    hn = (mid * scale_of(mid) * n2_ref[...]).astype(LOW)
    mid_ref[...] = mid
    hn_ref[...] = hn
    fetches[2].wait()
    fetches[3].wait()
    result = mid + b2_ref[...]
    for first in range(0, u_ref.shape[1], 512):
        cols = slice(first, first + 512)
        u = mul(hn, w1[:, cols]) + b1_ref[:, cols]
        act = gelu_parts(u)[0].astype(LOW)
        u_ref[:, cols] = u
        act_ref[:, cols] = act
        result = result + mul(act, w2[cols])
    result = jnp.where(valid_ref[...] > 0, result, 0.0).astype(LOW)
    local_ref[0] = result
    out_ref[...] = result

    @pl.loop(1, count)
    def _(step):
        outgoing(step).wait_send()

    @pl.loop(0, count // share)
    def _(index):
        block = share * index + part

        @pl.when(block != me)
        def _():
            returning(block).wait_send()

    save.wait()


def global_forward(x, mask, codes, valid, table, params):
    count = lax.axis_size("seq")
    utts, frames, width = x.shape
    rows, wide = utts * frames, params[6].shape[1]
    vmem = pl.BlockSpec(memory_space=pltpu.VMEM)
    hbm = pl.BlockSpec(memory_space=pl.ANY)
    return pl.pallas_call(
        functools.partial(attend_kernel, count),
        in_specs=[vmem] * 11 + [hbm] * 4,
        out_specs=[vmem, vmem, hbm] + [vmem] * 7,
        out_shape=[
            jax.ShapeDtypeStruct((rows, width), LOW),
            jax.ShapeDtypeStruct((rows, width), LOW),
            jax.ShapeDtypeStruct((count, 208, LANES), LOW),
            jax.ShapeDtypeStruct((count, 8, LANES), F32),
            jax.ShapeDtypeStruct((1 + CB, rows, width), LOW),
            jax.ShapeDtypeStruct((rows, width), F32),
            jax.ShapeDtypeStruct((rows, width), LOW),
            jax.ShapeDtypeStruct((rows, wide), F32),
            jax.ShapeDtypeStruct((rows, wide), LOW),
            jax.ShapeDtypeStruct((rows, width), LOW),
        ],
        scratch_shapes=[
            pltpu.VMEM((utts, 208, width), LOW),
            pltpu.VMEM((count, 208, LANES), LOW),
            pltpu.VMEM((utts, frames, width), LOW),
            pltpu.VMEM((count, HD, LANES), LOW),
            pltpu.VMEM((count * HD, LANES), F32),
            pltpu.VMEM((LANES, count * HD), LOW),
            pltpu.VMEM(table.shape, LOW),
            pltpu.VMEM(params[4].shape, LOW),
            pltpu.VMEM(params[6].shape, LOW),
            pltpu.VMEM(params[8].shape, LOW),
            pltpu.SemaphoreType.DMA((count,)),
            pltpu.SemaphoreType.DMA((count,)),
            pltpu.SemaphoreType.DMA((count,)),
            pltpu.SemaphoreType.DMA((16,)),
            pltpu.SemaphoreType.DMA,
            pltpu.SemaphoreType.DMA((4,)),
        ],
        compiler_params=pltpu.CompilerParams(
            collective_id=2, has_side_effects=True, vmem_limit_bytes=58 << 20
        ),
    )(
        x, mask, params[0].reshape(1, -1), params[1], params[2], params[3], codes, valid,
        params[5].reshape(1, -1), params[7].reshape(1, -1), params[9].reshape(1, -1), table,
        params[4], params[6], params[8],
    )


def settle_kernel(number, *refs):
    sources, targets, held = (refs[index * number : (index + 1) * number] for index in range(3))
    into = [
        pltpu.make_async_copy(sources[index], held[index], refs[-1].at[0, index])
        for index in range(number)
    ]
    out = [
        pltpu.make_async_copy(held[index], targets[index], refs[-1].at[1, index])
        for index in range(number)
    ]
    for copy in into:
        copy.start()
    for first, second in zip(into, out):
        first.wait()
        second.start()
    for copy in out:
        copy.wait()


def settle(arrays):
    hbm = pl.BlockSpec(memory_space=pl.ANY)
    return pl.pallas_call(
        functools.partial(settle_kernel, len(arrays)),
        in_specs=[hbm] * len(arrays),
        out_specs=[hbm] * len(arrays),
        out_shape=[jax.ShapeDtypeStruct(item.shape, item.dtype) for item in arrays],
        scratch_shapes=[pltpu.VMEM(item.shape, item.dtype) for item in arrays]
        + [pltpu.SemaphoreType.DMA((2, len(arrays)))],
        compiler_params=pltpu.CompilerParams(vmem_limit_bytes=62 << 20),
    )(*arrays)


def attend_back_kernel(
    count, grad_ref, held, log_ref,
    dqkv_ref,
    grads, landed, pieces, dk_acc, dv_acc, bias, k_t, send_sem, recv_sem, send_two, recv_two,
):
    share = count // 16
    me = lax.axis_index("seq")
    unit, part = me // share, me % share
    own_utt, own_pair = unit // 8, unit % 8
    own_cols = pl.ds(pl.multiple_of(own_pair * LANES, LANES), LANES)
    barrier = greet(count)
    k_t[...] = held[:, 64:128].reshape(count * HD, LANES).T
    fill_bias(bias, held[:, 192:208])
    dk_acc[...] = jnp.zeros_like(dk_acc)
    dv_acc[...] = jnp.zeros_like(dv_acc)
    pl.semaphore_wait(barrier, count - 1)

    def outgoing(other):
        cols = pl.ds(pl.multiple_of((other % 8) * LANES, LANES), LANES)
        place = other * share + part
        return place, remote(
            grad_ref.at[other // 8, :, cols], grads.at[me // share], send_sem.at[other],
            recv_sem.at[me // share], place,
        )

    @pl.loop(1, 16)
    def _(step):
        _, copy = outgoing(lax.rem(unit + step, 16))
        copy.start()

    grads[unit] = grad_ref[own_utt, :, own_cols]

    @pl.loop(1, 16)
    def _(step):
        other = lax.rem(unit + step, 16)
        here = grads.at[other]
        remote(here, here, send_sem.at[other], recv_sem.at[other], other * share + part).wait_recv()

    def returning(block):
        return remote(
            pieces.at[block],
            landed.at[part, :, own_utt, :, own_cols],
            send_two.at[block],
            recv_two.at[me],
            block,
        )

    for group in reversed(range(count // 4)):
        below = group * 256
        here = below + 256

        @pl.loop(0, 4 // share)
        def _(index):
            block = 4 * group + share * index + part
            query = two_heads(held[block, 0:64] * LOW(HD ** (-0.5)))
            grad = two_heads(grads[block // share])
            log_total = log_ref[block][0:1]
            near_v = held[4 * group : 4 * group + 4, 128:192].reshape(256, LANES)
            near_k = held[4 * group : 4 * group + 4, 64:128].reshape(256, LANES)
            near = masked_scores(mul_t(near_k, query), bias[below:here], below, block)
            near = jnp.exp(near - log_total)
            near_dp = mul_t(near_v, grad)
            delta = jnp.sum(near * near_dp, axis=0, keepdims=True)
            if group:
                far_v = held[0 : 4 * group, 128:192].reshape(below, LANES)
                far_k = held[0 : 4 * group, 64:128].reshape(below, LANES)
                far = jnp.exp(mul_t(far_k, query) + bias[0:below] - log_total)
                far_dp = mul_t(far_v, grad)
                delta = delta + jnp.sum(far * far_dp, axis=0, keepdims=True)
                far_ds = (far * (far_dp - delta)).astype(LOW)
                dk_acc[0:below] += mul(far_ds, query)
                dv_acc[0:below] += mul(far.astype(LOW), grad)
            near_ds = (near * (near_dp - delta)).astype(LOW)
            dk_acc[below:here] += mul(near_ds, query)
            dv_acc[below:here] += mul(near.astype(LOW), grad)
            dq = mul(k_t[:, below:here], near_ds)
            if group:
                dq = dq + mul(k_t[:, 0:below], far_ds)
            pieces[block, 0] = (join_heads(dq) * HD ** (-0.5)).astype(LOW)

        for block in range(4 * group, 4 * group + 4):
            rows = slice(block * HD, (block + 1) * HD)
            pieces[block, 1] = dk_acc[rows].astype(LOW)
            pieces[block, 2] = dv_acc[rows].astype(LOW)
            if share > 1:

                @pl.when(block % share != part)
                def _():
                    pieces[block, 0] = jnp.zeros((HD, LANES), LOW)

            @pl.when(block != me)
            def _():
                returning(block).start()

            @pl.when(block == me)
            def _():
                landed[part, :, own_utt, :, own_cols] = pieces[block]

    @pl.loop(1, count)
    def _(step):
        place = lax.rem(me + step, count)
        other, other_part = place // share, place % share
        cols = pl.ds(pl.multiple_of((other % 8) * LANES, LANES), LANES)
        here = landed.at[other_part, :, other // 8, :, cols]
        remote(here, here, send_two.at[place], recv_two.at[place], place).wait_recv()

    @pl.loop(1, 16)
    def _(step):
        _, copy = outgoing(lax.rem(unit + step, 16))
        copy.wait_send()

    @pl.loop(1, count)
    def _(step):
        returning(lax.rem(me + step, count)).wait_send()

    total = landed[0]
    for other_part in range(1, share):
        total = (total.astype(F32) + landed[other_part].astype(F32)).astype(LOW)
    dqkv_ref[...] = total


def global_attend_back(grad_mixed, saved, log_total):
    count = lax.axis_size("seq")
    utts, frames, width = grad_mixed.shape
    vmem = pl.BlockSpec(memory_space=pltpu.VMEM)
    return pl.pallas_call(
        functools.partial(attend_back_kernel, count),
        in_specs=[vmem] * 3,
        out_specs=vmem,
        out_shape=jax.ShapeDtypeStruct((3, utts, frames, width), LOW),
        scratch_shapes=[
            pltpu.VMEM((16, HD, LANES), LOW),
            pltpu.VMEM((count // 16, 3, utts, frames, width), LOW),
            pltpu.VMEM((count, 3, HD, LANES), LOW),
            pltpu.VMEM((count * HD, LANES), F32),
            pltpu.VMEM((count * HD, LANES), F32),
            pltpu.VMEM((count * HD, LANES), F32),
            pltpu.VMEM((LANES, count * HD), LOW),
            pltpu.SemaphoreType.DMA((16,)),
            pltpu.SemaphoreType.DMA((16,)),
            pltpu.SemaphoreType.DMA((count,)),
            pltpu.SemaphoreType.DMA((count,)),
        ],
        compiler_params=pltpu.CompilerParams(
            collective_id=3, has_side_effects=True, vmem_limit_bytes=48 << 20
        ),
    )(grad_mixed, saved, log_total)


SLOTS = 4
DEEP = 8
SROWS = 64
SCOLS = 512
ACOLS = 384
DRAIN = 8
PLAN = (
    (0, 8, 8), (8, 8, 2), (16, 2, 2), (18, 2, 2), (20, 2, 2), (22, 2, 2), (24, 6, 2),
    (30, 8, 2), (38, 8, 8), (46, 2, 2), (48, 2, 2), (50, 2, 2), (52, 2, 2), (54, 1, 1),
)
SLABS = 55
LOADED = 16
AT_LOCAL = 7
AT_HIDDEN = 16
AT_BACK = 20
AT_ATTEND = 27
AT_RETURN = 35
AT_LANDED = 45
PART = 32


def tail_kernel(names, out_count, *refs):
    r = types.SimpleNamespace(**dict(zip(names, refs)))
    outs = refs[names.index("out_0") : names.index("out_0") + out_count]
    utt = lax.axis_index("utt")
    seq = lax.axis_index("seq")
    count = 16
    pos = seq // 4
    col = (seq // 2) % 2
    core = seq % 2
    core_id = (utt, pos * 4 + col * 2 + 1 - core)
    col_id = (utt, pos * 4 + (1 - col) * 2 + core)
    utt_id = (1 - utt, seq)
    right_id = (utt, lax.rem(seq + 4, 16))
    left_id = (utt, lax.rem(seq + 12, 16))

    barrier = greet(count)
    pl.semaphore_signal(barrier, inc=1, device_id=utt_id, device_id_type=MESH_ID)

    def window(ref, spec, slab, lead):
        local = slab - spec[0]
        rows = pl.ds(pl.multiple_of((local // spec[2]) * SROWS, SROWS), SROWS)
        cols = pl.ds(pl.multiple_of((local % spec[2]) * SCOLS, SCOLS), SCOLS)
        return ref.at[lead + (rows, cols)]

    def load_start(slab):
        slot = slab % SLOTS

        @pl.when((slab >= PLAN[1][0]) & (slab < LOADED))
        def _():
            for side in range(2):
                pltpu.make_async_copy(
                    window(r.l_down, PLAN[1], slab, (slice(None), side)),
                    r.part.at[slot, side],
                    r.load_sem.at[slot, side],
                ).start()

    def load_wait(slot):
        for side in range(2):
            pltpu.make_async_copy(
                r.l_down.at[:, side, pl.ds(0, SROWS), pl.ds(0, SCOLS)],
                r.part.at[slot, side],
                r.load_sem.at[slot, side],
            ).wait()

    def weights(block, slot, up=r.g_w_up, down=r.g_w_down):
        start = block * SCOLS if isinstance(block, int) else pl.multiple_of(block * SCOLS, SCOLS)
        return (
            pltpu.make_async_copy(
                up.at[:, pl.ds(start, SCOLS)], r.up_buf.at[slot], r.weight_sem.at[slot, 0]
            ),
            pltpu.make_async_copy(
                down.at[pl.ds(start, SCOLS)], r.down_buf.at[slot], r.weight_sem.at[slot, 1]
            ),
        )

    fetches = (
        (r.g_w_o, r.square.at[0]), (r.g_w_q, r.square.at[1]), (r.g_w_k, r.square.at[2]),
        (r.g_w_v, r.square.at[3]), (r.saved, r.held), (r.l_normed, r.l_x.at[0]),
        (r.l_mixed, r.l_x.at[1]), (r.g_act, r.act_buf), (r.g_mixed, r.g_x.at[0]),
        (r.g_normed, r.g_x.at[1]), (r.l_w_o, r.square.at[0]), (r.l_w_q, r.square.at[1]),
        (r.l_w_k, r.square.at[2]), (r.l_w_v, r.square.at[3]), (r.l_hn, r.l_x.at[0]),
        (r.l_dout_flat, r.l_x.at[1]), (r.l_mid_flat, r.l_acc),
    )

    def fetch(*which):
        return [
            pltpu.make_async_copy(*fetches[index], r.fetch_sem.at[index]) for index in which
        ]

    def local_rows(step, slot):
        rows = pl.ds(step * PART if isinstance(step, int) else pl.multiple_of(step * PART, PART), PART)
        pairs = (
            (r.l_in, r.l_in_buf), (r.l_mid, r.l_mid_buf),
            (r.l_dout, r.l_dout_buf), (r.l_q, r.l_q_buf), (r.l_k, r.l_k_buf), (r.l_v, r.l_v_buf),
            (r.l_probs, r.l_probs_buf),
        )
        return [
            pltpu.make_async_copy(ref.at[:, rows], buffer.at[slot], r.local_sem.at[slot, index])
            for index, (ref, buffer) in enumerate(pairs)
        ]

    def local_weights(block, slot):
        return weights(block, slot, r.l_w_up, r.l_w_down)

    def kept(block, slot):
        return pltpu.make_async_copy(r.l_kept.at[slot], r.l_down.at[block], r.kept_sem.at[slot])

    result = pltpu.make_async_copy(r.l_x.at[0], r.y, r.result_sem.at[0])
    for copy in tuple(fetch(14, 15, 16)) + local_weights(0, 0):
        copy.start()

    def send(kind, slot, source, target, device):
        return pltpu.make_async_remote_copy(
            src_ref=source,
            dst_ref=target,
            send_sem=r.send_sem.at[kind, slot],
            recv_sem=r.recv_sem.at[kind, slot],
            device_id=device,
            device_id_type=MESH_ID,
        )

    def core_copy(slot):
        return send(0, slot, r.part.at[slot, 1 - core], r.recv_c.at[slot], core_id)

    def col_copy_a(slot):
        return send(1, slot, r.half_a.at[slot, 1 - col], r.recv_xa.at[slot], col_id)

    def utt_copy_b(slot):
        return send(2, slot, r.half_b.at[slot, 1 - utt], r.recv_yb.at[slot], utt_id)

    def col_copy_b(slot):
        return send(3, slot, r.sum_b.at[slot, 1 - col], r.recv_xb.at[slot], col_id)

    def utt_copy_a(slot, deep):
        return send(4, slot, r.sum_a.at[deep, pos], r.recv_ya.at[slot], utt_id)

    def utt_copy_b2(slot, deep):
        return send(5, slot, r.line_b.at[deep, pos], r.recv_yb2.at[slot], utt_id)

    def col_copy_c(slot, deep):
        return send(24, slot, r.line_c.at[deep, pos, 1 - col], r.recv_xc.at[slot], col_id)

    def utt_copy_c(slot):
        return send(25, slot, r.sum_c.at[slot], r.recv_yc.at[slot], utt_id)

    def line_right(kind, slot, deep, step, source, target):
        dest = jnp.minimum(4 - step + pos, 3)
        return send(kind + step - 1, slot, source.at[deep, dest], target.at[slot, step - 1], right_id)

    def line_left(kind, slot, deep, step, source, target):
        dest = jnp.maximum(pos - 4 + step, 0)
        return send(kind + step - 1, slot, source.at[deep, dest], target.at[slot, step - 1], left_id)

    def line_start(slot, deep, step, source, right, left, kind):
        @pl.when((pos <= step - 1) & (pos < 3))
        def _():
            line_right(kind, slot, deep, step, source, right).start()

        @pl.when((pos >= 4 - step) & (pos > 0))
        def _():
            line_left(kind + 3, slot, deep, step, source, left).start()

    def line_finish(slot, deep, step, source, right, left, kind):
        @pl.when((pos <= step - 1) & (pos < 3))
        def _():
            line_right(kind, slot, deep, step, source, right).wait_send()

        @pl.when((pos >= 4 - step) & (pos > 0))
        def _():
            line_left(kind + 3, slot, deep, step, source, left).wait_send()

        @pl.when((pos >= 1) & (pos <= step))
        def _():
            line_right(kind, slot, deep, step, source, right).wait_recv()
            dest = 3 - step + pos
            source[deep, dest] = (
                source[deep, dest].astype(F32) + right[slot, step - 1].astype(F32)
            ).astype(LOW)

        @pl.when((pos <= 2) & (pos >= 3 - step))
        def _():
            line_left(kind + 3, slot, deep, step, source, left).wait_recv()
            dest = pos + step - 3
            source[deep, dest] = (
                source[deep, dest].astype(F32) + left[slot, step - 1].astype(F32)
            ).astype(LOW)

    line_a = (r.sum_a, r.right_a, r.left_a, 6)
    line_bb = (r.line_b, r.right_b, r.left_b, 12)
    line_cc = (r.line_c, r.right_c, r.left_c, 18)

    def advance(tick):
        def stage(offset):
            slab = tick - offset
            return (
                slab,
                lax.rem(slab + SLOTS * 4, SLOTS),
                lax.rem(slab + DEEP, DEEP),
                pl.when((slab >= 0) & (slab < SLABS)),
                pl.when((slab >= 0) & (slab < SLABS - 1)),
            )

        slab, slot, _, guard, _ = stage(0)
        load_start(slab + 1)

        @pl.when((slab >= PLAN[1][0]) & (slab < LOADED))
        def _():
            load_wait(slot)

        @guard
        def _():
            core_copy(slot).start()

        _, slot1, deep1, guard, most = stage(1)

        @guard
        def _():
            core_copy(slot1).wait()
            for line in range(4):
                for side in range(2):
                    both = r.part[slot1, core, 2 * line + side].astype(F32) + r.recv_c[
                        slot1, 2 * line + side
                    ].astype(F32)
                    both = both.astype(LOW)
                    r.half_a[slot1, side, line] = both[:32, :ACOLS]
                    r.line_c[deep1, line, side] = both[:32, ACOLS:]
                    r.half_b[slot1, 0, side, line] = both[32:48]
                    r.half_b[slot1, 1, side, line] = both[48:]
            line_start(slot1, deep1, 1, *line_cc)

        @most
        def _():
            col_copy_a(slot1).start()
            utt_copy_b(slot1).start()

        _, slot2, deep2, guard, most = stage(2)

        @guard
        def _():
            line_finish(slot2, deep2, 1, *line_cc)
            line_start(slot2, deep2, 2, *line_cc)

        @most
        def _():
            col_copy_a(slot2).wait()
            r.sum_a[deep2] = (
                r.half_a[slot2, col].astype(F32) + r.recv_xa[slot2].astype(F32)
            ).astype(LOW)
            line_start(slot2, deep2, 1, *line_a)
            utt_copy_b(slot2).wait()
            r.sum_b[slot2] = (
                r.half_b[slot2, utt].astype(F32) + r.recv_yb[slot2].astype(F32)
            ).astype(LOW)
            col_copy_b(slot2).start()

        _, slot3, deep3, guard, most = stage(3)

        @guard
        def _():
            line_finish(slot3, deep3, 2, *line_cc)
            line_start(slot3, deep3, 3, *line_cc)

        @most
        def _():
            line_finish(slot3, deep3, 1, *line_a)
            line_start(slot3, deep3, 2, *line_a)
            col_copy_b(slot3).wait()
            r.line_b[deep3] = (
                r.sum_b[slot3, col].astype(F32) + r.recv_xb[slot3].astype(F32)
            ).astype(LOW)
            line_start(slot3, deep3, 1, *line_bb)

        _, slot4, deep4, guard, most = stage(4)

        @guard
        def _():
            line_finish(slot4, deep4, 3, *line_cc)
            col_copy_c(slot4, deep4).start()

        @most
        def _():
            line_finish(slot4, deep4, 2, *line_a)
            line_start(slot4, deep4, 3, *line_a)
            line_finish(slot4, deep4, 1, *line_bb)
            line_start(slot4, deep4, 2, *line_bb)

        _, slot5, deep5, guard, most = stage(5)

        @guard
        def _():
            col_copy_c(slot5, deep5).wait()
            r.sum_c[slot5] = (
                r.line_c[deep5, pos, col].astype(F32) + r.recv_xc[slot5].astype(F32)
            ).astype(LOW)
            utt_copy_c(slot5).start()

        @most
        def _():
            line_finish(slot5, deep5, 3, *line_a)
            utt_copy_a(slot5, deep5).start()
            line_finish(slot5, deep5, 2, *line_bb)
            line_start(slot5, deep5, 3, *line_bb)

        _, slot6, deep6, guard, most = stage(6)

        @guard
        def _():
            utt_copy_c(slot6).wait()
            r.staged[slot6, 0:32, ACOLS:] = r.sum_c[slot6].astype(F32) + r.recv_yc[slot6].astype(F32)

        @most
        def _():
            utt_copy_a(slot6, deep6).wait()
            r.staged[slot6, 0:32, :ACOLS] = r.sum_a[deep6, pos].astype(F32) + r.recv_ya[
                slot6
            ].astype(F32)
            line_finish(slot6, deep6, 3, *line_bb)
            utt_copy_b2(slot6, deep6).start()

        slab7, slot7, deep7, guard, most = stage(7)

        @most
        def _():
            utt_copy_b2(slot7, deep7).wait()
            mine = r.line_b[deep7, pos].astype(F32)
            theirs = r.recv_yb2[slot7].astype(F32)
            r.staged[slot7, 32:48] = jnp.where(utt == 0, mine, theirs)
            r.staged[slot7, 48:64] = jnp.where(utt == 0, theirs, mine)

        for ref, spec in zip(outs, PLAN):

            @pl.when((slab7 >= spec[0]) & (slab7 < spec[0] + spec[1]))
            def _():
                pltpu.make_async_copy(
                    r.staged.at[slot7], window(ref, spec, slab7, ()), r.out_sem.at[slot7]
                ).start()

        _, slot8, _, guard, _ = stage(8)

        @guard
        def _():
            pltpu.make_async_copy(
                r.staged.at[slot8], outs[0].at[pl.ds(0, SROWS), pl.ds(0, SCOLS)], r.out_sem.at[slot8]
            ).wait()

    def cols_of(index):
        return pl.ds(pl.multiple_of(index * SCOLS, SCOLS), SCOLS)

    def put(slot, dest, rows):
        r.part[slot, dest % 2, dest // 2] = rows.astype(LOW)

    def put_product(slot, left_of, right):
        for quarter in range(4):
            rows = mul(left_of(quarter), right)
            for index in range(4):
                put(slot, 4 * quarter + index, rows[64 * index : 64 * index + 64])

    def quarter_rows(ref, lead=()):
        return lambda quarter: ref[lead + (slice(256 * quarter, 256 * quarter + 256),)]

    def produce(slab):
        slot = slab % SLOTS

        def among(first, number):
            return pl.when((slab >= first) & (slab < first + number))

        @among(16, 8)
        def _():
            local = slab - 16
            put_product(slot, quarter_rows(r.l_x_t), r.l_g[local // 2, :, cols_of(local % 2)])

        @among(24, 6)
        def _():
            local = slab - 24
            for dest in range(16):
                place = 3 * dest + local // 2
                book = place // 16
                first = (place % 16) * SROWS
                ids = first + lax.broadcasted_iota(jnp.int32, (SROWS, LANES), 0)
                picked = (ids == r.codes[book][0:1]).astype(LOW)
                put(slot, dest, mul(picked, r.table_g[book, :, cols_of(local % 2)]))

        @among(30, 8)
        def _():
            local = slab - 30
            inner = local // 2

            def rows(quarter):
                return jnp.concatenate(
                    [
                        r.act_t[pl.ds(pl.multiple_of(256 * dest + 64 * inner, 64), 64)]
                        for dest in range(4 * quarter, 4 * quarter + 4)
                    ],
                    axis=0,
                )

            put_product(slot, rows, r.dout_low[:, cols_of(local % 2)])

        @among(38, 8)
        def _():
            put_product(slot, quarter_rows(r.g_hn_t), r.du[:, cols_of(slab - 38)])

        @among(46, 8)
        def _():
            local = slab - 46
            kind = local // 2
            put_product(
                slot,
                quarter_rows(r.g_x_t, (jnp.minimum(kind, 1),)),
                r.g_g[kind, :, cols_of(local % 2)],
            )

        @pl.when(slab == 54)
        def _():
            b_down = jnp.sum(r.dout_low[...].astype(F32), axis=0, keepdims=True)
            for dest in range(16):
                shared = slice(LANES * (dest // 2), LANES * (dest // 2) + LANES)
                rows = [r.dn1[:, shared], r.dn2[:, shared], b_down[:, shared]]
                for index in range(2):
                    first = 256 * (dest % 2) + LANES * index
                    rows.append(r.db1[dest // 2 : dest // 2 + 1, first : first + LANES])
                rows += [r.l_dn1[:, shared], r.l_dn2[:, shared], r.l_db2[:, shared]]
                for index in range(2):
                    first = 256 * dest + LANES * index
                    rows.append(r.l_db1[:, first : first + LANES])
                rows.append(jnp.zeros((6, LANES), F32))
                r.part[slot, dest % 2, dest // 2, 0:16, ACOLS:] = jnp.concatenate(
                    rows, axis=0
                ).astype(LOW)

    own_utt, own_pair = seq // 8, seq % 8
    own_cols = pl.ds(pl.multiple_of(own_pair * LANES, LANES), LANES)

    def pair_cols(other):
        return pl.ds(pl.multiple_of((other % 8) * LANES, LANES), LANES)

    def hand_out(other):
        return remote(
            r.dmix.at[other // 8, :, pair_cols(other)], r.grads.at[seq], r.send_one.at[other],
            r.recv_one.at[seq], other,
        )

    def hand_back(block):
        return remote(
            r.pieces.at[block], r.landed.at[:, own_utt, :, own_cols], r.send_two.at[block],
            r.recv_two.at[seq], block,
        )

    def others(body):
        @pl.loop(1, count)
        def _(step):
            body(lax.rem(seq + step, count))

    def compute(tick):
        def at(*ticks):
            hit = tick == ticks[0]
            for item in ticks[1:]:
                hit = hit | (tick == item)
            return pl.when(hit)

        @at(-1)
        def _():
            for copy in fetch(14, 15, 16):
                copy.wait()
            r.l_x_t[...] = r.l_x[0].T
            r.l_acc[...] += r.l_b2[...]
            r.l_dhn[...] = jnp.zeros_like(r.l_dhn)

        @pl.when(tick < AT_LOCAL)
        def _():
            block = tick + 1
            slot = block % 2
            for copy in local_weights(block, slot):
                copy.wait()

            @pl.when(block < 7)
            def _():
                for copy in local_weights(block + 1, 1 - slot):
                    copy.start()

            @pl.when(block >= 2)
            def _():
                kept(block - 2, slot).wait()

            cols = cols_of(block)
            u = mul(r.l_x[0], r.up_buf[slot]) + r.l_b1[:, cols]
            act, slope = gelu_parts(u)
            act = act.astype(LOW)
            r.l_acc[...] += mul(act, r.down_buf[slot])
            du = (mul_t(r.l_x[1], r.down_buf[slot]) * slope).astype(LOW)
            r.l_db1[:, cols] = jnp.sum(du.astype(F32), axis=0, keepdims=True)
            r.l_dhn[...] += mul_t(du, r.up_buf[slot])
            put_product(block % SLOTS, quarter_rows(r.l_x_t), du)
            r.l_kept[slot] = t_mul(act, r.l_x[1]).astype(LOW).reshape(r.l_kept.shape[1:])
            kept(block, slot).start()

        @at(1)
        def _():
            for copy in local_rows(0, 0) + fetch(10, 11, 12, 13):
                copy.start()

        @at(AT_LOCAL - 1)
        def _():
            kept(6, 0).wait()
            kept(7, 1).wait()
            r.l_db2[...] = jnp.sum(r.l_x[1].astype(F32), axis=0, keepdims=True)
            r.l_x[0] = r.l_acc[...].astype(LOW)
            result.start()

        since = tick - AT_LOCAL
        step = since // 2
        slot = step % 2

        @pl.when((since >= 0) & (since < 8) & (since % 2 == 0))
        def _():
            for copy in local_rows(step, slot):
                copy.wait()

            @pl.when(since == 0)
            def _():
                for copy in fetch(10):
                    copy.wait()
                r.l_dn1[...] = jnp.zeros_like(r.l_dn1)
                r.l_dn2[...] = jnp.zeros_like(r.l_dn2)

            @pl.when(step < 3)
            def _():
                for copy in local_rows(step + 1, 1 - slot):
                    copy.start()

            local_hidden_back(r, step, slot)
            local_attend_back(r, step, slot)

        @pl.when((since >= 0) & (since < 8) & (since % 2 == 1))
        def _():
            @pl.when(since == 1)
            def _():
                for copy in fetch(11, 12, 13):
                    copy.wait()

            local_project_back(r, step)
            local_input_back(r, step, slot)

        @at(9)
        def _():
            result.wait()

        @at(10)
        def _():
            for copy in weights(0, 0) + tuple(fetch(4, 5, 6)):
                copy.start()

        @at(AT_HIDDEN)
        def _():
            for copy in fetch(0, 1, 2, 3):
                copy.start()
            r.dout_low[...] = r.dout[...].astype(LOW)
            r.dhn[...] = jnp.zeros_like(r.dhn)

        @pl.when((tick >= AT_HIDDEN) & (tick < AT_HIDDEN + 4))
        def _():
            @pl.loop(0, 2)
            def _(index):
                block = 2 * (tick - AT_HIDDEN) + index
                slot = block % 2
                for copy in weights(block, slot):
                    copy.wait()

                @pl.when(block < 7)
                def _():
                    for copy in weights(block + 1, 1 - slot):
                        copy.start()

                cols = cols_of(block)
                _, slope = gelu_parts(r.u[:, cols])
                du = (mul_t(r.dout_low[...], r.down_buf[slot]) * slope).astype(LOW)
                r.du[:, cols] = du
                r.db1[pl.ds(block, 1), :] = jnp.sum(du.astype(F32), axis=0, keepdims=True)
                r.dhn[...] += mul_t(du, r.up_buf[slot])

        @at(15)
        def _():
            for copy in fetch(4, 5, 6):
                copy.wait()
            r.l_x_t[...] = r.l_x[0].T

        @at(18)
        def _():
            for copy in fetch(7, 8, 9):
                copy.start()

        @at(AT_BACK)
        def _():
            for copy in fetch(0):
                copy.wait()
            dmid, gain = scale_back(r.mid[...], r.n2[...], r.dhn[...])
            r.dn2[...] = jnp.sum(gain, axis=0, keepdims=True)
            dmid = dmid + r.dout[...]
            r.dmid[...] = dmid
            dattn = dmid.astype(LOW)
            r.g_g[0] = dattn
            r.dmix[...] = mul_t(dattn, r.square[0]).astype(LOW).reshape(r.dmix.shape)
            r.grads[seq] = r.dmix[own_utt, :, own_cols]

        @pl.when((tick >= AT_BACK) & (tick < AT_BACK + 5))
        def _():
            @pl.loop(0, 3)
            def _(index):
                hand_out(lax.rem(seq + 3 * (tick - AT_BACK) + index + 1, count)).start()

        @at(AT_BACK + 1)
        def _():
            r.k_t[...] = r.held[:, 64:128].reshape(count * HD, LANES).T
            fill_bias(r.bias, r.held[:, 192:208])
            r.dk_acc[...] = jnp.zeros_like(r.dk_acc)
            r.dv_acc[...] = jnp.zeros_like(r.dv_acc)

        @at(AT_ATTEND)
        def _():
            def arrived(other):
                here = r.grads.at[other]
                remote(here, here, r.send_one.at[other], r.recv_one.at[other], other).wait_recv()

            others(arrived)

        for order, group in enumerate(reversed(range(4))):
            below = group * 256
            here = below + 256
            begin = AT_ATTEND + 2 * order

            @at(begin, begin + 1)
            def _():
                @pl.loop(0, 2)
                def _(index):
                    attend_back_block(
                        r, group, below, here, 4 * group + 2 * (tick - begin) + index
                    )

            @at(begin + 1)
            def _():
                for block in range(4 * group, 4 * group + 4):
                    rows = slice(block * HD, (block + 1) * HD)
                    r.pieces[block, 1] = r.dk_acc[rows].astype(LOW)
                    r.pieces[block, 2] = r.dv_acc[rows].astype(LOW)

        @at(AT_RETURN)
        def _():
            r.landed[:, own_utt, :, own_cols] = r.pieces[seq]

        @pl.when((tick >= AT_RETURN) & (tick < AT_RETURN + 8))
        def _():
            hand_back(lax.rem(seq + 2 * (tick - AT_RETURN) + 1, count)).start()

        @pl.when((tick >= AT_RETURN) & (tick < AT_RETURN + 7))
        def _():
            hand_back(lax.rem(seq + 2 * (tick - AT_RETURN) + 2, count)).start()

        @at(AT_LANDED)
        def _():
            def arrived(other):
                here = r.landed.at[:, other // 8, :, pair_cols(other)]
                remote(here, here, r.send_two.at[other], r.recv_two.at[other], other).wait_recv()

            others(arrived)
            others(lambda other: hand_out(other).wait_send())
            others(lambda other: hand_back(other).wait_send())
            for index in range(3):
                r.g_g[1 + index] = r.landed[index].reshape(r.g_g.shape[1:])

        @at(AT_LANDED + 1)
        def _():
            for copy in fetch(1, 2, 3):
                copy.wait()
            r.dhn[...] = mul_t(r.g_g[1], r.square[1])

        @at(AT_LANDED + 2)
        def _():
            r.dhn[...] += mul_t(r.g_g[2], r.square[2])

        @at(AT_LANDED + 3)
        def _():
            dnormed = r.dhn[...] + mul_t(r.g_g[3], r.square[3])
            dx, gain = scale_back(r.x[...].astype(F32), r.n1[...], dnormed)
            r.dn1[...] = jnp.sum(gain, axis=0, keepdims=True)
            r.dx[...] = dx + r.dmid[...]

        @at(21)
        def _():
            r.l_x_t[...] = r.l_x[1].T

        @at(22)
        def _():
            for copy in fetch(7, 8, 9):
                copy.wait()

        @pl.when((tick >= 24) & (tick < 28))
        def _():
            cols = pl.ds(pl.multiple_of((tick - 24) * 1024, 1024), 1024)
            r.act_t[cols] = r.act_buf[:, cols].T

        @at(28)
        def _():
            r.g_hn_t[...] = r.hn[...].T

        @at(31, 32)
        def _():
            r.g_x_t[tick - 31] = r.g_x[tick - 31].T

    pl.semaphore_wait(barrier, count)

    @pl.loop(0, SLABS + DRAIN + 1)
    def _(index):
        tick = index - 1
        advance(tick)
        compute(tick)
        produce(tick + 1)


def local_hidden_back(r, step, slot):
    places, width = r.l_in_buf.shape[1], r.l_in_buf.shape[3]
    frames = r.l_in.shape[1]
    rows = places * PART

    def rows_of(place):
        return pl.ds(pl.multiple_of(place * frames + step * PART, PART), PART)

    mid = r.l_mid_buf[slot].reshape(rows, width)
    dmid, gain = scale_back(
        mid,
        r.l_n2[...],
        jnp.concatenate(
            [
                r.l_dhn[pl.ds(pl.multiple_of(place * frames + step * PART, PART), PART)]
                for place in range(places)
            ],
            axis=0,
        ),
    )
    r.l_dn2[...] += jnp.sum(gain, axis=0, keepdims=True)
    dmid = dmid + r.l_dout_buf[slot].astype(F32).reshape(rows, width)
    r.l_dmid[...] = dmid
    dattn = dmid.astype(LOW)
    for place in range(places):
        r.l_g[3, rows_of(place)] = dattn[place * PART : (place + 1) * PART]
    r.l_dmix[...] = mul_t(dattn, r.square[0]).astype(LOW).reshape(places, PART, width)


def local_attend_back(r, step, slot):
    places, width = r.l_in_buf.shape[1], r.l_in_buf.shape[3]
    frames = r.l_in.shape[1]

    def rows_of(place):
        return pl.ds(pl.multiple_of(place * frames + step * PART, PART), PART)

    sums, spread = head_sums(width), head_spread(width)
    add = lambda old, term: term if old is None else old + term
    pair = 0
    dk, dv = [None] * places, [None] * places
    for i in range(places):
        grad = r.l_dmix[i].astype(F32)
        query = r.l_q_buf[slot, i].astype(F32)
        dp = [sum_heads(grad * r.l_v_buf[slot, j].astype(F32), sums) for j in range(i + 1)]
        delta = None
        for j in range(i + 1):
            delta = add(delta, r.l_probs_buf[slot, pair + j] * dp[j])
        dq = None
        for j in range(i + 1):
            probs = r.l_probs_buf[slot, pair + j]
            ds = mul((probs * (dp[j] - delta)).astype(LOW), spread)
            dq = add(dq, ds * r.l_k_buf[slot, j].astype(F32))
            dk[j] = add(dk[j], ds * query)
            dv[j] = add(dv[j], mul(probs.astype(LOW), spread) * grad)
        pair += i + 1
        r.l_g[0, rows_of(i)] = (dq * HD ** (-0.5)).astype(LOW)
    for j in range(places):
        r.l_g[1, rows_of(j)] = (dk[j] * HD ** (-0.5)).astype(LOW)
        r.l_g[2, rows_of(j)] = dv[j].astype(LOW)


def local_project_back(r, step):
    places = r.l_in_buf.shape[1]
    frames = r.l_in.shape[1]
    dnormed = None
    for kind in range(3):
        grad = jnp.concatenate(
            [
                r.l_g[kind, pl.ds(pl.multiple_of(place * frames + step * PART, PART), PART)]
                for place in range(places)
            ],
            axis=0,
        )
        term = mul_t(grad, r.square[1 + kind])
        dnormed = term if dnormed is None else dnormed + term
    r.l_dnormed[...] = dnormed


def local_input_back(r, step, slot):
    places, width = r.l_in_buf.shape[1], r.l_in_buf.shape[3]
    rows = places * PART
    x = r.l_in_buf[slot].astype(F32).reshape(rows, width)
    dx, gain = scale_back(x, r.l_n1[...], r.l_dnormed[...])
    r.l_dn1[...] += jnp.sum(gain, axis=0, keepdims=True)
    dx = dx + r.l_dmid[...]
    here = pl.ds(pl.multiple_of(step * PART, PART), PART)
    total = r.cotan[here].astype(F32) + dx[:PART]
    r.dout[here] = jnp.where(r.valid[here] > 0, total, 0.0)
    for place in range(1, places):
        r.table_g[place - 1, here] = dx[place * PART : (place + 1) * PART].astype(LOW)


def attend_back_block(r, group, below, here, block):
    query = two_heads(r.held[block, 0:64] * LOW(HD ** (-0.5)))
    grad = two_heads(r.grads[block])
    log_total = r.log_total[block][0:1]
    near_v = r.held[4 * group : 4 * group + 4, 128:192].reshape(256, LANES)
    near_k = r.held[4 * group : 4 * group + 4, 64:128].reshape(256, LANES)
    near = masked_scores(mul_t(near_k, query), r.bias[below:here], below, block)
    near = jnp.exp(near - log_total)
    near_dp = mul_t(near_v, grad)
    delta = jnp.sum(near * near_dp, axis=0, keepdims=True)
    if group:
        far_v = r.held[0 : 4 * group, 128:192].reshape(below, LANES)
        far_k = r.held[0 : 4 * group, 64:128].reshape(below, LANES)
        far = jnp.exp(mul_t(far_k, query) + r.bias[0:below] - log_total)
        far_dp = mul_t(far_v, grad)
        delta = delta + jnp.sum(far * far_dp, axis=0, keepdims=True)
        far_ds = (far * (far_dp - delta)).astype(LOW)
        r.dk_acc[0:below] += mul(far_ds, query)
        r.dv_acc[0:below] += mul(far.astype(LOW), grad)
    near_ds = (near * (near_dp - delta)).astype(LOW)
    r.dk_acc[below:here] += mul(near_ds, query)
    r.dv_acc[below:here] += mul(near.astype(LOW), grad)
    dq = mul(r.k_t[:, below:here], near_ds)
    if group:
        dq = dq + mul(r.k_t[:, 0:below], far_ds)
    r.pieces[block, 0] = (join_heads(dq) * HD ** (-0.5)).astype(LOW)


def finish_on_slice(far, near):
    vmem = pl.BlockSpec(memory_space=pltpu.VMEM)
    hbm = pl.BlockSpec(memory_space=pl.ANY)
    rows, width = near["x"].shape
    wide = near["u"].shape[1]
    utts = rows // HD
    shapes = [
        (width // 16, wide), (wide // 16, width), (width // 16, width), (width // 16, width),
        (width // 16, width), (width // 16, width), (3 * 1024 // 16, width), (wide // 16, width),
        (width // 16, wide), (width // 16, width), (width // 16, width), (width // 16, width),
        (width // 16, width), (SROWS, SCOLS),
    ]
    out_names = ["dx", "y", "l_down"] + ["out_%d" % index for index in range(len(shapes))]
    rows_l = far["l_normed"].shape[0]
    places, pairs = far["l_in"].shape[0], far["l_probs"].shape[0]
    buffers = dict(
        part=((SLOTS, 2, 8, 64, SCOLS), LOW),
        recv_c=((SLOTS, 8, 64, SCOLS), LOW),
        half_a=((SLOTS, 2, 4, 32, ACOLS), LOW),
        half_b=((SLOTS, 2, 2, 4, 16, SCOLS), LOW),
        recv_xa=((SLOTS, 4, 32, ACOLS), LOW),
        recv_yb=((SLOTS, 2, 4, 16, SCOLS), LOW),
        sum_a=((DEEP, 4, 32, ACOLS), LOW),
        sum_b=((SLOTS, 2, 4, 16, SCOLS), LOW),
        recv_xb=((SLOTS, 4, 16, SCOLS), LOW),
        line_b=((DEEP, 4, 16, SCOLS), LOW),
        right_a=((SLOTS, 3, 32, ACOLS), LOW),
        left_a=((SLOTS, 3, 32, ACOLS), LOW),
        right_b=((SLOTS, 3, 16, SCOLS), LOW),
        left_b=((SLOTS, 3, 16, SCOLS), LOW),
        recv_ya=((SLOTS, 32, ACOLS), LOW),
        recv_yb2=((SLOTS, 16, SCOLS), LOW),
        line_c=((DEEP, 4, 2, 32, LANES), LOW),
        right_c=((SLOTS, 3, 2, 32, LANES), LOW),
        left_c=((SLOTS, 3, 2, 32, LANES), LOW),
        recv_xc=((SLOTS, 32, LANES), LOW),
        sum_c=((SLOTS, 32, LANES), LOW),
        recv_yc=((SLOTS, 32, LANES), LOW),
        staged=((SLOTS, 64, SCOLS), F32),
        up_buf=((2, width, SCOLS), LOW),
        down_buf=((2, SCOLS, width), LOW),
        square=((4, width, width), LOW),
        held=(far["saved"].shape, LOW),
        l_x=((2, rows_l, width), LOW),
        l_g=((4, rows_l, width), LOW),
        l_x_t=((width, rows_l), LOW),
        l_in_buf=((2, places, PART, width), LOW),
        l_mid_buf=((2, places, PART, width), F32),
        l_acc=((rows_l, width), F32),
        l_dhn=((rows_l, width), F32),
        l_kept=((2, 2, wide // 16, width), LOW),
        l_db1=((1, wide), F32),
        l_db2=((1, width), F32),
        l_dout_buf=((2, places, PART, width), LOW),
        l_q_buf=((2, places, PART, width), LOW),
        l_k_buf=((2, places, PART, width), LOW),
        l_v_buf=((2, places, PART, width), LOW),
        l_probs_buf=((2, pairs, PART, LANES), F32),
        l_dmid=((places * PART, width), F32),
        l_dnormed=((places * PART, width), F32),
        l_dmix=((places, PART, width), LOW),
        l_dn1=((1, width), F32),
        l_dn2=((1, width), F32),
        dout=((rows, width), F32),
        table_g=((places - 1, rows, width), LOW),
        act_buf=((rows, wide), LOW),
        act_t=((wide, rows), LOW),
        g_x=((2, rows, width), LOW),
        g_x_t=((2, width, rows), LOW),
        g_hn_t=((width, rows), LOW),
        g_g=((4, rows, width), LOW),
        dout_low=((rows, width), LOW),
        du=((rows, wide), LOW),
        db1=((8, SCOLS), F32),
        dn1=((1, width), F32),
        dn2=((1, width), F32),
        dhn=((rows, width), F32),
        dmid=((rows, width), F32),
        dmix=((utts, HD, width), LOW),
        grads=((16, HD, LANES), LOW),
        landed=((3, utts, HD, width), LOW),
        pieces=((16, 3, HD, LANES), LOW),
        dk_acc=((16 * HD, LANES), F32),
        dv_acc=((16 * HD, LANES), F32),
        bias=((16 * HD, LANES), F32),
        k_t=((LANES, 16 * HD), LOW),
    )
    semaphores = dict(
        load_sem=(SLOTS, 2), out_sem=(SLOTS,), send_sem=(26, SLOTS), recv_sem=(26, SLOTS),
        weight_sem=(2, 2), fetch_sem=(17,), local_sem=(2, 7), kept_sem=(2,), result_sem=(1,), send_one=(16,), recv_one=(16,), send_two=(16,),
        recv_two=(16,),
    )
    names = list(far) + list(near) + out_names + list(buffers) + list(semaphores)
    return pl.pallas_call(
        functools.partial(tail_kernel, names, len(shapes)),
        in_specs=[hbm] * len(far) + [vmem] * len(near),
        out_specs=[vmem] + [hbm] * (2 + len(shapes)),
        out_shape=[
            jax.ShapeDtypeStruct((rows, width), F32),
            jax.ShapeDtypeStruct((rows_l, width), LOW),
            jax.ShapeDtypeStruct((8, 2, wide // 16, width), LOW),
        ]
        + [jax.ShapeDtypeStruct(shape, F32) for shape in shapes],
        scratch_shapes=[pltpu.VMEM(*item) for item in buffers.values()]
        + [pltpu.SemaphoreType.DMA(item) for item in semaphores.values()],
        compiler_params=pltpu.CompilerParams(
            collective_id=1, has_side_effects=True, vmem_limit_bytes=63 << 20
        ),
    )(*far.values(), *near.values())


def normalize(values, gain_vec):
    return (
        values * lax.rsqrt(jnp.mean(values * values, axis=-1, keepdims=True) + EPSILON) * gain_vec
    )


def gelu_fn(values):
    return jax.nn.gelu(values, approximate=True)


def project_back(gradient, weight):
    return lax.dot_general(
        gradient, weight, (((1,), (1,)), ((), ())), preferred_element_type=jnp.float32
    )


def weight_grad(left_side, gradient):
    return lax.dot_general(
        left_side, gradient, (((0,), (0,)), ((), ())), preferred_element_type=jnp.float32
    )


def block_back(inputs, normed, mixed_rows, kept_parts, params, grad_out, attention_back):
    middle, middle_norm, pre_active, active = kept_parts
    grad_branch = grad_out.astype(jnp.bfloat16)
    grad_b_down = jnp.sum(grad_branch.astype(jnp.float32), axis=0)
    grad_w_down = weight_grad(active, grad_branch)
    grad_active = project_back(grad_branch, params[8])
    grad_pre = jax.vjp(gelu_fn, pre_active)[1](grad_active)[0].astype(jnp.bfloat16)
    grad_b_up = jnp.sum(grad_pre.astype(jnp.float32), axis=0)
    grad_w_up = weight_grad(middle_norm, grad_pre)
    middle_back = jax.vjp(normalize, middle, params[5])[1]
    grad_middle, grad_norm_two = middle_back(project_back(grad_pre, params[6]))
    grad_middle = grad_middle + grad_out
    grad_attn = grad_middle.astype(jnp.bfloat16)
    grad_w_output = weight_grad(mixed_rows, grad_attn)
    grad_mixed = project_back(grad_attn, params[4]).astype(jnp.bfloat16)
    grad_query, grad_key, grad_value = attention_back(grad_mixed)
    grad_normed = (
        project_back(grad_query, params[1])
        + project_back(grad_key, params[2])
        + project_back(grad_value, params[3])
    )
    input_back = jax.vjp(normalize, inputs, params[0])[1]
    grad_inputs, grad_norm_one = input_back(grad_normed)
    weight_grads = (
        grad_norm_one,
        weight_grad(normed, grad_query),
        weight_grad(normed, grad_key),
        weight_grad(normed, grad_value),
        grad_w_output,
        grad_norm_two,
        grad_w_up,
        grad_b_up,
        grad_w_down,
        grad_b_down,
    )
    return (grad_inputs + grad_middle, weight_grads)


def on_device(
    frames,
    codes,
    lengths,
    frame_mask,
    table,
    glob_norm_one,
    glob_w_query,
    glob_w_key,
    glob_w_value,
    glob_w_output,
    glob_norm_two,
    glob_w_up,
    glob_b_up,
    glob_w_down,
    glob_b_down,
    local_norm_one,
    local_w_query,
    local_w_key,
    local_w_value,
    local_w_output,
    local_norm_two,
    local_w_up,
    local_b_up,
    local_w_down,
    local_b_down,
    cotan_global,
    cotan_local,
):
    utter_count, frame_count, model_width = frames.shape
    row_count = utter_count * frame_count
    local_len = CB + 1
    positions = lax.axis_index("seq") * frame_count + jnp.arange(frame_count, dtype=jnp.int32)
    valid = positions[None, :] < lengths[:, None]
    usable = jnp.pad(frame_mask.astype(LOW), ((0, 0), (0, LANES - frame_count)))
    usable = jnp.broadcast_to(usable[:, None, :], (utter_count, 16, LANES))
    glob_params = (
        glob_norm_one,
        glob_w_query,
        glob_w_key,
        glob_w_value,
        glob_w_output,
        glob_norm_two,
        glob_w_up,
        glob_b_up,
        glob_w_down,
        glob_b_down,
    )
    local_params = (
        local_norm_one,
        local_w_query,
        local_w_key,
        local_w_value,
        local_w_output,
        local_norm_two,
        local_w_up,
        local_b_up,
        local_w_down,
        local_b_down,
    )
    code_rows = codes.transpose(2, 0, 1).reshape(CB, row_count)
    (
        glob_normed, glob_mixed, saved, log_total, local_in,
        glob_middle, glob_middle_norm, pre_active, active, global_rows,
    ) = global_forward(
        frames,
        usable,
        codes.reshape(row_count, CB),
        valid.reshape(row_count, 1).astype(F32),
        table,
        glob_params,
    )
    local_shape = (local_len, row_count, model_width)
    flat_shape = (local_len * row_count, model_width)
    normed, local_q, local_k, local_v, local_probs, mixed, middle, middle_norm = local_front(
        local_in, local_params
    )
    row_valid = valid.reshape(1, row_count, 1)
    local_cotan = cotan_local.transpose(2, 0, 1, 3).reshape(local_shape)
    local_cotan = jnp.where(row_valid, local_cotan, 0)

    def by_frame(result):
        result = jnp.where(row_valid, result.reshape(local_shape), 0)
        result = result.reshape(local_len, utter_count, frame_count, model_width)
        return result.transpose(1, 2, 0, 3)

    normed = normed.reshape(flat_shape)
    mixed = mixed.reshape(flat_shape)
    if lax.axis_size("seq") == 16 and lax.axis_size("utt") == 2:
        far = dict(
            l_w_up=local_w_up,
            l_w_down=local_w_down,
            l_hn=middle_norm.reshape(flat_shape),
            l_dout_flat=local_cotan.reshape(flat_shape),
            l_mid_flat=middle.reshape(flat_shape),
            g_w_up=glob_w_up,
            g_w_down=glob_w_down,
            g_w_o=glob_w_output,
            g_w_q=glob_w_query,
            g_w_k=glob_w_key,
            g_w_v=glob_w_value,
            saved=saved,
            l_normed=normed,
            l_mixed=mixed,
            l_in=local_in,
            l_mid=middle,
            l_dout=local_cotan,
            l_q=local_q,
            l_k=local_k,
            l_v=local_v,
            l_probs=local_probs,
            l_w_o=local_w_output,
            l_w_q=local_w_query,
            l_w_k=local_w_key,
            l_w_v=local_w_value,
            g_act=active,
            g_mixed=glob_mixed,
            g_normed=glob_normed,
        )
        near = dict(
            u=pre_active,
            cotan=cotan_global.reshape(row_count, model_width),
            valid=valid.reshape(row_count, 1).astype(F32),
            mid=glob_middle,
            hn=glob_middle_norm,
            x=frames.reshape(row_count, model_width),
            n1=glob_norm_one.reshape(1, -1),
            n2=glob_norm_two.reshape(1, -1),
            log_total=log_total,
            codes=jnp.broadcast_to(code_rows[:, None, :], (CB, 8, row_count)),
            l_n1=local_norm_one.reshape(1, -1),
            l_n2=local_norm_two.reshape(1, -1),
            l_b1=local_b_up.reshape(1, -1),
            l_b2=local_b_down.reshape(1, -1),
        )
        grad_inputs, local_result, _, *sums = finish_on_slice(far, near)
        grad_inputs, *sums = settle([grad_inputs] + sums)
        wide = dict(zip("12qkvot76pabc", sums[:-1]))
        half = lax.axis_index("seq") % 2
        rest = sums[-1]

        def piece(row):
            return jnp.where(half == 0, rest[row, ACOLS : ACOLS + LANES // 2], rest[row, ACOLS + LANES // 2 :])

        def piece_wide(row):
            return rest[row : row + 2, ACOLS:].reshape(-1)

        return (
            global_rows.reshape(utter_count, frame_count, model_width),
            by_frame(local_result),
            grad_inputs.reshape(utter_count, frame_count, model_width),
            wide["t"],
            piece(0),
            wide["a"],
            wide["b"],
            wide["c"],
            wide["p"],
            piece(1),
            wide["6"],
            piece_wide(3),
            wide["7"],
            piece(2),
            piece(5),
            wide["q"],
            wide["k"],
            wide["v"],
            wide["o"],
            piece(6),
            wide["1"],
            piece_wide(8),
            wide["2"],
            piece(7),
        )

    local_result, grad_hidden, grad_w_up, grad_w_down, grad_b_up, grad_b_down = local_ffn(
        middle_norm.reshape(flat_shape),
        local_cotan.reshape(flat_shape),
        middle.reshape(flat_shape),
        local_params,
    )
    grad_attn, grad_q, grad_k, grad_v, grad_first, grad_rest, grad_n1, grad_n2 = local_back(
        local_in,
        middle,
        grad_hidden.reshape(local_shape),
        local_cotan,
        local_q,
        local_k,
        local_v,
        local_probs,
        local_params,
    )
    grad_first = grad_first.reshape(utter_count, frame_count, model_width)
    glob_cotan = jnp.where(
        valid[:, :, None], cotan_global.astype(jnp.float32) + grad_first, 0.0
    )
    glob_cotan = glob_cotan.reshape(row_count, model_width)
    local_grads = (
        grad_n1[0],
        weight_grad(normed, grad_q.reshape(flat_shape)),
        weight_grad(normed, grad_k.reshape(flat_shape)),
        weight_grad(normed, grad_v.reshape(flat_shape)),
        weight_grad(mixed, grad_attn.reshape(flat_shape)),
        grad_n2[0],
        grad_w_up,
        grad_b_up[0],
        grad_w_down,
        grad_b_down[0],
    )
    picked = code_rows[:, None, :] == jnp.arange(VOCAB, dtype=jnp.int32)[None, :, None]
    grad_tab = jnp.einsum(
        "cvn,cnd->cvd", picked.astype(LOW), grad_rest, preferred_element_type=F32
    ).reshape(CB * VOCAB, model_width)

    def global_back(grad_mixed):
        grads = global_attend_back(
            grad_mixed.reshape(utter_count, frame_count, model_width), saved, log_total
        )
        return tuple(grads.reshape(3, row_count, model_width))

    global_in = frames.astype(F32).reshape(row_count, model_width)
    glob_kept = (glob_middle, glob_middle_norm, pre_active, active)
    grad_inputs, glob_grads = block_back(
        global_in, glob_normed, glob_mixed, glob_kept, glob_params, glob_cotan, global_back
    )
    reduced = reduce_all((grad_tab,) + glob_grads + local_grads)
    return (
        global_rows.reshape(utter_count, frame_count, model_width),
        by_frame(local_result),
        grad_inputs.reshape(utter_count, frame_count, model_width),
    ) + reduced


def solution(mesh):
    return jax.shard_map(
        on_device,
        mesh=mesh,
        in_specs=(
            P("utt", "seq", None),
            P("utt", "seq", None),
            P("utt"),
            P("utt", "seq"),
            P(),
            P(),
            P(),
            P(),
            P(),
            P(),
            P(),
            P(),
            P(),
            P(),
            P(),
            P(),
            P(),
            P(),
            P(),
            P(),
            P(),
            P(),
            P(),
            P(),
            P(),
            P("utt", "seq", None),
            P("utt", "seq", None, None),
        ),
        out_specs=(
            P("utt", "seq", None),
            P("utt", "seq", None, None),
            P("utt", "seq", None),
            P("seq", None),
            P("seq"),
            P("seq", None),
            P("seq", None),
            P("seq", None),
            P("seq", None),
            P("seq"),
            P("seq", None),
            P("seq"),
            P("seq", None),
            P("seq"),
            P("seq"),
            P("seq", None),
            P("seq", None),
            P("seq", None),
            P("seq", None),
            P("seq"),
            P("seq", None),
            P("seq"),
            P("seq", None),
            P("seq"),
        ),
        check_vma=False,
    )
```

```python
import functools
import types

import jax
import jax.numpy as jnp
from jax import lax
from jax.experimental import pallas as pl
from jax.experimental.pallas import tpu as pltpu
from jax.sharding import PartitionSpec as P

H = 16
HD = 64
CB = 3
VOCAB = 1024


EPSILON = 1e-05
NEGATIVE = -1e30
F32 = jnp.float32
LOW = jnp.bfloat16
LANES = 128
MESH_ID = pl.DeviceIdType.MESH


def reduce_all(grads):
    return tuple(
        lax.psum(
            lax.psum_scatter(item.astype(LOW), "seq", scatter_dimension=0, tiled=True), "utt"
        ).astype(F32)
        for item in grads
    )


def mul(left_side, right_side):
    return jnp.dot(left_side, right_side, preferred_element_type=F32)


def mul_t(left_side, right_side):
    return lax.dot_general(
        left_side, right_side, (((1,), (1,)), ((), ())), preferred_element_type=F32
    )


def t_mul(left_side, right_side):
    return lax.dot_general(
        left_side, right_side, (((0,), (0,)), ((), ())), preferred_element_type=F32
    )


def scale_of(values):
    return lax.rsqrt(jnp.mean(values * values, axis=-1, keepdims=True) + EPSILON)


def scale_back(values, gain, grad):
    scale = scale_of(values)
    inner = grad * gain
    shared = jnp.mean(values * inner, axis=-1, keepdims=True) * (scale * scale * scale)
    return inner * scale - values * shared, grad * values * scale


def head_sums(width):
    rows = lax.broadcasted_iota(jnp.int32, (width, 128), 0) // HD
    cols = lax.broadcasted_iota(jnp.int32, (width, 128), 1)
    return (rows == cols).astype(LOW)


def head_spread(width):
    rows = lax.broadcasted_iota(jnp.int32, (128, width), 0)
    cols = lax.broadcasted_iota(jnp.int32, (128, width), 1) // HD
    return (rows == cols).astype(LOW)


def sum_heads(product, sums):
    high = product.astype(LOW)
    rest = (product - high.astype(F32)).astype(LOW)
    return mul(high, sums) + mul(rest, sums)


def front_kernel(
    x_ref, n1_ref, wq_ref, wk_ref, wv_ref, wo_ref, n2_ref,
    normed_ref, q_ref, k_ref, v_ref, probs_ref, mixed_ref, mid_ref, mid_norm_ref,
):
    places, frames, width = x_ref.shape
    rows = places * frames
    x = x_ref[...].astype(F32).reshape(rows, width)
    normed = (x * scale_of(x) * n1_ref[...]).astype(LOW)
    normed_ref[...] = normed.reshape(places, frames, width)
    q_ref[...] = mul(normed, wq_ref[...]).astype(LOW).reshape(places, frames, width)
    k_ref[...] = mul(normed, wk_ref[...]).astype(LOW).reshape(places, frames, width)
    v_ref[...] = mul(normed, wv_ref[...]).astype(LOW).reshape(places, frames, width)
    sums, spread = head_sums(width), head_spread(width)
    pair = 0
    for i in range(places):
        query = q_ref[i].astype(F32)
        scores = [
            sum_heads(query * k_ref[j].astype(F32), sums) * HD ** (-0.5) for j in range(i + 1)
        ]
        peak = scores[0]
        for item in scores[1:]:
            peak = jnp.maximum(peak, item)
        raised = [jnp.exp(item - peak) for item in scores]
        total = raised[0]
        for item in raised[1:]:
            total = total + item
        mixed = None
        for j in range(i + 1):
            probs = raised[j] / total
            probs_ref[pair] = probs
            pair += 1
            term = mul(probs.astype(LOW), spread) * v_ref[j].astype(F32)
            mixed = term if mixed is None else mixed + term
        mixed_ref[i] = mixed.astype(LOW)
    mid = x + mul(mixed_ref[...].reshape(rows, width), wo_ref[...])
    mid_ref[...] = mid.reshape(places, frames, width)
    mid_norm_ref[...] = (
        (mid * scale_of(mid) * n2_ref[...]).astype(LOW).reshape(places, frames, width)
    )


def local_front(x, params):
    places, frames, width = x.shape
    pairs = places * (places + 1) // 2
    step = frames
    rows = pl.BlockSpec((places, step, width), lambda i: (0, i, 0))
    whole = lambda item: pl.BlockSpec(item.shape, lambda i: (0, 0), pipeline_mode=pl.Buffered(1))
    n1, n2 = params[0].reshape(1, -1), params[5].reshape(1, -1)
    operands = (x, n1, params[1], params[2], params[3], params[4], n2)
    like = lambda kind: jax.ShapeDtypeStruct((places, frames, width), kind)
    return pl.pallas_call(
        front_kernel,
        grid=(frames // step,),
        in_specs=[rows] + [whole(item) for item in operands[1:]],
        out_specs=[rows] * 4
        + [pl.BlockSpec((pairs, step, 128), lambda i: (0, i, 0))]
        + [rows] * 3,
        out_shape=[
            like(LOW), like(LOW), like(LOW), like(LOW),
            jax.ShapeDtypeStruct((pairs, frames, 128), F32),
            like(LOW), like(F32), like(LOW),
        ],
        compiler_params=pltpu.CompilerParams(vmem_limit_bytes=56 << 20),
    )(*operands)


def gelu_parts(u):
    scale = 0.7978845608028654
    inner = jnp.tanh(scale * (u + 0.044715 * u * u * u))
    half = 0.5 * (1.0 + inner)
    slope = half + 0.5 * u * (1.0 - inner * inner) * scale * (1.0 + 3 * 0.044715 * u * u)
    return u * half, slope


def ffn_kernel(
    hn_ref, dout_ref, mid_ref, w1_ref, b1_ref, w2_ref, b2_ref,
    y_ref, dhn_ref, dw1_ref, dw2_ref, db1_ref, db2_ref, acc_ref, hn_t_ref,
):
    at = pl.program_id(0)
    last = pl.num_programs(0) - 1

    @pl.when(at == 0)
    def _():
        hn_t_ref[...] = hn_ref[...].T
        acc_ref[...] = mid_ref[...] + b2_ref[...]
        dhn_ref[...] = jnp.zeros_like(dhn_ref)
        db2_ref[...] = jnp.sum(dout_ref[...].astype(F32), axis=0, keepdims=True)

    hn, dout = hn_ref[...], dout_ref[...]
    u = mul(hn, w1_ref[...]) + b1_ref[...]
    act, slope = gelu_parts(u)
    act = act.astype(LOW)
    acc_ref[...] += mul(act, w2_ref[...])
    du = (mul_t(dout, w2_ref[...]) * slope).astype(LOW)
    db1_ref[...] = jnp.sum(du.astype(F32), axis=0, keepdims=True)
    dhn_ref[...] += mul_t(du, w1_ref[...])
    dw1_ref[...] = mul(hn_t_ref[...], du).astype(LOW)
    dw2_ref[...] = t_mul(act, dout).astype(LOW)

    @pl.when(at == last)
    def _():
        y_ref[...] = acc_ref[...].astype(LOW)


def local_ffn(hn, dout, mid, params):
    rows, width = hn.shape
    wide = params[6].shape[1]
    step = 512
    whole = pl.BlockSpec((rows, width), lambda i: (0, 0), pipeline_mode=pl.Buffered(1))
    out_whole = pl.BlockSpec((rows, width), lambda i: (0, 0))
    return pl.pallas_call(
        ffn_kernel,
        grid=(wide // step,),
        in_specs=[
            whole, whole, whole,
            pl.BlockSpec((width, step), lambda i: (0, i)),
            pl.BlockSpec((1, step), lambda i: (0, i)),
            pl.BlockSpec((step, width), lambda i: (i, 0)),
            pl.BlockSpec((1, width), lambda i: (0, 0)),
        ],
        out_specs=[
            out_whole, out_whole,
            pl.BlockSpec((width, step), lambda i: (0, i)),
            pl.BlockSpec((step, width), lambda i: (i, 0)),
            pl.BlockSpec((1, step), lambda i: (0, i)),
            pl.BlockSpec((1, width), lambda i: (0, 0)),
        ],
        out_shape=[
            jax.ShapeDtypeStruct((rows, width), LOW),
            jax.ShapeDtypeStruct((rows, width), F32),
            jax.ShapeDtypeStruct((width, wide), LOW),
            jax.ShapeDtypeStruct((wide, width), LOW),
            jax.ShapeDtypeStruct((1, wide), F32),
            jax.ShapeDtypeStruct((1, width), F32),
        ],
        scratch_shapes=[pltpu.VMEM((rows, width), F32), pltpu.VMEM((width, rows), LOW)],
        compiler_params=pltpu.CompilerParams(vmem_limit_bytes=56 << 20),
    )(hn, dout, mid, params[6], params[7].reshape(1, -1), params[8], params[9].reshape(1, -1))


def back_kernel(
    x_ref, mid_ref, dhn_ref, dout_ref, q_ref, k_ref, v_ref, probs_ref,
    n1_ref, n2_ref, wq_ref, wk_ref, wv_ref, wo_ref,
    dattn_ref, dq_ref, dk_ref, dv_ref, first_ref, rest_ref, dn1_ref, dn2_ref,
    dmid_ref,
):
    places, frames, width = x_ref.shape
    rows = places * frames

    @pl.when(pl.program_id(0) == 0)
    def _():
        dn1_ref[...] = jnp.zeros_like(dn1_ref)
        dn2_ref[...] = jnp.zeros_like(dn2_ref)

    mid = mid_ref[...].reshape(rows, width)
    dmid, gain = scale_back(mid, n2_ref[...], dhn_ref[...].reshape(rows, width))
    dn2_ref[...] += jnp.sum(gain, axis=0, keepdims=True)
    dmid = dmid + dout_ref[...].astype(F32).reshape(rows, width)
    dmid_ref[...] = dmid
    dattn = dmid.astype(LOW)
    dattn_ref[...] = dattn.reshape(places, frames, width)
    dmixed = mul_t(dattn, wo_ref[...]).astype(LOW).reshape(places, frames, width)
    sums, spread = head_sums(width), head_spread(width)
    pair = 0
    dk, dv = [None] * places, [None] * places
    add = lambda old, term: term if old is None else old + term
    for i in range(places):
        grad = dmixed[i].astype(F32)
        query = q_ref[i].astype(F32)
        dp = [sum_heads(grad * v_ref[j].astype(F32), sums) for j in range(i + 1)]
        delta = None
        for j in range(i + 1):
            delta = add(delta, probs_ref[pair + j] * dp[j])
        dq = None
        for j in range(i + 1):
            probs = probs_ref[pair + j]
            ds = (probs * (dp[j] - delta)).astype(LOW)
            ds = mul(ds, spread)
            dq = add(dq, ds * k_ref[j].astype(F32))
            dk[j] = add(dk[j], ds * query)
            dv[j] = add(dv[j], mul(probs.astype(LOW), spread) * grad)
        pair += i + 1
        dq_ref[i] = (dq * HD ** (-0.5)).astype(LOW)
    for j in range(places):
        dk_ref[j] = (dk[j] * HD ** (-0.5)).astype(LOW)
        dv_ref[j] = dv[j].astype(LOW)
    dnormed = (
        mul_t(dq_ref[...].reshape(rows, width), wq_ref[...])
        + mul_t(dk_ref[...].reshape(rows, width), wk_ref[...])
        + mul_t(dv_ref[...].reshape(rows, width), wv_ref[...])
    )
    x = x_ref[...].astype(F32).reshape(rows, width)
    dx, gain = scale_back(x, n1_ref[...], dnormed)
    dn1_ref[...] += jnp.sum(gain, axis=0, keepdims=True)
    dx = (dx + dmid_ref[...]).reshape(places, frames, width)
    first_ref[...] = dx[0]
    rest_ref[...] = dx[1:].astype(LOW)


def local_back(x, mid, dhn, dout, q, k, v, probs, params):
    places, frames, width = x.shape
    pairs = probs.shape[0]
    step = 64
    rows = pl.BlockSpec((places, step, width), lambda i: (0, i, 0))
    whole = lambda item: pl.BlockSpec(item.shape, lambda i: (0, 0), pipeline_mode=pl.Buffered(1))
    like = lambda kind: jax.ShapeDtypeStruct((places, frames, width), kind)
    fixed = (params[0].reshape(1, -1), params[5].reshape(1, -1)) + tuple(params[1:5])
    vector = pl.BlockSpec((1, width), lambda i: (0, 0))
    return pl.pallas_call(
        back_kernel,
        grid=(frames // step,),
        in_specs=[rows] * 7
        + [pl.BlockSpec((pairs, step, 128), lambda i: (0, i, 0))]
        + [whole(item) for item in fixed],
        out_specs=[rows] * 4
        + [
            pl.BlockSpec((step, width), lambda i: (i, 0)),
            pl.BlockSpec((places - 1, step, width), lambda i: (0, i, 0)),
            vector, vector,
        ],
        out_shape=[
            like(LOW), like(LOW), like(LOW), like(LOW),
            jax.ShapeDtypeStruct((frames, width), F32),
            jax.ShapeDtypeStruct((places - 1, frames, width), LOW),
            jax.ShapeDtypeStruct((1, width), F32),
            jax.ShapeDtypeStruct((1, width), F32),
        ],
        scratch_shapes=[pltpu.VMEM((places * step, width), F32)],
        compiler_params=pltpu.CompilerParams(vmem_limit_bytes=60 << 20),
    )(x, mid, dhn, dout, q, k, v, probs, *fixed)


def greet(count):
    utt, me = lax.axis_index("utt"), lax.axis_index("seq")
    barrier = pltpu.get_barrier_semaphore()

    @pl.loop(1, count)
    def _(step):
        pl.semaphore_signal(
            barrier, inc=1, device_id=(utt, lax.rem(me + step, count)), device_id_type=MESH_ID
        )

    return barrier


def remote(source, target, send_sem, recv_sem, place):
    return pltpu.make_async_remote_copy(
        src_ref=source,
        dst_ref=target,
        send_sem=send_sem,
        recv_sem=recv_sem,
        device_id=(lax.axis_index("utt"), place),
        device_id_type=MESH_ID,
    )


def two_heads(rows):
    lane = lax.broadcasted_iota(jnp.int32, rows.shape, 1)
    zero = jnp.zeros_like(rows)
    return jnp.concatenate([jnp.where(lane < HD, rows, zero), jnp.where(lane < HD, zero, rows)], axis=0)


def join_heads(tall):
    rows = tall.T
    lane = lax.broadcasted_iota(jnp.int32, (HD, LANES), 1)
    return jnp.where(lane < HD, rows[:HD], rows[HD:])


def masked_scores(scores, bias, first, block):
    key = first + lax.broadcasted_iota(jnp.int32, scores.shape, 0)
    query = block * HD + lax.rem(lax.broadcasted_iota(jnp.int32, scores.shape, 1), HD)
    return jnp.where(key < query, scores + bias, jnp.where(key == query, scores, NEGATIVE))


def fill_bias(bias_ref, mask):
    for block in range(mask.shape[0]):
        row = lax.broadcasted_iota(jnp.int32, (HD, LANES), 0)
        lane = lax.broadcasted_iota(jnp.int32, (HD, LANES), 1)
        flags = jnp.broadcast_to(mask[block, 0:1, :], (HD, LANES))
        diagonal = jnp.where(row == lane, flags.astype(F32), 0.0).astype(LOW)
        usable = mul(diagonal, jnp.ones((LANES, LANES), LOW))
        bias_ref[block * HD : (block + 1) * HD, :] = (usable - 1.0) * 1e30


def attend_kernel(
    count, x_ref, mask_ref, n1_ref, wq_ref, wk_ref, wv_ref, codes_ref, valid_ref, n2_ref, b1_ref,
    b2_ref, table_ref, wo_ref, w1_ref, w2_ref,
    normed_ref, mixed_ref, saved_ref, log_ref, local_ref, mid_ref, hn_ref, u_ref, act_ref, out_ref,
    packed, held, mixed_all, pieces, bias, v_t, table, wo, w1, w2,
    send_sem, recv_sem, send_two, recv_two, save_sem, fetch_sem,
):
    share = count // 16
    me = lax.axis_index("seq")
    unit, part = me // share, me % share
    own_utt, own_pair = unit // 8, unit % 8
    own_cols = pl.ds(pl.multiple_of(own_pair * LANES, LANES), LANES)
    utts, frames, width = x_ref.shape
    rows = utts * frames
    barrier = greet(count)
    fetches = [
        pltpu.make_async_copy(source, target, fetch_sem.at[index])
        for index, (source, target) in enumerate(
            ((table_ref, table), (wo_ref, wo), (w1_ref, w1), (w2_ref, w2))
        )
    ]
    for copy in fetches:
        copy.start()

    x = x_ref[...].astype(F32).reshape(rows, width)
    normed = (x * scale_of(x) * n1_ref[...]).astype(LOW)
    normed_ref[...] = normed
    packed[:, 0:64] = (mul(normed, wq_ref[...]).astype(LOW)).reshape(utts, frames, width)
    packed[:, 64:128] = mul(normed, wk_ref[...]).astype(LOW).reshape(utts, frames, width)
    packed[:, 128:192] = mul(normed, wv_ref[...]).astype(LOW).reshape(utts, frames, width)
    for pair in range(8):
        packed[:, 192:208, pair * LANES : (pair + 1) * LANES] = jnp.broadcast_to(
            mask_ref[...], (utts, 16, LANES)
        )
    pl.semaphore_wait(barrier, count - 1)

    def outgoing(step):
        place = lax.rem(me + step, count)
        target = place // share
        cols = pl.ds(pl.multiple_of((target % 8) * LANES, LANES), LANES)
        return remote(
            packed.at[target // 8, :, cols], held.at[me], send_sem.at[step], recv_sem.at[step], place
        )

    @pl.loop(1, count)
    def _(step):
        outgoing(step).start()

    held[me] = packed[own_utt, :, own_cols]

    fetches[0].wait()
    vocab = table.shape[0] // CB
    for book in range(CB):
        ids = jnp.broadcast_to(codes_ref[:, book : book + 1], (rows, vocab))
        picked = (ids == lax.broadcasted_iota(jnp.int32, (rows, vocab), 1)).astype(LOW)
        local_ref[1 + book] = mul(picked, table[book * vocab : (book + 1) * vocab]).astype(LOW)

    save = pltpu.make_async_copy(held, saved_ref, save_sem)

    def returning(block):
        return remote(
            pieces.at[block],
            mixed_all.at[own_utt, :, own_cols],
            send_two.at[block],
            recv_two.at[unit],
            block,
        )

    for group in range(count // 4):
        below = group * 256
        here = below + 256
        for place in range(4 * group, 4 * group + 4):

            @pl.when(place != me)
            def _():
                step = lax.rem(me + count - place, count)
                remote(
                    held.at[place], held.at[place], send_sem.at[step], recv_sem.at[step], place
                ).wait_recv()

        v_t[:, below:here] = held[4 * group : 4 * group + 4, 128:192].reshape(256, LANES).T
        fill_bias(bias.at[below:here], held[4 * group : 4 * group + 4, 192:208])

        @pl.loop(0, 4 // share)
        def _(index):
            block = 4 * group + share * index + part
            query = two_heads(held[block, 0:64] * LOW(HD ** (-0.5)))
            keys = held[4 * group : 4 * group + 4, 64:128].reshape(256, LANES)
            near = masked_scores(mul_t(keys, query), bias[below:here], below, block)
            peak = jnp.max(near, axis=0, keepdims=True)
            if group:
                keys = held[0 : 4 * group, 64:128].reshape(below, LANES)
                far = mul_t(keys, query) + bias[0:below]
                peak = jnp.maximum(peak, jnp.max(far, axis=0, keepdims=True))
                far = jnp.exp(far - peak)
            near = jnp.exp(near - peak)
            total = jnp.sum(near, axis=0, keepdims=True)
            if group:
                total = total + jnp.sum(far, axis=0, keepdims=True)
            inverse = 1.0 / total
            mixed = mul(v_t[:, below:here], (near * inverse).astype(LOW))
            if group:
                mixed = mixed + mul(v_t[:, 0:below], (far * inverse).astype(LOW))
            log_ref[block] = jnp.broadcast_to(peak + jnp.log(total), (8, LANES))
            pieces[block] = join_heads(mixed).astype(LOW)

            @pl.when(block != me)
            def _():
                returning(block).start()

            @pl.when(block == me)
            def _():
                mixed_all[own_utt, :, own_cols] = pieces[block]

    save.start()

    @pl.loop(0, 16)
    def _(other):
        place = other * share + me % share
        cols = pl.ds(pl.multiple_of((other % 8) * LANES, LANES), LANES)

        @pl.when(place != me)
        def _():
            here = mixed_all.at[other // 8, :, cols]
            remote(here, here, send_two.at[0], recv_two.at[other], place).wait_recv()

    mixed = mixed_all[...].reshape(rows, width)
    mixed_ref[...] = mixed
    fetches[1].wait()
    mid = x_ref[...].astype(F32).reshape(rows, width) + mul(mixed, wo[...])
    hn = (mid * scale_of(mid) * n2_ref[...]).astype(LOW)
    mid_ref[...] = mid
    hn_ref[...] = hn
    fetches[2].wait()
    fetches[3].wait()
    result = mid + b2_ref[...]
    for first in range(0, u_ref.shape[1], 512):
        cols = slice(first, first + 512)
        u = mul(hn, w1[:, cols]) + b1_ref[:, cols]
        act = gelu_parts(u)[0].astype(LOW)
        u_ref[:, cols] = u
        act_ref[:, cols] = act
        result = result + mul(act, w2[cols])
    result = jnp.where(valid_ref[...] > 0, result, 0.0).astype(LOW)
    local_ref[0] = result
    out_ref[...] = result

    @pl.loop(1, count)
    def _(step):
        outgoing(step).wait_send()

    @pl.loop(0, count // share)
    def _(index):
        block = share * index + part

        @pl.when(block != me)
        def _():
            returning(block).wait_send()

    save.wait()


def global_forward(x, mask, codes, valid, table, params):
    count = lax.axis_size("seq")
    utts, frames, width = x.shape
    rows, wide = utts * frames, params[6].shape[1]
    vmem = pl.BlockSpec(memory_space=pltpu.VMEM)
    hbm = pl.BlockSpec(memory_space=pl.ANY)
    return pl.pallas_call(
        functools.partial(attend_kernel, count),
        in_specs=[vmem] * 11 + [hbm] * 4,
        out_specs=[vmem, vmem, hbm] + [vmem] * 7,
        out_shape=[
            jax.ShapeDtypeStruct((rows, width), LOW),
            jax.ShapeDtypeStruct((rows, width), LOW),
            jax.ShapeDtypeStruct((count, 208, LANES), LOW),
            jax.ShapeDtypeStruct((count, 8, LANES), F32),
            jax.ShapeDtypeStruct((1 + CB, rows, width), LOW),
            jax.ShapeDtypeStruct((rows, width), F32),
            jax.ShapeDtypeStruct((rows, width), LOW),
            jax.ShapeDtypeStruct((rows, wide), F32),
            jax.ShapeDtypeStruct((rows, wide), LOW),
            jax.ShapeDtypeStruct((rows, width), LOW),
        ],
        scratch_shapes=[
            pltpu.VMEM((utts, 208, width), LOW),
            pltpu.VMEM((count, 208, LANES), LOW),
            pltpu.VMEM((utts, frames, width), LOW),
            pltpu.VMEM((count, HD, LANES), LOW),
            pltpu.VMEM((count * HD, LANES), F32),
            pltpu.VMEM((LANES, count * HD), LOW),
            pltpu.VMEM(table.shape, LOW),
            pltpu.VMEM(params[4].shape, LOW),
            pltpu.VMEM(params[6].shape, LOW),
            pltpu.VMEM(params[8].shape, LOW),
            pltpu.SemaphoreType.DMA((count,)),
            pltpu.SemaphoreType.DMA((count,)),
            pltpu.SemaphoreType.DMA((count,)),
            pltpu.SemaphoreType.DMA((16,)),
            pltpu.SemaphoreType.DMA,
            pltpu.SemaphoreType.DMA((4,)),
        ],
        compiler_params=pltpu.CompilerParams(
            collective_id=2, has_side_effects=True, vmem_limit_bytes=58 << 20
        ),
    )(
        x, mask, params[0].reshape(1, -1), params[1], params[2], params[3], codes, valid,
        params[5].reshape(1, -1), params[7].reshape(1, -1), params[9].reshape(1, -1), table,
        params[4], params[6], params[8],
    )


def settle_kernel(number, *refs):
    sources, targets, held = (refs[index * number : (index + 1) * number] for index in range(3))
    into = [
        pltpu.make_async_copy(sources[index], held[index], refs[-1].at[0, index])
        for index in range(number)
    ]
    out = [
        pltpu.make_async_copy(held[index], targets[index], refs[-1].at[1, index])
        for index in range(number)
    ]
    for copy in into:
        copy.start()
    for first, second in zip(into, out):
        first.wait()
        second.start()
    for copy in out:
        copy.wait()


def settle(arrays):
    hbm = pl.BlockSpec(memory_space=pl.ANY)
    return pl.pallas_call(
        functools.partial(settle_kernel, len(arrays)),
        in_specs=[hbm] * len(arrays),
        out_specs=[hbm] * len(arrays),
        out_shape=[jax.ShapeDtypeStruct(item.shape, item.dtype) for item in arrays],
        scratch_shapes=[pltpu.VMEM(item.shape, item.dtype) for item in arrays]
        + [pltpu.SemaphoreType.DMA((2, len(arrays)))],
        compiler_params=pltpu.CompilerParams(vmem_limit_bytes=62 << 20),
    )(*arrays)


def attend_back_kernel(
    count, grad_ref, held, log_ref,
    dqkv_ref,
    grads, landed, pieces, dk_acc, dv_acc, bias, k_t, send_sem, recv_sem, send_two, recv_two,
):
    share = count // 16
    me = lax.axis_index("seq")
    unit, part = me // share, me % share
    own_utt, own_pair = unit // 8, unit % 8
    own_cols = pl.ds(pl.multiple_of(own_pair * LANES, LANES), LANES)
    barrier = greet(count)
    k_t[...] = held[:, 64:128].reshape(count * HD, LANES).T
    fill_bias(bias, held[:, 192:208])
    dk_acc[...] = jnp.zeros_like(dk_acc)
    dv_acc[...] = jnp.zeros_like(dv_acc)
    pl.semaphore_wait(barrier, count - 1)

    def outgoing(other):
        cols = pl.ds(pl.multiple_of((other % 8) * LANES, LANES), LANES)
        place = other * share + part
        return place, remote(
            grad_ref.at[other // 8, :, cols], grads.at[me // share], send_sem.at[other],
            recv_sem.at[me // share], place,
        )

    @pl.loop(1, 16)
    def _(step):
        _, copy = outgoing(lax.rem(unit + step, 16))
        copy.start()

    grads[unit] = grad_ref[own_utt, :, own_cols]

    @pl.loop(1, 16)
    def _(step):
        other = lax.rem(unit + step, 16)
        here = grads.at[other]
        remote(here, here, send_sem.at[other], recv_sem.at[other], other * share + part).wait_recv()

    def returning(block):
        return remote(
            pieces.at[block],
            landed.at[part, :, own_utt, :, own_cols],
            send_two.at[block],
            recv_two.at[me],
            block,
        )

    for group in reversed(range(count // 4)):
        below = group * 256
        here = below + 256

        @pl.loop(0, 4 // share)
        def _(index):
            block = 4 * group + share * index + part
            query = two_heads(held[block, 0:64] * LOW(HD ** (-0.5)))
            grad = two_heads(grads[block // share])
            log_total = log_ref[block][0:1]
            near_v = held[4 * group : 4 * group + 4, 128:192].reshape(256, LANES)
            near_k = held[4 * group : 4 * group + 4, 64:128].reshape(256, LANES)
            near = masked_scores(mul_t(near_k, query), bias[below:here], below, block)
            near = jnp.exp(near - log_total)
            near_dp = mul_t(near_v, grad)
            delta = jnp.sum(near * near_dp, axis=0, keepdims=True)
            if group:
                far_v = held[0 : 4 * group, 128:192].reshape(below, LANES)
                far_k = held[0 : 4 * group, 64:128].reshape(below, LANES)
                far = jnp.exp(mul_t(far_k, query) + bias[0:below] - log_total)
                far_dp = mul_t(far_v, grad)
                delta = delta + jnp.sum(far * far_dp, axis=0, keepdims=True)
                far_ds = (far * (far_dp - delta)).astype(LOW)
                dk_acc[0:below] += mul(far_ds, query)
                dv_acc[0:below] += mul(far.astype(LOW), grad)
            near_ds = (near * (near_dp - delta)).astype(LOW)
            dk_acc[below:here] += mul(near_ds, query)
            dv_acc[below:here] += mul(near.astype(LOW), grad)
            dq = mul(k_t[:, below:here], near_ds)
            if group:
                dq = dq + mul(k_t[:, 0:below], far_ds)
            pieces[block, 0] = (join_heads(dq) * HD ** (-0.5)).astype(LOW)

        for block in range(4 * group, 4 * group + 4):
            rows = slice(block * HD, (block + 1) * HD)
            pieces[block, 1] = dk_acc[rows].astype(LOW)
            pieces[block, 2] = dv_acc[rows].astype(LOW)
            if share > 1:

                @pl.when(block % share != part)
                def _():
                    pieces[block, 0] = jnp.zeros((HD, LANES), LOW)

            @pl.when(block != me)
            def _():
                returning(block).start()

            @pl.when(block == me)
            def _():
                landed[part, :, own_utt, :, own_cols] = pieces[block]

    @pl.loop(1, count)
    def _(step):
        place = lax.rem(me + step, count)
        other, other_part = place // share, place % share
        cols = pl.ds(pl.multiple_of((other % 8) * LANES, LANES), LANES)
        here = landed.at[other_part, :, other // 8, :, cols]
        remote(here, here, send_two.at[place], recv_two.at[place], place).wait_recv()

    @pl.loop(1, 16)
    def _(step):
        _, copy = outgoing(lax.rem(unit + step, 16))
        copy.wait_send()

    @pl.loop(1, count)
    def _(step):
        returning(lax.rem(me + step, count)).wait_send()

    total = landed[0]
    for other_part in range(1, share):
        total = (total.astype(F32) + landed[other_part].astype(F32)).astype(LOW)
    dqkv_ref[...] = total


def global_attend_back(grad_mixed, saved, log_total):
    count = lax.axis_size("seq")
    utts, frames, width = grad_mixed.shape
    vmem = pl.BlockSpec(memory_space=pltpu.VMEM)
    return pl.pallas_call(
        functools.partial(attend_back_kernel, count),
        in_specs=[vmem] * 3,
        out_specs=vmem,
        out_shape=jax.ShapeDtypeStruct((3, utts, frames, width), LOW),
        scratch_shapes=[
            pltpu.VMEM((16, HD, LANES), LOW),
            pltpu.VMEM((count // 16, 3, utts, frames, width), LOW),
            pltpu.VMEM((count, 3, HD, LANES), LOW),
            pltpu.VMEM((count * HD, LANES), F32),
            pltpu.VMEM((count * HD, LANES), F32),
            pltpu.VMEM((count * HD, LANES), F32),
            pltpu.VMEM((LANES, count * HD), LOW),
            pltpu.SemaphoreType.DMA((16,)),
            pltpu.SemaphoreType.DMA((16,)),
            pltpu.SemaphoreType.DMA((count,)),
            pltpu.SemaphoreType.DMA((count,)),
        ],
        compiler_params=pltpu.CompilerParams(
            collective_id=3, has_side_effects=True, vmem_limit_bytes=48 << 20
        ),
    )(grad_mixed, saved, log_total)


SLOTS = 4
DEEP = 8
SROWS = 64
SCOLS = 512
ACOLS = 384
DRAIN = 8
PLAN = (
    (0, 8, 8), (8, 8, 2), (16, 2, 2), (18, 2, 2), (20, 2, 2), (22, 2, 2), (24, 6, 2),
    (30, 8, 2), (38, 8, 8), (46, 2, 2), (48, 2, 2), (50, 2, 2), (52, 2, 2), (54, 1, 1),
)
SLABS = 55
LOADED = 16
AT_LOCAL = 7
AT_HIDDEN = 16
AT_BACK = 20
AT_ATTEND = 27
AT_RETURN = 35
AT_LANDED = 45
PART = 32


def tail_kernel(names, out_count, *refs):
    r = types.SimpleNamespace(**dict(zip(names, refs)))
    outs = refs[names.index("out_0") : names.index("out_0") + out_count]
    utt = lax.axis_index("utt")
    seq = lax.axis_index("seq")
    count = 16
    pos = seq // 4
    col = (seq // 2) % 2
    core = seq % 2
    core_id = (utt, pos * 4 + col * 2 + 1 - core)
    col_id = (utt, pos * 4 + (1 - col) * 2 + core)
    utt_id = (1 - utt, seq)
    right_id = (utt, lax.rem(seq + 4, 16))
    left_id = (utt, lax.rem(seq + 12, 16))

    barrier = greet(count)
    pl.semaphore_signal(barrier, inc=1, device_id=utt_id, device_id_type=MESH_ID)

    def window(ref, spec, slab, lead):
        local = slab - spec[0]
        rows = pl.ds(pl.multiple_of((local // spec[2]) * SROWS, SROWS), SROWS)
        cols = pl.ds(pl.multiple_of((local % spec[2]) * SCOLS, SCOLS), SCOLS)
        return ref.at[lead + (rows, cols)]

    def load_start(slab):
        slot = slab % SLOTS

        @pl.when((slab >= PLAN[1][0]) & (slab < LOADED))
        def _():
            for side in range(2):
                pltpu.make_async_copy(
                    window(r.l_down, PLAN[1], slab, (slice(None), side)),
                    r.part.at[slot, side],
                    r.load_sem.at[slot, side],
                ).start()

    def load_wait(slot):
        for side in range(2):
            pltpu.make_async_copy(
                r.l_down.at[:, side, pl.ds(0, SROWS), pl.ds(0, SCOLS)],
                r.part.at[slot, side],
                r.load_sem.at[slot, side],
            ).wait()

    def weights(block, slot, up=r.g_w_up, down=r.g_w_down):
        start = block * SCOLS if isinstance(block, int) else pl.multiple_of(block * SCOLS, SCOLS)
        return (
            pltpu.make_async_copy(
                up.at[:, pl.ds(start, SCOLS)], r.up_buf.at[slot], r.weight_sem.at[slot, 0]
            ),
            pltpu.make_async_copy(
                down.at[pl.ds(start, SCOLS)], r.down_buf.at[slot], r.weight_sem.at[slot, 1]
            ),
        )

    fetches = (
        (r.g_w_o, r.square.at[0]), (r.g_w_q, r.square.at[1]), (r.g_w_k, r.square.at[2]),
        (r.g_w_v, r.square.at[3]), (r.saved, r.held), (r.l_normed, r.l_x.at[0]),
        (r.l_mixed, r.l_x.at[1]), (r.g_act, r.act_buf), (r.g_mixed, r.g_x.at[0]),
        (r.g_normed, r.g_x.at[1]), (r.l_w_o, r.square.at[0]), (r.l_w_q, r.square.at[1]),
        (r.l_w_k, r.square.at[2]), (r.l_w_v, r.square.at[3]), (r.l_hn, r.l_x.at[0]),
        (r.l_dout_flat, r.l_x.at[1]), (r.l_mid_flat, r.l_acc),
    )

    def fetch(*which):
        return [
            pltpu.make_async_copy(*fetches[index], r.fetch_sem.at[index]) for index in which
        ]

    def local_rows(step, slot):
        rows = pl.ds(step * PART if isinstance(step, int) else pl.multiple_of(step * PART, PART), PART)
        pairs = (
            (r.l_in, r.l_in_buf), (r.l_mid, r.l_mid_buf),
            (r.l_dout, r.l_dout_buf), (r.l_q, r.l_q_buf), (r.l_k, r.l_k_buf), (r.l_v, r.l_v_buf),
            (r.l_probs, r.l_probs_buf),
        )
        return [
            pltpu.make_async_copy(ref.at[:, rows], buffer.at[slot], r.local_sem.at[slot, index])
            for index, (ref, buffer) in enumerate(pairs)
        ]

    def local_weights(block, slot):
        return weights(block, slot, r.l_w_up, r.l_w_down)

    def kept(block, slot):
        return pltpu.make_async_copy(r.l_kept.at[slot], r.l_down.at[block], r.kept_sem.at[slot])

    result = pltpu.make_async_copy(r.l_x.at[0], r.y, r.result_sem.at[0])
    for copy in tuple(fetch(14, 15, 16)) + local_weights(0, 0):
        copy.start()

    def send(kind, slot, source, target, device):
        return pltpu.make_async_remote_copy(
            src_ref=source,
            dst_ref=target,
            send_sem=r.send_sem.at[kind, slot],
            recv_sem=r.recv_sem.at[kind, slot],
            device_id=device,
            device_id_type=MESH_ID,
        )

    def core_copy(slot):
        return send(0, slot, r.part.at[slot, 1 - core], r.recv_c.at[slot], core_id)

    def col_copy_a(slot):
        return send(1, slot, r.half_a.at[slot, 1 - col], r.recv_xa.at[slot], col_id)

    def utt_copy_b(slot):
        return send(2, slot, r.half_b.at[slot, 1 - utt], r.recv_yb.at[slot], utt_id)

    def col_copy_b(slot):
        return send(3, slot, r.sum_b.at[slot, 1 - col], r.recv_xb.at[slot], col_id)

    def utt_copy_a(slot, deep):
        return send(4, slot, r.sum_a.at[deep, pos], r.recv_ya.at[slot], utt_id)

    def utt_copy_b2(slot, deep):
        return send(5, slot, r.line_b.at[deep, pos], r.recv_yb2.at[slot], utt_id)

    def col_copy_c(slot, deep):
        return send(24, slot, r.line_c.at[deep, pos, 1 - col], r.recv_xc.at[slot], col_id)

    def utt_copy_c(slot):
        return send(25, slot, r.sum_c.at[slot], r.recv_yc.at[slot], utt_id)

    def line_right(kind, slot, deep, step, source, target):
        dest = jnp.minimum(4 - step + pos, 3)
        return send(kind + step - 1, slot, source.at[deep, dest], target.at[slot, step - 1], right_id)

    def line_left(kind, slot, deep, step, source, target):
        dest = jnp.maximum(pos - 4 + step, 0)
        return send(kind + step - 1, slot, source.at[deep, dest], target.at[slot, step - 1], left_id)

    def line_start(slot, deep, step, source, right, left, kind):
        @pl.when((pos <= step - 1) & (pos < 3))
        def _():
            line_right(kind, slot, deep, step, source, right).start()

        @pl.when((pos >= 4 - step) & (pos > 0))
        def _():
            line_left(kind + 3, slot, deep, step, source, left).start()

    def line_finish(slot, deep, step, source, right, left, kind):
        @pl.when((pos <= step - 1) & (pos < 3))
        def _():
            line_right(kind, slot, deep, step, source, right).wait_send()

        @pl.when((pos >= 4 - step) & (pos > 0))
        def _():
            line_left(kind + 3, slot, deep, step, source, left).wait_send()

        @pl.when((pos >= 1) & (pos <= step))
        def _():
            line_right(kind, slot, deep, step, source, right).wait_recv()
            dest = 3 - step + pos
            source[deep, dest] = (
                source[deep, dest].astype(F32) + right[slot, step - 1].astype(F32)
            ).astype(LOW)

        @pl.when((pos <= 2) & (pos >= 3 - step))
        def _():
            line_left(kind + 3, slot, deep, step, source, left).wait_recv()
            dest = pos + step - 3
            source[deep, dest] = (
                source[deep, dest].astype(F32) + left[slot, step - 1].astype(F32)
            ).astype(LOW)

    line_a = (r.sum_a, r.right_a, r.left_a, 6)
    line_bb = (r.line_b, r.right_b, r.left_b, 12)
    line_cc = (r.line_c, r.right_c, r.left_c, 18)

    def advance(tick):
        def stage(offset):
            slab = tick - offset
            return (
                slab,
                lax.rem(slab + SLOTS * 4, SLOTS),
                lax.rem(slab + DEEP, DEEP),
                pl.when((slab >= 0) & (slab < SLABS)),
                pl.when((slab >= 0) & (slab < SLABS - 1)),
            )

        slab, slot, _, guard, _ = stage(0)
        load_start(slab + 1)

        @pl.when((slab >= PLAN[1][0]) & (slab < LOADED))
        def _():
            load_wait(slot)

        @guard
        def _():
            core_copy(slot).start()

        _, slot1, deep1, guard, most = stage(1)

        @guard
        def _():
            core_copy(slot1).wait()
            for line in range(4):
                for side in range(2):
                    both = r.part[slot1, core, 2 * line + side].astype(F32) + r.recv_c[
                        slot1, 2 * line + side
                    ].astype(F32)
                    both = both.astype(LOW)
                    r.half_a[slot1, side, line] = both[:32, :ACOLS]
                    r.line_c[deep1, line, side] = both[:32, ACOLS:]
                    r.half_b[slot1, 0, side, line] = both[32:48]
                    r.half_b[slot1, 1, side, line] = both[48:]
            line_start(slot1, deep1, 1, *line_cc)

        @most
        def _():
            col_copy_a(slot1).start()
            utt_copy_b(slot1).start()

        _, slot2, deep2, guard, most = stage(2)

        @guard
        def _():
            line_finish(slot2, deep2, 1, *line_cc)
            line_start(slot2, deep2, 2, *line_cc)

        @most
        def _():
            col_copy_a(slot2).wait()
            r.sum_a[deep2] = (
                r.half_a[slot2, col].astype(F32) + r.recv_xa[slot2].astype(F32)
            ).astype(LOW)
            line_start(slot2, deep2, 1, *line_a)
            utt_copy_b(slot2).wait()
            r.sum_b[slot2] = (
                r.half_b[slot2, utt].astype(F32) + r.recv_yb[slot2].astype(F32)
            ).astype(LOW)
            col_copy_b(slot2).start()

        _, slot3, deep3, guard, most = stage(3)

        @guard
        def _():
            line_finish(slot3, deep3, 2, *line_cc)
            line_start(slot3, deep3, 3, *line_cc)

        @most
        def _():
            line_finish(slot3, deep3, 1, *line_a)
            line_start(slot3, deep3, 2, *line_a)
            col_copy_b(slot3).wait()
            r.line_b[deep3] = (
                r.sum_b[slot3, col].astype(F32) + r.recv_xb[slot3].astype(F32)
            ).astype(LOW)
            line_start(slot3, deep3, 1, *line_bb)

        _, slot4, deep4, guard, most = stage(4)

        @guard
        def _():
            line_finish(slot4, deep4, 3, *line_cc)
            col_copy_c(slot4, deep4).start()

        @most
        def _():
            line_finish(slot4, deep4, 2, *line_a)
            line_start(slot4, deep4, 3, *line_a)
            line_finish(slot4, deep4, 1, *line_bb)
            line_start(slot4, deep4, 2, *line_bb)

        _, slot5, deep5, guard, most = stage(5)

        @guard
        def _():
            col_copy_c(slot5, deep5).wait()
            r.sum_c[slot5] = (
                r.line_c[deep5, pos, col].astype(F32) + r.recv_xc[slot5].astype(F32)
            ).astype(LOW)
            utt_copy_c(slot5).start()

        @most
        def _():
            line_finish(slot5, deep5, 3, *line_a)
            utt_copy_a(slot5, deep5).start()
            line_finish(slot5, deep5, 2, *line_bb)
            line_start(slot5, deep5, 3, *line_bb)

        _, slot6, deep6, guard, most = stage(6)

        @guard
        def _():
            utt_copy_c(slot6).wait()
            r.staged[slot6, 0:32, ACOLS:] = r.sum_c[slot6].astype(F32) + r.recv_yc[slot6].astype(F32)

        @most
        def _():
            utt_copy_a(slot6, deep6).wait()
            r.staged[slot6, 0:32, :ACOLS] = r.sum_a[deep6, pos].astype(F32) + r.recv_ya[
                slot6
            ].astype(F32)
            line_finish(slot6, deep6, 3, *line_bb)
            utt_copy_b2(slot6, deep6).start()

        slab7, slot7, deep7, guard, most = stage(7)

        @most
        def _():
            utt_copy_b2(slot7, deep7).wait()
            mine = r.line_b[deep7, pos].astype(F32)
            theirs = r.recv_yb2[slot7].astype(F32)
            r.staged[slot7, 32:48] = jnp.where(utt == 0, mine, theirs)
            r.staged[slot7, 48:64] = jnp.where(utt == 0, theirs, mine)

        for ref, spec in zip(outs, PLAN):

            @pl.when((slab7 >= spec[0]) & (slab7 < spec[0] + spec[1]))
            def _():
                pltpu.make_async_copy(
                    r.staged.at[slot7], window(ref, spec, slab7, ()), r.out_sem.at[slot7]
                ).start()

        _, slot8, _, guard, _ = stage(8)

        @guard
        def _():
            pltpu.make_async_copy(
                r.staged.at[slot8], outs[0].at[pl.ds(0, SROWS), pl.ds(0, SCOLS)], r.out_sem.at[slot8]
            ).wait()

    def cols_of(index):
        return pl.ds(pl.multiple_of(index * SCOLS, SCOLS), SCOLS)

    def put(slot, dest, rows):
        r.part[slot, dest % 2, dest // 2] = rows.astype(LOW)

    def put_product(slot, left_of, right):
        for quarter in range(4):
            rows = mul(left_of(quarter), right)
            for index in range(4):
                put(slot, 4 * quarter + index, rows[64 * index : 64 * index + 64])

    def quarter_rows(ref, lead=()):
        return lambda quarter: ref[lead + (slice(256 * quarter, 256 * quarter + 256),)]

    def produce(slab):
        slot = slab % SLOTS

        def among(first, number):
            return pl.when((slab >= first) & (slab < first + number))

        @among(16, 8)
        def _():
            local = slab - 16
            put_product(slot, quarter_rows(r.l_x_t), r.l_g[local // 2, :, cols_of(local % 2)])

        @among(24, 6)
        def _():
            local = slab - 24
            for dest in range(16):
                place = 3 * dest + local // 2
                book = place // 16
                first = (place % 16) * SROWS
                ids = first + lax.broadcasted_iota(jnp.int32, (SROWS, LANES), 0)
                picked = (ids == r.codes[book][0:1]).astype(LOW)
                put(slot, dest, mul(picked, r.table_g[book, :, cols_of(local % 2)]))

        @among(30, 8)
        def _():
            local = slab - 30
            inner = local // 2

            def rows(quarter):
                return jnp.concatenate(
                    [
                        r.act_t[pl.ds(pl.multiple_of(256 * dest + 64 * inner, 64), 64)]
                        for dest in range(4 * quarter, 4 * quarter + 4)
                    ],
                    axis=0,
                )

            put_product(slot, rows, r.dout_low[:, cols_of(local % 2)])

        @among(38, 8)
        def _():
            put_product(slot, quarter_rows(r.g_hn_t), r.du[:, cols_of(slab - 38)])

        @among(46, 8)
        def _():
            local = slab - 46
            kind = local // 2
            put_product(
                slot,
                quarter_rows(r.g_x_t, (jnp.minimum(kind, 1),)),
                r.g_g[kind, :, cols_of(local % 2)],
            )

        @pl.when(slab == 54)
        def _():
            b_down = jnp.sum(r.dout_low[...].astype(F32), axis=0, keepdims=True)
            for dest in range(16):
                shared = slice(LANES * (dest // 2), LANES * (dest // 2) + LANES)
                rows = [r.dn1[:, shared], r.dn2[:, shared], b_down[:, shared]]
                for index in range(2):
                    first = 256 * (dest % 2) + LANES * index
                    rows.append(r.db1[dest // 2 : dest // 2 + 1, first : first + LANES])
                rows += [r.l_dn1[:, shared], r.l_dn2[:, shared], r.l_db2[:, shared]]
                for index in range(2):
                    first = 256 * dest + LANES * index
                    rows.append(r.l_db1[:, first : first + LANES])
                rows.append(jnp.zeros((6, LANES), F32))
                r.part[slot, dest % 2, dest // 2, 0:16, ACOLS:] = jnp.concatenate(
                    rows, axis=0
                ).astype(LOW)

    own_utt, own_pair = seq // 8, seq % 8
    own_cols = pl.ds(pl.multiple_of(own_pair * LANES, LANES), LANES)

    def pair_cols(other):
        return pl.ds(pl.multiple_of((other % 8) * LANES, LANES), LANES)

    def hand_out(other):
        return remote(
            r.dmix.at[other // 8, :, pair_cols(other)], r.grads.at[seq], r.send_one.at[other],
            r.recv_one.at[seq], other,
        )

    def hand_back(block):
        return remote(
            r.pieces.at[block], r.landed.at[:, own_utt, :, own_cols], r.send_two.at[block],
            r.recv_two.at[seq], block,
        )

    def others(body):
        @pl.loop(1, count)
        def _(step):
            body(lax.rem(seq + step, count))

    def compute(tick):
        def at(*ticks):
            hit = tick == ticks[0]
            for item in ticks[1:]:
                hit = hit | (tick == item)
            return pl.when(hit)

        @at(-1)
        def _():
            for copy in fetch(14, 15, 16):
                copy.wait()
            r.l_x_t[...] = r.l_x[0].T
            r.l_acc[...] += r.l_b2[...]
            r.l_dhn[...] = jnp.zeros_like(r.l_dhn)

        @pl.when(tick < AT_LOCAL)
        def _():
            block = tick + 1
            slot = block % 2
            for copy in local_weights(block, slot):
                copy.wait()

            @pl.when(block < 7)
            def _():
                for copy in local_weights(block + 1, 1 - slot):
                    copy.start()

            @pl.when(block >= 2)
            def _():
                kept(block - 2, slot).wait()

            cols = cols_of(block)
            u = mul(r.l_x[0], r.up_buf[slot]) + r.l_b1[:, cols]
            act, slope = gelu_parts(u)
            act = act.astype(LOW)
            r.l_acc[...] += mul(act, r.down_buf[slot])
            du = (mul_t(r.l_x[1], r.down_buf[slot]) * slope).astype(LOW)
            r.l_db1[:, cols] = jnp.sum(du.astype(F32), axis=0, keepdims=True)
            r.l_dhn[...] += mul_t(du, r.up_buf[slot])
            put_product(block % SLOTS, quarter_rows(r.l_x_t), du)
            r.l_kept[slot] = t_mul(act, r.l_x[1]).astype(LOW).reshape(r.l_kept.shape[1:])
            kept(block, slot).start()

        @at(1)
        def _():
            for copy in local_rows(0, 0) + fetch(10, 11, 12, 13):
                copy.start()

        @at(AT_LOCAL - 1)
        def _():
            kept(6, 0).wait()
            kept(7, 1).wait()
            r.l_db2[...] = jnp.sum(r.l_x[1].astype(F32), axis=0, keepdims=True)
            r.l_x[0] = r.l_acc[...].astype(LOW)
            result.start()

        since = tick - AT_LOCAL
        step = since // 2
        slot = step % 2

        @pl.when((since >= 0) & (since < 8) & (since % 2 == 0))
        def _():
            for copy in local_rows(step, slot):
                copy.wait()

            @pl.when(since == 0)
            def _():
                for copy in fetch(10):
                    copy.wait()
                r.l_dn1[...] = jnp.zeros_like(r.l_dn1)
                r.l_dn2[...] = jnp.zeros_like(r.l_dn2)

            @pl.when(step < 3)
            def _():
                for copy in local_rows(step + 1, 1 - slot):
                    copy.start()

            local_hidden_back(r, step, slot)
            local_attend_back(r, step, slot)

        @pl.when((since >= 0) & (since < 8) & (since % 2 == 1))
        def _():
            @pl.when(since == 1)
            def _():
                for copy in fetch(11, 12, 13):
                    copy.wait()

            local_project_back(r, step)
            local_input_back(r, step, slot)

        @at(9)
        def _():
            result.wait()

        @at(10)
        def _():
            for copy in weights(0, 0) + tuple(fetch(4, 5, 6)):
                copy.start()

        @at(AT_HIDDEN)
        def _():
            for copy in fetch(0, 1, 2, 3):
                copy.start()
            r.dout_low[...] = r.dout[...].astype(LOW)
            r.dhn[...] = jnp.zeros_like(r.dhn)

        @pl.when((tick >= AT_HIDDEN) & (tick < AT_HIDDEN + 4))
        def _():
            @pl.loop(0, 2)
            def _(index):
                block = 2 * (tick - AT_HIDDEN) + index
                slot = block % 2
                for copy in weights(block, slot):
                    copy.wait()

                @pl.when(block < 7)
                def _():
                    for copy in weights(block + 1, 1 - slot):
                        copy.start()

                cols = cols_of(block)
                _, slope = gelu_parts(r.u[:, cols])
                du = (mul_t(r.dout_low[...], r.down_buf[slot]) * slope).astype(LOW)
                r.du[:, cols] = du
                r.db1[pl.ds(block, 1), :] = jnp.sum(du.astype(F32), axis=0, keepdims=True)
                r.dhn[...] += mul_t(du, r.up_buf[slot])

        @at(15)
        def _():
            for copy in fetch(4, 5, 6):
                copy.wait()
            r.l_x_t[...] = r.l_x[0].T

        @at(18)
        def _():
            for copy in fetch(7, 8, 9):
                copy.start()

        @at(AT_BACK)
        def _():
            for copy in fetch(0):
                copy.wait()
            dmid, gain = scale_back(r.mid[...], r.n2[...], r.dhn[...])
            r.dn2[...] = jnp.sum(gain, axis=0, keepdims=True)
            dmid = dmid + r.dout[...]
            r.dmid[...] = dmid
            dattn = dmid.astype(LOW)
            r.g_g[0] = dattn
            r.dmix[...] = mul_t(dattn, r.square[0]).astype(LOW).reshape(r.dmix.shape)
            r.grads[seq] = r.dmix[own_utt, :, own_cols]

        @pl.when((tick >= AT_BACK) & (tick < AT_BACK + 5))
        def _():
            @pl.loop(0, 3)
            def _(index):
                hand_out(lax.rem(seq + 3 * (tick - AT_BACK) + index + 1, count)).start()

        @at(AT_BACK + 1)
        def _():
            r.k_t[...] = r.held[:, 64:128].reshape(count * HD, LANES).T
            fill_bias(r.bias, r.held[:, 192:208])
            r.dk_acc[...] = jnp.zeros_like(r.dk_acc)
            r.dv_acc[...] = jnp.zeros_like(r.dv_acc)

        @at(AT_ATTEND)
        def _():
            def arrived(other):
                here = r.grads.at[other]
                remote(here, here, r.send_one.at[other], r.recv_one.at[other], other).wait_recv()

            others(arrived)

        for order, group in enumerate(reversed(range(4))):
            below = group * 256
            here = below + 256
            begin = AT_ATTEND + 2 * order

            @at(begin, begin + 1)
            def _():
                @pl.loop(0, 2)
                def _(index):
                    attend_back_block(
                        r, group, below, here, 4 * group + 2 * (tick - begin) + index
                    )

            @at(begin + 1)
            def _():
                for block in range(4 * group, 4 * group + 4):
                    rows = slice(block * HD, (block + 1) * HD)
                    r.pieces[block, 1] = r.dk_acc[rows].astype(LOW)
                    r.pieces[block, 2] = r.dv_acc[rows].astype(LOW)

        @at(AT_RETURN)
        def _():
            r.landed[:, own_utt, :, own_cols] = r.pieces[seq]

        @pl.when((tick >= AT_RETURN) & (tick < AT_RETURN + 8))
        def _():
            hand_back(lax.rem(seq + 2 * (tick - AT_RETURN) + 1, count)).start()

        @pl.when((tick >= AT_RETURN) & (tick < AT_RETURN + 7))
        def _():
            hand_back(lax.rem(seq + 2 * (tick - AT_RETURN) + 2, count)).start()

        @at(AT_LANDED)
        def _():
            def arrived(other):
                here = r.landed.at[:, other // 8, :, pair_cols(other)]
                remote(here, here, r.send_two.at[other], r.recv_two.at[other], other).wait_recv()

            others(arrived)
            others(lambda other: hand_out(other).wait_send())
            others(lambda other: hand_back(other).wait_send())
            for index in range(3):
                r.g_g[1 + index] = r.landed[index].reshape(r.g_g.shape[1:])

        @at(AT_LANDED + 1)
        def _():
            for copy in fetch(1, 2, 3):
                copy.wait()
            r.dhn[...] = mul_t(r.g_g[1], r.square[1])

        @at(AT_LANDED + 2)
        def _():
            r.dhn[...] += mul_t(r.g_g[2], r.square[2])

        @at(AT_LANDED + 3)
        def _():
            dnormed = r.dhn[...] + mul_t(r.g_g[3], r.square[3])
            dx, gain = scale_back(r.x[...].astype(F32), r.n1[...], dnormed)
            r.dn1[...] = jnp.sum(gain, axis=0, keepdims=True)
            r.dx[...] = dx + r.dmid[...]

        @at(21)
        def _():
            r.l_x_t[...] = r.l_x[1].T

        @at(22)
        def _():
            for copy in fetch(7, 8, 9):
                copy.wait()

        @pl.when((tick >= 24) & (tick < 28))
        def _():
            cols = pl.ds(pl.multiple_of((tick - 24) * 1024, 1024), 1024)
            r.act_t[cols] = r.act_buf[:, cols].T

        @at(28)
        def _():
            r.g_hn_t[...] = r.hn[...].T

        @at(31, 32)
        def _():
            r.g_x_t[tick - 31] = r.g_x[tick - 31].T

    pl.semaphore_wait(barrier, count)

    @pl.loop(0, SLABS + DRAIN + 1)
    def _(index):
        tick = index - 1
        advance(tick)
        compute(tick)
        produce(tick + 1)


def local_hidden_back(r, step, slot):
    places, width = r.l_in_buf.shape[1], r.l_in_buf.shape[3]
    frames = r.l_in.shape[1]
    rows = places * PART

    def rows_of(place):
        return pl.ds(pl.multiple_of(place * frames + step * PART, PART), PART)

    mid = r.l_mid_buf[slot].reshape(rows, width)
    dmid, gain = scale_back(
        mid,
        r.l_n2[...],
        jnp.concatenate(
            [
                r.l_dhn[pl.ds(pl.multiple_of(place * frames + step * PART, PART), PART)]
                for place in range(places)
            ],
            axis=0,
        ),
    )
    r.l_dn2[...] += jnp.sum(gain, axis=0, keepdims=True)
    dmid = dmid + r.l_dout_buf[slot].astype(F32).reshape(rows, width)
    r.l_dmid[...] = dmid
    dattn = dmid.astype(LOW)
    for place in range(places):
        r.l_g[3, rows_of(place)] = dattn[place * PART : (place + 1) * PART]
    r.l_dmix[...] = mul_t(dattn, r.square[0]).astype(LOW).reshape(places, PART, width)


def local_attend_back(r, step, slot):
    places, width = r.l_in_buf.shape[1], r.l_in_buf.shape[3]
    frames = r.l_in.shape[1]

    def rows_of(place):
        return pl.ds(pl.multiple_of(place * frames + step * PART, PART), PART)

    sums, spread = head_sums(width), head_spread(width)
    add = lambda old, term: term if old is None else old + term
    pair = 0
    dk, dv = [None] * places, [None] * places
    for i in range(places):
        grad = r.l_dmix[i].astype(F32)
        query = r.l_q_buf[slot, i].astype(F32)
        dp = [sum_heads(grad * r.l_v_buf[slot, j].astype(F32), sums) for j in range(i + 1)]
        delta = None
        for j in range(i + 1):
            delta = add(delta, r.l_probs_buf[slot, pair + j] * dp[j])
        dq = None
        for j in range(i + 1):
            probs = r.l_probs_buf[slot, pair + j]
            ds = mul((probs * (dp[j] - delta)).astype(LOW), spread)
            dq = add(dq, ds * r.l_k_buf[slot, j].astype(F32))
            dk[j] = add(dk[j], ds * query)
            dv[j] = add(dv[j], mul(probs.astype(LOW), spread) * grad)
        pair += i + 1
        r.l_g[0, rows_of(i)] = (dq * HD ** (-0.5)).astype(LOW)
    for j in range(places):
        r.l_g[1, rows_of(j)] = (dk[j] * HD ** (-0.5)).astype(LOW)
        r.l_g[2, rows_of(j)] = dv[j].astype(LOW)


def local_project_back(r, step):
    places = r.l_in_buf.shape[1]
    frames = r.l_in.shape[1]
    dnormed = None
    for kind in range(3):
        grad = jnp.concatenate(
            [
                r.l_g[kind, pl.ds(pl.multiple_of(place * frames + step * PART, PART), PART)]
                for place in range(places)
            ],
            axis=0,
        )
        term = mul_t(grad, r.square[1 + kind])
        dnormed = term if dnormed is None else dnormed + term
    r.l_dnormed[...] = dnormed


def local_input_back(r, step, slot):
    places, width = r.l_in_buf.shape[1], r.l_in_buf.shape[3]
    rows = places * PART
    x = r.l_in_buf[slot].astype(F32).reshape(rows, width)
    dx, gain = scale_back(x, r.l_n1[...], r.l_dnormed[...])
    r.l_dn1[...] += jnp.sum(gain, axis=0, keepdims=True)
    dx = dx + r.l_dmid[...]
    here = pl.ds(pl.multiple_of(step * PART, PART), PART)
    total = r.cotan[here].astype(F32) + dx[:PART]
    r.dout[here] = jnp.where(r.valid[here] > 0, total, 0.0)
    for place in range(1, places):
        r.table_g[place - 1, here] = dx[place * PART : (place + 1) * PART].astype(LOW)


def attend_back_block(r, group, below, here, block):
    query = two_heads(r.held[block, 0:64] * LOW(HD ** (-0.5)))
    grad = two_heads(r.grads[block])
    log_total = r.log_total[block][0:1]
    near_v = r.held[4 * group : 4 * group + 4, 128:192].reshape(256, LANES)
    near_k = r.held[4 * group : 4 * group + 4, 64:128].reshape(256, LANES)
    near = masked_scores(mul_t(near_k, query), r.bias[below:here], below, block)
    near = jnp.exp(near - log_total)
    near_dp = mul_t(near_v, grad)
    delta = jnp.sum(near * near_dp, axis=0, keepdims=True)
    if group:
        far_v = r.held[0 : 4 * group, 128:192].reshape(below, LANES)
        far_k = r.held[0 : 4 * group, 64:128].reshape(below, LANES)
        far = jnp.exp(mul_t(far_k, query) + r.bias[0:below] - log_total)
        far_dp = mul_t(far_v, grad)
        delta = delta + jnp.sum(far * far_dp, axis=0, keepdims=True)
        far_ds = (far * (far_dp - delta)).astype(LOW)
        r.dk_acc[0:below] += mul(far_ds, query)
        r.dv_acc[0:below] += mul(far.astype(LOW), grad)
    near_ds = (near * (near_dp - delta)).astype(LOW)
    r.dk_acc[below:here] += mul(near_ds, query)
    r.dv_acc[below:here] += mul(near.astype(LOW), grad)
    dq = mul(r.k_t[:, below:here], near_ds)
    if group:
        dq = dq + mul(r.k_t[:, 0:below], far_ds)
    r.pieces[block, 0] = (join_heads(dq) * HD ** (-0.5)).astype(LOW)


def finish_on_slice(far, near):
    vmem = pl.BlockSpec(memory_space=pltpu.VMEM)
    hbm = pl.BlockSpec(memory_space=pl.ANY)
    rows, width = near["x"].shape
    wide = near["u"].shape[1]
    utts = rows // HD
    shapes = [
        (width // 16, wide), (wide // 16, width), (width // 16, width), (width // 16, width),
        (width // 16, width), (width // 16, width), (3 * 1024 // 16, width), (wide // 16, width),
        (width // 16, wide), (width // 16, width), (width // 16, width), (width // 16, width),
        (width // 16, width), (SROWS, SCOLS),
    ]
    out_names = ["dx", "y", "l_down"] + ["out_%d" % index for index in range(len(shapes))]
    rows_l = far["l_normed"].shape[0]
    places, pairs = far["l_in"].shape[0], far["l_probs"].shape[0]
    buffers = dict(
        part=((SLOTS, 2, 8, 64, SCOLS), LOW),
        recv_c=((SLOTS, 8, 64, SCOLS), LOW),
        half_a=((SLOTS, 2, 4, 32, ACOLS), LOW),
        half_b=((SLOTS, 2, 2, 4, 16, SCOLS), LOW),
        recv_xa=((SLOTS, 4, 32, ACOLS), LOW),
        recv_yb=((SLOTS, 2, 4, 16, SCOLS), LOW),
        sum_a=((DEEP, 4, 32, ACOLS), LOW),
        sum_b=((SLOTS, 2, 4, 16, SCOLS), LOW),
        recv_xb=((SLOTS, 4, 16, SCOLS), LOW),
        line_b=((DEEP, 4, 16, SCOLS), LOW),
        right_a=((SLOTS, 3, 32, ACOLS), LOW),
        left_a=((SLOTS, 3, 32, ACOLS), LOW),
        right_b=((SLOTS, 3, 16, SCOLS), LOW),
        left_b=((SLOTS, 3, 16, SCOLS), LOW),
        recv_ya=((SLOTS, 32, ACOLS), LOW),
        recv_yb2=((SLOTS, 16, SCOLS), LOW),
        line_c=((DEEP, 4, 2, 32, LANES), LOW),
        right_c=((SLOTS, 3, 2, 32, LANES), LOW),
        left_c=((SLOTS, 3, 2, 32, LANES), LOW),
        recv_xc=((SLOTS, 32, LANES), LOW),
        sum_c=((SLOTS, 32, LANES), LOW),
        recv_yc=((SLOTS, 32, LANES), LOW),
        staged=((SLOTS, 64, SCOLS), F32),
        up_buf=((2, width, SCOLS), LOW),
        down_buf=((2, SCOLS, width), LOW),
        square=((4, width, width), LOW),
        held=(far["saved"].shape, LOW),
        l_x=((2, rows_l, width), LOW),
        l_g=((4, rows_l, width), LOW),
        l_x_t=((width, rows_l), LOW),
        l_in_buf=((2, places, PART, width), LOW),
        l_mid_buf=((2, places, PART, width), F32),
        l_acc=((rows_l, width), F32),
        l_dhn=((rows_l, width), F32),
        l_kept=((2, 2, wide // 16, width), LOW),
        l_db1=((1, wide), F32),
        l_db2=((1, width), F32),
        l_dout_buf=((2, places, PART, width), LOW),
        l_q_buf=((2, places, PART, width), LOW),
        l_k_buf=((2, places, PART, width), LOW),
        l_v_buf=((2, places, PART, width), LOW),
        l_probs_buf=((2, pairs, PART, LANES), F32),
        l_dmid=((places * PART, width), F32),
        l_dnormed=((places * PART, width), F32),
        l_dmix=((places, PART, width), LOW),
        l_dn1=((1, width), F32),
        l_dn2=((1, width), F32),
        dout=((rows, width), F32),
        table_g=((places - 1, rows, width), LOW),
        act_buf=((rows, wide), LOW),
        act_t=((wide, rows), LOW),
        g_x=((2, rows, width), LOW),
        g_x_t=((2, width, rows), LOW),
        g_hn_t=((width, rows), LOW),
        g_g=((4, rows, width), LOW),
        dout_low=((rows, width), LOW),
        du=((rows, wide), LOW),
        db1=((8, SCOLS), F32),
        dn1=((1, width), F32),
        dn2=((1, width), F32),
        dhn=((rows, width), F32),
        dmid=((rows, width), F32),
        dmix=((utts, HD, width), LOW),
        grads=((16, HD, LANES), LOW),
        landed=((3, utts, HD, width), LOW),
        pieces=((16, 3, HD, LANES), LOW),
        dk_acc=((16 * HD, LANES), F32),
        dv_acc=((16 * HD, LANES), F32),
        bias=((16 * HD, LANES), F32),
        k_t=((LANES, 16 * HD), LOW),
    )
    semaphores = dict(
        load_sem=(SLOTS, 2), out_sem=(SLOTS,), send_sem=(26, SLOTS), recv_sem=(26, SLOTS),
        weight_sem=(2, 2), fetch_sem=(17,), local_sem=(2, 7), kept_sem=(2,), result_sem=(1,), send_one=(16,), recv_one=(16,), send_two=(16,),
        recv_two=(16,),
    )
    names = list(far) + list(near) + out_names + list(buffers) + list(semaphores)
    return pl.pallas_call(
        functools.partial(tail_kernel, names, len(shapes)),
        in_specs=[hbm] * len(far) + [vmem] * len(near),
        out_specs=[vmem] + [hbm] * (2 + len(shapes)),
        out_shape=[
            jax.ShapeDtypeStruct((rows, width), F32),
            jax.ShapeDtypeStruct((rows_l, width), LOW),
            jax.ShapeDtypeStruct((8, 2, wide // 16, width), LOW),
        ]
        + [jax.ShapeDtypeStruct(shape, F32) for shape in shapes],
        scratch_shapes=[pltpu.VMEM(*item) for item in buffers.values()]
        + [pltpu.SemaphoreType.DMA(item) for item in semaphores.values()],
        compiler_params=pltpu.CompilerParams(
            collective_id=1, has_side_effects=True, vmem_limit_bytes=63 << 20
        ),
    )(*far.values(), *near.values())


def normalize(values, gain_vec):
    return (
        values * lax.rsqrt(jnp.mean(values * values, axis=-1, keepdims=True) + EPSILON) * gain_vec
    )


def gelu_fn(values):
    return jax.nn.gelu(values, approximate=True)


def project_back(gradient, weight):
    return lax.dot_general(
        gradient, weight, (((1,), (1,)), ((), ())), preferred_element_type=jnp.float32
    )


def weight_grad(left_side, gradient):
    return lax.dot_general(
        left_side, gradient, (((0,), (0,)), ((), ())), preferred_element_type=jnp.float32
    )


def block_back(inputs, normed, mixed_rows, kept_parts, params, grad_out, attention_back):
    middle, middle_norm, pre_active, active = kept_parts
    grad_branch = grad_out.astype(jnp.bfloat16)
    grad_b_down = jnp.sum(grad_branch.astype(jnp.float32), axis=0)
    grad_w_down = weight_grad(active, grad_branch)
    grad_active = project_back(grad_branch, params[8])
    grad_pre = jax.vjp(gelu_fn, pre_active)[1](grad_active)[0].astype(jnp.bfloat16)
    grad_b_up = jnp.sum(grad_pre.astype(jnp.float32), axis=0)
    grad_w_up = weight_grad(middle_norm, grad_pre)
    middle_back = jax.vjp(normalize, middle, params[5])[1]
    grad_middle, grad_norm_two = middle_back(project_back(grad_pre, params[6]))
    grad_middle = grad_middle + grad_out
    grad_attn = grad_middle.astype(jnp.bfloat16)
    grad_w_output = weight_grad(mixed_rows, grad_attn)
    grad_mixed = project_back(grad_attn, params[4]).astype(jnp.bfloat16)
    grad_query, grad_key, grad_value = attention_back(grad_mixed)
    grad_normed = (
        project_back(grad_query, params[1])
        + project_back(grad_key, params[2])
        + project_back(grad_value, params[3])
    )
    input_back = jax.vjp(normalize, inputs, params[0])[1]
    grad_inputs, grad_norm_one = input_back(grad_normed)
    weight_grads = (
        grad_norm_one,
        weight_grad(normed, grad_query),
        weight_grad(normed, grad_key),
        weight_grad(normed, grad_value),
        grad_w_output,
        grad_norm_two,
        grad_w_up,
        grad_b_up,
        grad_w_down,
        grad_b_down,
    )
    return (grad_inputs + grad_middle, weight_grads)


def on_device(
    frames,
    codes,
    lengths,
    frame_mask,
    table,
    glob_norm_one,
    glob_w_query,
    glob_w_key,
    glob_w_value,
    glob_w_output,
    glob_norm_two,
    glob_w_up,
    glob_b_up,
    glob_w_down,
    glob_b_down,
    local_norm_one,
    local_w_query,
    local_w_key,
    local_w_value,
    local_w_output,
    local_norm_two,
    local_w_up,
    local_b_up,
    local_w_down,
    local_b_down,
    cotan_global,
    cotan_local,
):
    utter_count, frame_count, model_width = frames.shape
    row_count = utter_count * frame_count
    local_len = CB + 1
    positions = lax.axis_index("seq") * frame_count + jnp.arange(frame_count, dtype=jnp.int32)
    valid = positions[None, :] < lengths[:, None]
    usable = jnp.pad(frame_mask.astype(LOW), ((0, 0), (0, LANES - frame_count)))
    usable = jnp.broadcast_to(usable[:, None, :], (utter_count, 16, LANES))
    glob_params = (
        glob_norm_one,
        glob_w_query,
        glob_w_key,
        glob_w_value,
        glob_w_output,
        glob_norm_two,
        glob_w_up,
        glob_b_up,
        glob_w_down,
        glob_b_down,
    )
    local_params = (
        local_norm_one,
        local_w_query,
        local_w_key,
        local_w_value,
        local_w_output,
        local_norm_two,
        local_w_up,
        local_b_up,
        local_w_down,
        local_b_down,
    )
    code_rows = codes.transpose(2, 0, 1).reshape(CB, row_count)
    (
        glob_normed, glob_mixed, saved, log_total, local_in,
        glob_middle, glob_middle_norm, pre_active, active, global_rows,
    ) = global_forward(
        frames,
        usable,
        codes.reshape(row_count, CB),
        valid.reshape(row_count, 1).astype(F32),
        table,
        glob_params,
    )
    local_shape = (local_len, row_count, model_width)
    flat_shape = (local_len * row_count, model_width)
    normed, local_q, local_k, local_v, local_probs, mixed, middle, middle_norm = local_front(
        local_in, local_params
    )
    row_valid = valid.reshape(1, row_count, 1)
    local_cotan = cotan_local.transpose(2, 0, 1, 3).reshape(local_shape)
    local_cotan = lax.optimization_barrier(jnp.where(row_valid, local_cotan, 0))

    def by_frame(result):
        result = jnp.where(row_valid, result.reshape(local_shape), 0)
        result = result.reshape(local_len, utter_count, frame_count, model_width)
        return result.transpose(1, 2, 0, 3)

    normed = normed.reshape(flat_shape)
    mixed = mixed.reshape(flat_shape)
    if lax.axis_size("seq") == 16 and lax.axis_size("utt") == 2:
        far = dict(
            l_w_up=local_w_up,
            l_w_down=local_w_down,
            l_hn=middle_norm.reshape(flat_shape),
            l_dout_flat=local_cotan.reshape(flat_shape),
            l_mid_flat=middle.reshape(flat_shape),
            g_w_up=glob_w_up,
            g_w_down=glob_w_down,
            g_w_o=glob_w_output,
            g_w_q=glob_w_query,
            g_w_k=glob_w_key,
            g_w_v=glob_w_value,
            saved=saved,
            l_normed=normed,
            l_mixed=mixed,
            l_in=local_in,
            l_mid=middle,
            l_dout=local_cotan,
            l_q=local_q,
            l_k=local_k,
            l_v=local_v,
            l_probs=local_probs,
            l_w_o=local_w_output,
            l_w_q=local_w_query,
            l_w_k=local_w_key,
            l_w_v=local_w_value,
            g_act=active,
            g_mixed=glob_mixed,
            g_normed=glob_normed,
        )
        near = dict(
            u=pre_active,
            cotan=cotan_global.reshape(row_count, model_width),
            valid=valid.reshape(row_count, 1).astype(F32),
            mid=glob_middle,
            hn=glob_middle_norm,
            x=frames.reshape(row_count, model_width),
            n1=glob_norm_one.reshape(1, -1),
            n2=glob_norm_two.reshape(1, -1),
            log_total=log_total,
            codes=jnp.broadcast_to(code_rows[:, None, :], (CB, 8, row_count)),
            l_n1=local_norm_one.reshape(1, -1),
            l_n2=local_norm_two.reshape(1, -1),
            l_b1=local_b_up.reshape(1, -1),
            l_b2=local_b_down.reshape(1, -1),
        )
        grad_inputs, local_result, _, *sums = finish_on_slice(far, near)
        grad_inputs, *sums = settle([grad_inputs] + sums)
        wide = dict(zip("12qkvot76pabc", sums[:-1]))
        half = lax.axis_index("seq") % 2
        rest = sums[-1]

        def piece(row):
            return jnp.where(half == 0, rest[row, ACOLS : ACOLS + LANES // 2], rest[row, ACOLS + LANES // 2 :])

        def piece_wide(row):
            return rest[row : row + 2, ACOLS:].reshape(-1)

        return (
            global_rows.reshape(utter_count, frame_count, model_width),
            by_frame(local_result),
            grad_inputs.reshape(utter_count, frame_count, model_width),
            wide["t"],
            piece(0),
            wide["a"],
            wide["b"],
            wide["c"],
            wide["p"],
            piece(1),
            wide["6"],
            piece_wide(3),
            wide["7"],
            piece(2),
            piece(5),
            wide["q"],
            wide["k"],
            wide["v"],
            wide["o"],
            piece(6),
            wide["1"],
            piece_wide(8),
            wide["2"],
            piece(7),
        )

    local_result, grad_hidden, grad_w_up, grad_w_down, grad_b_up, grad_b_down = local_ffn(
        middle_norm.reshape(flat_shape),
        local_cotan.reshape(flat_shape),
        middle.reshape(flat_shape),
        local_params,
    )
    grad_attn, grad_q, grad_k, grad_v, grad_first, grad_rest, grad_n1, grad_n2 = local_back(
        local_in,
        middle,
        grad_hidden.reshape(local_shape),
        local_cotan,
        local_q,
        local_k,
        local_v,
        local_probs,
        local_params,
    )
    grad_first = grad_first.reshape(utter_count, frame_count, model_width)
    glob_cotan = jnp.where(
        valid[:, :, None], cotan_global.astype(jnp.float32) + grad_first, 0.0
    )
    glob_cotan = glob_cotan.reshape(row_count, model_width)
    local_grads = (
        grad_n1[0],
        weight_grad(normed, grad_q.reshape(flat_shape)),
        weight_grad(normed, grad_k.reshape(flat_shape)),
        weight_grad(normed, grad_v.reshape(flat_shape)),
        weight_grad(mixed, grad_attn.reshape(flat_shape)),
        grad_n2[0],
        grad_w_up,
        grad_b_up[0],
        grad_w_down,
        grad_b_down[0],
    )
    picked = code_rows[:, None, :] == jnp.arange(VOCAB, dtype=jnp.int32)[None, :, None]
    grad_tab = jnp.einsum(
        "cvn,cnd->cvd", picked.astype(LOW), grad_rest, preferred_element_type=F32
    ).reshape(CB * VOCAB, model_width)

    def global_back(grad_mixed):
        grads = global_attend_back(
            grad_mixed.reshape(utter_count, frame_count, model_width), saved, log_total
        )
        return tuple(grads.reshape(3, row_count, model_width))

    global_in = frames.astype(F32).reshape(row_count, model_width)
    glob_kept = (glob_middle, glob_middle_norm, pre_active, active)
    grad_inputs, glob_grads = block_back(
        global_in, glob_normed, glob_mixed, glob_kept, glob_params, glob_cotan, global_back
    )
    reduced = reduce_all((grad_tab,) + glob_grads + local_grads)
    return (
        global_rows.reshape(utter_count, frame_count, model_width),
        by_frame(local_result),
        grad_inputs.reshape(utter_count, frame_count, model_width),
    ) + reduced


def solution(mesh):
    return jax.shard_map(
        on_device,
        mesh=mesh,
        in_specs=(
            P("utt", "seq", None),
            P("utt", "seq", None),
            P("utt"),
            P("utt", "seq"),
            P(),
            P(),
            P(),
            P(),
            P(),
            P(),
            P(),
            P(),
            P(),
            P(),
            P(),
            P(),
            P(),
            P(),
            P(),
            P(),
            P(),
            P(),
            P(),
            P(),
            P(),
            P("utt", "seq", None),
            P("utt", "seq", None, None),
        ),
        out_specs=(
            P("utt", "seq", None),
            P("utt", "seq", None, None),
            P("utt", "seq", None),
            P("seq", None),
            P("seq"),
            P("seq", None),
            P("seq", None),
            P("seq", None),
            P("seq", None),
            P("seq"),
            P("seq", None),
            P("seq"),
            P("seq", None),
            P("seq"),
            P("seq"),
            P("seq", None),
            P("seq", None),
            P("seq", None),
            P("seq", None),
            P("seq"),
            P("seq", None),
            P("seq"),
            P("seq", None),
            P("seq"),
        ),
        check_vma=False,
    )
```
